32 devices in a mesh: dp: 8 (over y, x, core), tensor: 4 (over z).
Axes of the slice: x: 2, y: 2, z: 4, core: 2. Of those that a mesh axis runs over, the one named last changes fastest.
Arguments:
- tokens_in: bfloat16 [12288, 768], P('dp'), may hold values from -6 to 6
- segment_ids: int32 [8, 1536], P('dp'), may hold values from 0 to 11, never falling along the last dimension, each value on 1 to 216 neighbouring positions
- first_gain: float32 [768], replicated, may hold values from 0.25 to 1.75
- first_shift: float32 [768], replicated, may hold values from -3 to 3
- qkv_weight: bfloat16 [3, 768, 768], P(None, None, 'tensor'), may hold values from -0.21875 to 0.21875
- query_value_bias: float32 [2, 768], P(None, 'tensor'), may hold values from -1.2 to 1.2
- out_weight: bfloat16 [768, 768], P('tensor'), may hold values from -0.875 to 0.875
- out_bias: float32 [768], replicated, may hold values from -3 to 3
- second_gain: float32 [768], replicated, may hold values from 0.25 to 1.75
- second_shift: float32 [768], replicated, may hold values from -3 to 3
- up_weight: bfloat16 [768, 3072], P(None, 'tensor'), may hold values from -0.21875 to 0.21875
- up_bias: float32 [3072], P('tensor'), may hold values from -3 to 3
- down_weight: bfloat16 [3072, 768], P('tensor'), may hold values from -0.109375 to 0.109375
- down_bias: float32 [768], replicated, may hold values from -3 to 3
- cotangent: bfloat16 [12288, 768], P('dp'), may hold values from -6 to 6
Outputs:
- result: bfloat16 [12288, 768], P('dp')
- input_grad: bfloat16 [12288, 768], P('dp')
- first_gain_grad: float32 [768], replicated
- first_shift_grad: float32 [768], replicated
- qkv_weight_grad: float32 [3, 768, 768], P(None, None, 'tensor')
- query_value_bias_grad: float32 [2, 768], P(None, 'tensor')
- out_weight_grad: float32 [768, 768], P('tensor')
- out_bias_grad: float32 [768], replicated
- second_gain_grad: float32 [768], replicated
- second_shift_grad: float32 [768], replicated
- up_weight_grad: float32 [768, 3072], P(None, 'tensor')
- up_bias_grad: float32 [3072], P('tensor')
- down_weight_grad: float32 [3072, 768], P('tensor')
- down_bias_grad: float32 [768], replicated
The draws below stay inside these ranges and needn't reach their ends.
Inputs may be any that keep to these rules, and one draw needn't show every extreme that they name: `segment_ids`: in each sequence the ids never fall; each crop holds 1 to 216 tokens, one exactly 216.
All inputs are finite; a program needn't handle non-finite values.
Results may differ from the reference program's by a relative error of at most 0.018.
Values may be sent and summed in bfloat16 or wider, within the bound.
A program may use at most 192 MiB of HBM per device.

```python
import math
import jax
import jax.numpy as jnp
import numpy as np
from jax import lax

D = 768
HEADS = 12
FF = 3072
HEAD_DIM = 64
SEQ_LEN = 1536
CROP = 216
SEGS = 12
SEQS = 8
TOKENS = 12288
N_DP = 8
N_TENSOR = 4


def steps_of(key, shape, split, least, largest):
    factor_of = 1.0
    for dim, blocks in split:
        steps = jax.random.uniform(jax.random.fold_in(jax.random.fold_in(key, 6), dim), (blocks,), jnp.float32, least / len(split), largest / len(split))
        factor_of = factor_of * jnp.repeat(jnp.exp(steps), shape[dim] // blocks).reshape((-1,) + (1,) * (len(shape) - 1 - dim))
    return factor_of


def split_up(number_of, total, bound, lean):
    loads = [(1 << 20) // math.isqrt(rank ** lean) + 1 for rank in range(2, number_of + 1)]
    surplus, holding = total - bound - (number_of - 1), [1] * (number_of - 1)
    while surplus > 0:
        free = [i for i in range(number_of - 1) if holding[i] < bound]
        mass, remaining = sum([loads[i] for i in free]), surplus
        for i in free:
            extra = min(bound - holding[i], max(1, remaining * loads[i] // mass), surplus)
            holding[i] = holding[i] + extra
            surplus = surplus - extra
    return np.array([bound] + holding)


def ragged(rng, amount, total, most, slope):
    if amount == 2:
        one = jax.random.randint(rng, (), max(1, total - most), min(most, total - 1) + 1)
        return jnp.stack([one, total - one])
    lengths = jnp.asarray(split_up(amount, total, most, slope), jnp.int32)
    twos = (amount - 1) // 2
    donor, taker = lengths[1:1 + 2 * twos:2], lengths[2:2 + 2 * twos:2]
    margin = jnp.minimum(donor - 1, most - taker)
    moved = jax.random.randint(jax.random.fold_in(rng, 1), (twos,), 0, 1 << 20) % (margin + 1)
    lengths = lengths.at[1:1 + 2 * twos:2].set(donor - moved).at[2:2 + 2 * twos:2].set(taker + moved)
    return lengths[jax.random.permutation(jax.random.fold_in(rng, 2), amount)]


def normal_values(key, dims, deviation, reach, pieces=(), held_as=jnp.bfloat16):
    gain = steps_of(key, dims, pieces, -0.22, 0.18) if pieces else 1.0
    values = jax.random.normal(key, dims, jnp.float32) * deviation * gain
    return jnp.minimum(jnp.maximum(values, -reach), reach).astype(held_as)


def setup_inputs(seed: int = 0) -> dict:
    splits = jax.random.split(jax.random.key(seed), 16)
    return {
        "tokens_in": normal_values(splits[0], (TOKENS, D), 1.0, 6.0, ((0, 8),)),
        "segment_ids": jax.vmap(lambda own: jnp.searchsorted(jnp.cumsum(ragged(own, SEGS, SEQ_LEN, CROP, 0)), jnp.arange(SEQ_LEN), side="right"))(jax.random.split(splits[1], SEQS)).reshape((SEQS, SEQ_LEN)).astype(jnp.int32),
        "first_gain": jnp.clip(1.0 + 0.15 * jax.random.normal(splits[2], (D,), jnp.float32), 0.25, 1.75),
        "first_shift": normal_values(splits[3], (D,), 0.5, 3.0, (), jnp.float32),
        "qkv_weight": normal_values(splits[4], (3, D, D), D ** -0.5, 0.21875, ((2, 4),)),
        "query_value_bias": normal_values(splits[5], (2, D), 0.2, 1.2, ((1, 4),), jnp.float32),
        "out_weight": normal_values(splits[6], (D, D), (D // 16) ** -0.5, 0.875, ((0, 4),)),
        "out_bias": normal_values(splits[7], (D,), 0.5, 3.0, (), jnp.float32),
        "second_gain": jnp.clip(1.0 + 0.15 * jax.random.normal(splits[8], (D,), jnp.float32), 0.25, 1.75),
        "second_shift": normal_values(splits[9], (D,), 0.5, 3.0, (), jnp.float32),
        "up_weight": normal_values(splits[10], (D, FF), D ** -0.5, 0.21875, ((1, 4),)),
        "up_bias": normal_values(splits[11], (FF,), 0.5, 3.0, ((0, 4),), jnp.float32),
        "down_weight": normal_values(splits[12], (FF, D), FF ** -0.5, 0.109375, ((0, 4),)),
        "down_bias": normal_values(splits[13], (D,), 0.5, 3.0, (), jnp.float32),
        "cotangent": normal_values(splits[14], (TOKENS, D), 1.0, 6.0, ((0, 8),)),
    }


@jax.custom_vjp
def low(v):
    return lax.optimization_barrier(v.astype(jnp.bfloat16)).astype(jnp.float32)

@jax.custom_vjp
def low_back(v):
    return v

def low_keep(v):
    return (low(v), None)

def low_pass(kept, grad):
    return (grad,)

def back_keep(v):
    return (v, None)

def back_low(kept, grad):
    return (low(grad),)
low.defvjp(low_keep, low_pass)
low_back.defvjp(back_keep, back_low)
highest = lax.Precision.HIGHEST
norm_eps = 1e-06

def layer_norm(inputs, scaling, offset):
    center = inputs - lax.optimization_barrier(jnp.mean(inputs, axis=-1, keepdims=True))
    spread = lax.optimization_barrier(jnp.mean(center * center, axis=-1, keepdims=True))
    return center * lax.rsqrt(spread + norm_eps) * scaling + offset

def attend(query_rows, segment_rows, key_all, value_all, segment_all):
    scores = jnp.einsum('qhd,khd->hqk', query_rows, key_all, precision=highest) * HEAD_DIM ** (-0.5)
    scores = low_back(scores)
    allowed = segment_rows[:, None] == segment_all[None, :]
    scores = jnp.where(allowed[None], scores, -1000000000.0)
    probs_full = jax.nn.softmax(scores, axis=-1)
    probs_low = low(probs_full)
    return jnp.einsum('hqk,khd->qhd', probs_low, value_all, precision=highest)

def forward(params, tokens, segments):
    first_gain, first_shift, qkv_weight, query_value_bias, out_weight, out_bias, second_gain, second_shift, up_weight, up_bias, down_weight, down_bias = params
    length = tokens.shape[0]
    groups = N_TENSOR
    normed = low(layer_norm(tokens, first_gain, first_shift))
    copies = low_back(jnp.broadcast_to(normed, (groups, length, D)))
    split_weight = qkv_weight.reshape(3, D, groups, D // groups)
    projected = jnp.einsum('gtd,sdgc->stgc', copies, split_weight, precision=highest).reshape(3, length, D)
    query_all = low(low_back(projected[0] + query_value_bias[0])).reshape(length, HEADS, HEAD_DIM)
    key_all = low(low_back(projected[1])).reshape(length, HEADS, HEAD_DIM)
    value_all = low(low_back(projected[2] + query_value_bias[1])).reshape(length, HEADS, HEAD_DIM)
    block_rows = min(512, length)
    count_blocks = length // block_rows
    attend_saved = jax.checkpoint(attend)

    def one_block(operands):
        return attend_saved(operands[0], operands[1], key_all, value_all, segments)
    mixed_rows = lax.map(one_block, (query_all.reshape(count_blocks, block_rows, HEADS, HEAD_DIM), segments.reshape(count_blocks, block_rows)))
    heads_out = low(low_back(mixed_rows.reshape(length, D)))
    parts = jnp.einsum('tgc,gcd->gtd', heads_out.reshape(length, groups, D // groups), out_weight.reshape(groups, D // groups, D), precision=highest)
    branch = low_back(lax.optimization_barrier(jnp.sum(low(parts), axis=0)))
    hidden = tokens + branch + out_bias
    normed_two = low(layer_norm(hidden, second_gain, second_shift))
    copies_two = low_back(jnp.broadcast_to(normed_two, (groups, length, D)))
    pre_act = jnp.einsum('gtd,dgc->tgc', copies_two, up_weight.reshape(D, groups, FF // groups), precision=highest).reshape(length, FF)
    pre_act = low_back(pre_act + up_bias)
    activated = low(jax.nn.gelu(pre_act, approximate=False))
    parts_two = jnp.einsum('tgc,gcd->gtd', activated.reshape(length, groups, FF // groups), down_weight.reshape(groups, FF // groups, D), precision=highest)
    mlp_out = low_back(lax.optimization_barrier(jnp.sum(low(parts_two), axis=0)))
    return hidden + mlp_out + down_bias

def reference(tokens_in, segment_ids, first_gain, first_shift, qkv_weight, query_value_bias, out_weight, out_bias, second_gain, second_shift, up_weight, up_bias, down_weight, down_bias, cotangent):
    params = jax.tree.map(lambda tensor: tensor.astype(jnp.float32), (first_gain, first_shift, qkv_weight, query_value_bias, out_weight, out_bias, second_gain, second_shift, up_weight, up_bias, down_weight, down_bias))
    tokens_seq = tokens_in.astype(jnp.float32).reshape(SEQS, SEQ_LEN, D)
    cotangent_seq = cotangent.astype(jnp.float32).reshape(SEQS, SEQ_LEN, D)
    starting = jax.tree.map(jnp.zeros_like, params)

    def one_sequence(totals, operands):
        tokens, segments, grad_out = operands

        def apply_layer(weights, inputs):
            return forward(weights, inputs, segments)
        output_rows, pullback = jax.vjp(apply_layer, params, tokens)
        grad_params, grad_tokens = pullback(grad_out)
        totals = jax.tree.map(jnp.add, totals, grad_params)
        return (totals, (output_rows, grad_tokens))
    totals, (outputs, input_grads) = lax.scan(one_sequence, starting, (tokens_seq, segment_ids, cotangent_seq))
    grads = jax.tree.map(lambda tensor: tensor / N_DP, totals)
    return (outputs.reshape(TOKENS, D).astype(jnp.bfloat16), input_grads.reshape(TOKENS, D).astype(jnp.bfloat16), grads[0], grads[1], grads[2], grads[3], grads[4], grads[5], grads[6], grads[7], grads[8], grads[9], grads[10], grads[11])
```

```python
import functools

import jax
import jax.numpy as jnp
from jax import lax
from jax.experimental import pallas as pl
from jax.experimental.pallas import tpu as pltpu
from jax.sharding import PartitionSpec as P

HEAD_DIM = 64
HALO = 256
BLOCK = 128
EPS = 1e-06
F32 = jnp.float32
BF16 = jnp.bfloat16
MESH = pl.DeviceIdType.MESH
VMEM_LIMIT = 60 << 20


def place():
    d, t = lax.axis_index("dp"), lax.axis_index("tensor")
    return d, t, lax.rem(d, 2), lax.rem(d // 2, 2), lax.rem(d // 4, 2)


def flip(d, value):
    return d + value * (1 - 2 * lax.rem(d // value, 2))


def remote(src, dst, send, recv, **axis):
    return pltpu.make_async_remote_copy(
        src_ref=src, dst_ref=dst, send_sem=send, recv_sem=recv,
        device_id=axis, device_id_type=MESH)


def greet(nt, bits, far=False):
    d, t = lax.axis_index("dp"), lax.axis_index("tensor")
    barrier = pltpu.get_barrier_semaphore()

    @pl.when(t > 0)
    def _():
        pl.semaphore_signal(barrier, inc=1, device_id={"tensor": t - 1}, device_id_type=MESH)

    @pl.when(t < nt - 1)
    def _():
        pl.semaphore_signal(barrier, inc=1, device_id={"tensor": t + 1}, device_id_type=MESH)

    for bit in bits:
        pl.semaphore_signal(barrier, inc=1, device_id={"dp": flip(d, bit)}, device_id_type=MESH)
    if far:
        pl.semaphore_signal(barrier, inc=1, device_id={"tensor": flip(t, 2)}, device_id_type=MESH)
    peers = len(bits) + int(far) + (t > 0).astype(jnp.int32) + (t < nt - 1).astype(jnp.int32)
    pl.semaphore_wait(barrier, peers)


def ordered(tasks):
    for _, _, task in sorted(tasks, key=lambda item: item[:2]):
        task()


def relay_tasks(nt, chunks, own, full, sems, start, hop, place_of, arrived):
    send, recv = sems
    tasks = []
    t = lax.axis_index("tensor")
    for k in range(chunks):
        for j in range(nt):
            def step(k=k, j=j):
                for way in (0, 1):
                    sign = 1 - 2 * way
                    shard = t - sign * j
                    inside = (shard >= 0) & (shard < nt)
                    if j > 0:
                        @pl.when(inside)
                        def _():
                            remote(full(shard, k), full(shard, k), send.at[k, j - 1, way], recv.at[k, j - 1, way],
                                   tensor=t).wait_recv()
                            arrived(k, j, way, shard)
                    if j < nt - 1:
                        goal = t + sign
                        @pl.when(inside & (goal >= 0) & (goal < nt))
                        def _():
                            source = own(k) if j == 0 else full(shard, k)
                            remote(source, full(shard, k), send.at[k, j, way], recv.at[k, j, way],
                                   tensor=goal).start()
            tasks.append((start(k, j), len(tasks), step))

    def finish():
        for k in range(chunks):
            for j in range(nt - 1):
                for way in (0, 1):
                    sign = 1 - 2 * way
                    shard, goal = t - sign * j, t + sign
                    @pl.when((shard >= 0) & (shard < nt) & (goal >= 0) & (goal < nt))
                    def _():
                        source = own(k) if j == 0 else full(shard, k)
                        remote(source, full(shard, k), send.at[k, j, way], recv.at[k, j, way],
                               tensor=goal).wait_send()
    return tasks, finish


def gather_kernel(nt, chunks, pack, w, zs, zr, ps, pr, cs, cr, ls):
    d, t, b0, b1, b2 = place()
    local = pltpu.make_async_copy(pack, w.at[t], ls)
    local.start()
    greet(nt, (1, 2, 4))
    tasks = []

    def one(shard, k, q, way, j):
        if q == 0:
            return remote(w.at[shard, k, b0, b2, b1, 0], w.at[shard, k, b0, b2, b1, 0],
                       ps.at[k, j, way, 0], pr.at[k, j, way, 0], dp=flip(d, 2))
        return remote(w.at[shard, k, b0, b2, b1, 1], w.at[shard, k, b0, b2, b1, 1],
                   ps.at[k, j, way, 1], pr.at[k, j, way, 1], dp=flip(d, 4))

    def two(shard, k, q, way, j):
        if q == 0:
            return remote(w.at[shard, k, b0, b2, :, 0], w.at[shard, k, b0, b2, :, 0],
                       ps.at[k, j, way, 2], pr.at[k, j, way, 2], dp=flip(d, 4))
        return remote(w.at[shard, k, b0, :, b1, 1], w.at[shard, k, b0, :, b1, 1],
                   ps.at[k, j, way, 3], pr.at[k, j, way, 3], dp=flip(d, 2))

    def core(shard, k, way, j):
        return remote(w.at[shard, k, b0], w.at[shard, k, b0], cs.at[k, j, way], cr.at[k, j, way], dp=flip(d, 1))

    def arrived(k, j, way, shard):
        one(shard, k, 0, way, j - 1).start()
        one(shard, k, 1, way, j - 1).start()

    def each(k, j, body):
        for way in (0, 1):
            shard = t - (1 - 2 * way) * (j + 1)
            @pl.when((shard >= 0) & (shard < nt))
            def _():
                body(shard, k, way, j)

    z_tasks, z_finish = relay_tasks(
        nt, chunks, lambda k: pack.at[k, b0, b2, b1], lambda s, k: w.at[s, k, b0, b2, b1], (zs, zr),
        lambda k, j: 16.0 * k + 4.0 * j, None, None, arrived)
    tasks += z_tasks
    for k in range(chunks):
        for j in range(nt - 1):
            def second(k=k, j=j):
                def body(shard, k, way, j):
                    for q in (0, 1):
                        one(shard, k, q, way, j).wait_recv()
                    for q in (0, 1):
                        two(shard, k, q, way, j).start()
                each(k, j, body)

            def third(k=k, j=j):
                def body(shard, k, way, j):
                    for q in (0, 1):
                        two(shard, k, q, way, j).wait_recv()
                    core(shard, k, way, j).start()
                each(k, j, body)
            tasks.append((16.0 * k + 4.0 * j + 9.0, len(tasks), second))
            tasks.append((16.0 * k + 4.0 * j + 16.5, len(tasks), third))
    ordered(tasks)
    local.wait()
    z_finish()
    for k in range(chunks):
        for j in range(nt - 1):
            def last(shard, k, way, j):
                core(shard, k, way, j).wait()
                for q in (0, 1):
                    one(shard, k, q, way, j).wait_send()
                    two(shard, k, q, way, j).wait_send()
            each(k, j, last)


def gather_weights(pack, nt):
    chunks, rows = pack.shape[0], pack.shape[-2]
    width = pack.shape[-1]
    dma = pltpu.SemaphoreType.DMA
    return pl.pallas_call(
        functools.partial(gather_kernel, nt, chunks),
        name="gather_weights",
        out_shape=jax.ShapeDtypeStruct((nt,) + pack.shape, pack.dtype),
        in_specs=[pl.BlockSpec(memory_space=pl.ANY)],
        out_specs=pl.BlockSpec(memory_space=pltpu.VMEM),
        scratch_shapes=[
            dma((chunks, nt - 1, 2)), dma((chunks, nt - 1, 2)),
            dma((chunks, nt - 1, 2, 4)), dma((chunks, nt - 1, 2, 4)),
            dma((chunks, nt - 1, 2)), dma((chunks, nt - 1, 2)), dma(()),
        ],
        compiler_params=pltpu.CompilerParams(collective_id=1, has_side_effects=True, vmem_limit_bytes=VMEM_LIMIT),
    )(pack)


def add_bf16(ref, other):
    ref[...] = (ref[...].astype(F32) + other[...].astype(F32)).astype(BF16)


def reduce_kernel(nt, chunks, extra, outs, grads, small, own_rows, total, small_out, gathered,
                  s1, rc, ra, rb, rz, rx, sv, sr,
                  ls, cs, cr, ps, pr, zs, zr, xs, xr, fs, fr, os_, or_, ss, sm, lo):
    d, t, b0, b1, b2 = place()
    bits = (1, 2, 4) + tuple(extra)
    order = tuple(range(chunks))[::-1]
    units = [(k, s) for k in order for s in range(nt)]

    def own_copy(k, s):
        return pltpu.make_async_copy(grads.at[s, k, b0], s1.at[s, k], ls.at[s, k])

    for k, s in units:
        own_copy(k, s).start()
    own_small = pltpu.make_async_copy(small, sv, lo.at[0])
    own_small.start()
    keep = [pltpu.make_async_copy(own_rows.at[o], gathered.at[o, t], lo.at[1 + o]) for o in range(outs)]
    for copy in keep:
        copy.start()
    greet(nt, bits, nt > 2)

    def core(k, s):
        return remote(grads.at[s, k, 1 - b0], rc.at[s, k], cs.at[s, k], cr.at[s, k], dp=flip(d, 1))

    def one(k, s, q):
        if q == 0:
            return remote(s1.at[s, k, 1 - b2, :, 0], ra.at[s, k], ps.at[s, k, 0], pr.at[s, k, 0], dp=flip(d, 4))
        return remote(s1.at[s, k, :, 1 - b1, 1], rb.at[s, k], ps.at[s, k, 1], pr.at[s, k, 1], dp=flip(d, 2))

    def two(k, s, q):
        if q == 0:
            return remote(s1.at[s, k, b2, 1 - b1, 0], rz.at[s, k, 0], ps.at[s, k, 2], pr.at[s, k, 2], dp=flip(d, 2))
        return remote(s1.at[s, k, 1 - b2, b1, 1], rz.at[s, k, 1], ps.at[s, k, 3], pr.at[s, k, 3], dp=flip(d, 4))

    def up(k, s):
        return remote(s1.at[s, k, b2, b1], rx.at[s, k, 0], zs.at[s, k, 0], zr.at[s, k, 0], tensor=t + 1)

    def down(k, s):
        return remote(s1.at[s, k, b2, b1], rx.at[s, k, 1], zs.at[s, k, 1], zr.at[s, k, 1], tensor=t - 1)

    tasks = []

    def task(when, body):
        tasks.append((when, len(tasks), body))

    pace = 5.4
    for n, (k, s) in enumerate(units):
        def first(k=k, s=s):
            core(k, s).start()

        def second(k=k, s=s):
            own_copy(k, s).wait()
            core(k, s).wait_recv()
            add_bf16(s1.at[s, k], rc.at[s, k])
            one(k, s, 0).start()
            one(k, s, 1).start()

        def third(k=k, s=s):
            one(k, s, 0).wait_recv()
            one(k, s, 1).wait_recv()
            add_bf16(s1.at[s, k, b2, :, 0], ra.at[s, k])
            add_bf16(s1.at[s, k, :, b1, 1], rb.at[s, k])
            two(k, s, 0).start()
            two(k, s, 1).start()

        def fourth(k=k, s=s):
            two(k, s, 0).wait_recv()
            two(k, s, 1).wait_recv()
            add_bf16(s1.at[s, k, b2, b1, 0], rz.at[s, k, 0])
            add_bf16(s1.at[s, k, b2, b1, 1], rz.at[s, k, 1])
        task(n * pace - 12.0, first)
        task(n * pace, second)
        task(n * pace + 6.0, third)
        task(n * pace + 11.5, fourth)

    for c, k in enumerate(order):
        for hop in range(nt):
            def chain(k=k, hop=hop):
                @pl.when(t == hop)
                def _():
                    for s in reversed(range(nt)):
                        @pl.when(s >= t)
                        def _():
                            if hop > 0:
                                up(k, s).wait_recv()
                                add_bf16(s1.at[s, k, b2, b1], rx.at[s, k, 0])
                            if hop < nt - 1:
                                @pl.when(s > t)
                                def _():
                                    up(k, s).start()

                @pl.when(t == nt - 1 - hop)
                def _():
                    for s in range(nt):
                        @pl.when(s <= t)
                        def _():
                            if hop > 0:
                                down(k, s).wait_recv()
                                add_bf16(s1.at[s, k, b2, b1], rx.at[s, k, 1])
                            if hop < nt - 1:
                                @pl.when(s < t)
                                def _():
                                    down(k, s).start()
            task((c + 1) * nt * pace + 8.0 + 5.0 * hop, chain)

        def settle(k=k):
            pltpu.sync_copy(s1.at[t, k, b2, b1], total.at[k, b0, b2, b1])
        base = (c + 1) * nt * pace + 8.0 + 5.0 * nt
        if not extra:
            task(base, settle)
        else:
            for e, bit in enumerate(extra):
                def more(k=k, e=e, bit=bit):
                    swap = remote(s1.at[t, k, b2, b1], rx.at[e, k, 2], xs.at[e, k], xr.at[e, k], dp=flip(d, bit))
                    swap.start()
                    swap.wait()
                    add_bf16(s1.at[t, k, b2, b1], rx.at[e, k, 2])
                task(base + 0.01 * e, more)
            task(base + 0.5, settle)

        def gone(k, q):
            if q == 0:
                return remote(total.at[k, b0, b2, b1, 0], total.at[k, b0, b2, b1, 0], fs.at[k, 0], fr.at[k, 0], dp=flip(d, 2))
            return remote(total.at[k, b0, b2, b1, 1], total.at[k, b0, b2, b1, 1], fs.at[k, 1], fr.at[k, 1], dp=flip(d, 4))

        def gtwo(k, q):
            if q == 0:
                return remote(total.at[k, b0, b2, :, 0], total.at[k, b0, b2, :, 0], fs.at[k, 2], fr.at[k, 2], dp=flip(d, 4))
            return remote(total.at[k, b0, :, b1, 1], total.at[k, b0, :, b1, 1], fs.at[k, 3], fr.at[k, 3], dp=flip(d, 2))

        def gcore(k):
            return remote(total.at[k, b0], total.at[k, b0], fs.at[k, 4], fr.at[k, 4], dp=flip(d, 1))

        def spread_one(k=k):
            for q in (0, 1):
                gone(k, q).start()

        def spread_two(k=k):
            for q in (0, 1):
                gone(k, q).wait_recv()
            for q in (0, 1):
                gtwo(k, q).start()

        def spread_core(k=k):
            for q in (0, 1):
                gtwo(k, q).wait_recv()
            gcore(k).start()

        def spread_end(k=k):
            gcore(k).wait()
            for q in (0, 1):
                gone(k, q).wait_send()
                gtwo(k, q).wait_send()
        task(base + 1.0, spread_one)
        task(base + 4.0, spread_two)
        task(base + 8.0, spread_core)
        task(1e6, spread_end)

    z_tasks, z_finish = relay_tasks(
        nt, outs, lambda o: own_rows.at[o], lambda s, o: gathered.at[o, s], (os_, or_),
        lambda o, j: 1.0 + 46.0 * o + 14.0 * j, None, None, lambda *a: None)
    tasks += [(w, 1000 + n, b) for w, n, b in z_tasks]

    exchanges = [("dp", bit) for bit in bits]
    step = 1
    while step < nt:
        exchanges.append(("tensor", step))
        step *= 2
    for e, (axis, bit) in enumerate(exchanges):
        def swap(e=e, axis=axis, bit=bit):
            goal = {axis: flip(lax.axis_index(axis), bit)}
            return remote(sv, sr.at[e], ss.at[e], sm.at[e], **goal)

        def begin(e=e, swap=swap):
            if e == 0:
                own_small.wait()
            swap().start()

        def end(e=e, swap=swap):
            swap().wait()
            sv[...] = sv[...] + sr[e]
        task(2.0 + 6.0 * e, begin)
        task(6.0 + 6.0 * e, end)

    ordered(tasks)
    small_out[...] = sv[...]
    for copy in keep:
        copy.wait()
    z_finish()
    for k, s in units:
        core(k, s).wait_send()
        for q in (0, 1):
            one(k, s, q).wait_send()
            two(k, s, q).wait_send()

        @pl.when(s > t)
        def _():
            up(k, s).wait_send()

        @pl.when(s < t)
        def _():
            down(k, s).wait_send()


def reduce_grads(grads, small, own_rows, nt, extra):
    chunks, cols, outs = grads.shape[1], grads.shape[-1], own_rows.shape[0]
    dma = pltpu.SemaphoreType.DMA
    piece = grads.shape[-2]
    hops = 3 + len(extra) + (nt - 1).bit_length()
    any_ = pl.BlockSpec(memory_space=pl.ANY)
    return pl.pallas_call(
        functools.partial(reduce_kernel, nt, chunks, extra, outs),
        name="reduce_grads",
        out_shape=(
            jax.ShapeDtypeStruct(grads.shape[1:], BF16),
            jax.ShapeDtypeStruct(small.shape, F32),
            jax.ShapeDtypeStruct((outs, nt) + own_rows.shape[1:], BF16),
        ),
        in_specs=[any_, any_, any_],
        out_specs=(pl.BlockSpec(memory_space=pltpu.VMEM),) * 3,
        scratch_shapes=[
            pltpu.VMEM((nt, chunks, 2, 2, 2, piece, cols), BF16),
            pltpu.VMEM((nt, chunks, 2, 2, 2, piece, cols), BF16),
            pltpu.VMEM((nt, chunks, 2, piece, cols), BF16),
            pltpu.VMEM((nt, chunks, 2, piece, cols), BF16),
            pltpu.VMEM((nt, chunks, 2, piece, cols), BF16),
            pltpu.VMEM((nt, chunks, 3 if extra else 2, 2, piece, cols), BF16),
            pltpu.VMEM(small.shape, F32),
            pltpu.VMEM((hops,) + small.shape, F32),
            dma((nt, chunks)), dma((nt, chunks)), dma((nt, chunks)),
            dma((nt, chunks, 4)), dma((nt, chunks, 4)),
            dma((nt, chunks, 2)), dma((nt, chunks, 2)),
            dma((max(1, len(extra)), chunks)), dma((max(1, len(extra)), chunks)),
            dma((chunks, 5)), dma((chunks, 5)),
            dma((outs, nt - 1, 2)), dma((outs, nt - 1, 2)),
            dma((hops,)), dma((hops,)), dma((1 + outs,)),
        ],
        compiler_params=pltpu.CompilerParams(
            collective_id=2, has_side_effects=True, vmem_limit_bytes=VMEM_LIMIT),
    )(grads, small, own_rows)


def stacked(pair):
    lane = lax.broadcasted_iota(jnp.int32, pair.shape, 1)
    zero = jnp.zeros_like(pair)
    return jnp.concatenate([jnp.where(lane < HEAD_DIM, pair, zero), jnp.where(lane < HEAD_DIM, zero, pair)], axis=0)


def dot(a, b, dims):
    return lax.dot_general(a, b, (dims, ((), ())), preferred_element_type=F32)


NN = ((1,), (0,))
NT = ((1,), (1,))


def untangle(both):
    half = both.shape[1] // 2
    return jnp.concatenate([both[:HEAD_DIM, :half], both[HEAD_DIM:, half:]], axis=0).T


def attend_kernel(own, q_ref, k_ref, v_ref, segc, segr, o_ref, lse_ref):
    blocks = own // BLOCK
    for b in range(blocks):
        first, count = BLOCK * b, BLOCK + 2 * HALO
        q0 = HALO + BLOCK * b
        row = segr[:, q0:q0 + BLOCK]
        allowed = segc[first:first + count, :] == row
        allowed = jnp.concatenate([allowed, allowed], axis=1)

        def pair(j, carry):
            cols = pl.ds(pl.multiple_of(j * 128, 128), 128)
            q2 = stacked(q_ref[q0:q0 + BLOCK, cols])
            k2 = k_ref[first:first + count, cols]
            v2 = v_ref[first:first + count, cols]
            s = dot(k2, q2, NT) * (HEAD_DIM ** -0.5)
            s = jnp.where(allowed, s, -1e9)
            m = jnp.max(s, axis=0, keepdims=True)
            p = jnp.exp(s - m)
            l = jnp.sum(p, axis=0, keepdims=True)
            low = (p * (1.0 / l)).astype(BF16)
            out = dot(v2.T, low, NN)
            o_ref[b * BLOCK:(b + 1) * BLOCK, cols] = untangle(out).astype(BF16)
            lse_ref[j, b] = m + jnp.log(l)
            return carry
        lax.fori_loop(0, q_ref.shape[1] // 128, pair, 0)


def attend(q, k, v, segc, segr, own):
    width = q.shape[1]
    return pl.pallas_call(
        functools.partial(attend_kernel, own),
        name="attend",
        out_shape=(jax.ShapeDtypeStruct((own, width), BF16),
                   jax.ShapeDtypeStruct((width // 128, own // BLOCK, 1, 2 * BLOCK), F32)),
        compiler_params=pltpu.CompilerParams(vmem_limit_bytes=VMEM_LIMIT),
    )(q, k, v, segc, segr)


def attend_back_kernel(own, q_ref, k_ref, v_ref, g_ref, lse_ref, delta_ref, segc, segr, dq_ref, dk_ref, dv_ref, dk, dv):
    scale = HEAD_DIM ** -0.5
    window = own + 2 * HALO
    blocks = window // BLOCK
    mine = range(HALO // BLOCK, HALO // BLOCK + own // BLOCK)
    reach = HALO // BLOCK

    def pair(j, carry):
        cols = pl.ds(pl.multiple_of(j * 128, 128), 128)
        dk[...] = jnp.zeros_like(dk)
        dv[...] = jnp.zeros_like(dv)
        for w in range(blocks):
            low_block, high_block = max(0, w - reach), min(blocks, w + reach + 1)
            if w not in mine:
                low_block, high_block = max(low_block, mine[0]), min(high_block, mine[-1] + 1)
            k0, k1 = low_block * BLOCK, high_block * BLOCK
            q0 = w * BLOCK
            q2 = stacked(q_ref[q0:q0 + BLOCK, cols])
            g2 = stacked(g_ref[q0:q0 + BLOCK, cols])
            k2 = k_ref[k0:k1, cols]
            v2 = v_ref[k0:k1, cols]
            allowed = segc[k0:k1, :] == segr[:, q0:q0 + BLOCK]
            allowed = jnp.concatenate([allowed, allowed], axis=1)
            s = dot(k2, q2, NT) * scale
            p = jnp.exp(jnp.where(allowed, s - lse_ref[j, w], -1e9))
            low = p.astype(BF16)
            dp = dot(v2, g2, NT)
            ds = (p * (dp - delta_ref[j, w])).astype(BF16)
            o0, o1 = max(k0, HALO), min(k1, HALO + own)
            dst = slice(o0 - HALO, o1 - HALO)
            src = slice(o0 - k0, o1 - k0)
            dk[dst, :] += dot(ds[src], q2, NN)
            dv[dst, :] += dot(low[src], g2, NN)
            if w in mine:
                out = dot(k2.T, ds, NN)
                i = w - mine[0]
                dq_ref[i * BLOCK:(i + 1) * BLOCK, cols] = (untangle(out) * scale).astype(BF16)
        dk_ref[:, cols] = (dk[...] * scale).astype(BF16)
        dv_ref[:, cols] = dv[...].astype(BF16)
        return carry
    lax.fori_loop(0, q_ref.shape[1] // 128, pair, 0)


def attend_back(q, k, v, g, lse, delta, segc, segr, own):
    width = q.shape[1]
    shape = jax.ShapeDtypeStruct((own, width), BF16)
    return pl.pallas_call(
        functools.partial(attend_back_kernel, own),
        name="attend_back",
        out_shape=(shape, shape, shape),
        scratch_shapes=[pltpu.VMEM((own, 128), F32), pltpu.VMEM((own, 128), F32)],
        compiler_params=pltpu.CompilerParams(vmem_limit_bytes=VMEM_LIMIT),
    )(q, k, v, g, lse, delta, segc, segr)


def standardize(rows):
    center = rows - jnp.mean(rows, axis=-1, keepdims=True)
    r = lax.rsqrt(jnp.mean(center * center, axis=-1, keepdims=True) + EPS)
    return center * r, r


def norm_back(e, xhat, r):
    return r * (e - jnp.mean(e, axis=-1, keepdims=True) - xhat * jnp.mean(e * xhat, axis=-1, keepdims=True))


def body(tokens_in, segment_ids, first_gain, first_shift, qkv_weight, query_value_bias, out_weight, out_bias,
         second_gain, second_shift, up_weight, up_bias, down_weight, down_bias, cotangent):
    nt, ndp = lax.axis_size("tensor"), lax.axis_size("dp")
    t = lax.axis_index("tensor")
    length, width = tokens_in.shape
    own = length // nt
    local = qkv_weight.shape[2]
    hidden_local = up_weight.shape[1]
    start = t * own
    pack = jnp.concatenate([
        qkv_weight.transpose(0, 2, 1).reshape(3 * local, width), out_weight, up_weight, down_weight], axis=0)
    piece = width // 16
    pack = pack.reshape(-1, 2, 2, 2, 2, piece, width)
    chunks = pack.shape[0]
    whole = gather_weights(pack, nt).reshape(nt, chunks * width, width)
    up_all = lax.all_gather(up_bias, "tensor", tiled=True)
    qv_bias = lax.all_gather(query_value_bias, "tensor", axis=1, tiled=True)
    w_qkv = whole[:, :3 * local].reshape(nt, 3, local, width)
    w_out = whole[:, 3 * local:width]
    w_up = whole[:, width:2 * width]
    w_down = whole[:, 2 * width:]

    padded = jnp.pad(tokens_in, ((HALO, HALO), (0, 0)))
    tokens = lax.dynamic_slice_in_dim(padded, start, own + 2 * HALO).astype(F32)
    segs = lax.dynamic_slice_in_dim(jnp.pad(segment_ids[0], (HALO, HALO), constant_values=-1), start, own + 2 * HALO)
    segr = segs[None, :]
    segc = jnp.broadcast_to(segs[:, None], (own + 2 * HALO, BLOCK))
    cot = lax.dynamic_slice_in_dim(cotangent, start, own)
    xhat_all, r_all = standardize(tokens)
    normed = (xhat_all * first_gain + first_shift).astype(BF16)
    own_rows = slice(HALO, HALO + own)

    def project(s):
        return jnp.einsum("td,gcd->tgc", normed, w_qkv[:, s], preferred_element_type=F32).reshape(-1, width)
    q = (project(0) + qv_bias[0]).astype(BF16)
    k = project(1).astype(BF16)
    v = (project(2) + qv_bias[1]).astype(BF16)
    heads_out, lse = attend(q, k, v, segc, segr, own)
    heads_groups = heads_out.reshape(own, nt, local)
    branch = jnp.einsum("tgc,gcd->td", heads_groups, w_out, preferred_element_type=F32)
    hidden = tokens[own_rows] + branch + out_bias
    xhat2, r2 = standardize(hidden)
    normed_two = (xhat2 * second_gain + second_shift).astype(BF16)
    pre_act = jnp.einsum("td,gdf->tgf", normed_two, w_up, preferred_element_type=F32) + up_all.reshape(nt, -1)
    activated_full, gelu_back = jax.vjp(lambda a: jax.nn.gelu(a, approximate=False), pre_act)
    activated = activated_full.astype(BF16)
    mlp_out = jnp.einsum("tgf,gfd->td", activated, w_down, preferred_element_type=F32)
    result = (hidden + mlp_out + down_bias).astype(BF16)

    cot32 = cot.astype(F32)
    down_grad = jnp.einsum("tgf,td->gfd", activated, cot, preferred_element_type=F32).astype(BF16)
    grad_act = jnp.einsum("td,gfd->tgf", cot, w_down, preferred_element_type=F32)
    grad_pre = gelu_back(grad_act)[0].astype(BF16)
    up_bias_grad = jnp.sum(grad_pre.astype(F32), axis=0)
    up_grad = jnp.einsum("td,tgf->gdf", normed_two, grad_pre, preferred_element_type=F32).astype(BF16)
    grad_two = jnp.einsum("tgf,gdf->td", grad_pre, w_up, preferred_element_type=F32)
    second_gain_grad = jnp.sum(grad_two * xhat2, axis=0)
    second_shift_grad = jnp.sum(grad_two, axis=0)
    grad_hidden = cot32 + norm_back(grad_two * second_gain, xhat2, r2)
    out_bias_grad = jnp.sum(grad_hidden, axis=0)
    grad_branch = grad_hidden.astype(BF16)
    out_grad = jnp.einsum("tgc,td->gcd", heads_groups, grad_branch, preferred_element_type=F32).astype(BF16)
    grad_heads = jnp.einsum("td,gcd->tgc", grad_branch, w_out, preferred_element_type=F32).astype(BF16)
    grad_heads = grad_heads.reshape(own, width)

    products = (grad_heads.astype(F32) * heads_out.astype(F32)).reshape(own // BLOCK, BLOCK, width // 128, 2, HEAD_DIM)
    delta = jnp.sum(products, axis=-1).transpose(2, 0, 3, 1).reshape(width // 128, own // BLOCK, 1, 2 * BLOCK)
    stats = jnp.concatenate([lse, delta], axis=2)
    upward = [(i, i + 1) for i in range(nt - 1)]
    downward = [(i + 1, i) for i in range(nt - 1)]
    span = HALO // BLOCK
    g_all = jnp.concatenate([
        lax.ppermute(grad_heads[own - HALO:], "tensor", upward), grad_heads,
        lax.ppermute(grad_heads[:HALO], "tensor", downward)], axis=0)
    stats_all = jnp.concatenate([
        lax.ppermute(stats[:, own // BLOCK - span:], "tensor", upward), stats,
        lax.ppermute(stats[:, :span], "tensor", downward)], axis=1)
    dq, dk, dv = attend_back(q, k, v, g_all, stats_all[:, :, :1], stats_all[:, :, 1:], segc, segr, own)

    grad_qkv = jnp.stack([dq, dk, dv])
    normed_own = normed[own_rows]
    split = grad_qkv.reshape(3, own, nt, local)
    qkv_grad = jnp.einsum("stgc,td->gscd", split, normed_own, preferred_element_type=F32).astype(BF16)
    grad_normed = jnp.einsum("stgc,gscd->td", split, w_qkv, preferred_element_type=F32)
    xhat1, r1 = xhat_all[own_rows], r_all[own_rows]
    first_gain_grad = jnp.sum(grad_normed * xhat1, axis=0)
    first_shift_grad = jnp.sum(grad_normed, axis=0)
    input_grad = (grad_hidden + norm_back(grad_normed * first_gain, xhat1, r1)).astype(BF16)

    small = jnp.concatenate([
        jnp.stack([first_gain_grad, first_shift_grad, out_bias_grad, second_gain_grad, second_shift_grad,
                   jnp.sum(cot32, axis=0), jnp.sum(dq.astype(F32), axis=0), jnp.sum(dv.astype(F32), axis=0)]),
        up_bias_grad.reshape(-1, width)], axis=0)
    small = jnp.pad(small, ((0, -small.shape[0] % 8), (0, 0)))
    grads = jnp.concatenate([qkv_grad.reshape(nt, 3 * local, width), out_grad, up_grad, down_grad], axis=1)
    grads = grads.reshape((nt,) + pack.shape)
    extra = []
    bit = 8
    while bit < ndp:
        extra.append(bit)
        bit *= 2
    total, small, outs = reduce_grads(grads, small, jnp.stack([result, input_grad]), nt, tuple(extra))
    total = total.reshape(chunks * width, width).astype(F32) / ndp
    small = small / ndp
    up_rows = hidden_local // width
    return (
        outs[0].reshape(length, width),
        outs[1].reshape(length, width),
        small[0],
        small[1],
        total[:3 * local].reshape(3, local, width).transpose(0, 2, 1),
        lax.dynamic_slice_in_dim(small[6:8], t * local, local, axis=1),
        total[3 * local:width],
        small[2],
        small[3],
        small[4],
        total[width:2 * width],
        lax.dynamic_slice_in_dim(small, 8 + t * up_rows, up_rows).reshape(-1),
        total[2 * width:],
        small[5],
    )


def solution(mesh):
    placed = (
        P("dp", None), P("dp", None), P(), P(), P(None, None, "tensor"), P(None, "tensor"), P("tensor", None), P(),
        P(), P(), P(None, "tensor"), P("tensor"), P("tensor", None), P(), P("dp", None),
    )
    return jax.shard_map(
        body,
        mesh=mesh,
        in_specs=placed,
        out_specs=(
            P("dp", None), P("dp", None), P(), P(), P(None, None, "tensor"), P(None, "tensor"), P("tensor", None),
            P(), P(), P(), P(None, "tensor"), P("tensor"), P("tensor", None), P(),
        ),
        check_vma=False,
    )
```

```python
import functools

import jax
import jax.numpy as jnp
from jax import lax
from jax.experimental import pallas as pl
from jax.experimental.pallas import tpu as pltpu
from jax.sharding import PartitionSpec as P

HEAD_DIM = 64
HALO = 256
BLOCK = 128
EPS = 1e-06
F32 = jnp.float32
BF16 = jnp.bfloat16
MESH = pl.DeviceIdType.MESH
VMEM_LIMIT = 60 << 20


def place():
    d, t = lax.axis_index("dp"), lax.axis_index("tensor")
    return d, t, lax.rem(d, 2), lax.rem(d // 2, 2), lax.rem(d // 4, 2)


def flip(d, value):
    return d + value * (1 - 2 * lax.rem(d // value, 2))


def remote(src, dst, send, recv, **axis):
    return pltpu.make_async_remote_copy(
        src_ref=src, dst_ref=dst, send_sem=send, recv_sem=recv,
        device_id=axis, device_id_type=MESH)


def greet(nt, bits, far=False):
    d, t = lax.axis_index("dp"), lax.axis_index("tensor")
    barrier = pltpu.get_barrier_semaphore()

    @pl.when(t > 0)
    def _():
        pl.semaphore_signal(barrier, inc=1, device_id={"tensor": t - 1}, device_id_type=MESH)

    @pl.when(t < nt - 1)
    def _():
        pl.semaphore_signal(barrier, inc=1, device_id={"tensor": t + 1}, device_id_type=MESH)

    for bit in bits:
        pl.semaphore_signal(barrier, inc=1, device_id={"dp": flip(d, bit)}, device_id_type=MESH)
    if far:
        pl.semaphore_signal(barrier, inc=1, device_id={"tensor": flip(t, 2)}, device_id_type=MESH)
    peers = len(bits) + int(far) + (t > 0).astype(jnp.int32) + (t < nt - 1).astype(jnp.int32)
    pl.semaphore_wait(barrier, peers)


def ordered(tasks):
    for _, _, task in sorted(tasks, key=lambda item: item[:2]):
        task()


def relay_tasks(nt, chunks, own, full, sems, start, arrived):
    send, recv = sems
    tasks = []
    t = lax.axis_index("tensor")
    for k in range(chunks):
        for j in range(nt):
            def step(k=k, j=j):
                for way in (0, 1):
                    sign = 1 - 2 * way
                    shard = t - sign * j
                    inside = (shard >= 0) & (shard < nt)
                    if j > 0:
                        @pl.when(inside)
                        def _():
                            remote(full(shard, k), full(shard, k), send.at[k, j - 1, way], recv.at[k, j - 1, way],
                                   tensor=t).wait_recv()
                            arrived(k, j, way, shard)
                    if j < nt - 1:
                        goal = t + sign
                        @pl.when(inside & (goal >= 0) & (goal < nt))
                        def _():
                            source = own(k) if j == 0 else full(shard, k)
                            remote(source, full(shard, k), send.at[k, j, way], recv.at[k, j, way],
                                   tensor=goal).start()
            tasks.append((start(k, j), len(tasks), step))

    def finish():
        for k in range(chunks):
            for j in range(nt - 1):
                for way in (0, 1):
                    sign = 1 - 2 * way
                    shard, goal = t - sign * j, t + sign
                    @pl.when((shard >= 0) & (shard < nt) & (goal >= 0) & (goal < nt))
                    def _():
                        source = own(k) if j == 0 else full(shard, k)
                        remote(source, full(shard, k), send.at[k, j, way], recv.at[k, j, way],
                               tensor=goal).wait_send()
    return tasks, finish


def add_bf16(ref, other):
    ref[...] = (ref[...].astype(F32) + other[...].astype(F32)).astype(BF16)


def reduce_kernel(nt, chunks, extra, outs, grads, small, own_rows, total, small_out, gathered,
                  s1, rc, ra, rb, rz, rx, sv, sr,
                  ls, cs, cr, ps, pr, zs, zr, xs, xr, fs, fr, os_, or_, ss, sm, lo):
    d, t, b0, b1, b2 = place()
    bits = (1, 2, 4) + tuple(extra)
    order = tuple(range(chunks))[::-1]
    units = [(k, s) for k in order for s in range(nt)]

    def own_copy(k, s):
        return pltpu.make_async_copy(grads.at[s, k, b0], s1.at[s, k], ls.at[s, k])

    for k, s in units:
        own_copy(k, s).start()
    own_small = pltpu.make_async_copy(small, sv, lo.at[0])
    own_small.start()
    keep = [pltpu.make_async_copy(own_rows.at[o], gathered.at[o, t], lo.at[1 + o]) for o in range(outs)]
    for copy in keep:
        copy.start()
    greet(nt, bits, nt > 2)

    def core(k, s):
        return remote(grads.at[s, k, 1 - b0], rc.at[s, k], cs.at[s, k], cr.at[s, k], dp=flip(d, 1))

    def one(k, s, q):
        if q == 0:
            return remote(s1.at[s, k, 1 - b2, :, 0], ra.at[s, k], ps.at[s, k, 0], pr.at[s, k, 0], dp=flip(d, 4))
        return remote(s1.at[s, k, :, 1 - b1, 1], rb.at[s, k], ps.at[s, k, 1], pr.at[s, k, 1], dp=flip(d, 2))

    def two(k, s, q):
        if q == 0:
            return remote(s1.at[s, k, b2, 1 - b1, 0], rz.at[s, k, 0], ps.at[s, k, 2], pr.at[s, k, 2], dp=flip(d, 2))
        return remote(s1.at[s, k, 1 - b2, b1, 1], rz.at[s, k, 1], ps.at[s, k, 3], pr.at[s, k, 3], dp=flip(d, 4))

    def up(k, s):
        return remote(s1.at[s, k, b2, b1], rx.at[s, k, 0], zs.at[s, k, 0], zr.at[s, k, 0], tensor=t + 1)

    def down(k, s):
        return remote(s1.at[s, k, b2, b1], rx.at[s, k, 1], zs.at[s, k, 1], zr.at[s, k, 1], tensor=t - 1)

    tasks = []

    def task(when, body):
        tasks.append((when, len(tasks), body))

    pace = 5.4
    for n, (k, s) in enumerate(units):
        def first(k=k, s=s):
            core(k, s).start()

        def second(k=k, s=s):
            own_copy(k, s).wait()
            core(k, s).wait_recv()
            add_bf16(s1.at[s, k], rc.at[s, k])
            one(k, s, 0).start()
            one(k, s, 1).start()

        def third(k=k, s=s):
            one(k, s, 0).wait_recv()
            one(k, s, 1).wait_recv()
            add_bf16(s1.at[s, k, b2, :, 0], ra.at[s, k])
            add_bf16(s1.at[s, k, :, b1, 1], rb.at[s, k])
            two(k, s, 0).start()
            two(k, s, 1).start()

        def fourth(k=k, s=s):
            two(k, s, 0).wait_recv()
            two(k, s, 1).wait_recv()
            add_bf16(s1.at[s, k, b2, b1, 0], rz.at[s, k, 0])
            add_bf16(s1.at[s, k, b2, b1, 1], rz.at[s, k, 1])
        task(n * pace - 12.0, first)
        task(n * pace, second)
        task(n * pace + 6.0, third)
        task(n * pace + 11.5, fourth)

    for c, k in enumerate(order):
        for hop in range(nt):
            def chain(k=k, hop=hop):
                @pl.when(t == hop)
                def _():
                    for s in reversed(range(nt)):
                        @pl.when(s >= t)
                        def _():
                            if hop > 0:
                                up(k, s).wait_recv()
                                add_bf16(s1.at[s, k, b2, b1], rx.at[s, k, 0])
                            if hop < nt - 1:
                                @pl.when(s > t)
                                def _():
                                    up(k, s).start()

                @pl.when(t == nt - 1 - hop)
                def _():
                    for s in range(nt):
                        @pl.when(s <= t)
                        def _():
                            if hop > 0:
                                down(k, s).wait_recv()
                                add_bf16(s1.at[s, k, b2, b1], rx.at[s, k, 1])
                            if hop < nt - 1:
                                @pl.when(s < t)
                                def _():
                                    down(k, s).start()
            task((c + 1) * nt * pace + 8.0 + 5.0 * hop, chain)

        def settle(k=k):
            pltpu.sync_copy(s1.at[t, k, b2, b1], total.at[k, b0, b2, b1])
        base = (c + 1) * nt * pace + 8.0 + 5.0 * nt
        if not extra:
            task(base, settle)
        else:
            for e, bit in enumerate(extra):
                def more(k=k, e=e, bit=bit):
                    swap = remote(s1.at[t, k, b2, b1], rx.at[e, k, 2], xs.at[e, k], xr.at[e, k], dp=flip(d, bit))
                    swap.start()
                    swap.wait()
                    add_bf16(s1.at[t, k, b2, b1], rx.at[e, k, 2])
                task(base + 0.01 * e, more)
            task(base + 0.5, settle)

        def gone(k, q):
            if q == 0:
                return remote(total.at[k, b0, b2, b1, 0], total.at[k, b0, b2, b1, 0], fs.at[k, 0], fr.at[k, 0], dp=flip(d, 2))
            return remote(total.at[k, b0, b2, b1, 1], total.at[k, b0, b2, b1, 1], fs.at[k, 1], fr.at[k, 1], dp=flip(d, 4))

        def gtwo(k, q):
            if q == 0:
                return remote(total.at[k, b0, b2, :, 0], total.at[k, b0, b2, :, 0], fs.at[k, 2], fr.at[k, 2], dp=flip(d, 4))
            return remote(total.at[k, b0, :, b1, 1], total.at[k, b0, :, b1, 1], fs.at[k, 3], fr.at[k, 3], dp=flip(d, 2))

        def gcore(k):
            return remote(total.at[k, b0], total.at[k, b0], fs.at[k, 4], fr.at[k, 4], dp=flip(d, 1))

        def spread_one(k=k):
            for q in (0, 1):
                gone(k, q).start()

        def spread_two(k=k):
            for q in (0, 1):
                gone(k, q).wait_recv()
            for q in (0, 1):
                gtwo(k, q).start()

        def spread_core(k=k):
            for q in (0, 1):
                gtwo(k, q).wait_recv()
            gcore(k).start()

        def spread_end(k=k):
            gcore(k).wait()
            for q in (0, 1):
                gone(k, q).wait_send()
                gtwo(k, q).wait_send()
        task(base + 1.0, spread_one)
        task(base + 4.0, spread_two)
        task(base + 8.0, spread_core)
        task(1e6, spread_end)

    z_tasks, z_finish = relay_tasks(
        nt, outs, lambda o: own_rows.at[o], lambda s, o: gathered.at[o, s], (os_, or_),
        lambda o, j: 1.0 + 46.0 * o + 14.0 * j, lambda *a: None)
    tasks += [(w, 1000 + n, b) for w, n, b in z_tasks]

    exchanges = [("dp", bit) for bit in bits]
    step = 1
    while step < nt:
        exchanges.append(("tensor", step))
        step *= 2
    for e, (axis, bit) in enumerate(exchanges):
        def swap(e=e, axis=axis, bit=bit):
            goal = {axis: flip(lax.axis_index(axis), bit)}
            return remote(sv, sr.at[e], ss.at[e], sm.at[e], **goal)

        def begin(e=e, swap=swap):
            if e == 0:
                own_small.wait()
            swap().start()

        def end(e=e, swap=swap):
            swap().wait()
            sv[...] = sv[...] + sr[e]
        task(2.0 + 6.0 * e, begin)
        task(6.0 + 6.0 * e, end)

    ordered(tasks)
    small_out[...] = sv[...]
    for copy in keep:
        copy.wait()
    z_finish()
    for k, s in units:
        core(k, s).wait_send()
        for q in (0, 1):
            one(k, s, q).wait_send()
            two(k, s, q).wait_send()

        @pl.when(s > t)
        def _():
            up(k, s).wait_send()

        @pl.when(s < t)
        def _():
            down(k, s).wait_send()


def reduce_grads(grads, small, own_rows, nt, extra):
    chunks, cols, outs = grads.shape[1], grads.shape[-1], own_rows.shape[0]
    dma = pltpu.SemaphoreType.DMA
    piece = grads.shape[-2]
    hops = 3 + len(extra) + (nt - 1).bit_length()
    any_ = pl.BlockSpec(memory_space=pl.ANY)
    return pl.pallas_call(
        functools.partial(reduce_kernel, nt, chunks, extra, outs),
        name="reduce_grads",
        out_shape=(
            jax.ShapeDtypeStruct(grads.shape[1:], BF16),
            jax.ShapeDtypeStruct(small.shape, F32),
            jax.ShapeDtypeStruct((outs, nt) + own_rows.shape[1:], BF16),
        ),
        in_specs=[any_, any_, any_],
        out_specs=(pl.BlockSpec(memory_space=pltpu.VMEM),) * 3,
        scratch_shapes=[
            pltpu.VMEM((nt, chunks, 2, 2, 2, piece, cols), BF16),
            pltpu.VMEM((nt, chunks, 2, 2, 2, piece, cols), BF16),
            pltpu.VMEM((nt, chunks, 2, piece, cols), BF16),
            pltpu.VMEM((nt, chunks, 2, piece, cols), BF16),
            pltpu.VMEM((nt, chunks, 2, piece, cols), BF16),
            pltpu.VMEM((nt, chunks, 3 if extra else 2, 2, piece, cols), BF16),
            pltpu.VMEM(small.shape, F32),
            pltpu.VMEM((hops,) + small.shape, F32),
            dma((nt, chunks)), dma((nt, chunks)), dma((nt, chunks)),
            dma((nt, chunks, 4)), dma((nt, chunks, 4)),
            dma((nt, chunks, 2)), dma((nt, chunks, 2)),
            dma((max(1, len(extra)), chunks)), dma((max(1, len(extra)), chunks)),
            dma((chunks, 5)), dma((chunks, 5)),
            dma((outs, nt - 1, 2)), dma((outs, nt - 1, 2)),
            dma((hops,)), dma((hops,)), dma((1 + outs,)),
        ],
        compiler_params=pltpu.CompilerParams(
            collective_id=2, has_side_effects=True, vmem_limit_bytes=VMEM_LIMIT),
    )(grads, small, own_rows)


def stacked(pair):
    lane = lax.broadcasted_iota(jnp.int32, pair.shape, 1)
    zero = jnp.zeros_like(pair)
    return jnp.concatenate([jnp.where(lane < HEAD_DIM, pair, zero), jnp.where(lane < HEAD_DIM, zero, pair)], axis=0)


def dot(a, b, dims):
    return lax.dot_general(a, b, (dims, ((), ())), preferred_element_type=F32)


NN = ((1,), (0,))
NT = ((1,), (1,))


def untangle(both):
    half = both.shape[1] // 2
    return jnp.concatenate([both[:HEAD_DIM, :half], both[HEAD_DIM:, half:]], axis=0).T


def attend_back_kernel(own, q_ref, k_ref, v_ref, g_ref, lse_ref, delta_ref, segc, segr, dq_ref, dk_ref, dv_ref, dk, dv):
    scale = HEAD_DIM ** -0.5
    window = own + 2 * HALO
    blocks = window // BLOCK
    mine = range(HALO // BLOCK, HALO // BLOCK + own // BLOCK)
    reach = HALO // BLOCK

    def pair(j, carry):
        cols = pl.ds(pl.multiple_of(j * 128, 128), 128)
        dk[...] = jnp.zeros_like(dk)
        dv[...] = jnp.zeros_like(dv)
        for w in range(blocks):
            low_block, high_block = max(0, w - reach), min(blocks, w + reach + 1)
            if w not in mine:
                low_block, high_block = max(low_block, mine[0]), min(high_block, mine[-1] + 1)
            k0, k1 = low_block * BLOCK, high_block * BLOCK
            q0 = w * BLOCK
            q2 = stacked(q_ref[q0:q0 + BLOCK, cols])
            g2 = stacked(g_ref[q0:q0 + BLOCK, cols])
            k2 = k_ref[k0:k1, cols]
            v2 = v_ref[k0:k1, cols]
            allowed = segc[k0:k1, :] == segr[:, q0:q0 + BLOCK]
            allowed = jnp.concatenate([allowed, allowed], axis=1)
            s = dot(k2, q2, NT) * scale
            p = jnp.exp(jnp.where(allowed, s - lse_ref[j, w], -1e9))
            low = p.astype(BF16)
            dp = dot(v2, g2, NT)
            ds = (p * (dp - delta_ref[j, w])).astype(BF16)
            o0, o1 = max(k0, HALO), min(k1, HALO + own)
            dst = slice(o0 - HALO, o1 - HALO)
            src = slice(o0 - k0, o1 - k0)
            dk[dst, :] += dot(ds[src], q2, NN)
            dv[dst, :] += dot(low[src], g2, NN)
            if w in mine:
                out = dot(k2.T, ds, NN)
                i = w - mine[0]
                dq_ref[i * BLOCK:(i + 1) * BLOCK, cols] = (untangle(out) * scale).astype(BF16)
        dk_ref[:, cols] = (dk[...] * scale).astype(BF16)
        dv_ref[:, cols] = dv[...].astype(BF16)
        return carry
    lax.fori_loop(0, q_ref.shape[1] // 128, pair, 0)


def attend_back(q, k, v, g, lse, delta, segc, segr, own):
    width = q.shape[1]
    shape = jax.ShapeDtypeStruct((own, width), BF16)
    return pl.pallas_call(
        functools.partial(attend_back_kernel, own),
        name="attend_back",
        out_shape=(shape, shape, shape),
        scratch_shapes=[pltpu.VMEM((own, 128), F32), pltpu.VMEM((own, 128), F32)],
        compiler_params=pltpu.CompilerParams(vmem_limit_bytes=VMEM_LIMIT),
    )(q, k, v, g, lse, delta, segc, segr)


def standardize(rows):
    center = rows - jnp.mean(rows, axis=-1, keepdims=True)
    r = lax.rsqrt(jnp.mean(center * center, axis=-1, keepdims=True) + EPS)
    return center * r, r


def norm_back(e, xhat, r):
    return r * (e - jnp.mean(e, axis=-1, keepdims=True) - xhat * jnp.mean(e * xhat, axis=-1, keepdims=True))


def grid_rows(block):
    return block.reshape(-1, block.shape[-1])


def nearest(nt):
    return [sorted(range(nt), key=lambda s: (abs(s - p), s if p < nt // 2 else -s)) for p in range(nt)]


def pick(table, position):
    t = lax.axis_index("tensor")
    return sum((t == p).astype(jnp.int32) * row[position] for p, row in enumerate(table))


def gelu_parts(x):
    cdf = 0.5 * (1.0 + lax.erf(x * (0.5 ** 0.5)))
    pdf = jnp.exp(-0.5 * x * x) * ((2.0 * jnp.pi) ** -0.5)
    return x * cdf, cdf + x * pdf


Z_TIMES = ((0.0, 4.0, 8.0, 12.0), (16.0, 24.0, 32.0, 40.0), (20.0, 28.0, 36.0, 44.0))


def forward_kernel(nt, chunks, own,
                   tok, cot, segc, segr, vecs, bias, pack,
                   result, grad_hidden, q_ref, k_ref, v_ref, normed, g_ref, stats, small, out_g, grads, w0,
                   w, bias_all, bias_sem, bias_recv, heads, heads_t, hidden, normed_two, n2t, cot_t, mlp, gtwo,
                   gbuf, pre_s, gact_s, act, gpre, gsem, zs, zr, ps, pr, cs, cr, ls):
    d, t, b0, b1, b2 = place()
    window, width = tok.shape
    local = width // nt
    blocks = own // BLOCK
    local_copy = pltpu.make_async_copy(pack, w.at[t], ls.at[0])
    local_copy.start()
    bias_copy = pltpu.make_async_copy(bias, bias_all.at[t], ls.at[1])
    bias_copy.start()

    barrier = pltpu.get_barrier_semaphore()
    for bit in (1, 2, 4):
        pl.semaphore_signal(barrier, inc=1, device_id={"dp": flip(d, bit)}, device_id_type=MESH)
    for j in range(1, nt):
        pl.semaphore_signal(barrier, inc=1, device_id={"tensor": lax.rem(t + j, nt)}, device_id_type=MESH)
    pl.semaphore_wait(barrier, 3 + nt - 1)
    tasks = []

    def task(when, body):
        tasks.append((when, len(tasks), body))

    def bias_send(j):
        return remote(bias, bias_all.at[t], bias_sem.at[j], bias_recv.at[j], tensor=lax.rem(t + j + 1, nt))

    def bias_get(j):
        source = lax.rem(t + nt - j - 1, nt)
        return remote(bias, bias_all.at[source], bias_sem.at[j], bias_recv.at[j], tensor=source)

    def one(shard, k, q, way, j):
        if q == 0:
            return remote(w.at[shard, k, b0, b2, b1, 0], w.at[shard, k, b0, b2, b1, 0],
                          ps.at[k, j, way, 0], pr.at[k, j, way, 0], dp=flip(d, 2))
        return remote(w.at[shard, k, b0, b2, b1, 1], w.at[shard, k, b0, b2, b1, 1],
                      ps.at[k, j, way, 1], pr.at[k, j, way, 1], dp=flip(d, 4))

    def two(shard, k, q, way, j):
        if q == 0:
            return remote(w.at[shard, k, b0, b2, :, 0], w.at[shard, k, b0, b2, :, 0],
                          ps.at[k, j, way, 2], pr.at[k, j, way, 2], dp=flip(d, 4))
        return remote(w.at[shard, k, b0, :, b1, 1], w.at[shard, k, b0, :, b1, 1],
                      ps.at[k, j, way, 3], pr.at[k, j, way, 3], dp=flip(d, 2))

    def core(shard, k, way, j):
        return remote(w.at[shard, k, b0], w.at[shard, k, b0], cs.at[k, j, way], cr.at[k, j, way], dp=flip(d, 1))

    def arrived(k, j, way, shard):
        one(shard, k, 0, way, j - 1).start()
        one(shard, k, 1, way, j - 1).start()

    def each(k, j, act):
        for way in (0, 1):
            shard = t - (1 - 2 * way) * (j + 1)

            @pl.when((shard >= 0) & (shard < nt))
            def _():
                act(shard, k, way, j)

    z_tasks, z_finish = relay_tasks(
        nt, chunks, lambda k: pack.at[k, b0, b2, b1], lambda s, k: w.at[s, k, b0, b2, b1], (zs, zr),
        lambda k, j: Z_TIMES[k][j], arrived)
    tasks += z_tasks
    for k in range(chunks):
        for j in range(nt - 1):
            def second(k=k, j=j):
                def act(shard, k, way, j):
                    for q in (0, 1):
                        one(shard, k, q, way, j).wait_recv()
                    for q in (0, 1):
                        two(shard, k, q, way, j).start()
                each(k, j, act)

            def third(k=k, j=j):
                def act(shard, k, way, j):
                    for q in (0, 1):
                        two(shard, k, q, way, j).wait_recv()
                    core(shard, k, way, j).start()
                each(k, j, act)

            def fourth(k=k, j=j):
                def act(shard, k, way, j):
                    core(shard, k, way, j).wait_recv()
                each(k, j, act)
            arrive = Z_TIMES[k][j + 1]
            task(arrive + 5.0, second)
            task(arrive + 12.0, third)
            task(arrive + 16.0, fourth)

    def bias_begin():
        for j in range(nt - 1):
            bias_send(j).start()

    def bias_end():
        bias_copy.wait()
        for j in range(nt - 1):
            bias_get(j).wait_recv()
    task(0.2, bias_begin)
    task(10.0, bias_end)

    g1, s1, ob, g2, s2, db = (vecs[i:i + 1, :] for i in range(6))

    for i in range(window // BLOCK):
        def norm_rows(i=i):
            def part(n, carry):
                rows = pl.ds(pl.multiple_of(i * BLOCK + n * 32, 32), 32)
                xhat, _ = standardize(tok[rows, :].astype(F32))
                normed[rows, :] = (xhat * g1 + s1).astype(BF16)
                return carry
            lax.fori_loop(0, BLOCK // 32, part, 0)
        task(0.5 + 0.7 * i, norm_rows)

    def transposes():
        cot_t[...] = cot[...].T
        small[5:6, :] = jnp.sum(cot[...].astype(F32), axis=0, keepdims=True)
    task(6.0, transposes)

    half_rows = window // 2
    group = 2 * local

    def project(u, kind, part):
        rows = slice(part * half_rows, (part + 1) * half_rows)
        weight = w[pl.ds(2 * u, 2), 0, kind // 2, kind % 2].reshape(group, width)
        out = dot(normed[rows, :], weight, NT)
        if kind != 1:
            line = 1 + kind // 2
            out = out + jnp.concatenate([bias_all[2 * u, line:line + 1, :local], bias_all[2 * u + 1, line:line + 1, :local]], axis=1)
        target = (q_ref, k_ref, v_ref)[kind]
        target[rows, pl.ds(pl.multiple_of(u * group, 128), group)] = out.astype(BF16)

    def attention(u, b):
        first, count = BLOCK * b + 32, BLOCK + 448
        q0 = HALO + BLOCK * b
        allowed = segc[first:first + count, :] == segr[:, q0:q0 + BLOCK]
        allowed = jnp.concatenate([allowed, allowed], axis=1)

        def pair(j, carry):
            at = u * (group // 128) + j
            cols = pl.ds(pl.multiple_of(at * 128, 128), 128)
            q2 = stacked(q_ref[q0:q0 + BLOCK, cols])
            k2 = k_ref[first:first + count, cols]
            v2 = v_ref[first:first + count, cols]
            s = dot(k2, q2, NT) * (HEAD_DIM ** -0.5)
            s = jnp.where(allowed, s, -1e9)
            m = jnp.max(s, axis=0, keepdims=True)
            p = jnp.exp(s - m)
            l = jnp.sum(p, axis=0, keepdims=True)
            low = (p * (1.0 / l)).astype(BF16)
            out = dot(v2.T, low, NN)
            half = out.shape[1] // 2
            both = jnp.concatenate([out[:HEAD_DIM, :half], out[HEAD_DIM:, half:]], axis=0).astype(BF16)
            heads_t[cols, b * BLOCK:(b + 1) * BLOCK] = both
            heads[b * BLOCK:(b + 1) * BLOCK, cols] = both.T
            stats[at, b, 0:1, :] = m + jnp.log(l)
            return carry
        lax.fori_loop(0, group // 128, pair, 0)

    def out_project(u, fresh):
        weight = w[pl.ds(2 * u, 2), 0, 1, 1].reshape(group, width)
        part = dot(heads[:, pl.ds(pl.multiple_of(u * group, 128), group)], weight, NN)
        if fresh:
            hidden[...] = part
        else:
            hidden[...] += part

    first_half = t // 2
    at = 7.0
    for n in range(nt // 2):
        u = lax.rem(first_half + n, nt // 2)
        if n == 0:
            def own_ready():
                local_copy.wait()
            task(20.8, own_ready)
            at = 20.9
        else:
            at = max(at, 28.5)
        for kind in range(3):
            for part in range(2):
                def run(u=u, kind=kind, part=part):
                    project(u, kind, part)
                task(at, run)
                at += 0.7
        for b in range(blocks):
            def run(u=u, b=b):
                attention(u, b)
            task(at, run)
            at += 3.0

        def run(u=u, n=n):
            out_project(u, n == 0)
        task(at, run)
        at += 0.6

    def rows_of(i):
        return slice(i * BLOCK, (i + 1) * BLOCK)

    for i in range(blocks):
        def norm_two(i=i):
            rows = rows_of(i)
            token = tok[HALO + i * BLOCK:HALO + (i + 1) * BLOCK, :].astype(F32)
            whole = hidden[rows, :] + token + ob
            hidden[rows, :] = whole
            xhat, _ = standardize(whole)
            low = (xhat * g2 + s2).astype(BF16)
            normed_two[rows, :] = low
            n2t[:, rows] = low.T
        task(at, norm_two)
        at += 0.7

    table = nearest(nt)
    slab = 32

    def grads_out(slot, shard):
        return pltpu.make_async_copy(gbuf.at[slot], grads.at[shard], gsem.at[slot])

    def mlp_shard(position, shard):
        slot = position % 2
        up = w[shard, 1].reshape(width, width)
        down = w[shard, 2].reshape(width, width)
        pre_s[...] = dot(normed_two[...], up, NN) + bias_all[shard, 0:1, :]
        gact_s[...] = dot(cot[...], down, NT)

        def step(i, total):
            rows = pl.ds(pl.multiple_of(i * slab, slab), slab)
            value, slope = gelu_parts(pre_s[rows, :])
            act[rows, :] = value.astype(BF16)
            low = (gact_s[rows, :] * slope).astype(BF16)
            gpre[rows, :] = low
            return total + low.astype(F32)
        total = lax.fori_loop(0, own // slab, step, jnp.zeros((slab, width), F32))
        small[pl.ds(8 + shard, 1), :] = jnp.sum(total, axis=0, keepdims=True)
        if position == 0:
            mlp[...] = dot(act[...], down, NN)
            gtwo[...] = dot(gpre[...], up, NT)
        else:
            mlp[...] += dot(act[...], down, NN)
            gtwo[...] += dot(gpre[...], up, NT)
        if position >= 2:
            grads_out(slot, shard).wait()
        gbuf[slot, 0] = dot(n2t[...], gpre[...], NN).astype(BF16).reshape(gbuf.shape[2:])
        gbuf[slot, 1] = dot(cot_t[...], act[...], NN).astype(BF16).reshape(gbuf.shape[2:])
        grads_out(slot, shard).start()

    for position in range(nt):
        def run(position=position):
            mlp_shard(position, pick(table, position))
        if position > 0:
            at = max(at, Z_TIMES[2][position] + 16.5)
        task(at, run)
        at += 6.0

    for i in range(blocks):
        def finish_rows(i=i):
            rows = rows_of(i)
            whole = hidden[rows, :]
            result[rows, :] = (whole + mlp[rows, :] + db).astype(BF16)
            xhat, r = standardize(whole)
            grad = gtwo[rows, :]
            gh = cot[rows, :].astype(F32) + norm_back(grad * g2, xhat, r)
            grad_hidden[rows, :] = gh
            sums = (jnp.sum(gh, axis=0, keepdims=True), jnp.sum(grad * xhat, axis=0, keepdims=True),
                    jnp.sum(grad, axis=0, keepdims=True))
            for n, value in enumerate(sums):
                if i == 0:
                    small[2 + n:3 + n, :] = value
                else:
                    small[2 + n:3 + n, :] += value
            normed_two[rows, :] = gh.astype(BF16)
        task(at, finish_rows)
        at += 0.8

    def out_back():
        outw = w[:, 0, 1, 1].reshape(width, width)
        branch = normed_two[...]
        g_ref[...] = dot(branch, outw, NT).astype(BF16)
        g_t = dot(outw, branch, NT).astype(BF16).astype(F32)
        product = g_t * heads_t[...].astype(F32)
        for h in range(width // HEAD_DIM):
            line = jnp.sum(product[h * HEAD_DIM:(h + 1) * HEAD_DIM, :], axis=0, keepdims=True)
            for b in range(blocks):
                stats[h // 2, b, 1:2, (h % 2) * BLOCK:(h % 2 + 1) * BLOCK] = line[:, b * BLOCK:(b + 1) * BLOCK]
    task(at, out_back)

    def out_grad():
        out_g[...] = dot(heads_t[...], normed_two[...], NN).astype(BF16)
    task(at + 2.0, out_grad)

    def keep_copy():
        return pltpu.make_async_copy(w.at[:, 0], w0, ls.at[0])

    def keep_first():
        keep_copy().start()
    task(at - 0.1, keep_first)
    ordered(tasks)
    grads_out(0, 0).wait()
    grads_out(1, 0).wait()
    keep_copy().wait()
    for n in (0, 1, 6, 7):
        small[n:n + 1, :] = jnp.zeros((1, width), F32)
    if small.shape[0] > 8 + nt:
        small[8 + nt:, :] = jnp.zeros((small.shape[0] - 8 - nt, width), F32)
    z_finish()
    for j in range(nt - 1):
        bias_send(j).wait_send()
    for k in range(chunks):
        for j in range(nt - 1):
            def end(shard, k, way, j):
                core(shard, k, way, j).wait_send()
                for q in (0, 1):
                    one(shard, k, q, way, j).wait_send()
                    two(shard, k, q, way, j).wait_send()
            each(k, j, end)


def forward(tok, cot, segc, segr, vecs, bias, pack, nt):
    chunks, piece, width = pack.shape[0], pack.shape[-2], pack.shape[-1]
    window, own = tok.shape[0], cot.shape[0]
    lines = 8 + nt + -nt % 8
    dma = pltpu.SemaphoreType.DMA
    vmem, any_ = pl.BlockSpec(memory_space=pltpu.VMEM), pl.BlockSpec(memory_space=pl.ANY)

    def shape(dims, kind):
        return jax.ShapeDtypeStruct(dims, kind)
    return pl.pallas_call(
        functools.partial(forward_kernel, nt, chunks, own),
        name="forward",
        out_shape=(
            shape((own, width), BF16), shape((own, width), F32),
            shape((window, width), BF16), shape((window, width), BF16), shape((window, width), BF16),
            shape((window, width), BF16), shape((own, width), BF16),
            shape((width // 128, own // BLOCK, 2, 2 * BLOCK), F32), shape((lines, width), F32),
            shape((width, width), BF16), shape((nt, chunks - 1) + pack.shape[1:], BF16),
            shape((nt,) + pack.shape[1:], BF16),
        ),
        in_specs=[vmem] * 6 + [any_],
        out_specs=(vmem,) * 10 + (any_, any_),
        scratch_shapes=[
            pltpu.VMEM((nt,) + pack.shape, BF16), pltpu.VMEM((nt,) + bias.shape, F32), dma((nt - 1,)), dma((nt - 1,)),
            pltpu.VMEM((own, width), BF16), pltpu.VMEM((width, own), BF16), pltpu.VMEM((own, width), F32),
            pltpu.VMEM((own, width), BF16), pltpu.VMEM((width, own), BF16), pltpu.VMEM((width, own), BF16),
            pltpu.VMEM((own, width), F32), pltpu.VMEM((own, width), F32),
            pltpu.VMEM((2, chunks - 1) + pack.shape[1:], BF16),
            pltpu.VMEM((own, width), F32), pltpu.VMEM((own, width), F32),
            pltpu.VMEM((own, width), BF16), pltpu.VMEM((own, width), BF16),
            dma((2,)),
            dma((chunks, nt - 1, 2)), dma((chunks, nt - 1, 2)),
            dma((chunks, nt - 1, 2, 4)), dma((chunks, nt - 1, 2, 4)),
            dma((chunks, nt - 1, 2)), dma((chunks, nt - 1, 2)), dma((2,)),
        ],
        compiler_params=pltpu.CompilerParams(
            collective_id=1, has_side_effects=True, vmem_limit_bytes=VMEM_LIMIT),
    )(tok, cot, segc, segr, vecs, bias, pack)


def body(tokens_in, segment_ids, first_gain, first_shift, qkv_weight, query_value_bias, out_weight, out_bias,
         second_gain, second_shift, up_weight, up_bias, down_weight, down_bias, cotangent):
    nt, ndp = lax.axis_size("tensor"), lax.axis_size("dp")
    t = lax.axis_index("tensor")
    length, width = tokens_in.shape
    own = length // nt
    local = qkv_weight.shape[2]
    hidden_local = up_weight.shape[1]
    start = t * own
    pack = jnp.concatenate([
        qkv_weight.transpose(0, 2, 1).reshape(3 * local, width), out_weight, up_weight, down_weight], axis=0)
    piece = width // 16
    pack = pack.reshape(-1, 2, 2, 2, 2, piece, width)
    chunks = pack.shape[0]
    padded = jnp.pad(tokens_in, ((HALO, HALO), (0, 0)))
    tokens = lax.dynamic_slice_in_dim(padded, start, own + 2 * HALO)
    segs = lax.dynamic_slice_in_dim(jnp.pad(segment_ids[0], (HALO, HALO), constant_values=-1), start, own + 2 * HALO)
    segr = segs[None, :]
    segc = jnp.broadcast_to(segs[:, None], (own + 2 * HALO, BLOCK))
    cot = lax.dynamic_slice_in_dim(cotangent, start, own)
    vecs = jnp.pad(jnp.stack([first_gain, first_shift, out_bias, second_gain, second_shift, down_bias]), ((0, 2), (0, 0)))
    bias = jnp.pad(jnp.concatenate([up_bias[None], jnp.pad(query_value_bias, ((0, 0), (0, width - local)))]), ((0, 5), (0, 0)))
    result, grad_hidden, q, k, v, normed, grad_heads, stats, small1, out_grad, mlp_grads, w_first = forward(
        tokens, cot, segc, segr, vecs, bias, pack, nt)
    own_rows = slice(HALO, HALO + own)
    w_qkv = w_first.reshape(nt, width, width)[:, :3 * local].reshape(nt, 3, local, width)
    upward = [(i, i + 1) for i in range(nt - 1)]
    downward = [(i + 1, i) for i in range(nt - 1)]
    span = HALO // BLOCK
    g_all = jnp.concatenate([
        lax.ppermute(grad_heads[own - HALO:], "tensor", upward), grad_heads,
        lax.ppermute(grad_heads[:HALO], "tensor", downward)], axis=0)
    stats_all = jnp.concatenate([
        lax.ppermute(stats[:, own // BLOCK - span:], "tensor", upward), stats,
        lax.ppermute(stats[:, :span], "tensor", downward)], axis=1)
    dq, dk, dv = attend_back(q, k, v, g_all, stats_all[:, :, :1], stats_all[:, :, 1:], segc, segr, own)

    grad_qkv = jnp.stack([dq, dk, dv])
    normed_own = normed[own_rows]
    split = grad_qkv.reshape(3, own, nt, local)
    qkv_grad = jnp.einsum("stgc,td->gscd", split, normed_own, preferred_element_type=F32).astype(BF16)
    grad_normed = jnp.einsum("stgc,gscd->td", split, w_qkv, preferred_element_type=F32)
    xhat1, r1 = standardize(tokens[own_rows].astype(F32))
    first_gain_grad = jnp.sum(grad_normed * xhat1, axis=0)
    first_shift_grad = jnp.sum(grad_normed, axis=0)
    input_grad = (grad_hidden + norm_back(grad_normed * first_gain, xhat1, r1)).astype(BF16)

    small = small1.at[:2].set(jnp.stack([first_gain_grad, first_shift_grad])).at[6:8].set(
        jnp.stack([jnp.sum(dq.astype(F32), axis=0), jnp.sum(dv.astype(F32), axis=0)]))
    first = jnp.concatenate([qkv_grad.reshape(nt, 3 * local, width), out_grad.reshape(nt, local, width)], axis=1)
    grads = jnp.concatenate([first.reshape((nt, 1) + pack.shape[1:]), mlp_grads], axis=1)
    extra = []
    bit = 8
    while bit < ndp:
        extra.append(bit)
        bit *= 2
    total, small, outs = reduce_grads(grads, small, jnp.stack([result, input_grad]), nt, tuple(extra))
    total = total.reshape(chunks * width, width).astype(F32) / ndp
    small = small / ndp
    up_rows = hidden_local // width
    return (
        outs[0].reshape(length, width),
        outs[1].reshape(length, width),
        small[0],
        small[1],
        total[:3 * local].reshape(3, local, width).transpose(0, 2, 1),
        lax.dynamic_slice_in_dim(small[6:8], t * local, local, axis=1),
        total[3 * local:width],
        small[2],
        small[3],
        small[4],
        total[width:2 * width],
        lax.dynamic_slice_in_dim(small, 8 + t * up_rows, up_rows).reshape(-1),
        total[2 * width:].T,
        small[5],
    )


def solution(mesh):
    placed = (
        P("dp", None), P("dp", None), P(), P(), P(None, None, "tensor"), P(None, "tensor"), P("tensor", None), P(),
        P(), P(), P(None, "tensor"), P("tensor"), P("tensor", None), P(), P("dp", None),
    )
    return jax.shard_map(
        body,
        mesh=mesh,
        in_specs=placed,
        out_specs=(
            P("dp", None), P("dp", None), P(), P(), P(None, None, "tensor"), P(None, "tensor"), P("tensor", None),
            P(), P(), P(), P(None, "tensor"), P("tensor"), P("tensor", None), P(),
        ),
        check_vma=False,
    )
```

```python
import functools

import jax
import jax.numpy as jnp
from jax import lax
from jax.experimental import pallas as pl
from jax.experimental.pallas import tpu as pltpu
from jax.sharding import PartitionSpec as P

HEAD_DIM = 64
HALO = 256
REACH = 224
BLOCK = 128
EPS = 1e-06
F32 = jnp.float32
BF16 = jnp.bfloat16
MESH = pl.DeviceIdType.MESH
VMEM_LIMIT = 60 << 20


def place():
    d, t = lax.axis_index("dp"), lax.axis_index("tensor")
    return d, t, lax.rem(d, 2), lax.rem(d // 2, 2), lax.rem(d // 4, 2)


def flip(d, value):
    return d + value * (1 - 2 * lax.rem(d // value, 2))


def remote(src, dst, send, recv, **axis):
    return pltpu.make_async_remote_copy(
        src_ref=src, dst_ref=dst, send_sem=send, recv_sem=recv,
        device_id=axis, device_id_type=MESH)


def greet(nt, bits, far=False):
    d, t = lax.axis_index("dp"), lax.axis_index("tensor")
    barrier = pltpu.get_barrier_semaphore()

    @pl.when(t > 0)
    def _():
        pl.semaphore_signal(barrier, inc=1, device_id={"tensor": t - 1}, device_id_type=MESH)

    @pl.when(t < nt - 1)
    def _():
        pl.semaphore_signal(barrier, inc=1, device_id={"tensor": t + 1}, device_id_type=MESH)

    for bit in bits:
        pl.semaphore_signal(barrier, inc=1, device_id={"dp": flip(d, bit)}, device_id_type=MESH)
    if far:
        pl.semaphore_signal(barrier, inc=1, device_id={"tensor": flip(t, 2)}, device_id_type=MESH)
    peers = len(bits) + int(far) + (t > 0).astype(jnp.int32) + (t < nt - 1).astype(jnp.int32)
    pl.semaphore_wait(barrier, peers)


def ordered(tasks):
    for _, _, task in sorted(tasks, key=lambda item: item[:2]):
        task()


def relay_tasks(nt, chunks, own, full, sems, start, arrived):
    send, recv = sems
    tasks = []
    t = lax.axis_index("tensor")
    for k in range(chunks):
        for j in range(nt):
            def step(k=k, j=j):
                for way in (0, 1):
                    sign = 1 - 2 * way
                    shard = t - sign * j
                    inside = (shard >= 0) & (shard < nt)
                    if j > 0:
                        @pl.when(inside)
                        def _():
                            remote(full(shard, k), full(shard, k), send.at[k, j - 1, way], recv.at[k, j - 1, way],
                                   tensor=t).wait_recv()
                            arrived(k, j, way, shard)
                    if j < nt - 1:
                        goal = t + sign
                        @pl.when(inside & (goal >= 0) & (goal < nt))
                        def _():
                            source = own(k) if j == 0 else full(shard, k)
                            remote(source, full(shard, k), send.at[k, j, way], recv.at[k, j, way],
                                   tensor=goal).start()
            tasks.append((start(k, j), len(tasks), step))

    def finish():
        for k in range(chunks):
            for j in range(nt - 1):
                for way in (0, 1):
                    sign = 1 - 2 * way
                    shard, goal = t - sign * j, t + sign
                    @pl.when((shard >= 0) & (shard < nt) & (goal >= 0) & (goal < nt))
                    def _():
                        source = own(k) if j == 0 else full(shard, k)
                        remote(source, full(shard, k), send.at[k, j, way], recv.at[k, j, way],
                               tensor=goal).wait_send()
    return tasks, finish


def add_bf16(ref, other):
    ref[...] = (ref[...].astype(F32) + other[...].astype(F32)).astype(BF16)


def stacked(pair):
    lane = lax.broadcasted_iota(jnp.int32, pair.shape, 1)
    zero = jnp.zeros_like(pair)
    return jnp.concatenate([jnp.where(lane < HEAD_DIM, pair, zero), jnp.where(lane < HEAD_DIM, zero, pair)], axis=0)


def dot(a, b, dims):
    return lax.dot_general(a, b, (dims, ((), ())), preferred_element_type=F32)


NN = ((1,), (0,))
NT = ((1,), (1,))


def untangle(both):
    half = both.shape[1] // 2
    return jnp.concatenate([both[:HEAD_DIM, :half], both[HEAD_DIM:, half:]], axis=0).T


def standardize(rows):
    center = rows - jnp.mean(rows, axis=-1, keepdims=True)
    r = lax.rsqrt(jnp.mean(center * center, axis=-1, keepdims=True) + EPS)
    return center * r, r


def norm_back(e, xhat, r):
    return r * (e - jnp.mean(e, axis=-1, keepdims=True) - xhat * jnp.mean(e * xhat, axis=-1, keepdims=True))


def grid_rows(block):
    return block.reshape(-1, block.shape[-1])


def nearest(nt):
    return [sorted(range(nt), key=lambda s: (abs(s - p), s if p < nt // 2 else -s)) for p in range(nt)]


def pick(table, position):
    t = lax.axis_index("tensor")
    return sum((t == p).astype(jnp.int32) * row[position] for p, row in enumerate(table))


def gelu_parts(x):
    cdf = 0.5 * (1.0 + lax.erf(x * (0.5 ** 0.5)))
    pdf = jnp.exp(-0.5 * x * x) * ((2.0 * jnp.pi) ** -0.5)
    return x * cdf, cdf + x * pdf


Z_TIMES = ((0.0, 4.0, 8.0, 12.0), (16.0, 24.0, 32.0, 40.0), (20.0, 28.0, 36.0, 44.0))


def forward_kernel(nt, chunks, own,
                   tok, cot, segc, segr, vecs, bias, pack,
                   result, grad_hidden, q_ref, k_ref, v_ref, normed_own, g_ref, stats, small, out_g, grads, w0,
                   normed, w, bias_all, bias_sem, bias_recv, heads, heads_t, hidden, normed_two, n2t, cot_t, mlp, gtwo,
                   gbuf, pre_s, gact_s, act, gpre, gsem, zs, zr, ps, pr, cs, cr, ls):
    d, t, b0, b1, b2 = place()
    window, width = tok.shape
    local = width // nt
    blocks = own // BLOCK
    local_copy = pltpu.make_async_copy(pack, w.at[t], ls.at[0])
    local_copy.start()
    bias_copy = pltpu.make_async_copy(bias, bias_all.at[t], ls.at[1])
    bias_copy.start()

    barrier = pltpu.get_barrier_semaphore()
    for bit in (1, 2, 4):
        pl.semaphore_signal(barrier, inc=1, device_id={"dp": flip(d, bit)}, device_id_type=MESH)
    for j in range(1, nt):
        pl.semaphore_signal(barrier, inc=1, device_id={"tensor": lax.rem(t + j, nt)}, device_id_type=MESH)
    pl.semaphore_wait(barrier, 3 + nt - 1)
    tasks = []

    def task(when, body):
        tasks.append((when, len(tasks), body))

    def bias_send(j):
        return remote(bias, bias_all.at[t], bias_sem.at[j], bias_recv.at[j], tensor=lax.rem(t + j + 1, nt))

    def bias_get(j):
        source = lax.rem(t + nt - j - 1, nt)
        return remote(bias, bias_all.at[source], bias_sem.at[j], bias_recv.at[j], tensor=source)

    def one(shard, k, q, way, j):
        if q == 0:
            return remote(w.at[shard, k, b0, b2, b1, 0], w.at[shard, k, b0, b2, b1, 0],
                          ps.at[k, j, way, 0], pr.at[k, j, way, 0], dp=flip(d, 2))
        return remote(w.at[shard, k, b0, b2, b1, 1], w.at[shard, k, b0, b2, b1, 1],
                      ps.at[k, j, way, 1], pr.at[k, j, way, 1], dp=flip(d, 4))

    def two(shard, k, q, way, j):
        if q == 0:
            return remote(w.at[shard, k, b0, b2, :, 0], w.at[shard, k, b0, b2, :, 0],
                          ps.at[k, j, way, 2], pr.at[k, j, way, 2], dp=flip(d, 4))
        return remote(w.at[shard, k, b0, :, b1, 1], w.at[shard, k, b0, :, b1, 1],
                      ps.at[k, j, way, 3], pr.at[k, j, way, 3], dp=flip(d, 2))

    def core(shard, k, way, j):
        return remote(w.at[shard, k, b0], w.at[shard, k, b0], cs.at[k, j, way], cr.at[k, j, way], dp=flip(d, 1))

    def arrived(k, j, way, shard):
        one(shard, k, 0, way, j - 1).start()
        one(shard, k, 1, way, j - 1).start()

    def each(k, j, act):
        for way in (0, 1):
            shard = t - (1 - 2 * way) * (j + 1)

            @pl.when((shard >= 0) & (shard < nt))
            def _():
                act(shard, k, way, j)

    z_tasks, z_finish = relay_tasks(
        nt, chunks, lambda k: pack.at[k, b0, b2, b1], lambda s, k: w.at[s, k, b0, b2, b1], (zs, zr),
        lambda k, j: Z_TIMES[k][j], arrived)
    tasks += z_tasks
    for k in range(chunks):
        for j in range(nt - 1):
            def second(k=k, j=j):
                def act(shard, k, way, j):
                    for q in (0, 1):
                        one(shard, k, q, way, j).wait_recv()
                    for q in (0, 1):
                        two(shard, k, q, way, j).start()
                each(k, j, act)

            def third(k=k, j=j):
                def act(shard, k, way, j):
                    for q in (0, 1):
                        two(shard, k, q, way, j).wait_recv()
                    core(shard, k, way, j).start()
                each(k, j, act)

            def fourth(k=k, j=j):
                def act(shard, k, way, j):
                    core(shard, k, way, j).wait_recv()
                each(k, j, act)
            arrive = Z_TIMES[k][j + 1]
            task(arrive + 5.0, second)
            task(arrive + 12.0, third)
            task(arrive + 16.0, fourth)

    def bias_begin():
        for j in range(nt - 1):
            bias_send(j).start()

    def bias_end():
        bias_copy.wait()
        for j in range(nt - 1):
            bias_get(j).wait_recv()
    task(0.2, bias_begin)

    def clear():
        stats[...] = jnp.zeros(stats.shape, F32)
    task(0.3, clear)
    task(10.0, bias_end)

    g1, s1, ob, g2, s2, db = (vecs[i:i + 1, :] for i in range(6))

    for i in range(window // BLOCK):
        def norm_rows(i=i):
            def part(n, carry):
                rows = pl.ds(pl.multiple_of(i * BLOCK + n * 32, 32), 32)
                xhat, _ = standardize(tok[rows, :].astype(F32))
                normed[rows, :] = (xhat * g1 + s1).astype(BF16)
                return carry
            lax.fori_loop(0, BLOCK // 32, part, 0)
        task(0.5 + 0.7 * i, norm_rows)

    def transposes():
        normed_own[...] = normed[HALO:HALO + own, :]
        cot_t[...] = cot[...].T
        small[5:6, :] = jnp.sum(cot[...].astype(F32), axis=0, keepdims=True)
    task(6.0, transposes)

    half_rows = window // 2
    group = 2 * local

    def project(u, kind, part):
        rows = slice(part * half_rows, (part + 1) * half_rows)
        weight = w[pl.ds(2 * u, 2), 0, kind // 2, kind % 2].reshape(group, width)
        out = dot(normed[rows, :], weight, NT)
        if kind != 1:
            line = 1 + kind // 2
            out = out + jnp.concatenate([bias_all[2 * u, line:line + 1, :local], bias_all[2 * u + 1, line:line + 1, :local]], axis=1)
        target = (q_ref, k_ref, v_ref)[kind]
        target[rows, pl.ds(pl.multiple_of(u * group, 128), group)] = out.astype(BF16)

    def attention(u, b):
        first, count = BLOCK * b + 32, BLOCK + 448
        q0 = HALO + BLOCK * b
        allowed = segc[first:first + count, :] == segr[:, q0:q0 + BLOCK]
        allowed = jnp.concatenate([allowed, allowed], axis=1)

        def pair(j, carry):
            at = u * (group // 128) + j
            cols = pl.ds(pl.multiple_of(at * 128, 128), 128)
            q2 = stacked(q_ref[q0:q0 + BLOCK, cols])
            k2 = k_ref[first:first + count, cols]
            v2 = v_ref[first:first + count, cols]
            s = dot(k2, q2, NT) * (HEAD_DIM ** -0.5)
            s = jnp.where(allowed, s, -1e9)
            m = jnp.max(s, axis=0, keepdims=True)
            p = jnp.exp(s - m)
            l = jnp.sum(p, axis=0, keepdims=True)
            low = (p * (1.0 / l)).astype(BF16)
            out = dot(v2.T, low, NN)
            half = out.shape[1] // 2
            both = jnp.concatenate([out[:HEAD_DIM, :half], out[HEAD_DIM:, half:]], axis=0).astype(BF16)
            heads_t[cols, b * BLOCK:(b + 1) * BLOCK] = both
            heads[b * BLOCK:(b + 1) * BLOCK, cols] = both.T
            stats[b, pl.ds(at, 1), :] = m + jnp.log(l)
            return carry
        lax.fori_loop(0, group // 128, pair, 0)

    def out_project(u, fresh):
        weight = w[pl.ds(2 * u, 2), 0, 1, 1].reshape(group, width)
        part = dot(heads[:, pl.ds(pl.multiple_of(u * group, 128), group)], weight, NN)
        if fresh:
            hidden[...] = part
        else:
            hidden[...] += part

    first_half = t // 2
    at = 7.0
    for n in range(nt // 2):
        u = lax.rem(first_half + n, nt // 2)
        if n == 0:
            def own_ready():
                local_copy.wait()
            task(20.8, own_ready)
            at = 20.9
        else:
            at = max(at, 28.5)
        for kind in range(3):
            for part in range(2):
                def run(u=u, kind=kind, part=part):
                    project(u, kind, part)
                task(at, run)
                at += 0.7
        for b in range(blocks):
            def run(u=u, b=b):
                attention(u, b)
            task(at, run)
            at += 3.0

        def run(u=u, n=n):
            out_project(u, n == 0)
        task(at, run)
        at += 0.6

    def rows_of(i):
        return slice(i * BLOCK, (i + 1) * BLOCK)

    for i in range(blocks):
        def norm_two(i=i):
            rows = rows_of(i)
            token = tok[HALO + i * BLOCK:HALO + (i + 1) * BLOCK, :].astype(F32)
            whole = hidden[rows, :] + token + ob
            hidden[rows, :] = whole
            xhat, _ = standardize(whole)
            low = (xhat * g2 + s2).astype(BF16)
            normed_two[rows, :] = low
            n2t[:, rows] = low.T
        task(at, norm_two)
        at += 0.7

    table = nearest(nt)
    slab = 32

    def grads_out(slot, shard):
        return pltpu.make_async_copy(gbuf.at[slot], grads.at[shard], gsem.at[slot])

    def mlp_shard(position, shard):
        slot = position % 2
        up = w[shard, 1].reshape(width, width)
        down = w[shard, 2].reshape(width, width)
        pre_s[...] = dot(normed_two[...], up, NN) + bias_all[shard, 0:1, :]
        gact_s[...] = dot(cot[...], down, NT)

        def step(i, total):
            rows = pl.ds(pl.multiple_of(i * slab, slab), slab)
            value, slope = gelu_parts(pre_s[rows, :])
            act[rows, :] = value.astype(BF16)
            low = (gact_s[rows, :] * slope).astype(BF16)
            gpre[rows, :] = low
            return total + low.astype(F32)
        total = lax.fori_loop(0, own // slab, step, jnp.zeros((slab, width), F32))
        small[pl.ds(8 + shard, 1), :] = jnp.sum(total, axis=0, keepdims=True)
        if position == 0:
            mlp[...] = dot(act[...], down, NN)
            gtwo[...] = dot(gpre[...], up, NT)
        else:
            mlp[...] += dot(act[...], down, NN)
            gtwo[...] += dot(gpre[...], up, NT)
        if position >= 2:
            grads_out(slot, shard).wait()
        gbuf[slot, 0] = dot(n2t[...], gpre[...], NN).astype(BF16).reshape(gbuf.shape[2:])
        gbuf[slot, 1] = dot(cot_t[...], act[...], NN).astype(BF16).reshape(gbuf.shape[2:])
        grads_out(slot, shard).start()

    for position in range(nt):
        def run(position=position):
            mlp_shard(position, pick(table, position))
        if position > 0:
            at = max(at, Z_TIMES[2][position] + 16.5)
        task(at, run)
        at += 6.0

    for i in range(blocks):
        def finish_rows(i=i):
            rows = rows_of(i)
            whole = hidden[rows, :]
            result[rows, :] = (whole + mlp[rows, :] + db).astype(BF16)
            xhat, r = standardize(whole)
            grad = gtwo[rows, :]
            gh = cot[rows, :].astype(F32) + norm_back(grad * g2, xhat, r)
            grad_hidden[rows, :] = gh
            sums = (jnp.sum(gh, axis=0, keepdims=True), jnp.sum(grad * xhat, axis=0, keepdims=True),
                    jnp.sum(grad, axis=0, keepdims=True))
            for n, value in enumerate(sums):
                if i == 0:
                    small[2 + n:3 + n, :] = value
                else:
                    small[2 + n:3 + n, :] += value
            normed_two[rows, :] = gh.astype(BF16)
        task(at, finish_rows)
        at += 0.8

    def out_back():
        outw = w[:, 0, 1, 1].reshape(width, width)
        branch = normed_two[...]
        g_ref[...] = dot(branch, outw, NT).astype(BF16)
        g_t = dot(outw, branch, NT).astype(BF16).astype(F32)
        product = g_t * heads_t[...].astype(F32)
        for h in range(width // HEAD_DIM):
            line = jnp.sum(product[h * HEAD_DIM:(h + 1) * HEAD_DIM, :], axis=0, keepdims=True)
            for b in range(blocks):
                stats[b, 8 + h // 2:9 + h // 2, (h % 2) * BLOCK:(h % 2 + 1) * BLOCK] = line[:, b * BLOCK:(b + 1) * BLOCK]
    task(at, out_back)

    def out_grad():
        out_g[...] = dot(heads_t[...], normed_two[...], NN).astype(BF16)
    task(at + 2.0, out_grad)

    def keep_copy():
        return pltpu.make_async_copy(w.at[:, 0], w0, ls.at[0])

    def keep_first():
        keep_copy().start()
    task(at - 0.1, keep_first)
    ordered(tasks)
    grads_out(0, 0).wait()
    grads_out(1, 0).wait()
    keep_copy().wait()
    for n in (0, 1, 6, 7):
        small[n:n + 1, :] = jnp.zeros((1, width), F32)
    if small.shape[0] > 8 + nt:
        small[8 + nt:, :] = jnp.zeros((small.shape[0] - 8 - nt, width), F32)
    z_finish()
    for j in range(nt - 1):
        bias_send(j).wait_send()
    for k in range(chunks):
        for j in range(nt - 1):
            def end(shard, k, way, j):
                core(shard, k, way, j).wait_send()
                for q in (0, 1):
                    one(shard, k, q, way, j).wait_send()
                    two(shard, k, q, way, j).wait_send()
            each(k, j, end)


def forward(tok, cot, segc, segr, vecs, bias, pack, nt):
    chunks, piece, width = pack.shape[0], pack.shape[-2], pack.shape[-1]
    window, own = tok.shape[0], cot.shape[0]
    lines = 8 + nt + -nt % 8
    dma = pltpu.SemaphoreType.DMA
    vmem, any_ = pl.BlockSpec(memory_space=pltpu.VMEM), pl.BlockSpec(memory_space=pl.ANY)

    def shape(dims, kind):
        return jax.ShapeDtypeStruct(dims, kind)
    return pl.pallas_call(
        functools.partial(forward_kernel, nt, chunks, own),
        name="forward",
        out_shape=(
            shape((own, width), BF16), shape((own, width), F32),
            shape((window, width), BF16), shape((window, width), BF16), shape((window, width), BF16),
            shape((own, width), BF16), shape((own, width), BF16),
            shape((own // BLOCK, 16, 2 * BLOCK), F32), shape((lines, width), F32),
            shape((width, width), BF16), shape((nt, chunks - 1) + pack.shape[1:], BF16),
            shape((nt,) + pack.shape[1:], BF16),
        ),
        in_specs=[vmem] * 6 + [any_],
        out_specs=(vmem,) * 10 + (any_, any_),
        scratch_shapes=[
            pltpu.VMEM((window, width), BF16),
            pltpu.VMEM((nt,) + pack.shape, BF16), pltpu.VMEM((nt,) + bias.shape, F32), dma((nt - 1,)), dma((nt - 1,)),
            pltpu.VMEM((own, width), BF16), pltpu.VMEM((width, own), BF16), pltpu.VMEM((own, width), F32),
            pltpu.VMEM((own, width), BF16), pltpu.VMEM((width, own), BF16), pltpu.VMEM((width, own), BF16),
            pltpu.VMEM((own, width), F32), pltpu.VMEM((own, width), F32),
            pltpu.VMEM((2, chunks - 1) + pack.shape[1:], BF16),
            pltpu.VMEM((own, width), F32), pltpu.VMEM((own, width), F32),
            pltpu.VMEM((own, width), BF16), pltpu.VMEM((own, width), BF16),
            dma((2,)),
            dma((chunks, nt - 1, 2)), dma((chunks, nt - 1, 2)),
            dma((chunks, nt - 1, 2, 4)), dma((chunks, nt - 1, 2, 4)),
            dma((chunks, nt - 1, 2)), dma((chunks, nt - 1, 2)), dma((2,)),
        ],
        compiler_params=pltpu.CompilerParams(
            collective_id=1, has_side_effects=True, vmem_limit_bytes=VMEM_LIMIT),
    )(tok, cot, segc, segr, vecs, bias, pack)


def backward_kernel(nt, chunks, extra,
                    result, grad_hidden, q_ref, k_ref, v_ref, normed, g_ref, stats, small1, out_g, segc, segr, vecs,
                    tok, grads, w0,
                    total, small, gathered,
                    s1, rc, ra, rb, rz, rx, rt, sr, g0, w_first, token, halo_g, halo_s, dk, dv, dq, d_t, gn, own_ig,
                    ls, cs, cr, ps, pr, zs, zr, xs, xr, fs, fr, os_, or_, ss, sm, hs, hr, lo):
    d, t, b0, b1, b2 = place()
    own, width = result.shape
    local = width // nt
    blocks = own // BLOCK
    scale = HEAD_DIM ** -0.5
    bits = (1, 2, 4) + tuple(extra)
    order = tuple(range(chunks))[::-1]
    units = [(k, s) for k in order for s in range(nt)]

    def own_copy(k, s):
        return pltpu.make_async_copy(grads.at[s, k - 1, b0], s1.at[s, k], ls.at[s, k])

    for k, s in units:
        if k > 0:
            own_copy(k, s).start()
    fetch_w = pltpu.make_async_copy(w0, w_first, lo.at[0])
    fetch_w.start()
    fetch_t = pltpu.make_async_copy(tok.at[pl.ds(HALO, own)], token, lo.at[1])
    fetch_t.start()
    greet(nt, bits, nt > 2)
    tasks = []

    def task(when, body):
        tasks.append((when, len(tasks), body))

    def core(k, s):
        source = g0.at[s, 1 - b0] if k == 0 else grads.at[s, k - 1, 1 - b0]
        return remote(source, rc.at[s, k], cs.at[s, k], cr.at[s, k], dp=flip(d, 1))

    def one(k, s, q):
        if q == 0:
            return remote(s1.at[s, k, 1 - b2, :, 0], ra.at[s, k], ps.at[s, k, 0], pr.at[s, k, 0], dp=flip(d, 4))
        return remote(s1.at[s, k, :, 1 - b1, 1], rb.at[s, k], ps.at[s, k, 1], pr.at[s, k, 1], dp=flip(d, 2))

    def two(k, s, q):
        if q == 0:
            return remote(s1.at[s, k, b2, 1 - b1, 0], rz.at[s, k, 0], ps.at[s, k, 2], pr.at[s, k, 2], dp=flip(d, 2))
        return remote(s1.at[s, k, 1 - b2, b1, 1], rz.at[s, k, 1], ps.at[s, k, 3], pr.at[s, k, 3], dp=flip(d, 4))

    def up(k, s):
        return remote(s1.at[s, k, b2, b1], rx.at[s, k], zs.at[s, k, 0], zr.at[s, k, 0], tensor=t + 1)

    def down(k, s, last):
        goal = rt.at[k] if last else rx.at[s, k]
        return remote(s1.at[s, k, b2, b1], goal, zs.at[s, k, 1], zr.at[s, k, 1], tensor=t - 1)

    def halo(n):
        if n == 0:
            return remote(g_ref.at[pl.ds(own - REACH, REACH)], halo_g.at[0, pl.ds(HALO - REACH, REACH)],
                          hs.at[0], hr.at[0], tensor=t + 1)
        if n == 1:
            return remote(g_ref.at[pl.ds(0, REACH)], halo_g.at[1, pl.ds(0, REACH)], hs.at[1], hr.at[1], tensor=t - 1)
        span = HALO // BLOCK
        if n == 2:
            return remote(stats.at[pl.ds(blocks - span, span)], halo_s.at[0], hs.at[2], hr.at[2], tensor=t + 1)
        return remote(stats.at[pl.ds(0, span)], halo_s.at[1], hs.at[3], hr.at[3], tensor=t - 1)

    def halo_start():
        @pl.when(t < nt - 1)
        def _():
            halo(0).start()
            halo(2).start()

        @pl.when(t > 0)
        def _():
            halo(1).start()
            halo(3).start()
        pad = HALO - REACH
        halo_g[0, 0:pad, :] = jnp.zeros((pad, width), BF16)
        halo_g[1, REACH:HALO, :] = jnp.zeros((pad, width), BF16)

        @pl.when(t == 0)
        def _():
            halo_g[0] = jnp.zeros((HALO, width), BF16)
            halo_s[0] = jnp.zeros(halo_s.shape[1:], F32)

        @pl.when(t == nt - 1)
        def _():
            halo_g[1] = jnp.zeros((HALO, width), BF16)
            halo_s[1] = jnp.zeros(halo_s.shape[1:], F32)

    def halo_end():
        @pl.when(t > 0)
        def _():
            halo(0).wait_recv()
            halo(2).wait_recv()

        @pl.when(t < nt - 1)
        def _():
            halo(1).wait_recv()
            halo(3).wait_recv()
    task(-20.0, halo_start)

    def attend_block(w, cols, row):
        q0 = w * BLOCK
        middle = HALO // BLOCK <= w < HALO // BLOCK + blocks
        k0, k1 = max(0, q0 - REACH), q0 + BLOCK + REACH
        if not middle:
            k0, k1 = max(k0, HALO), min(k1, HALO + own)
        q2 = stacked(q_ref[q0:q0 + BLOCK, cols])
        if middle:
            i = w - HALO // BLOCK
            g_rows = g_ref[i * BLOCK:(i + 1) * BLOCK, cols]
            lse, delta = stats[i, pl.ds(row, 1), :], stats[i, pl.ds(8 + row, 1), :]
        else:
            side = int(w > HALO // BLOCK)
            i = w if side == 0 else w - HALO // BLOCK - blocks
            g_rows = halo_g[side, i * BLOCK:(i + 1) * BLOCK, cols]
            lse, delta = halo_s[side, i, pl.ds(row, 1), :], halo_s[side, i, pl.ds(8 + row, 1), :]
        g2 = stacked(g_rows)
        k2, v2 = k_ref[k0:k1, cols], v_ref[k0:k1, cols]
        allowed = segc[k0:k1, :] == segr[:, q0:q0 + BLOCK]
        allowed = jnp.concatenate([allowed, allowed], axis=1)
        s = dot(k2, q2, NT) * scale
        p = jnp.exp(jnp.where(allowed, s - lse, -1e9))
        low = p.astype(BF16)
        ds = (p * (dot(v2, g2, NT) - delta)).astype(BF16)
        o0, o1 = max(k0, HALO), min(k1, HALO + own)
        dst, src = slice(o0 - HALO, o1 - HALO), slice(o0 - k0, o1 - k0)
        dk[dst, cols] += dot(ds[src], q2, NN)
        dv[dst, cols] += dot(low[src], g2, NN)
        if middle:
            out = dot(k2.T, ds, NN) * scale
            half = out.shape[1] // 2
            both = jnp.concatenate([out[:HEAD_DIM, :half], out[HEAD_DIM:, half:]], axis=0).astype(BF16)
            d_t[0, cols, i * BLOCK:(i + 1) * BLOCK] = both
            dq[0, i * BLOCK:(i + 1) * BLOCK, cols] = both.T

    def attention(first, count, mine):
        def pair(j, carry):
            cols = pl.ds(pl.multiple_of(j * 128, 128), 128)
            if mine:
                dk[:, cols] = jnp.zeros((own, 128), F32)
                dv[:, cols] = jnp.zeros((own, 128), F32)
                for b in range(blocks):
                    attend_block(HALO // BLOCK + b, cols, j)
            else:
                for w in tuple(range(HALO // BLOCK)) + tuple(range(HALO // BLOCK + blocks, 2 * HALO // BLOCK + blocks)):
                    attend_block(w, cols, j)
                for n, (ref, factor) in enumerate(((dk, scale), (dv, 1.0))):
                    value = (ref[:, cols] * factor).astype(BF16)
                    dq[1 + n, :, cols] = value
                    d_t[1 + n, cols, :] = value.T
            return carry
        lax.fori_loop(first, first + count, pair, 0)

    at = 0.5
    pairs = width // 128
    for first in range(0, pairs, 2):
        def run(first=first):
            attention(first, 2, True)
        task(at, run)
        at += 4.0
    at = max(at, 13.0)
    task(at, halo_end)
    for first in range(0, pairs, 2):
        def run(first=first):
            attention(first, 2, False)
        task(at, run)
        at += 3.0

    def weight_of(kind):
        return w_first[:, kind // 2, kind % 2].reshape(width, width)

    def back_project():
        fetch_w.wait()
        gn[...] = dot(dq[0], weight_of(0), NN)
        gn[...] += dot(dq[1], weight_of(1), NN)
        gn[...] += dot(dq[2], weight_of(2), NN)
    task(at, back_project)
    at += 2.5

    def norm_one():
        fetch_t.wait()
        g1 = vecs[0:1, :]

        def part(n, carry):
            rows = pl.ds(pl.multiple_of(n * 32, 32), 32)
            xhat, r = standardize(token[rows, :].astype(F32))
            grad = gn[rows, :]
            own_ig[rows, :] = (grad_hidden[rows, :] + norm_back(grad * g1, xhat, r)).astype(BF16)
            return (carry[0] + grad * xhat, carry[1] + grad, carry[2] + dq[0, rows, :].astype(F32),
                    carry[3] + dq[2, rows, :].astype(F32))
        zero = jnp.zeros((32, width), F32)
        sums = lax.fori_loop(0, own // 32, part, (zero, zero, zero, zero))
        small[...] = small1[...]
        for line, value in zip((0, 1, 6, 7), sums):
            small[line:line + 1, :] = jnp.sum(value, axis=0, keepdims=True)
        gathered[1, t] = own_ig[...]
    task(at, norm_one)
    at += 3.0
    ready = at
    for kind in range(3):
        def run(kind=kind):
            value = dot(d_t[kind], normed[...], NN).astype(BF16)
            g0[:, kind // 2, kind % 2] = value.reshape(nt, 2, 2, width // 16, width)
        task(at, run)
        at += 1.2

    def place_out():
        g0[:, 1, 1] = out_g[...].reshape(nt, 2, 2, width // 16, width)
    task(at, place_out)
    at += 0.5
    late = at

    pace = 5.4
    for n, (k, s) in enumerate(units):
        base = n * pace if k > 0 else max(n * pace, late + 4.0 + (n - nt * (chunks - 1)) * pace)

        def first(k=k, s=s):
            core(k, s).start()

        def second(k=k, s=s):
            core(k, s).wait_recv()
            if k > 0:
                own_copy(k, s).wait()
                add_bf16(s1.at[s, k], rc.at[s, k])
            else:
                s1[s, k] = (g0[s, b0].astype(F32) + rc[s, k].astype(F32)).astype(BF16)
            one(k, s, 0).start()
            one(k, s, 1).start()

        def third(k=k, s=s):
            one(k, s, 0).wait_recv()
            one(k, s, 1).wait_recv()
            add_bf16(s1.at[s, k, b2, :, 0], ra.at[s, k])
            add_bf16(s1.at[s, k, :, b1, 1], rb.at[s, k])
            two(k, s, 0).start()
            two(k, s, 1).start()

        def fourth(k=k, s=s):
            two(k, s, 0).wait_recv()
            two(k, s, 1).wait_recv()
            add_bf16(s1.at[s, k, b2, b1, 0], rz.at[s, k, 0])
            add_bf16(s1.at[s, k, b2, b1, 1], rz.at[s, k, 1])
        task(max(base - 12.0, -10.0) if k > 0 else max(base - 12.0, late + 0.01), first)
        task(base + 2.5, second)
        task(base + 8.5, third)
        task(base + 14.0, fourth)
        if s == nt - 1:
            end_of_chunk = base + 14.0
        else:
            continue

        for hop in range(nt):
            def chain(k=k, hop=hop):
                @pl.when(t == hop)
                def _():
                    for s in reversed(range(nt)):
                        @pl.when(s >= t)
                        def _():
                            if hop > 0:
                                up(k, s).wait_recv()
                                add_bf16(s1.at[s, k, b2, b1], rx.at[s, k])
                            if hop < nt - 1:
                                @pl.when(s > t)
                                def _():
                                    up(k, s).start()

                @pl.when(t == nt - 1 - hop)
                def _():
                    for s in range(nt):
                        if hop > 0:
                            @pl.when(s < t)
                            def _():
                                down(k, s, False).wait_recv()
                                add_bf16(s1.at[s, k, b2, b1], rx.at[s, k])

                            @pl.when(s == t)
                            def _():
                                down(k, s, True).wait_recv()
                                add_bf16(s1.at[s, k, b2, b1], rt.at[k])
                        if hop < nt - 1:
                            @pl.when(s == t - 1)
                            def _():
                                down(k, s, True).start()

                            @pl.when(s < t - 1)
                            def _():
                                down(k, s, False).start()
            task(end_of_chunk + 0.5 + 5.0 * hop, chain)
        base = end_of_chunk + 0.5 + 5.0 * nt

        for e, bit in enumerate(extra):
            def more(k=k, e=e, bit=bit):
                swap = remote(s1.at[t, k, b2, b1], rx.at[nt + e, k], xs.at[e, k], xr.at[e, k], dp=flip(d, bit))
                swap.start()
                swap.wait()
                add_bf16(s1.at[t, k, b2, b1], rx.at[nt + e, k])
            task(base + 0.01 * e, more)

        def settle(k=k):
            total[k, b0, b2, b1] = s1[t, k, b2, b1]

        def gone(k, q):
            if q == 0:
                return remote(total.at[k, b0, b2, b1, 0], total.at[k, b0, b2, b1, 0], fs.at[k, 0], fr.at[k, 0], dp=flip(d, 2))
            return remote(total.at[k, b0, b2, b1, 1], total.at[k, b0, b2, b1, 1], fs.at[k, 1], fr.at[k, 1], dp=flip(d, 4))

        def gtwo(k, q):
            if q == 0:
                return remote(total.at[k, b0, b2, :, 0], total.at[k, b0, b2, :, 0], fs.at[k, 2], fr.at[k, 2], dp=flip(d, 4))
            return remote(total.at[k, b0, :, b1, 1], total.at[k, b0, :, b1, 1], fs.at[k, 3], fr.at[k, 3], dp=flip(d, 2))

        def gcore(k):
            return remote(total.at[k, b0], total.at[k, b0], fs.at[k, 4], fr.at[k, 4], dp=flip(d, 1))

        def spread_one(k=k):
            for q in (0, 1):
                gone(k, q).start()

        def spread_two(k=k):
            for q in (0, 1):
                gone(k, q).wait_recv()
            for q in (0, 1):
                gtwo(k, q).start()

        def spread_core(k=k):
            for q in (0, 1):
                gtwo(k, q).wait_recv()
            gcore(k).start()

        def spread_end(k=k):
            gcore(k).wait()
            for q in (0, 1):
                gone(k, q).wait_send()
                gtwo(k, q).wait_send()
        task(base + 0.5, settle)
        task(base + 1.0, spread_one)
        task(base + 4.0, spread_two)
        task(base + 8.0, spread_core)
        task(1e6, spread_end)

    def keep_result():
        gathered[0, t] = result[...]
    task(0.2, keep_result)

    z_tasks, z_finish = relay_tasks(
        nt, 2, lambda o: (result, own_ig)[o], lambda s, o: gathered.at[o, s], (os_, or_),
        lambda o, j: (-5.0, ready)[o] + 14.0 * j + (0.01 if j == 0 else 1.0), lambda *a: None)
    tasks += [(w, 1000 + n, b) for w, n, b in z_tasks]

    exchanges = [("dp", bit) for bit in bits]
    step = 1
    while step < nt:
        exchanges.append(("tensor", step))
        step *= 2
    for e, (axis, bit) in enumerate(exchanges):
        def swap(e=e, axis=axis, bit=bit):
            goal = {axis: flip(lax.axis_index(axis), bit)}
            return remote(small, sr.at[e], ss.at[e], sm.at[e], **goal)

        def begin(swap=swap):
            swap().start()

        def end(e=e, swap=swap):
            swap().wait()
            small[...] = small[...] + sr[e]
        task(late + 1.0 + 5.0 * e, begin)
        task(late + 5.5 + 5.0 * e, end)

    ordered(tasks)
    z_finish()

    @pl.when(t < nt - 1)
    def _():
        halo(0).wait_send()
        halo(2).wait_send()

    @pl.when(t > 0)
    def _():
        halo(1).wait_send()
        halo(3).wait_send()
    for k, s in units:
        core(k, s).wait_send()
        for q in (0, 1):
            one(k, s, q).wait_send()
            two(k, s, q).wait_send()

        @pl.when(s > t)
        def _():
            up(k, s).wait_send()

        @pl.when(s < t)
        def _():
            down(k, s, False).wait_send()


def backward(result, grad_hidden, q, k, v, normed, g, stats, small1, out_g, segc, segr, vecs, tok, grads, w0, nt, extra):
    own, width = result.shape
    piece = width // 16
    chunks = grads.shape[1] + 1
    dma = pltpu.SemaphoreType.DMA
    hops = 3 + len(extra) + (nt - 1).bit_length()
    vmem, any_ = pl.BlockSpec(memory_space=pltpu.VMEM), pl.BlockSpec(memory_space=pl.ANY)
    unit = (2, 2, 2, piece, width)
    return pl.pallas_call(
        functools.partial(backward_kernel, nt, chunks, extra),
        name="backward",
        out_shape=(
            jax.ShapeDtypeStruct((chunks, 2) + unit, BF16),
            jax.ShapeDtypeStruct(small1.shape, F32),
            jax.ShapeDtypeStruct((2, nt, own, width), BF16),
        ),
        in_specs=[vmem] * 13 + [any_] * 3,
        out_specs=(vmem,) * 3,
        scratch_shapes=[
            pltpu.VMEM((nt, chunks) + unit, BF16),
            pltpu.VMEM((nt, chunks) + unit, BF16),
            pltpu.VMEM((nt, chunks, 2, piece, width), BF16),
            pltpu.VMEM((nt, chunks, 2, piece, width), BF16),
            pltpu.VMEM((nt, chunks, 2, piece, width), BF16),
            pltpu.VMEM((nt + len(extra), chunks, 2, piece, width), BF16),
            pltpu.VMEM((chunks, 2, piece, width), BF16),
            pltpu.VMEM((hops,) + small1.shape, F32),
            pltpu.VMEM((nt, 2) + unit, BF16),
            pltpu.VMEM((nt, 2) + unit, BF16),
            pltpu.VMEM((own, width), BF16),
            pltpu.VMEM((2, HALO, width), BF16),
            pltpu.VMEM((2, HALO // BLOCK) + stats.shape[1:], F32),
            pltpu.VMEM((own, width), F32), pltpu.VMEM((own, width), F32),
            pltpu.VMEM((3, own, width), BF16), pltpu.VMEM((3, width, own), BF16),
            pltpu.VMEM((own, width), F32), pltpu.VMEM((own, width), BF16),
            dma((nt, chunks)), dma((nt, chunks)), dma((nt, chunks)),
            dma((nt, chunks, 4)), dma((nt, chunks, 4)),
            dma((nt, chunks, 2)), dma((nt, chunks, 2)),
            dma((max(1, len(extra)), chunks)), dma((max(1, len(extra)), chunks)),
            dma((chunks, 5)), dma((chunks, 5)),
            dma((2, nt - 1, 2)), dma((2, nt - 1, 2)),
            dma((hops,)), dma((hops,)), dma((4,)), dma((4,)), dma((2,)),
        ],
        compiler_params=pltpu.CompilerParams(
            collective_id=2, has_side_effects=True, vmem_limit_bytes=VMEM_LIMIT),
    )(result, grad_hidden, q, k, v, normed, g, stats, small1, out_g, segc, segr, vecs, tok, grads, w0)


def body(tokens_in, segment_ids, first_gain, first_shift, qkv_weight, query_value_bias, out_weight, out_bias,
         second_gain, second_shift, up_weight, up_bias, down_weight, down_bias, cotangent):
    nt, ndp = lax.axis_size("tensor"), lax.axis_size("dp")
    t = lax.axis_index("tensor")
    length, width = tokens_in.shape
    own = length // nt
    local = qkv_weight.shape[2]
    hidden_local = up_weight.shape[1]
    start = t * own
    pack = jnp.concatenate([
        qkv_weight.transpose(0, 2, 1).reshape(3 * local, width), out_weight, up_weight, down_weight], axis=0)
    piece = width // 16
    pack = pack.reshape(-1, 2, 2, 2, 2, piece, width)
    chunks = pack.shape[0]
    padded = jnp.pad(tokens_in, ((HALO, HALO), (0, 0)))
    tokens = lax.dynamic_slice_in_dim(padded, start, own + 2 * HALO)
    segs = lax.dynamic_slice_in_dim(jnp.pad(segment_ids[0], (HALO, HALO), constant_values=-1), start, own + 2 * HALO)
    segr = segs[None, :]
    segc = jnp.broadcast_to(segs[:, None], (own + 2 * HALO, BLOCK))
    cot = lax.dynamic_slice_in_dim(cotangent, start, own)
    vecs = jnp.pad(jnp.stack([first_gain, first_shift, out_bias, second_gain, second_shift, down_bias]), ((0, 2), (0, 0)))
    bias = jnp.pad(jnp.concatenate([up_bias[None], jnp.pad(query_value_bias, ((0, 0), (0, width - local)))]), ((0, 5), (0, 0)))
    result, grad_hidden, q, k, v, normed, grad_heads, stats, small1, out_grad, mlp_grads, w_first = forward(
        tokens, cot, segc, segr, vecs, bias, pack, nt)
    extra = []
    bit = 8
    while bit < ndp:
        extra.append(bit)
        bit *= 2
    total, small, outs = backward(result, grad_hidden, q, k, v, normed, grad_heads, stats, small1, out_grad,
                                  segc, segr, vecs, tokens, mlp_grads, w_first, nt, tuple(extra))
    total = total.reshape(chunks * width, width).astype(F32) / ndp
    small = small / ndp
    up_rows = hidden_local // width
    return (
        outs[0].reshape(length, width),
        outs[1].reshape(length, width),
        small[0],
        small[1],
        total[:3 * local].reshape(3, local, width).transpose(0, 2, 1),
        lax.dynamic_slice_in_dim(small[6:8], t * local, local, axis=1),
        total[3 * local:width],
        small[2],
        small[3],
        small[4],
        total[width:2 * width],
        lax.dynamic_slice_in_dim(small, 8 + t * up_rows, up_rows).reshape(-1),
        total[2 * width:].T,
        small[5],
    )


def solution(mesh):
    placed = (
        P("dp", None), P("dp", None), P(), P(), P(None, None, "tensor"), P(None, "tensor"), P("tensor", None), P(),
        P(), P(), P(None, "tensor"), P("tensor"), P("tensor", None), P(), P("dp", None),
    )
    return jax.shard_map(
        body,
        mesh=mesh,
        in_specs=placed,
        out_specs=(
            P("dp", None), P("dp", None), P(), P(), P(None, None, "tensor"), P(None, "tensor"), P("tensor", None),
            P(), P(), P(), P(None, "tensor"), P("tensor"), P("tensor", None), P(),
        ),
        check_vma=False,
    )
```

```python
import functools

import jax
import jax.numpy as jnp
from jax import lax
from jax.experimental import pallas as pl
from jax.experimental.pallas import tpu as pltpu
from jax.sharding import PartitionSpec as P

HEAD_DIM = 64
HALO = 256
REACH = 224
BLOCK = 128
EPS = 1e-06
F32 = jnp.float32
BF16 = jnp.bfloat16
MESH = pl.DeviceIdType.MESH
VMEM_LIMIT = 60 << 20


def place():
    d, t = lax.axis_index("dp"), lax.axis_index("tensor")
    return d, t, lax.rem(d, 2), lax.rem(d // 2, 2), lax.rem(d // 4, 2)


def flip(d, value):
    return d + value * (1 - 2 * lax.rem(d // value, 2))


def remote(src, dst, send, recv, **axis):
    return pltpu.make_async_remote_copy(
        src_ref=src, dst_ref=dst, send_sem=send, recv_sem=recv,
        device_id=axis, device_id_type=MESH)


def greet(nt, bits, far=False):
    d, t = lax.axis_index("dp"), lax.axis_index("tensor")
    barrier = pltpu.get_barrier_semaphore()

    @pl.when(t > 0)
    def _():
        pl.semaphore_signal(barrier, inc=1, device_id={"tensor": t - 1}, device_id_type=MESH)

    @pl.when(t < nt - 1)
    def _():
        pl.semaphore_signal(barrier, inc=1, device_id={"tensor": t + 1}, device_id_type=MESH)

    for bit in bits:
        pl.semaphore_signal(barrier, inc=1, device_id={"dp": flip(d, bit)}, device_id_type=MESH)
    if far:
        pl.semaphore_signal(barrier, inc=1, device_id={"tensor": flip(t, 2)}, device_id_type=MESH)
    peers = len(bits) + int(far) + (t > 0).astype(jnp.int32) + (t < nt - 1).astype(jnp.int32)
    pl.semaphore_wait(barrier, peers)


def ordered(tasks):
    for _, _, task in sorted(tasks, key=lambda item: item[:2]):
        task()


def relay_tasks(nt, chunks, own, full, sems, start, arrived):
    send, recv = sems
    tasks = []
    t = lax.axis_index("tensor")
    for k in range(chunks):
        for j in range(nt):
            def step(k=k, j=j):
                for way in (0, 1):
                    sign = 1 - 2 * way
                    shard = t - sign * j
                    inside = (shard >= 0) & (shard < nt)
                    if j > 0:
                        @pl.when(inside)
                        def _():
                            remote(full(shard, k), full(shard, k), send.at[k, j - 1, way], recv.at[k, j - 1, way],
                                   tensor=t).wait_recv()
                            arrived(k, j, way, shard)
                    if j < nt - 1:
                        goal = t + sign
                        @pl.when(inside & (goal >= 0) & (goal < nt))
                        def _():
                            source = own(k) if j == 0 else full(shard, k)
                            remote(source, full(shard, k), send.at[k, j, way], recv.at[k, j, way],
                                   tensor=goal).start()
            tasks.append((start(k, j), len(tasks), step))

    def finish():
        for k in range(chunks):
            for j in range(nt - 1):
                for way in (0, 1):
                    sign = 1 - 2 * way
                    shard, goal = t - sign * j, t + sign
                    @pl.when((shard >= 0) & (shard < nt) & (goal >= 0) & (goal < nt))
                    def _():
                        source = own(k) if j == 0 else full(shard, k)
                        remote(source, full(shard, k), send.at[k, j, way], recv.at[k, j, way],
                               tensor=goal).wait_send()
    return tasks, finish


def add_bf16(ref, other):
    ref[...] = (ref[...].astype(F32) + other[...].astype(F32)).astype(BF16)


def stacked(pair):
    lane = lax.broadcasted_iota(jnp.int32, pair.shape, 1)
    zero = jnp.zeros_like(pair)
    return jnp.concatenate([jnp.where(lane < HEAD_DIM, pair, zero), jnp.where(lane < HEAD_DIM, zero, pair)], axis=0)


def dot(a, b, dims):
    return lax.dot_general(a, b, (dims, ((), ())), preferred_element_type=F32)


NN = ((1,), (0,))
NT = ((1,), (1,))


def untangle(both):
    half = both.shape[1] // 2
    return jnp.concatenate([both[:HEAD_DIM, :half], both[HEAD_DIM:, half:]], axis=0).T


def standardize(rows):
    center = rows - jnp.mean(rows, axis=-1, keepdims=True)
    r = lax.rsqrt(jnp.mean(center * center, axis=-1, keepdims=True) + EPS)
    return center * r, r


def norm_back(e, xhat, r):
    return r * (e - jnp.mean(e, axis=-1, keepdims=True) - xhat * jnp.mean(e * xhat, axis=-1, keepdims=True))


def window_segments(segments, padded, row, column):
    length, window = segments.shape[1], row.shape[1]
    padded[...] = jnp.full(padded.shape, -1, jnp.int32)
    padded[:, HALO:HALO + length] = segments[...]
    own = window - 2 * HALO
    for i in range(window // BLOCK):
        first = pl.multiple_of(lax.axis_index("tensor") * own + i * BLOCK, BLOCK)
        line = padded[:, pl.ds(first, BLOCK)]
        row[:, i * BLOCK:(i + 1) * BLOCK] = line
        column[i * BLOCK:(i + 1) * BLOCK, :] = jnp.broadcast_to(line, (BLOCK, BLOCK)).T


def nearest(nt):
    return [sorted(range(nt), key=lambda s: (abs(s - p), s if p < nt // 2 else -s)) for p in range(nt)]


def pick(table, position):
    t = lax.axis_index("tensor")
    return sum((t == p).astype(jnp.int32) * row[position] for p, row in enumerate(table))


def gelu_parts(x):
    cdf = 0.5 * (1.0 + lax.erf(x * (0.5 ** 0.5)))
    pdf = jnp.exp(-0.5 * x * x) * ((2.0 * jnp.pi) ** -0.5)
    return x * cdf, cdf + x * pdf


LINE, PLANE, LEAD, LAGS = 3.5, 0.0, 0.0, (6.0, 12.0, 16.0)


def forward_kernel(nt, chunks, own,
                   tokens_in, cotangent, segments, gain_1, shift_1, qkv_in, qv_bias, out_in, out_bias, gain_2, shift_2,
                   up_in, up_bias, down_in, down_bias,
                   result, hidden, q_ref, k_ref, v_ref, normed_own, heads_t, gtwo, lse_ref, small, grads, w0,
                   tok, cot, segp, segr, segc, bias, normed, w, bias_all, bias_sem, bias_recv, heads, normed_two, n2t,
                   cot_t, mlp, gbuf, pre_s, gact_s, act, gpre, gsem, zs, zr, ps, pr, cs, cr, ls):
    d, t, b0, b1, b2 = place()
    window, width = tok.shape
    local = width // nt
    blocks = own // BLOCK
    local_copies = [
        pltpu.make_async_copy(out_in, w.at[t, 0, 1, 1], ls.at[0]),
        pltpu.make_async_copy(up_in, w.at[t, 1], ls.at[1]),
        pltpu.make_async_copy(down_in, w.at[t, 2], ls.at[2]),
    ]
    for copy in local_copies:
        copy.start()
    cot_copy = pltpu.make_async_copy(cotangent.at[pl.ds(pl.multiple_of(t * own, own), own)], cot, ls.at[3])
    cot_copy.start()

    def token_copy(place):
        rows = own + HALO
        if place == 0:
            return pltpu.make_async_copy(tokens_in.at[pl.ds(0, rows)], tok.at[pl.ds(HALO, rows)], ls.at[4])
        if place == 1:
            return pltpu.make_async_copy(tokens_in.at[pl.ds((nt - 1) * own - HALO, rows)], tok.at[pl.ds(0, rows)], ls.at[4])
        first = pl.multiple_of(t * own - HALO, BLOCK)
        return pltpu.make_async_copy(tokens_in.at[pl.ds(first, window)], tok, ls.at[4])

    def tokens(act):
        @pl.when(t == 0)
        def _():
            act(token_copy(0))

        @pl.when(t == nt - 1)
        def _():
            act(token_copy(1))

        @pl.when((t > 0) & (t < nt - 1))
        def _():
            act(token_copy(2))
    tokens(lambda copy: copy.start())

    @pl.when(t == 0)
    def _():
        tok[0:HALO, :] = jnp.zeros((HALO, width), BF16)

    @pl.when(t == nt - 1)
    def _():
        tok[window - HALO:window, :] = jnp.zeros((HALO, width), BF16)

    barrier = pltpu.get_barrier_semaphore()
    for bit in (1, 2, 4):
        pl.semaphore_signal(barrier, inc=1, device_id={"dp": flip(d, bit)}, device_id_type=MESH)
    for j in range(1, nt):
        pl.semaphore_signal(barrier, inc=1, device_id={"tensor": lax.rem(t + j, nt)}, device_id_type=MESH)
    for kind in range(3):
        w[t, 0, kind // 2, kind % 2] = qkv_in[kind].T.reshape(2, 2, width // 16, width)
    bias[...] = jnp.zeros(bias.shape, F32)
    bias[0:1, :] = up_bias[...].reshape(1, width)
    bias[1:3, 0:local] = qv_bias[...]
    bias_all[t] = bias[...]
    window_segments(segments, segp, segr, segc)
    for copy in local_copies:
        copy.wait()
    pl.semaphore_wait(barrier, 3 + nt - 1)
    tasks = []

    def task(when, body):
        tasks.append((when, len(tasks), body))

    def bias_send(j):
        return remote(bias, bias_all.at[t], bias_sem.at[j], bias_recv.at[j], tensor=lax.rem(t + j + 1, nt))

    def bias_get(j):
        source = lax.rem(t + nt - j - 1, nt)
        return remote(bias, bias_all.at[source], bias_sem.at[j], bias_recv.at[j], tensor=source)

    def one(shard, k, q, way, j):
        if q == 0:
            mine = w.at[shard, k, b0, b2, b1, 0]
            return remote(mine, mine, ps.at[k, j, way, 0], pr.at[k, j, way, 0], dp=flip(d, 2))
        mine = w.at[shard, k, b0, b2, b1, 1]
        return remote(mine, mine, ps.at[k, j, way, 1], pr.at[k, j, way, 1], dp=flip(d, 4))

    def two(shard, k, q, way, j):
        if q == 0:
            mine = w.at[shard, k, b0, b2, :, 0]
            return remote(mine, mine, ps.at[k, j, way, 2], pr.at[k, j, way, 2], dp=flip(d, 4))
        mine = w.at[shard, k, b0, :, b1, 1]
        return remote(mine, mine, ps.at[k, j, way, 3], pr.at[k, j, way, 3], dp=flip(d, 2))

    def core(shard, k, way, j):
        return remote(w.at[shard, k, b0], w.at[shard, k, b0], cs.at[k, j, way], cr.at[k, j, way], dp=flip(d, 1))

    def each(k, j, act):
        for way in (0, 1):
            shard = t - (1 - 2 * way) * (j + 1)

            @pl.when((shard >= 0) & (shard < nt))
            def _():
                act(shard, k, way, j)

    def line_time(k, j):
        return LINE * (k * (nt - 1) + j)

    z_tasks, z_finish = relay_tasks(
        nt, chunks, lambda k: w.at[t, k, b0, b2, b1], lambda s, k: w.at[s, k, b0, b2, b1], (zs, zr),
        line_time, lambda *a: None)
    tasks += z_tasks
    ready_at = {}
    for k in range(chunks):
        for j in range(nt - 1):
            def begin(k=k, j=j):
                def act(shard, k, way, j):
                    for q in (0, 1):
                        one(shard, k, q, way, j).start()
                each(k, j, act)

            def second(k=k, j=j):
                def act(shard, k, way, j):
                    for q in (0, 1):
                        one(shard, k, q, way, j).wait_recv()
                    for q in (0, 1):
                        two(shard, k, q, way, j).start()
                each(k, j, act)

            def third(k=k, j=j):
                def act(shard, k, way, j):
                    for q in (0, 1):
                        two(shard, k, q, way, j).wait_recv()
                    core(shard, k, way, j).start()
                each(k, j, act)

            def fourth(k=k, j=j):
                def act(shard, k, way, j):
                    core(shard, k, way, j).wait_recv()
                each(k, j, act)
            n = k * (nt - 1) + j
            base = max(line_time(k, j + 1) + 0.1, LEAD + PLANE * n)
            task(base, begin)
            task(base + LAGS[0], second)
            task(base + LAGS[1], third)
            task(base + LAGS[2], fourth)
            ready_at[k, j] = base + LAGS[2] + 0.1

    def bias_begin():
        for j in range(nt - 1):
            bias_send(j).start()

    def bias_end():
        for j in range(nt - 1):
            bias_get(j).wait_recv()
    task(0.2, bias_begin)
    task(10.0, bias_end)

    g1, s1, ob, g2, s2, db = (ref[...].reshape(1, width) for ref in (gain_1, shift_1, out_bias, gain_2, shift_2, down_bias))

    def tokens_here():
        tokens(lambda copy: copy.wait())
    task(0.4, tokens_here)
    for i in range(window // BLOCK):
        def norm_rows(i=i):
            def part(n, carry):
                rows = pl.ds(pl.multiple_of(i * BLOCK + n * 32, 32), 32)
                xhat, _ = standardize(tok[rows, :].astype(F32))
                normed[rows, :] = (xhat * g1 + s1).astype(BF16)
                return carry
            lax.fori_loop(0, BLOCK // 32, part, 0)
        task(0.5 + 0.7 * i, norm_rows)

    def transposes():
        normed_own[...] = normed[HALO:HALO + own, :]
        cot_copy.wait()
        cot_t[...] = cot[...].T
        small[5:6, :] = jnp.sum(cot[...].astype(F32), axis=0, keepdims=True)
    task(6.0, transposes)

    half_rows = window // 2
    group = 2 * local

    def project(u, kind, part):
        rows = slice(part * half_rows, (part + 1) * half_rows)
        weight = w[pl.ds(2 * u, 2), 0, kind // 2, kind % 2].reshape(group, width)
        out = dot(normed[rows, :], weight, NT)
        if kind != 1:
            line = 1 + kind // 2
            out = out + jnp.concatenate([bias_all[2 * u, line:line + 1, :local], bias_all[2 * u + 1, line:line + 1, :local]], axis=1)
        target = (q_ref, k_ref, v_ref)[kind]
        target[rows, pl.ds(pl.multiple_of(u * group, 128), group)] = out.astype(BF16)

    def attention(u, b):
        first, count = BLOCK * b + 32, BLOCK + 448
        q0 = HALO + BLOCK * b
        allowed = segc[first:first + count, :] == segr[:, q0:q0 + BLOCK]
        allowed = jnp.concatenate([allowed, allowed], axis=1)

        def pair(j, carry):
            at = u * (group // 128) + j
            cols = pl.ds(pl.multiple_of(at * 128, 128), 128)
            q2 = stacked(q_ref[q0:q0 + BLOCK, cols])
            k2 = k_ref[first:first + count, cols]
            v2 = v_ref[first:first + count, cols]
            s = dot(k2, q2, NT) * (HEAD_DIM ** -0.5)
            s = jnp.where(allowed, s, -1e9)
            m = jnp.max(s, axis=0, keepdims=True)
            p = jnp.exp(s - m)
            l = jnp.sum(p, axis=0, keepdims=True)
            low = (p * (1.0 / l)).astype(BF16)
            out = dot(v2.T, low, NN)
            half = out.shape[1] // 2
            both = jnp.concatenate([out[:HEAD_DIM, :half], out[HEAD_DIM:, half:]], axis=0).astype(BF16)
            heads_t[cols, b * BLOCK:(b + 1) * BLOCK] = both
            heads[b * BLOCK:(b + 1) * BLOCK, cols] = both.T
            lse_ref[b, pl.ds(at, 1), :] = m + jnp.log(l)
            return carry
        lax.fori_loop(0, group // 128, pair, 0)

    def out_project(u, fresh):
        weight = w[pl.ds(2 * u, 2), 0, 1, 1].reshape(group, width)
        part = dot(heads[:, pl.ds(pl.multiple_of(u * group, 128), group)], weight, NN)
        if fresh:
            hidden[...] = part
        else:
            hidden[...] += part

    first_half = t // 2
    at = 7.0
    for n in range(nt // 2):
        u = lax.rem(first_half + n, nt // 2)
        if n == 0:
            at = max(at, ready_at[0, 0])
        else:
            at = max(at, ready_at[0, nt - 2])
        for kind in range(3):
            for part in range(2):
                def run(u=u, kind=kind, part=part):
                    project(u, kind, part)
                task(at, run)
                at += 0.7
        for b in range(blocks):
            def run(u=u, b=b):
                attention(u, b)
            task(at, run)
            at += 3.0

        def run(u=u, n=n):
            out_project(u, n == 0)
        task(at, run)
        at += 0.6

    def rows_of(i):
        return slice(i * BLOCK, (i + 1) * BLOCK)

    for i in range(blocks):
        def norm_two(i=i):
            rows = rows_of(i)
            token = tok[HALO + i * BLOCK:HALO + (i + 1) * BLOCK, :].astype(F32)
            whole = hidden[rows, :] + token + ob
            hidden[rows, :] = whole
            xhat, _ = standardize(whole)
            low = (xhat * g2 + s2).astype(BF16)
            normed_two[rows, :] = low
            n2t[:, rows] = low.T
        task(at, norm_two)
        at += 0.7

    table = nearest(nt)
    slab = 32

    def grads_out(slot, shard):
        return pltpu.make_async_copy(gbuf.at[slot], grads.at[shard], gsem.at[slot])

    def mlp_shard(position, shard):
        slot = position % 2
        up = w[shard, 1].reshape(width, width)
        down = w[shard, 2].reshape(width, width)
        pre_s[...] = dot(normed_two[...], up, NN) + bias_all[shard, 0:1, :]
        gact_s[...] = dot(cot[...], down, NT)

        def step(i, total):
            rows = pl.ds(pl.multiple_of(i * slab, slab), slab)
            value, slope = gelu_parts(pre_s[rows, :])
            act[rows, :] = value.astype(BF16)
            low = (gact_s[rows, :] * slope).astype(BF16)
            gpre[rows, :] = low
            return total + low.astype(F32)
        total = lax.fori_loop(0, own // slab, step, jnp.zeros((slab, width), F32))
        small[pl.ds(8 + shard, 1), :] = jnp.sum(total, axis=0, keepdims=True)
        if position == 0:
            mlp[...] = dot(act[...], down, NN)
            gtwo[...] = dot(gpre[...], up, NT)
        else:
            mlp[...] += dot(act[...], down, NN)
            gtwo[...] += dot(gpre[...], up, NT)
        if position >= 2:
            grads_out(slot, shard).wait()
        shape = gbuf.shape[2:]
        gbuf[slot, 0] = dot(n2t[...], gpre[...], NN).astype(BF16).reshape(shape)
        gbuf[slot, 1] = dot(cot_t[...], act[...], NN).astype(BF16).reshape(shape)
        grads_out(slot, shard).start()

    for position in range(nt):
        def run(position=position):
            mlp_shard(position, pick(table, position))
        if position > 0:
            at = max([at] + [ready_at[k, position - 1] for k in range(1, chunks)])
        task(at, run)
        at += 6.0

    def finish():
        def part(n, carry):
            rows = pl.ds(pl.multiple_of(n * 32, 32), 32)
            result[rows, :] = (hidden[rows, :] + mlp[rows, :] + db).astype(BF16)
            return carry
        lax.fori_loop(0, own // 32, part, 0)
    task(at, finish)

    def keep_copy():
        return pltpu.make_async_copy(w.at[:, 0], w0, ls.at[0])

    def keep_first():
        keep_copy().start()
    task(at - 10.0, keep_first)
    ordered(tasks)
    grads_out(0, 0).wait()
    grads_out(1, 0).wait()
    keep_copy().wait()
    for n in (0, 1, 2, 3, 4, 6, 7):
        small[n:n + 1, :] = jnp.zeros((1, width), F32)
    if small.shape[0] > 8 + nt:
        small[8 + nt:, :] = jnp.zeros((small.shape[0] - 8 - nt, width), F32)
    z_finish()
    for j in range(nt - 1):
        bias_send(j).wait_send()
    for k in range(chunks):
        for j in range(nt - 1):
            def end(shard, k, way, j):
                core(shard, k, way, j).wait_send()
                for q in (0, 1):
                    one(shard, k, q, way, j).wait_send()
                    two(shard, k, q, way, j).wait_send()
            each(k, j, end)


def forward(arrays, nt):
    length, width = arrays[0].shape
    own = length // nt
    window = own + 2 * HALO
    piece = width // 16
    unit = (2, 2, 2, 2, piece, width)
    rows = width + 2 * arrays[12].shape[0]
    chunks = rows // (16 * piece)
    lines = 8 + nt + -nt % 8
    dma = pltpu.SemaphoreType.DMA
    vmem, any_ = pl.BlockSpec(memory_space=pltpu.VMEM), pl.BlockSpec(memory_space=pl.ANY)

    def shape(dims, kind):
        return jax.ShapeDtypeStruct(dims, kind)

    def low(*dims):
        return pltpu.VMEM(dims, BF16)

    def wide(*dims):
        return pltpu.VMEM(dims, F32)
    views = list(arrays)
    for n in (7, 11, 13):
        views[n] = arrays[n].reshape(unit[2:] if n == 7 else unit)
    return pl.pallas_call(
        functools.partial(forward_kernel, nt, chunks, own),
        name="forward",
        out_shape=(
            shape((own, width), BF16), shape((own, width), F32),
            shape((window, width), BF16), shape((window, width), BF16), shape((window, width), BF16),
            shape((own, width), BF16), shape((width, own), BF16), shape((own, width), F32),
            shape((own // BLOCK, 8, 2 * BLOCK), F32), shape((lines, width), F32),
            shape((nt, chunks - 1) + unit, BF16), shape((nt,) + unit, BF16),
        ),
        in_specs=[any_, any_] + [vmem] * 5 + [any_] + [vmem] * 3 + [any_, vmem, any_, vmem],
        out_specs=(vmem,) * 10 + (any_, any_),
        scratch_shapes=[
            low(window, width), low(own, width), pltpu.VMEM((1, length + 2 * HALO), jnp.int32),
            pltpu.VMEM((1, window), jnp.int32), pltpu.VMEM((window, BLOCK), jnp.int32), wide(8, width),
            low(window, width), low(nt, chunks, *unit), wide(nt, 8, width), dma((nt - 1,)), dma((nt - 1,)),
            low(own, width), low(own, width), low(width, own), low(width, own), wide(own, width),
            low(2, chunks - 1, *unit), wide(own, width), wide(own, width), low(own, width), low(own, width),
            dma((2,)),
            dma((chunks, nt - 1, 2)), dma((chunks, nt - 1, 2)),
            dma((chunks, nt - 1, 2, 4)), dma((chunks, nt - 1, 2, 4)),
            dma((chunks, nt - 1, 2)), dma((chunks, nt - 1, 2)), dma((5,)),
        ],
        compiler_params=pltpu.CompilerParams(
            collective_id=1, has_side_effects=True, vmem_limit_bytes=VMEM_LIMIT),
    )(*views)


PIECES = 2
PACE, STEPS, HOP = 5.4, (2.5, 8.5, 14.0), 5.0


def backward_kernel(nt, chunks, extra,
                    result, hidden, q_ref, k_ref, v_ref, normed, heads_t, gtwo, lse_ref, small1, segments, gain_1, gain_2,
                    cotangent, tokens_in, grads, w0,
                    total, small, gathered_r, gathered_g,
                    s1, rc, ra, rb, rz, rx, rt, sr, g0, w_first, token, cot, segp, segr, segc, branch, g_ref, stats,
                    halo_g, halo_s, dk, dv, dq, d_t, gtwo_out, own_ig,
                    ls, cs, cr, ps, pr, zs, zr, xs, xr, fs, fr, os_, or_, ss, sm, hs, hr, lo):
    d, t, b0, b1, b2 = place()
    own, width = result.shape
    blocks = own // BLOCK
    scale = HEAD_DIM ** -0.5
    gathered = (gathered_r, gathered_g)
    bits = (1, 2, 4) + tuple(extra)
    order = tuple(range(chunks))[::-1]
    units = [(k, s) for k in order for s in range(nt)]

    def own_copy(k, s):
        return pltpu.make_async_copy(grads.at[s, k - 1, b0], s1.at[s, k], ls.at[s, k])

    for k, s in units:
        if k > 0:
            own_copy(k, s).start()
    fetch_w = pltpu.make_async_copy(w0, w_first, lo.at[0])
    fetch_w.start()
    mine = pl.ds(pl.multiple_of(t * own, own), own)
    fetch_t = pltpu.make_async_copy(tokens_in.at[mine], token, lo.at[1])
    fetch_t.start()
    fetch_c = pltpu.make_async_copy(cotangent.at[mine], cot, lo.at[2])
    fetch_c.start()
    window_segments(segments, segp, segr, segc)
    greet(nt, bits, nt > 2)
    tasks = []

    def task(when, body):
        tasks.append((when, len(tasks), body))

    def core(k, s):
        source = g0.at[s, 1 - b0] if k == 0 else grads.at[s, k - 1, 1 - b0]
        return remote(source, rc.at[s, k], cs.at[s, k], cr.at[s, k], dp=flip(d, 1))

    def one(k, s, q):
        if q == 0:
            return remote(s1.at[s, k, 1 - b2, :, 0], ra.at[s, k], ps.at[s, k, 0], pr.at[s, k, 0], dp=flip(d, 4))
        return remote(s1.at[s, k, :, 1 - b1, 1], rb.at[s, k], ps.at[s, k, 1], pr.at[s, k, 1], dp=flip(d, 2))

    def two(k, s, q):
        if q == 0:
            return remote(s1.at[s, k, b2, 1 - b1, 0], rz.at[s, k, 0], ps.at[s, k, 2], pr.at[s, k, 2], dp=flip(d, 2))
        return remote(s1.at[s, k, 1 - b2, b1, 1], rz.at[s, k, 1], ps.at[s, k, 3], pr.at[s, k, 3], dp=flip(d, 4))

    def up(k, s):
        return remote(s1.at[s, k, b2, b1], rx.at[s, k], zs.at[s, k, 0], zr.at[s, k, 0], tensor=t + 1)

    def down(k, s, last):
        goal = rt.at[k] if last else rx.at[s, k]
        return remote(s1.at[s, k, b2, b1], goal, zs.at[s, k, 1], zr.at[s, k, 1], tensor=t - 1)

    def halo(n):
        if n == 0:
            return remote(g_ref.at[pl.ds(own - REACH, REACH)], halo_g.at[0, pl.ds(HALO - REACH, REACH)],
                          hs.at[0], hr.at[0], tensor=t + 1)
        if n == 1:
            return remote(g_ref.at[pl.ds(0, REACH)], halo_g.at[1, pl.ds(0, REACH)], hs.at[1], hr.at[1], tensor=t - 1)
        span = HALO // BLOCK
        if n == 2:
            return remote(stats.at[pl.ds(blocks - span, span)], halo_s.at[0], hs.at[2], hr.at[2], tensor=t + 1)
        return remote(stats.at[pl.ds(0, span)], halo_s.at[1], hs.at[3], hr.at[3], tensor=t - 1)

    def halo_start():
        @pl.when(t < nt - 1)
        def _():
            halo(0).start()
            halo(2).start()

        @pl.when(t > 0)
        def _():
            halo(1).start()
            halo(3).start()
        pad = HALO - REACH
        halo_g[0, 0:pad, :] = jnp.zeros((pad, width), BF16)
        halo_g[1, REACH:HALO, :] = jnp.zeros((pad, width), BF16)

        @pl.when(t == 0)
        def _():
            halo_g[0] = jnp.zeros((HALO, width), BF16)
            halo_s[0] = jnp.zeros(halo_s.shape[1:], F32)

        @pl.when(t == nt - 1)
        def _():
            halo_g[1] = jnp.zeros((HALO, width), BF16)
            halo_s[1] = jnp.zeros(halo_s.shape[1:], F32)

    def halo_end():
        @pl.when(t > 0)
        def _():
            halo(0).wait_recv()
            halo(2).wait_recv()

        @pl.when(t < nt - 1)
        def _():
            halo(1).wait_recv()
            halo(3).wait_recv()

    def attend_block(w, cols, row):
        q0 = w * BLOCK
        middle = HALO // BLOCK <= w < HALO // BLOCK + blocks
        k0, k1 = max(0, q0 - REACH), q0 + BLOCK + REACH
        if not middle:
            k0, k1 = max(k0, HALO), min(k1, HALO + own)
        q2 = stacked(q_ref[q0:q0 + BLOCK, cols])
        if middle:
            i = w - HALO // BLOCK
            g_rows = g_ref[i * BLOCK:(i + 1) * BLOCK, cols]
            lse, delta = stats[i, pl.ds(row, 1), :], stats[i, pl.ds(8 + row, 1), :]
        else:
            side = int(w > HALO // BLOCK)
            i = w if side == 0 else w - HALO // BLOCK - blocks
            g_rows = halo_g[side, i * BLOCK:(i + 1) * BLOCK, cols]
            lse, delta = halo_s[side, i, pl.ds(row, 1), :], halo_s[side, i, pl.ds(8 + row, 1), :]
        g2 = stacked(g_rows)
        k2, v2 = k_ref[k0:k1, cols], v_ref[k0:k1, cols]
        allowed = segc[k0:k1, :] == segr[:, q0:q0 + BLOCK]
        allowed = jnp.concatenate([allowed, allowed], axis=1)
        s = dot(k2, q2, NT) * scale
        p = jnp.exp(jnp.where(allowed, s - lse, -1e9))
        low = p.astype(BF16)
        ds = (p * (dot(v2, g2, NT) - delta)).astype(BF16)
        o0, o1 = max(k0, HALO), min(k1, HALO + own)
        dst, src = slice(o0 - HALO, o1 - HALO), slice(o0 - k0, o1 - k0)
        dk[dst, cols] += dot(ds[src], q2, NN)
        dv[dst, cols] += dot(low[src], g2, NN)
        if middle:
            out = dot(k2.T, ds, NN) * scale
            half = out.shape[1] // 2
            both = jnp.concatenate([out[:HEAD_DIM, :half], out[HEAD_DIM:, half:]], axis=0).astype(BF16)
            d_t[0, cols, i * BLOCK:(i + 1) * BLOCK] = both
            dq[0, i * BLOCK:(i + 1) * BLOCK, cols] = both.T

    def attention(first, count, mine):
        def pair(j, carry):
            cols = pl.ds(pl.multiple_of(j * 128, 128), 128)
            if mine:
                dk[:, cols] = jnp.zeros((own, 128), F32)
                dv[:, cols] = jnp.zeros((own, 128), F32)
                for b in range(blocks):
                    attend_block(HALO // BLOCK + b, cols, j)
            else:
                for w in tuple(range(HALO // BLOCK)) + tuple(range(HALO // BLOCK + blocks, 2 * HALO // BLOCK + blocks)):
                    attend_block(w, cols, j)
                for n, (ref, factor) in enumerate(((dk, scale), (dv, 1.0))):
                    value = (ref[:, cols] * factor).astype(BF16)
                    dq[1 + n, :, cols] = value
                    d_t[1 + n, cols, :] = value.T
            return carry
        lax.fori_loop(first, first + count, pair, 0)

    g1, g2 = gain_1[...].reshape(1, width), gain_2[...].reshape(1, width)

    def norm_two_back():
        fetch_c.wait()

        def part(n, carry):
            rows = pl.ds(pl.multiple_of(n * 32, 32), 32)
            xhat, r = standardize(hidden[rows, :])
            grad = gtwo[rows, :]
            gh = cot[rows, :].astype(F32) + norm_back(grad * g2, xhat, r)
            gtwo_out[rows, :] = gh
            branch[rows, :] = gh.astype(BF16)
            return carry[0] + gh, carry[1] + grad * xhat, carry[2] + grad
        zero = jnp.zeros((32, width), F32)
        sums = lax.fori_loop(0, own // 32, part, (zero, zero, zero))
        small[...] = small1[...]
        for line, value in zip((2, 3, 4), sums):
            small[line:line + 1, :] = jnp.sum(value, axis=0, keepdims=True)

    def out_back():
        fetch_w.wait()
        outw = w_first[:, 1, 1].reshape(width, width)
        rows = branch[...]
        g_ref[...] = dot(rows, outw, NT).astype(BF16)
        g_t = dot(outw, rows, NT).astype(BF16).astype(F32)
        product = g_t * heads_t[...].astype(F32)
        for b in range(blocks):
            stats[b, 0:8, :] = lse_ref[b]
            for h in range(width // HEAD_DIM):
                line = jnp.sum(product[h * HEAD_DIM:(h + 1) * HEAD_DIM, b * BLOCK:(b + 1) * BLOCK], axis=0, keepdims=True)
                stats[b, 8 + h // 2:9 + h // 2, (h % 2) * BLOCK:(h % 2 + 1) * BLOCK] = line
            stats[b, 8 + width // 128:16, :] = jnp.zeros((8 - width // 128, 2 * BLOCK), F32)

    def out_grad():
        value = dot(heads_t[...], branch[...], NN).astype(BF16)
        g0[:, 1, 1] = value.reshape((nt,) + g0.shape[3:])
    task(0.3, norm_two_back)
    task(3.0, out_back)
    task(5.5, halo_start)
    task(6.0, out_grad)
    at = 7.0
    pairs = width // 128
    for first in range(0, pairs, 2):
        def run(first=first):
            attention(first, 2, True)
        task(at, run)
        at += 4.0
    at = max(at, 24.0)
    task(at, halo_end)
    for first in range(0, pairs, 2):
        def run(first=first):
            attention(first, 2, False)
        task(at, run)
        at += 3.0

    def weight_of(kind):
        return w_first[:, kind // 2, kind % 2].reshape(width, width)

    def back_project():
        dk[...] = dot(dq[0], weight_of(0), NN)
        dk[...] += dot(dq[1], weight_of(1), NN)
        dk[...] += dot(dq[2], weight_of(2), NN)
    task(at, back_project)
    at += 2.5

    def norm_one():
        fetch_t.wait()

        def part(n, carry):
            rows = pl.ds(pl.multiple_of(n * 32, 32), 32)
            xhat, r = standardize(token[rows, :].astype(F32))
            grad = dk[rows, :]
            own_ig[rows, :] = (gtwo_out[rows, :] + norm_back(grad * g1, xhat, r)).astype(BF16)
            return (carry[0] + grad * xhat, carry[1] + grad, carry[2] + dq[0, rows, :].astype(F32),
                    carry[3] + dq[2, rows, :].astype(F32))
        zero = jnp.zeros((32, width), F32)
        sums = lax.fori_loop(0, own // 32, part, (zero, zero, zero, zero))
        for line, value in zip((0, 1, 6, 7), sums):
            small[line:line + 1, :] = jnp.sum(value, axis=0, keepdims=True)
        gathered_g[t] = own_ig[...]
    task(at, norm_one)
    at += 3.0
    ready = at
    for kind in range(3):
        def run(kind=kind):
            value = dot(d_t[kind], normed[...], NN).astype(BF16)
            g0[:, kind // 2, kind % 2] = value.reshape((nt,) + g0.shape[3:])
        task(at, run)
        at += 1.2

    late = at

    pace = PACE
    for n, (k, s) in enumerate(units):
        base = n * pace if k > 0 else max(n * pace, late + 3.0 + (n - nt * (chunks - 1)) * pace)

        def first(k=k, s=s):
            core(k, s).start()

        def second(k=k, s=s):
            core(k, s).wait_recv()
            if k > 0:
                own_copy(k, s).wait()
                add_bf16(s1.at[s, k], rc.at[s, k])
            else:
                s1[s, k] = (g0[s, b0].astype(F32) + rc[s, k].astype(F32)).astype(BF16)
            one(k, s, 0).start()
            one(k, s, 1).start()

        def third(k=k, s=s):
            one(k, s, 0).wait_recv()
            one(k, s, 1).wait_recv()
            add_bf16(s1.at[s, k, b2, :, 0], ra.at[s, k])
            add_bf16(s1.at[s, k, :, b1, 1], rb.at[s, k])
            two(k, s, 0).start()
            two(k, s, 1).start()

        def fourth(k=k, s=s):
            two(k, s, 0).wait_recv()
            two(k, s, 1).wait_recv()
            add_bf16(s1.at[s, k, b2, b1, 0], rz.at[s, k, 0])
            add_bf16(s1.at[s, k, b2, b1, 1], rz.at[s, k, 1])
        task(max(base - 12.0, -10.0) if k > 0 else max(base - 12.0, late + 0.01), first)
        task(base + STEPS[0], second)
        task(base + STEPS[1], third)
        task(base + STEPS[2], fourth)
        if s == nt - 1:
            end_of_chunk = base + STEPS[2]
        else:
            continue

        for hop in range(nt):
            def chain(k=k, hop=hop):
                @pl.when(t == hop)
                def _():
                    for s in reversed(range(nt)):
                        @pl.when(s >= t)
                        def _():
                            if hop > 0:
                                up(k, s).wait_recv()
                                add_bf16(s1.at[s, k, b2, b1], rx.at[s, k])
                            if hop < nt - 1:
                                @pl.when(s > t)
                                def _():
                                    up(k, s).start()

                @pl.when(t == nt - 1 - hop)
                def _():
                    for s in range(nt):
                        if hop > 0:
                            @pl.when(s < t)
                            def _():
                                down(k, s, False).wait_recv()
                                add_bf16(s1.at[s, k, b2, b1], rx.at[s, k])

                            @pl.when(s == t)
                            def _():
                                down(k, s, True).wait_recv()
                                add_bf16(s1.at[s, k, b2, b1], rt.at[k])
                        if hop < nt - 1:
                            @pl.when(s == t - 1)
                            def _():
                                down(k, s, True).start()

                            @pl.when(s < t - 1)
                            def _():
                                down(k, s, False).start()
            task(end_of_chunk + 0.5 + HOP * hop, chain)
        base = end_of_chunk + 0.5 + HOP * nt

        for e, bit in enumerate(extra):
            def more(k=k, e=e, bit=bit):
                swap = remote(s1.at[t, k, b2, b1], rx.at[nt + e, k], xs.at[e, k], xr.at[e, k], dp=flip(d, bit))
                swap.start()
                swap.wait()
                add_bf16(s1.at[t, k, b2, b1], rx.at[nt + e, k])
            task(base + 0.01 * e, more)

        def settle(k=k):
            total[k, b0, b2, b1] = s1[t, k, b2, b1]

        def give_one(k, q):
            if q == 0:
                piece = total.at[k, b0, b2, b1, 0]
                return remote(piece, piece, fs.at[k, 0], fr.at[k, 0], dp=flip(d, 2))
            piece = total.at[k, b0, b2, b1, 1]
            return remote(piece, piece, fs.at[k, 1], fr.at[k, 1], dp=flip(d, 4))

        def give_two(k, q):
            if q == 0:
                piece = total.at[k, b0, b2, :, 0]
                return remote(piece, piece, fs.at[k, 2], fr.at[k, 2], dp=flip(d, 4))
            piece = total.at[k, b0, :, b1, 1]
            return remote(piece, piece, fs.at[k, 3], fr.at[k, 3], dp=flip(d, 2))

        def give_core(k):
            return remote(total.at[k, b0], total.at[k, b0], fs.at[k, 4], fr.at[k, 4], dp=flip(d, 1))

        def spread_one(k=k):
            for q in (0, 1):
                give_one(k, q).start()

        def spread_two(k=k):
            for q in (0, 1):
                give_one(k, q).wait_recv()
            for q in (0, 1):
                give_two(k, q).start()

        def spread_core(k=k):
            for q in (0, 1):
                give_two(k, q).wait_recv()
            give_core(k).start()

        def spread_end(k=k):
            give_core(k).wait()
            for q in (0, 1):
                give_one(k, q).wait_send()
                give_two(k, q).wait_send()
        task(base + 0.5, settle)
        task(base + 1.0, spread_one)
        task(base + 4.0, spread_two)
        task(base + 8.0, spread_core)
        task(1e6, spread_end)

    def keep_result():
        gathered_r[t] = result[...]
    task(0.2, keep_result)

    part = own // PIECES

    def piece_of(ref, n):
        return ref.at[pl.ds(n % PIECES * part, part)]
    z_tasks, z_finish = relay_tasks(
        nt, 2 * PIECES, lambda n: piece_of((result, own_ig)[n // PIECES], n),
        lambda s, n: piece_of(gathered[n // PIECES].at[s], n), (os_, or_),
        lambda n, j: (-5.0, ready)[n // PIECES] + 14.0 / PIECES * (n % PIECES) + 14.0 * j + (0.01 if j == 0 else 1.0),
        lambda *a: None)
    tasks += [(w, 1000 + n, b) for w, n, b in z_tasks]

    exchanges = [("dp", bit) for bit in bits]
    step = 1
    while step < nt:
        exchanges.append(("tensor", step))
        step *= 2
    for e, (axis, bit) in enumerate(exchanges):
        def swap(e=e, axis=axis, bit=bit):
            goal = {axis: flip(lax.axis_index(axis), bit)}
            return remote(small, sr.at[e], ss.at[e], sm.at[e], **goal)

        def begin(swap=swap):
            swap().start()

        def end(e=e, swap=swap):
            swap().wait()
            small[...] = small[...] + sr[e]
        task(late + 1.0 + 5.0 * e, begin)
        task(late + 5.5 + 5.0 * e, end)

    ordered(tasks)
    z_finish()

    @pl.when(t < nt - 1)
    def _():
        halo(0).wait_send()
        halo(2).wait_send()

    @pl.when(t > 0)
    def _():
        halo(1).wait_send()
        halo(3).wait_send()
    for k, s in units:
        core(k, s).wait_send()
        for q in (0, 1):
            one(k, s, q).wait_send()
            two(k, s, q).wait_send()

        @pl.when(s > t)
        def _():
            up(k, s).wait_send()

        @pl.when(s < t)
        def _():
            down(k, s, False).wait_send()


def backward(vmem_arrays, hbm_arrays, nt, extra):
    own, width = vmem_arrays[0].shape
    grads, segments = hbm_arrays[2], vmem_arrays[10]
    small_shape = vmem_arrays[9].shape
    piece, chunks = width // 16, grads.shape[1] + 1
    window = own + 2 * HALO
    dma = pltpu.SemaphoreType.DMA
    hops = 3 + len(extra) + (nt - 1).bit_length()
    vmem, any_ = pl.BlockSpec(memory_space=pltpu.VMEM), pl.BlockSpec(memory_space=pl.ANY)
    unit = (2, 2, 2, piece, width)
    blocks = own // BLOCK

    def low(*dims):
        return pltpu.VMEM(dims, BF16)

    def wide(*dims):
        return pltpu.VMEM(dims, F32)
    return pl.pallas_call(
        functools.partial(backward_kernel, nt, chunks, extra),
        name="backward",
        out_shape=(
            jax.ShapeDtypeStruct((chunks, 2) + unit, BF16),
            jax.ShapeDtypeStruct(small_shape, F32),
            jax.ShapeDtypeStruct((nt, own, width), BF16),
            jax.ShapeDtypeStruct((nt, own, width), BF16),
        ),
        in_specs=[vmem] * len(vmem_arrays) + [any_] * len(hbm_arrays),
        out_specs=(vmem,) * 4,
        scratch_shapes=[
            low(nt, chunks, *unit), low(nt, chunks, *unit),
            low(nt, chunks, 2, piece, width), low(nt, chunks, 2, piece, width), low(nt, chunks, 2, piece, width),
            low(nt + len(extra), chunks, 2, piece, width), low(chunks, 2, piece, width),
            wide(hops, *small_shape), low(nt, 2, *unit), low(nt, 2, *unit),
            low(own, width), low(own, width), pltpu.VMEM((1, segments.shape[1] + 2 * HALO), jnp.int32),
            pltpu.VMEM((1, window), jnp.int32), pltpu.VMEM((window, BLOCK), jnp.int32),
            low(own, width), low(own, width), wide(blocks, 16, 2 * BLOCK),
            low(2, HALO, width), wide(2, HALO // BLOCK, 16, 2 * BLOCK),
            wide(own, width), wide(own, width), low(3, own, width), low(3, width, own),
            wide(own, width), low(own, width),
            dma((nt, chunks)), dma((nt, chunks)), dma((nt, chunks)),
            dma((nt, chunks, 4)), dma((nt, chunks, 4)),
            dma((nt, chunks, 2)), dma((nt, chunks, 2)),
            dma((max(1, len(extra)), chunks)), dma((max(1, len(extra)), chunks)),
            dma((chunks, 5)), dma((chunks, 5)),
            dma((2 * PIECES, nt - 1, 2)), dma((2 * PIECES, nt - 1, 2)),
            dma((hops,)), dma((hops,)), dma((4,)), dma((4,)), dma((3,)),
        ],
        compiler_params=pltpu.CompilerParams(
            collective_id=2, has_side_effects=True, vmem_limit_bytes=VMEM_LIMIT),
    )(*vmem_arrays, *hbm_arrays)


def finish_kernel(nt, ndp, total, small, g1, s1, qkv, qvb, out_w, out_b, g2, s2, up, up_b, down, down_b):
    t = lax.axis_index("tensor")
    width = small.shape[1]
    local = width // nt
    scale = 1.0 / ndp

    def rows(k, b):
        return total[0, k, b].reshape(local, width).astype(F32) * scale
    for kind in range(3):
        qkv[kind] = rows(kind // 2, kind % 2).T
    out_w[...] = rows(1, 1)
    up[...] = total[1].reshape(width, width).astype(F32) * scale
    down[...] = (total[2].reshape(width, width).astype(F32) * scale).T
    for ref, line in ((g1, 0), (s1, 1), (out_b, 2), (g2, 3), (s2, 4), (down_b, 5)):
        ref[...] = small[line:line + 1, :].reshape(width) * scale
    up_b[...] = small[pl.ds(8 + t, 1), :].reshape(width) * scale
    for place in range(nt):
        @pl.when(t == place)
        def _():
            qvb[...] = small[6:8, place * local:(place + 1) * local] * scale


def finish_up(total, small, nt, ndp):
    width = small.shape[1]
    local = width // nt

    def shape(*dims):
        return jax.ShapeDtypeStruct(dims, F32)
    return pl.pallas_call(
        functools.partial(finish_kernel, nt, ndp),
        name="finish",
        out_shape=(shape(width), shape(width), shape(3, width, local), shape(2, local), shape(local, width), shape(width),
                   shape(width), shape(width), shape(width, width), shape(width), shape(width, width), shape(width)),
        compiler_params=pltpu.CompilerParams(vmem_limit_bytes=VMEM_LIMIT),
    )(total, small)


def body(tokens_in, segment_ids, first_gain, first_shift, qkv_weight, query_value_bias, out_weight, out_bias,
         second_gain, second_shift, up_weight, up_bias, down_weight, down_bias, cotangent):
    nt, ndp = lax.axis_size("tensor"), lax.axis_size("dp")
    length, width = tokens_in.shape
    (result, hidden, q, k, v, normed, heads_t, grad_two, lse, small, mlp_grads, w_first) = forward(
        (tokens_in, cotangent, segment_ids, first_gain, first_shift, qkv_weight, query_value_bias, out_weight, out_bias,
         second_gain, second_shift, up_weight, up_bias, down_weight, down_bias), nt)
    extra = []
    bit = 8
    while bit < ndp:
        extra.append(bit)
        bit *= 2
    total, small, results, input_grads = backward(
        (result, hidden, q, k, v, normed, heads_t, grad_two, lse, small, segment_ids, first_gain, second_gain),
        (cotangent, tokens_in, mlp_grads, w_first), nt, tuple(extra))
    grads = finish_up(total, small, nt, ndp)
    return (results.reshape(length, width), input_grads.reshape(length, width)) + tuple(grads)


def solution(mesh):
    placed = (
        P("dp", None), P("dp", None), P(), P(), P(None, None, "tensor"), P(None, "tensor"), P("tensor", None), P(),
        P(), P(), P(None, "tensor"), P("tensor"), P("tensor", None), P(), P("dp", None),
    )
    return jax.shard_map(
        body,
        mesh=mesh,
        in_specs=placed,
        out_specs=(
            P("dp", None), P("dp", None), P(), P(), P(None, None, "tensor"), P(None, "tensor"), P("tensor", None),
            P(), P(), P(), P(None, "tensor"), P("tensor"), P("tensor", None), P(),
        ),
        check_vma=False,
    )
```

```python
import functools

import jax
import jax.numpy as jnp
from jax import lax
from jax.experimental import pallas as pl
from jax.experimental.pallas import tpu as pltpu
from jax.sharding import PartitionSpec as P

HEAD_DIM = 64
HALO = 256
REACH = 224
BLOCK = 128
EPS = 1e-06
F32 = jnp.float32
BF16 = jnp.bfloat16
MESH = pl.DeviceIdType.MESH
VMEM_LIMIT = 60 << 20


def place():
    d, t = lax.axis_index("dp"), lax.axis_index("tensor")
    return d, t, lax.rem(d, 2), lax.rem(d // 2, 2), lax.rem(d // 4, 2)


def flip(d, value):
    return d + value * (1 - 2 * lax.rem(d // value, 2))


def remote(src, dst, send, recv, **axis):
    return pltpu.make_async_remote_copy(
        src_ref=src, dst_ref=dst, send_sem=send, recv_sem=recv,
        device_id=axis, device_id_type=MESH)


def greet(nt, bits, far=False):
    d, t = lax.axis_index("dp"), lax.axis_index("tensor")
    barrier = pltpu.get_barrier_semaphore()

    @pl.when(t > 0)
    def _():
        pl.semaphore_signal(barrier, inc=1, device_id={"tensor": t - 1}, device_id_type=MESH)

    @pl.when(t < nt - 1)
    def _():
        pl.semaphore_signal(barrier, inc=1, device_id={"tensor": t + 1}, device_id_type=MESH)

    for bit in bits:
        pl.semaphore_signal(barrier, inc=1, device_id={"dp": flip(d, bit)}, device_id_type=MESH)
    if far:
        pl.semaphore_signal(barrier, inc=1, device_id={"tensor": flip(t, 2)}, device_id_type=MESH)
    peers = len(bits) + int(far) + (t > 0).astype(jnp.int32) + (t < nt - 1).astype(jnp.int32)
    pl.semaphore_wait(barrier, peers)


def ordered(tasks):
    for _, _, task in sorted(tasks, key=lambda item: item[:2]):
        task()


def relay_tasks(nt, chunks, own, full, sems, start, arrived):
    send, recv = sems
    tasks = []
    t = lax.axis_index("tensor")
    for k in range(chunks):
        for j in range(nt):
            def step(k=k, j=j):
                for way in (0, 1):
                    sign = 1 - 2 * way
                    shard = t - sign * j
                    inside = (shard >= 0) & (shard < nt)
                    if j > 0:
                        @pl.when(inside)
                        def _():
                            remote(full(shard, k), full(shard, k), send.at[k, j - 1, way], recv.at[k, j - 1, way],
                                   tensor=t).wait_recv()
                            arrived(k, j, way, shard)
                    if j < nt - 1:
                        goal = t + sign
                        @pl.when(inside & (goal >= 0) & (goal < nt))
                        def _():
                            source = own(k) if j == 0 else full(shard, k)
                            remote(source, full(shard, k), send.at[k, j, way], recv.at[k, j, way],
                                   tensor=goal).start()
            tasks.append((start(k, j), len(tasks), step))

    def finish():
        for k in range(chunks):
            for j in range(nt - 1):
                for way in (0, 1):
                    sign = 1 - 2 * way
                    shard, goal = t - sign * j, t + sign
                    @pl.when((shard >= 0) & (shard < nt) & (goal >= 0) & (goal < nt))
                    def _():
                        source = own(k) if j == 0 else full(shard, k)
                        remote(source, full(shard, k), send.at[k, j, way], recv.at[k, j, way],
                               tensor=goal).wait_send()
    return tasks, finish


def add_bf16(ref, other):
    ref[...] = (ref[...].astype(F32) + other[...].astype(F32)).astype(BF16)


def stacked(pair):
    lane = lax.broadcasted_iota(jnp.int32, pair.shape, 1)
    zero = jnp.zeros_like(pair)
    return jnp.concatenate([jnp.where(lane < HEAD_DIM, pair, zero), jnp.where(lane < HEAD_DIM, zero, pair)], axis=0)


def dot(a, b, dims):
    return lax.dot_general(a, b, (dims, ((), ())), preferred_element_type=F32)


NN = ((1,), (0,))
NT = ((1,), (1,))


def untangle(both):
    half = both.shape[1] // 2
    return jnp.concatenate([both[:HEAD_DIM, :half], both[HEAD_DIM:, half:]], axis=0).T


def standardize(rows):
    center = rows - jnp.mean(rows, axis=-1, keepdims=True)
    r = lax.rsqrt(jnp.mean(center * center, axis=-1, keepdims=True) + EPS)
    return center * r, r


def norm_back(e, xhat, r):
    return r * (e - jnp.mean(e, axis=-1, keepdims=True) - xhat * jnp.mean(e * xhat, axis=-1, keepdims=True))


def window_segments(segments, padded, row, column):
    length, window = segments.shape[1], row.shape[1]
    padded[...] = jnp.full(padded.shape, -1, jnp.int32)
    padded[:, HALO:HALO + length] = segments[...]
    own = window - 2 * HALO
    for i in range(window // BLOCK):
        first = pl.multiple_of(lax.axis_index("tensor") * own + i * BLOCK, BLOCK)
        line = padded[:, pl.ds(first, BLOCK)]
        row[:, i * BLOCK:(i + 1) * BLOCK] = line
        column[i * BLOCK:(i + 1) * BLOCK, :] = jnp.broadcast_to(line, (BLOCK, BLOCK)).T


def nearest(nt):
    return [sorted(range(nt), key=lambda s: (abs(s - p), s if p < nt // 2 else -s)) for p in range(nt)]


def pick(table, position):
    t = lax.axis_index("tensor")
    return sum((t == p).astype(jnp.int32) * row[position] for p, row in enumerate(table))


def gelu_parts(x):
    cdf = 0.5 * (1.0 + lax.erf(x * (0.5 ** 0.5)))
    pdf = jnp.exp(-0.5 * x * x) * ((2.0 * jnp.pi) ** -0.5)
    return x * cdf, cdf + x * pdf


ATTEND = 1.0
DIRECT = 2
LINE, PLANE, LEAD, LAGS = 4.5, 0.0, 0.0, (7.0, 14.0, 18.0)


def forward_kernel(nt, chunks, own,
                   tokens_in, cotangent, segments, gain_1, shift_1, qkv_in, qv_bias, out_in, out_bias, gain_2, shift_2,
                   up_in, up_bias, down_in, down_bias,
                   result_out, hidden_out, q_out, k_out, v_out, normed_out, heads_out, gtwo_out, lse_ref, small, grads, w0,
                   result, hidden, q_ref, k_ref, v_ref, heads_t, gtwo, tok, cot, segp, segr, segc, bias, normed, w, bias_all, bias_sem, bias_recv, heads, normed_two, n2t,
                   cot_t, mlp, gbuf, pre_s, gact_s, act, gpre, gsem, zs, zr, ps, pr, cs, cr, ls, out_sem):
    d, t, b0, b1, b2 = place()
    window, width = tok.shape
    local = width // nt
    blocks = own // BLOCK
    local_copies = [pltpu.make_async_copy(qkv_in.at[kind], w.at[t, 0, kind // 2, kind % 2], ls.at[5 + kind])
                    for kind in range(3)] + [
        pltpu.make_async_copy(out_in, w.at[t, 0, 1, 1], ls.at[0]),
        pltpu.make_async_copy(up_in, w.at[t, 1], ls.at[1]),
        pltpu.make_async_copy(down_in, w.at[t, 2], ls.at[2]),
    ]
    for copy in local_copies:
        copy.start()
    cot_copy = pltpu.make_async_copy(cotangent.at[pl.ds(pl.multiple_of(t * own, own), own)], cot, ls.at[3])
    cot_copy.start()

    def token_copy(place):
        rows = own + HALO
        if place == 0:
            return pltpu.make_async_copy(tokens_in.at[pl.ds(0, rows)], tok.at[pl.ds(HALO, rows)], ls.at[4])
        if place == 1:
            return pltpu.make_async_copy(tokens_in.at[pl.ds((nt - 1) * own - HALO, rows)], tok.at[pl.ds(0, rows)], ls.at[4])
        first = pl.multiple_of(t * own - HALO, BLOCK)
        return pltpu.make_async_copy(tokens_in.at[pl.ds(first, window)], tok, ls.at[4])

    def tokens(act):
        @pl.when(t == 0)
        def _():
            act(token_copy(0))

        @pl.when(t == nt - 1)
        def _():
            act(token_copy(1))

        @pl.when((t > 0) & (t < nt - 1))
        def _():
            act(token_copy(2))
    tokens(lambda copy: copy.start())

    @pl.when(t == 0)
    def _():
        tok[0:HALO, :] = jnp.zeros((HALO, width), BF16)

    @pl.when(t == nt - 1)
    def _():
        tok[window - HALO:window, :] = jnp.zeros((HALO, width), BF16)

    barrier = pltpu.get_barrier_semaphore()
    for bit in (1, 2, 4):
        pl.semaphore_signal(barrier, inc=1, device_id={"dp": flip(d, bit)}, device_id_type=MESH)
    for j in range(1, nt):
        pl.semaphore_signal(barrier, inc=1, device_id={"tensor": lax.rem(t + j, nt)}, device_id_type=MESH)
    bias[...] = jnp.zeros(bias.shape, F32)
    bias[0:1, :] = up_bias[...].reshape(1, width)
    bias[1:3, 0:local] = qv_bias[...]
    bias_all[t] = bias[...]
    window_segments(segments, segp, segr, segc)
    for copy in local_copies:
        copy.wait()
    pl.semaphore_wait(barrier, 3 + nt - 1)
    tasks = []

    def task(when, body):
        tasks.append((when, len(tasks), body))

    def bias_send(j):
        return remote(bias, bias_all.at[t], bias_sem.at[j], bias_recv.at[j], tensor=lax.rem(t + j + 1, nt))

    def bias_get(j):
        source = lax.rem(t + nt - j - 1, nt)
        return remote(bias, bias_all.at[source], bias_sem.at[j], bias_recv.at[j], tensor=source)

    parity = lax.rem(b1 + b2, 2)

    def line_piece(shard, n):
        if n < DIRECT:
            return w.at[shard, n, b0, b2, b1]
        k, side = DIRECT + (n - DIRECT) // 2, (n - DIRECT) % 2
        return w.at[shard, k, b0, side, parity if side == 0 else 1 - parity]

    def one(shard, k, q, way, j):
        if k >= DIRECT:
            mine = line_piece(shard, DIRECT + 2 * (k - DIRECT) + q)
            return remote(mine, mine, ps.at[k, j, way, q], pr.at[k, j, way, q], dp=flip(d, 2 + 2 * q))
        if q == 0:
            mine = w.at[shard, k, b0, b2, b1, 0]
            return remote(mine, mine, ps.at[k, j, way, 0], pr.at[k, j, way, 0], dp=flip(d, 2))
        mine = w.at[shard, k, b0, b2, b1, 1]
        return remote(mine, mine, ps.at[k, j, way, 1], pr.at[k, j, way, 1], dp=flip(d, 4))

    def two(shard, k, q, way, j):
        if q == 0:
            mine = w.at[shard, k, b0, b2, :, 0]
            return remote(mine, mine, ps.at[k, j, way, 2], pr.at[k, j, way, 2], dp=flip(d, 4))
        mine = w.at[shard, k, b0, :, b1, 1]
        return remote(mine, mine, ps.at[k, j, way, 3], pr.at[k, j, way, 3], dp=flip(d, 2))

    def core(shard, k, way, j):
        return remote(w.at[shard, k, b0], w.at[shard, k, b0], cs.at[k, j, way], cr.at[k, j, way], dp=flip(d, 1))

    def each(k, j, act):
        for way in (0, 1):
            shard = t - (1 - 2 * way) * (j + 1)

            @pl.when((shard >= 0) & (shard < nt))
            def _():
                act(shard, k, way, j)

    def piece_time(n, j):
        if n < DIRECT:
            return LINE * (n * (nt - 1) + j)
        pair, side = (n - DIRECT) // 2, (n - DIRECT) % 2
        return LINE * ((DIRECT + 2 * pair) * (nt - 1) + 2 * j - (j > 0) + side)

    def line_time(k, j):
        return piece_time(k, j) if k < DIRECT else piece_time(DIRECT + 2 * (k - DIRECT) + 1, j)

    z_tasks, z_finish = relay_tasks(
        nt, 2 * chunks - DIRECT, lambda n: line_piece(t, n), line_piece, (zs, zr), piece_time, lambda *a: None)
    tasks += z_tasks
    ready_at = {}
    for k in range(chunks):
        for j in range(nt - 1):
            def begin(k=k, j=j):
                def act(shard, k, way, j):
                    for q in (0, 1):
                        one(shard, k, q, way, j).start()
                each(k, j, act)

            def second(k=k, j=j):
                def act(shard, k, way, j):
                    for q in (0, 1):
                        one(shard, k, q, way, j).wait_recv()
                    for q in (0, 1):
                        two(shard, k, q, way, j).start()
                each(k, j, act)

            def third(k=k, j=j):
                def act(shard, k, way, j):
                    for q in (0, 1):
                        (two if k < DIRECT else one)(shard, k, q, way, j).wait_recv()
                    core(shard, k, way, j).start()
                each(k, j, act)

            def fourth(k=k, j=j):
                def act(shard, k, way, j):
                    core(shard, k, way, j).wait_recv()
                each(k, j, act)
            n = k * (nt - 1) + j
            base = max(line_time(k, j + 1) + 0.1, LEAD + PLANE * n)
            task(base, begin)
            if k < DIRECT:
                task(base + LAGS[0], second)
                task(base + LAGS[1], third)
                task(base + LAGS[2], fourth)
                ready_at[k, j] = base + LAGS[2] + 0.1
            else:
                task(base + LAGS[1] - LAGS[0], third)
                task(base + LAGS[2] - LAGS[0], fourth)
                ready_at[k, j] = base + LAGS[2] - LAGS[0] + 0.1

    def bias_begin():
        for j in range(nt - 1):
            bias_send(j).start()

    def bias_end():
        for j in range(nt - 1):
            bias_get(j).wait_recv()
    task(0.2, bias_begin)
    task(10.0, bias_end)

    g1, s1, ob, g2, s2, db = (ref[...].reshape(1, width) for ref in (gain_1, shift_1, out_bias, gain_2, shift_2, down_bias))

    def tokens_here():
        tokens(lambda copy: copy.wait())
    task(0.4, tokens_here)
    for i in range(window // BLOCK):
        def norm_rows(i=i):
            def part(n, carry):
                rows = pl.ds(pl.multiple_of(i * BLOCK + n * 32, 32), 32)
                xhat, _ = standardize(tok[rows, :].astype(F32))
                normed[rows, :] = (xhat * g1 + s1).astype(BF16)
                return carry
            lax.fori_loop(0, BLOCK // 32, part, 0)
        task(0.5 + 0.7 * i, norm_rows)

    kept = [pltpu.make_async_copy(source, goal, out_sem.at[n]) for n, (source, goal) in enumerate((
        (result, result_out), (hidden, hidden_out), (q_ref, q_out), (k_ref, k_out), (v_ref, v_out),
        (normed.at[pl.ds(HALO, own)], normed_out), (heads_t, heads_out), (gtwo, gtwo_out)))]

    def transposes():
        kept[5].start()
        cot_copy.wait()
        cot_t[...] = cot[...].T
        small[5:6, :] = jnp.sum(cot[...].astype(F32), axis=0, keepdims=True)
    task(6.0, transposes)

    half_rows = window // 2
    group = 2 * local

    def project(u, kind, part):
        rows = slice(part * half_rows, (part + 1) * half_rows)
        weight = w[pl.ds(2 * u, 2), 0, kind // 2, kind % 2].reshape(group, width)
        out = dot(normed[rows, :], weight, NT)
        if kind != 1:
            line = 1 + kind // 2
            out = out + jnp.concatenate([bias_all[2 * u, line:line + 1, :local], bias_all[2 * u + 1, line:line + 1, :local]], axis=1)
        target = (q_ref, k_ref, v_ref)[kind]
        target[rows, pl.ds(pl.multiple_of(u * group, 128), group)] = out.astype(BF16)

    def attention(u, b, only):
        first, count = BLOCK * b + 32, BLOCK + 448
        q0 = HALO + BLOCK * b
        allowed = segc[first:first + count, :] == segr[:, q0:q0 + BLOCK]
        allowed = jnp.concatenate([allowed, allowed], axis=1)

        def pair(j, carry):
            at = u * (group // 128) + j
            cols = pl.ds(pl.multiple_of(at * 128, 128), 128)
            q2 = stacked(q_ref[q0:q0 + BLOCK, cols])
            k2 = k_ref[first:first + count, cols]
            v2 = v_ref[first:first + count, cols]
            s = dot(k2, q2, NT) * (HEAD_DIM ** -0.5)
            s = jnp.where(allowed, s, -1e9)
            m = jnp.max(s, axis=0, keepdims=True)
            p = jnp.exp(s - m)
            l = jnp.sum(p, axis=0, keepdims=True)
            low = (p * (1.0 / l)).astype(BF16)
            out = dot(v2.T, low, NN)
            half = out.shape[1] // 2
            both = jnp.concatenate([out[:HEAD_DIM, :half], out[HEAD_DIM:, half:]], axis=0).astype(BF16)
            heads_t[cols, b * BLOCK:(b + 1) * BLOCK] = both
            heads[b * BLOCK:(b + 1) * BLOCK, cols] = both.T
            lse_ref[b, pl.ds(at, 1), :] = m + jnp.log(l)
            return carry
        pair(only, 0)

    def out_project(u, fresh):
        weight = w[pl.ds(2 * u, 2), 0, 1, 1].reshape(group, width)
        part = dot(heads[:, pl.ds(pl.multiple_of(u * group, 128), group)], weight, NN)
        if fresh:
            hidden[...] = part
        else:
            hidden[...] += part

    first_half = t // 2
    at = 7.0
    for n in range(nt // 2):
        u = lax.rem(first_half + n, nt // 2)
        if n == 0:
            at = max(at, ready_at[0, 0])
        else:
            at = max(at, ready_at[0, nt - 2])
        for kind in range(3):
            for part in range(2):
                def run(u=u, kind=kind, part=part):
                    project(u, kind, part)
                task(at, run)
                at += 0.7
        for b in range(blocks):
            for only in range(group // 128):
                def run(u=u, b=b, only=only):
                    attention(u, b, only)
                task(at, run)
                at += ATTEND

        def run(u=u, n=n):
            out_project(u, n == 0)
        task(at, run)
        at += 0.6

    def keep_heads():
        for n in (2, 3, 4, 6):
            kept[n].start()
    task(at, keep_heads)

    def rows_of(i):
        return slice(i * BLOCK, (i + 1) * BLOCK)

    for i in range(blocks):
        def norm_two(i=i):
            rows = rows_of(i)
            token = tok[HALO + i * BLOCK:HALO + (i + 1) * BLOCK, :].astype(F32)
            whole = hidden[rows, :] + token + ob
            hidden[rows, :] = whole
            xhat, _ = standardize(whole)
            low = (xhat * g2 + s2).astype(BF16)
            normed_two[rows, :] = low
            n2t[:, rows] = low.T
        task(at, norm_two)
        at += 0.7

    def keep_hidden():
        kept[1].start()
    task(at, keep_hidden)
    table = nearest(nt)
    slab = 32

    def grads_out(slot, shard):
        return pltpu.make_async_copy(gbuf.at[slot], grads.at[shard], gsem.at[slot])

    def mlp_steps(position):
        shard, slot = pick(table, position), position % 2

        def up():
            return w[shard, 1].reshape(width, width)

        def down():
            return w[shard, 2].reshape(width, width)

        def begin():
            pre_s[...] = dot(normed_two[...], up(), NN) + bias_all[shard, 0:1, :]

        def begin_back():
            gact_s[...] = dot(cot[...], down(), NT)

        def middle():
            def step(i, total):
                rows = pl.ds(pl.multiple_of(i * slab, slab), slab)
                value, slope = gelu_parts(pre_s[rows, :])
                act[rows, :] = value.astype(BF16)
                low = (gact_s[rows, :] * slope).astype(BF16)
                gpre[rows, :] = low
                return total + low.astype(F32)
            total = lax.fori_loop(0, own // slab, step, jnp.zeros((slab, width), F32))
            small[pl.ds(8 + shard, 1), :] = jnp.sum(total, axis=0, keepdims=True)

        def end():
            if position == 0:
                mlp[...] = dot(act[...], down(), NN)
                gtwo[...] = dot(gpre[...], up(), NT)
            else:
                mlp[...] += dot(act[...], down(), NN)
                gtwo[...] += dot(gpre[...], up(), NT)

        def grad_up():
            if position >= 2:
                grads_out(slot, shard).wait()
            gbuf[slot, 0] = dot(n2t[...], gpre[...], NN).astype(BF16).reshape(gbuf.shape[2:])

        def grad_down():
            gbuf[slot, 1] = dot(cot_t[...], act[...], NN).astype(BF16).reshape(gbuf.shape[2:])
            grads_out(slot, shard).start()
        return (begin, 0.8), (begin_back, 0.8), (middle, 1.5), (end, 1.6), (grad_up, 0.7), (grad_down, 0.7)

    for position in range(nt):
        if position > 0:
            at = max([at] + [ready_at[k, position - 1] for k in range(1, chunks)])
        for run, length in mlp_steps(position):
            task(at, run)
            at += length

    def finish():
        for k in range(chunks):
            for j in range(nt - 1):
                for way in (0, 1):
                    sign = 1 - 2 * way
                    shard, goal = t - sign * j, t + sign
                    @pl.when((shard >= 0) & (shard < nt) & (goal >= 0) & (goal < nt))
                    def _():
                        source = own(k) if j == 0 else full(shard, k)
                        remote(source, full(shard, k), send.at[k, j, way], recv.at[k, j, way],
                               tensor=goal).wait_send()
    return tasks, finish


def add_bf16(ref, other):
    ref[...] = (ref[...].astype(F32) + other[...].astype(F32)).astype(BF16)


def stacked(pair):
    lane = lax.broadcasted_iota(jnp.int32, pair.shape, 1)
    zero = jnp.zeros_like(pair)
    return jnp.concatenate([jnp.where(lane < HEAD_DIM, pair, zero), jnp.where(lane < HEAD_DIM, zero, pair)], axis=0)


def dot(a, b, dims):
    return lax.dot_general(a, b, (dims, ((), ())), preferred_element_type=F32)


NN = ((1,), (0,))
NT = ((1,), (1,))


def untangle(both):
    half = both.shape[1] // 2
    return jnp.concatenate([both[:HEAD_DIM, :half], both[HEAD_DIM:, half:]], axis=0).T


def standardize(rows):
    center = rows - jnp.mean(rows, axis=-1, keepdims=True)
    r = lax.rsqrt(jnp.mean(center * center, axis=-1, keepdims=True) + EPS)
    return center * r, r


def norm_back(e, xhat, r):
    return r * (e - jnp.mean(e, axis=-1, keepdims=True) - xhat * jnp.mean(e * xhat, axis=-1, keepdims=True))


def window_segments(segments, padded, row, column):
    length, window = segments.shape[1], row.shape[1]
    padded[...] = jnp.full(padded.shape, -1, jnp.int32)
    padded[:, HALO:HALO + length] = segments[...]
    own = window - 2 * HALO
    for i in range(window // BLOCK):
        first = pl.multiple_of(lax.axis_index("tensor") * own + i * BLOCK, BLOCK)
        line = padded[:, pl.ds(first, BLOCK)]
        row[:, i * BLOCK:(i + 1) * BLOCK] = line
        column[i * BLOCK:(i + 1) * BLOCK, :] = jnp.broadcast_to(line, (BLOCK, BLOCK)).T


def nearest(nt):
    return [sorted(range(nt), key=lambda s: (abs(s - p), s if p < nt // 2 else -s)) for p in range(nt)]


def pick(table, position):
    t = lax.axis_index("tensor")
    return sum((t == p).astype(jnp.int32) * row[position] for p, row in enumerate(table))


def gelu_parts(x):
    cdf = 0.5 * (1.0 + lax.erf(x * (0.5 ** 0.5)))
    pdf = jnp.exp(-0.5 * x * x) * ((2.0 * jnp.pi) ** -0.5)
    return x * cdf, cdf + x * pdf


ATTEND = 1.0
DIRECT = 2
LINE, PLANE, LEAD, LAGS = 4.5, 0.0, 0.0, (7.0, 14.0, 18.0)


def forward_kernel(nt, chunks, own,
                   tokens_in, cotangent, segments, gain_1, shift_1, qkv_in, qv_bias, out_in, out_bias, gain_2, shift_2,
                   up_in, up_bias, down_in, down_bias,
                   result_out, hidden_out, q_out, k_out, v_out, normed_out, heads_out, gtwo_out, lse_ref, small, grads, w0,
                   result, hidden, q_ref, k_ref, v_ref, heads_t, gtwo, tok, cot, segp, segr, segc, bias, normed, w, bias_all, bias_sem, bias_recv, heads, normed_two, n2t,
                   cot_t, mlp, gbuf, pre_s, gact_s, act, gpre, gsem, zs, zr, ps, pr, cs, cr, ls, out_sem):
    d, t, b0, b1, b2 = place()
    window, width = tok.shape
    local = width // nt
    blocks = own // BLOCK
    local_copies = [pltpu.make_async_copy(qkv_in.at[kind], w.at[t, 0, kind // 2, kind % 2], ls.at[5 + kind])
                    for kind in range(3)] + [
        pltpu.make_async_copy(out_in, w.at[t, 0, 1, 1], ls.at[0]),
        pltpu.make_async_copy(up_in, w.at[t, 1], ls.at[1]),
        pltpu.make_async_copy(down_in, w.at[t, 2], ls.at[2]),
    ]
    for copy in local_copies:
        copy.start()
    cot_copy = pltpu.make_async_copy(cotangent.at[pl.ds(pl.multiple_of(t * own, own), own)], cot, ls.at[3])
    cot_copy.start()

    def token_copy(place):
        rows = own + HALO
        if place == 0:
            return pltpu.make_async_copy(tokens_in.at[pl.ds(0, rows)], tok.at[pl.ds(HALO, rows)], ls.at[4])
        if place == 1:
            return pltpu.make_async_copy(tokens_in.at[pl.ds((nt - 1) * own - HALO, rows)], tok.at[pl.ds(0, rows)], ls.at[4])
        first = pl.multiple_of(t * own - HALO, BLOCK)
        return pltpu.make_async_copy(tokens_in.at[pl.ds(first, window)], tok, ls.at[4])

    def tokens(act):
        @pl.when(t == 0)
        def _():
            act(token_copy(0))

        @pl.when(t == nt - 1)
        def _():
            act(token_copy(1))

        @pl.when((t > 0) & (t < nt - 1))
        def _():
            act(token_copy(2))
    tokens(lambda copy: copy.start())

    @pl.when(t == 0)
    def _():
        tok[0:HALO, :] = jnp.zeros((HALO, width), BF16)

    @pl.when(t == nt - 1)
    def _():
        tok[window - HALO:window, :] = jnp.zeros((HALO, width), BF16)

    barrier = pltpu.get_barrier_semaphore()
    for bit in (1, 2, 4):
        pl.semaphore_signal(barrier, inc=1, device_id={"dp": flip(d, bit)}, device_id_type=MESH)
    for j in range(1, nt):
        pl.semaphore_signal(barrier, inc=1, device_id={"tensor": lax.rem(t + j, nt)}, device_id_type=MESH)
    bias[...] = jnp.zeros(bias.shape, F32)
    bias[0:1, :] = up_bias[...].reshape(1, width)
    bias[1:3, 0:local] = qv_bias[...]
    bias_all[t] = bias[...]
    window_segments(segments, segp, segr, segc)
    for copy in local_copies:
        copy.wait()
    pl.semaphore_wait(barrier, 3 + nt - 1)
    tasks = []

    def task(when, body):
        tasks.append((when, len(tasks), body))

    def bias_send(j):
        return remote(bias, bias_all.at[t], bias_sem.at[j], bias_recv.at[j], tensor=lax.rem(t + j + 1, nt))

    def bias_get(j):
        source = lax.rem(t + nt - j - 1, nt)
        return remote(bias, bias_all.at[source], bias_sem.at[j], bias_recv.at[j], tensor=source)

    parity = lax.rem(b1 + b2, 2)

    def line_piece(shard, n):
        if n < DIRECT:
            return w.at[shard, n, b0, b2, b1]
        k, side = DIRECT + (n - DIRECT) // 2, (n - DIRECT) % 2
        return w.at[shard, k, b0, side, parity if side == 0 else 1 - parity]

    def one(shard, k, q, way, j):
        if k >= DIRECT:
            mine = line_piece(shard, DIRECT + 2 * (k - DIRECT) + q)
            return remote(mine, mine, ps.at[k, j, way, q], pr.at[k, j, way, q], dp=flip(d, 2 + 2 * q))
        if q == 0:
            mine = w.at[shard, k, b0, b2, b1, 0]
            return remote(mine, mine, ps.at[k, j, way, 0], pr.at[k, j, way, 0], dp=flip(d, 2))
        mine = w.at[shard, k, b0, b2, b1, 1]
        return remote(mine, mine, ps.at[k, j, way, 1], pr.at[k, j, way, 1], dp=flip(d, 4))

    def two(shard, k, q, way, j):
        if q == 0:
            mine = w.at[shard, k, b0, b2, :, 0]
            return remote(mine, mine, ps.at[k, j, way, 2], pr.at[k, j, way, 2], dp=flip(d, 4))
        mine = w.at[shard, k, b0, :, b1, 1]
        return remote(mine, mine, ps.at[k, j, way, 3], pr.at[k, j, way, 3], dp=flip(d, 2))

    def core(shard, k, way, j):
        return remote(w.at[shard, k, b0], w.at[shard, k, b0], cs.at[k, j, way], cr.at[k, j, way], dp=flip(d, 1))

    def each(k, j, act):
        for way in (0, 1):
            shard = t - (1 - 2 * way) * (j + 1)

            @pl.when((shard >= 0) & (shard < nt))
            def _():
                act(shard, k, way, j)

    def piece_time(n, j):
        if n < DIRECT:
            return LINE * (n * (nt - 1) + j)
        pair, side = (n - DIRECT) // 2, (n - DIRECT) % 2
        return LINE * ((DIRECT + 2 * pair) * (nt - 1) + 2 * j - (j > 0) + side)

    def line_time(k, j):
        return piece_time(k, j) if k < DIRECT else piece_time(DIRECT + 2 * (k - DIRECT) + 1, j)

    z_tasks, z_finish = relay_tasks(
        nt, 2 * chunks - DIRECT, lambda n: line_piece(t, n), line_piece, (zs, zr), piece_time, lambda *a: None)
    tasks += z_tasks
    ready_at = {}
    for k in range(chunks):
        for j in range(nt - 1):
            def begin(k=k, j=j):
                def act(shard, k, way, j):
                    for q in (0, 1):
                        one(shard, k, q, way, j).start()
                each(k, j, act)

            def second(k=k, j=j):
                def act(shard, k, way, j):
                    for q in (0, 1):
                        one(shard, k, q, way, j).wait_recv()
                    for q in (0, 1):
                        two(shard, k, q, way, j).start()
                each(k, j, act)

            def third(k=k, j=j):
                def act(shard, k, way, j):
                    for q in (0, 1):
                        (two if k < DIRECT else one)(shard, k, q, way, j).wait_recv()
                    core(shard, k, way, j).start()
                each(k, j, act)

            def fourth(k=k, j=j):
                def act(shard, k, way, j):
                    core(shard, k, way, j).wait_recv()
                each(k, j, act)
            n = k * (nt - 1) + j
            base = max(line_time(k, j + 1) + 0.1, LEAD + PLANE * n)
            task(base, begin)
            if k < DIRECT:
                task(base + LAGS[0], second)
                task(base + LAGS[1], third)
                task(base + LAGS[2], fourth)
                ready_at[k, j] = base + LAGS[2] + 0.1
            else:
                task(base + LAGS[1] - LAGS[0], third)
                task(base + LAGS[2] - LAGS[0], fourth)
                ready_at[k, j] = base + LAGS[2] - LAGS[0] + 0.1

    def bias_begin():
        for j in range(nt - 1):
            bias_send(j).start()

    def bias_end():
        for j in range(nt - 1):
            bias_get(j).wait_recv()
    task(0.2, bias_begin)
    task(10.0, bias_end)

    g1, s1, ob, g2, s2, db = (ref[...].reshape(1, width) for ref in (gain_1, shift_1, out_bias, gain_2, shift_2, down_bias))

    def tokens_here():
        tokens(lambda copy: copy.wait())
    task(0.4, tokens_here)
    for i in range(window // BLOCK):
        def norm_rows(i=i):
            def part(n, carry):
                rows = pl.ds(pl.multiple_of(i * BLOCK + n * 32, 32), 32)
                xhat, _ = standardize(tok[rows, :].astype(F32))
                normed[rows, :] = (xhat * g1 + s1).astype(BF16)
                return carry
            lax.fori_loop(0, BLOCK // 32, part, 0)
        task(0.5 + 0.7 * i, norm_rows)

    kept = [pltpu.make_async_copy(source, goal, out_sem.at[n]) for n, (source, goal) in enumerate((
        (result, result_out), (hidden, hidden_out), (q_ref, q_out), (k_ref, k_out), (v_ref, v_out),
        (normed.at[pl.ds(HALO, own)], normed_out), (heads_t, heads_out), (gtwo, gtwo_out)))]

    def transposes():
        kept[5].start()
        cot_copy.wait()
        cot_t[...] = cot[...].T
        small[5:6, :] = jnp.sum(cot[...].astype(F32), axis=0, keepdims=True)
    task(6.0, transposes)

    half_rows = window // 2
    group = 2 * local

    def project(u, kind, part):
        rows = slice(part * half_rows, (part + 1) * half_rows)
        weight = w[pl.ds(2 * u, 2), 0, kind // 2, kind % 2].reshape(group, width)
        out = dot(normed[rows, :], weight, NT)
        if kind != 1:
            line = 1 + kind // 2
            out = out + jnp.concatenate([bias_all[2 * u, line:line + 1, :local], bias_all[2 * u + 1, line:line + 1, :local]], axis=1)
        target = (q_ref, k_ref, v_ref)[kind]
        target[rows, pl.ds(pl.multiple_of(u * group, 128), group)] = out.astype(BF16)

    def attention(u, b, only):
        first, count = BLOCK * b + 32, BLOCK + 448
        q0 = HALO + BLOCK * b
        allowed = segc[first:first + count, :] == segr[:, q0:q0 + BLOCK]
        allowed = jnp.concatenate([allowed, allowed], axis=1)

        def pair(j, carry):
            at = u * (group // 128) + j
            cols = pl.ds(pl.multiple_of(at * 128, 128), 128)
            q2 = stacked(q_ref[q0:q0 + BLOCK, cols])
            k2 = k_ref[first:first + count, cols]
            v2 = v_ref[first:first + count, cols]
            s = dot(k2, q2, NT) * (HEAD_DIM ** -0.5)
            s = jnp.where(allowed, s, -1e9)
            m = jnp.max(s, axis=0, keepdims=True)
            p = jnp.exp(s - m)
            l = jnp.sum(p, axis=0, keepdims=True)
            low = (p * (1.0 / l)).astype(BF16)
            out = dot(v2.T, low, NN)
            half = out.shape[1] // 2
            both = jnp.concatenate([out[:HEAD_DIM, :half], out[HEAD_DIM:, half:]], axis=0).astype(BF16)
            heads_t[cols, b * BLOCK:(b + 1) * BLOCK] = both
            heads[b * BLOCK:(b + 1) * BLOCK, cols] = both.T
            lse_ref[b, pl.ds(at, 1), :] = m + jnp.log(l)
            return carry
        pair(only, 0)

    def out_project(u, fresh):
        weight = w[pl.ds(2 * u, 2), 0, 1, 1].reshape(group, width)
        part = dot(heads[:, pl.ds(pl.multiple_of(u * group, 128), group)], weight, NN)
        if fresh:
            hidden[...] = part
        else:
            hidden[...] += part

    first_half = t // 2
    at = 7.0
    for n in range(nt // 2):
        u = lax.rem(first_half + n, nt // 2)
        if n == 0:
            at = max(at, ready_at[0, 0])
        else:
            at = max(at, ready_at[0, nt - 2])
        for kind in range(3):
            for part in range(2):
                def run(u=u, kind=kind, part=part):
                    project(u, kind, part)
                task(at, run)
                at += 0.7
        for b in range(blocks):
            for only in range(group // 128):
                def run(u=u, b=b, only=only):
                    attention(u, b, only)
                task(at, run)
                at += ATTEND

        def run(u=u, n=n):
            out_project(u, n == 0)
        task(at, run)
        at += 0.6

    def keep_heads():
        for n in (2, 3, 4, 6):
            kept[n].start()
    task(at, keep_heads)

    def rows_of(i):
        return slice(i * BLOCK, (i + 1) * BLOCK)

    for i in range(blocks):
        def norm_two(i=i):
            rows = rows_of(i)
            token = tok[HALO + i * BLOCK:HALO + (i + 1) * BLOCK, :].astype(F32)
            whole = hidden[rows, :] + token + ob
            hidden[rows, :] = whole
            xhat, _ = standardize(whole)
            low = (xhat * g2 + s2).astype(BF16)
            normed_two[rows, :] = low
            n2t[:, rows] = low.T
        task(at, norm_two)
        at += 0.7

    def keep_hidden():
        kept[1].start()
    task(at, keep_hidden)
    table = nearest(nt)
    slab = 32

    def grads_out(slot, shard):
        return pltpu.make_async_copy(gbuf.at[slot], grads.at[shard], gsem.at[slot])

    def mlp_shard(position, shard):
        slot = position % 2
        up = w[shard, 1].reshape(width, width)
        down = w[shard, 2].reshape(width, width)
        pre_s[...] = dot(normed_two[...], up, NN) + bias_all[shard, 0:1, :]
        gact_s[...] = dot(cot[...], down, NT)

        def step(i, total):
            rows = pl.ds(pl.multiple_of(i * slab, slab), slab)
            value, slope = gelu_parts(pre_s[rows, :])
            act[rows, :] = value.astype(BF16)
            low = (gact_s[rows, :] * slope).astype(BF16)
            gpre[rows, :] = low
            return total + low.astype(F32)
        total = lax.fori_loop(0, own // slab, step, jnp.zeros((slab, width), F32))
        small[pl.ds(8 + shard, 1), :] = jnp.sum(total, axis=0, keepdims=True)
        if position == 0:
            mlp[...] = dot(act[...], down, NN)
            gtwo[...] = dot(gpre[...], up, NT)
        else:
            mlp[...] += dot(act[...], down, NN)
            gtwo[...] += dot(gpre[...], up, NT)
        if position >= 2:
            grads_out(slot, shard).wait()
        shape = gbuf.shape[2:]
        gbuf[slot, 0] = dot(n2t[...], gpre[...], NN).astype(BF16).reshape(shape)
        gbuf[slot, 1] = dot(cot_t[...], act[...], NN).astype(BF16).reshape(shape)
        grads_out(slot, shard).start()

    for position in range(nt):
        def run(position=position):
            mlp_shard(position, pick(table, position))
        if position > 0:
            at = max([at] + [ready_at[k, position - 1] for k in range(1, chunks)])
        task(at, run)
        at += 6.0

    def finish():
        def part(n, carry):
            rows = pl.ds(pl.multiple_of(n * 32, 32), 32)
            result[rows, :] = (hidden[rows, :] + mlp[rows, :] + db).astype(BF16)
            return carry
        kept[7].start()
        lax.fori_loop(0, own // 32, part, 0)
        kept[0].start()
    task(at, finish)

    def keep_copy():
        return pltpu.make_async_copy(w.at[:, 0], w0, ls.at[0])

    def keep_first():
        keep_copy().start()
    task(at - 10.0, keep_first)
    ordered(tasks)
    grads_out(0, 0).wait()
    grads_out(1, 0).wait()
    keep_copy().wait()
    for copy in kept:
        copy.wait()
    for n in (0, 1, 2, 3, 4, 6, 7):
        small[n:n + 1, :] = jnp.zeros((1, width), F32)
    if small.shape[0] > 8 + nt:
        small[8 + nt:, :] = jnp.zeros((small.shape[0] - 8 - nt, width), F32)
    z_finish()
    for j in range(nt - 1):
        bias_send(j).wait_send()
    for k in range(chunks):
        for j in range(nt - 1):
            def end(shard, k, way, j):
                core(shard, k, way, j).wait_send()
                for q in (0, 1):
                    one(shard, k, q, way, j).wait_send()
                    if k < DIRECT:
                        two(shard, k, q, way, j).wait_send()
            each(k, j, end)


def forward(arrays, nt):
    length, width = arrays[0].shape
    own = length // nt
    window = own + 2 * HALO
    piece = width // 16
    unit = (2, 2, 2, 2, piece, width)
    rows = width + 2 * arrays[12].shape[0]
    chunks = rows // (16 * piece)
    lines = 8 + nt + -nt % 8
    dma = pltpu.SemaphoreType.DMA
    vmem, any_ = pl.BlockSpec(memory_space=pltpu.VMEM), pl.BlockSpec(memory_space=pl.ANY)

    def shape(dims, kind):
        return jax.ShapeDtypeStruct(dims, kind)

    def low(*dims):
        return pltpu.VMEM(dims, BF16)

    def wide(*dims):
        return pltpu.VMEM(dims, F32)
    views = list(arrays)
    for n in (7, 11, 13):
        views[n] = arrays[n].reshape(unit[2:] if n == 7 else unit)
    views[5] = arrays[5].transpose(0, 2, 1).reshape((3,) + unit[2:])
    return pl.pallas_call(
        functools.partial(forward_kernel, nt, chunks, own),
        name="forward",
        out_shape=(
            shape((own, width), BF16), shape((own, width), F32),
            shape((window, width), BF16), shape((window, width), BF16), shape((window, width), BF16),
            shape((own, width), BF16), shape((width, own), BF16), shape((own, width), F32),
            shape((own // BLOCK, 8, 2 * BLOCK), F32), shape((lines, width), F32),
            shape((nt, chunks - 1) + unit, BF16), shape((nt,) + unit, BF16),
        ),
        in_specs=[any_, any_] + [vmem] * 3 + [any_, vmem, any_] + [vmem] * 3 + [any_, vmem, any_, vmem],
        out_specs=(any_,) * 8 + (vmem, vmem, any_, any_),
        scratch_shapes=[
            low(own, width), wide(own, width), low(window, width), low(window, width), low(window, width),
            low(width, own), wide(own, width),
            low(window, width), low(own, width), pltpu.VMEM((1, length + 2 * HALO), jnp.int32),
            pltpu.VMEM((1, window), jnp.int32), pltpu.VMEM((window, BLOCK), jnp.int32), wide(8, width),
            low(window, width), low(nt, chunks, *unit), wide(nt, 8, width), dma((nt - 1,)), dma((nt - 1,)),
            low(own, width), low(own, width), low(width, own), low(width, own), wide(own, width),
            low(2, chunks - 1, *unit), wide(own, width), wide(own, width), low(own, width), low(own, width),
            dma((2,)),
            dma((2 * chunks - DIRECT, nt - 1, 2)), dma((2 * chunks - DIRECT, nt - 1, 2)),
            dma((chunks, nt - 1, 2, 4)), dma((chunks, nt - 1, 2, 4)),
            dma((chunks, nt - 1, 2)), dma((chunks, nt - 1, 2)), dma((8,)), dma((8,)),
        ],
        compiler_params=pltpu.CompilerParams(
            collective_id=1, has_side_effects=True, vmem_limit_bytes=VMEM_LIMIT),
    )(*views)


PIECES = 3
OWN_TIME, SIDE_TIME = 2.0, 1.5
PACE, STEPS, HOP = 6.0, (2.5, 9.5, 16.0), 6.0


def backward_kernel(nt, chunks, extra,
                    lse_ref, small1, segments, gain_1, gain_2,
                    cotangent, tokens_in, grads, w0, result, hidden_in, q_in, k_in, v_in, normed_in, heads_in, gtwo_in,
                    total, small, gathered_r, gathered_g,
                    hidden, q_ref, k_ref, v_ref, normed, heads_t, gtwo,
                    s1, rc, ra, rb, rz, rx, rt, sr, g0, w_first, token, cot, segp, segr, segc, branch, g_ref, stats,
                    halo_g, halo_s, dk, dv, dq, d_t, gtwo_out, own_ig,
                    ls, cs, cr, ps, pr, zs, zr, xs, xr, fs, fr, os_, or_, ss, sm, hs, hr, lo, in_sem):
    d, t, b0, b1, b2 = place()
    own, width = hidden.shape
    blocks = own // BLOCK
    scale = HEAD_DIM ** -0.5
    gathered = (gathered_r, gathered_g)
    bits = (1, 2, 4) + tuple(extra)
    order = tuple(range(chunks))[::-1]
    units = [(k, s) for k in order for s in range(nt)]

    def own_copy(k, s):
        return pltpu.make_async_copy(grads.at[s, k - 1, b0], s1.at[s, k], ls.at[s, k])

    arrivals = [pltpu.make_async_copy(source, goal, in_sem.at[n]) for n, (source, goal) in enumerate((
        (hidden_in, hidden), (gtwo_in, gtwo), (heads_in, heads_t), (q_in, q_ref), (k_in, k_ref), (v_in, v_ref),
        (normed_in, normed), (result, gathered_r.at[t])))]
    fetch_w = pltpu.make_async_copy(w0, w_first, lo.at[0])
    mine = pl.ds(pl.multiple_of(t * own, own), own)
    fetch_t = pltpu.make_async_copy(tokens_in.at[mine], token, lo.at[1])
    fetch_t.start()
    fetch_c = pltpu.make_async_copy(cotangent.at[mine], cot, lo.at[2])
    fetch_c.start()
    for copy in arrivals[:3]:
        copy.start()
    fetch_w.start()
    for copy in arrivals[3:]:
        copy.start()
    for k, s in units:
        if k > 0:
            own_copy(k, s).start()
    window_segments(segments, segp, segr, segc)
    greet(nt, bits, nt > 2)
    tasks = []

    def task(when, body):
        tasks.append((when, len(tasks), body))

    def core(k, s):
        source = g0.at[s, 1 - b0] if k == 0 else grads.at[s, k - 1, 1 - b0]
        return remote(source, rc.at[s, k], cs.at[s, k], cr.at[s, k], dp=flip(d, 1))

    def one(k, s, q):
        if q == 0:
            return remote(s1.at[s, k, 1 - b2, :, 0], ra.at[s, k], ps.at[s, k, 0], pr.at[s, k, 0], dp=flip(d, 4))
        return remote(s1.at[s, k, :, 1 - b1, 1], rb.at[s, k], ps.at[s, k, 1], pr.at[s, k, 1], dp=flip(d, 2))

    def two(k, s, q):
        if q == 0:
            return remote(s1.at[s, k, b2, 1 - b1, 0], rz.at[s, k, 0], ps.at[s, k, 2], pr.at[s, k, 2], dp=flip(d, 2))
        return remote(s1.at[s, k, 1 - b2, b1, 1], rz.at[s, k, 1], ps.at[s, k, 3], pr.at[s, k, 3], dp=flip(d, 4))

    def up(k, s):
        return remote(s1.at[s, k, b2, b1], rx.at[s, k], zs.at[s, k, 0], zr.at[s, k, 0], tensor=t + 1)

    def down(k, s, last):
        goal = rt.at[k] if last else rx.at[s, k]
        return remote(s1.at[s, k, b2, b1], goal, zs.at[s, k, 1], zr.at[s, k, 1], tensor=t - 1)

    def halo(n):
        if n == 0:
            return remote(g_ref.at[pl.ds(own - REACH, REACH)], halo_g.at[0, pl.ds(HALO - REACH, REACH)],
                          hs.at[0], hr.at[0], tensor=t + 1)
        if n == 1:
            return remote(g_ref.at[pl.ds(0, REACH)], halo_g.at[1, pl.ds(0, REACH)], hs.at[1], hr.at[1], tensor=t - 1)
        span = HALO // BLOCK
        if n == 2:
            return remote(stats.at[pl.ds(blocks - span, span)], halo_s.at[0], hs.at[2], hr.at[2], tensor=t + 1)
        return remote(stats.at[pl.ds(0, span)], halo_s.at[1], hs.at[3], hr.at[3], tensor=t - 1)

    def halo_start():
        @pl.when(t < nt - 1)
        def _():
            halo(0).start()
            halo(2).start()

        @pl.when(t > 0)
        def _():
            halo(1).start()
            halo(3).start()
        pad = HALO - REACH
        halo_g[0, 0:pad, :] = jnp.zeros((pad, width), BF16)
        halo_g[1, REACH:HALO, :] = jnp.zeros((pad, width), BF16)

        @pl.when(t == 0)
        def _():
            halo_g[0] = jnp.zeros((HALO, width), BF16)
            halo_s[0] = jnp.zeros(halo_s.shape[1:], F32)

        @pl.when(t == nt - 1)
        def _():
            halo_g[1] = jnp.zeros((HALO, width), BF16)
            halo_s[1] = jnp.zeros(halo_s.shape[1:], F32)

    def halo_end():
        @pl.when(t > 0)
        def _():
            halo(0).wait_recv()
            halo(2).wait_recv()

        @pl.when(t < nt - 1)
        def _():
            halo(1).wait_recv()
            halo(3).wait_recv()

    def attend_block(w, cols, row):
        q0 = w * BLOCK
        middle = HALO // BLOCK <= w < HALO // BLOCK + blocks
        k0, k1 = max(0, q0 - REACH), q0 + BLOCK + REACH
        if not middle:
            k0, k1 = max(k0, HALO), min(k1, HALO + own)
        q2 = stacked(q_ref[q0:q0 + BLOCK, cols])
        if middle:
            i = w - HALO // BLOCK
            g_rows = g_ref[i * BLOCK:(i + 1) * BLOCK, cols]
            lse, delta = stats[i, pl.ds(row, 1), :], stats[i, pl.ds(8 + row, 1), :]
        else:
            side = int(w > HALO // BLOCK)
            i = w if side == 0 else w - HALO // BLOCK - blocks
            g_rows = halo_g[side, i * BLOCK:(i + 1) * BLOCK, cols]
            lse, delta = halo_s[side, i, pl.ds(row, 1), :], halo_s[side, i, pl.ds(8 + row, 1), :]
        g2 = stacked(g_rows)
        k2, v2 = k_ref[k0:k1, cols], v_ref[k0:k1, cols]
        allowed = segc[k0:k1, :] == segr[:, q0:q0 + BLOCK]
        allowed = jnp.concatenate([allowed, allowed], axis=1)
        s = dot(k2, q2, NT) * scale
        p = jnp.exp(jnp.where(allowed, s - lse, -1e9))
        low = p.astype(BF16)
        ds = (p * (dot(v2, g2, NT) - delta)).astype(BF16)
        o0, o1 = max(k0, HALO), min(k1, HALO + own)
        dst, src = slice(o0 - HALO, o1 - HALO), slice(o0 - k0, o1 - k0)
        dk[dst, cols] += dot(ds[src], q2, NN)
        dv[dst, cols] += dot(low[src], g2, NN)
        if middle:
            out = dot(k2.T, ds, NN) * scale
            half = out.shape[1] // 2
            both = jnp.concatenate([out[:HEAD_DIM, :half], out[HEAD_DIM:, half:]], axis=0).astype(BF16)
            d_t[0, cols, i * BLOCK:(i + 1) * BLOCK] = both
            dq[0, i * BLOCK:(i + 1) * BLOCK, cols] = both.T

    def attention(first, count, mine):
        def pair(j, carry):
            cols = pl.ds(pl.multiple_of(j * 128, 128), 128)
            if mine:
                dk[:, cols] = jnp.zeros((own, 128), F32)
                dv[:, cols] = jnp.zeros((own, 128), F32)
                for b in range(blocks):
                    attend_block(HALO // BLOCK + b, cols, j)
            else:
                for w in tuple(range(HALO // BLOCK)) + tuple(range(HALO // BLOCK + blocks, 2 * HALO // BLOCK + blocks)):
                    attend_block(w, cols, j)
                for n, (ref, factor) in enumerate(((dk, scale), (dv, 1.0))):
                    value = (ref[:, cols] * factor).astype(BF16)
                    dq[1 + n, :, cols] = value
                    d_t[1 + n, cols, :] = value.T
            return carry
        for j in range(first, first + count):
            pair(j, 0)

    g1, g2 = gain_1[...].reshape(1, width), gain_2[...].reshape(1, width)

    def norm_two_back():
        fetch_c.wait()
        arrivals[0].wait()
        arrivals[1].wait()

        def part(n, carry):
            rows = pl.ds(pl.multiple_of(n * 32, 32), 32)
            xhat, r = standardize(hidden[rows, :])
            grad = gtwo[rows, :]
            gh = cot[rows, :].astype(F32) + norm_back(grad * g2, xhat, r)
            gtwo_out[rows, :] = gh
            branch[rows, :] = gh.astype(BF16)
            return carry[0] + gh, carry[1] + grad * xhat, carry[2] + grad
        zero = jnp.zeros((32, width), F32)
        sums = lax.fori_loop(0, own // 32, part, (zero, zero, zero))
        small[...] = small1[...]
        for line, value in zip((2, 3, 4), sums):
            small[line:line + 1, :] = jnp.sum(value, axis=0, keepdims=True)

    def out_back():
        fetch_w.wait()
        arrivals[2].wait()
        outw = w_first[:, 1, 1].reshape(width, width)
        rows = branch[...]
        g_ref[...] = dot(rows, outw, NT).astype(BF16)
        g_t = dot(outw, rows, NT).astype(BF16).astype(F32)
        product = g_t * heads_t[...].astype(F32)
        for b in range(blocks):
            stats[b, 0:8, :] = lse_ref[b]
            for h in range(width // HEAD_DIM):
                line = jnp.sum(product[h * HEAD_DIM:(h + 1) * HEAD_DIM, b * BLOCK:(b + 1) * BLOCK], axis=0, keepdims=True)
                stats[b, 8 + h // 2:9 + h // 2, (h % 2) * BLOCK:(h % 2 + 1) * BLOCK] = line
            stats[b, 8 + width // 128:16, :] = jnp.zeros((8 - width // 128, 2 * BLOCK), F32)

    def out_grad():
        value = dot(heads_t[...], branch[...], NN).astype(BF16)
        g0[:, 1, 1] = value.reshape((nt,) + g0.shape[3:])
    task(0.3, norm_two_back)
    task(3.0, out_back)
    task(5.5, halo_start)
    task(6.0, out_grad)
    at = 7.0
    pairs = width // 128

    def attend_ready():
        for copy in arrivals[3:]:
            copy.wait()
    task(at, attend_ready)
    for first in range(pairs):
        def run(first=first):
            attention(first, 1, True)
        task(at, run)
        at += OWN_TIME
    at = max(at, 24.0)
    task(at, halo_end)
    for first in range(pairs):
        def run(first=first):
            attention(first, 1, False)
        task(at, run)
        at += SIDE_TIME

    def weight_of(kind):
        return w_first[:, kind // 2, kind % 2].reshape(width, width)

    def back_project():
        dk[...] = dot(dq[0], weight_of(0), NN)
        dk[...] += dot(dq[1], weight_of(1), NN)
        dk[...] += dot(dq[2], weight_of(2), NN)
    task(at, back_project)
    at += 2.5

    def norm_one():
        fetch_t.wait()

        def part(n, carry):
            rows = pl.ds(pl.multiple_of(n * 32, 32), 32)
            xhat, r = standardize(token[rows, :].astype(F32))
            grad = dk[rows, :]
            own_ig[rows, :] = (gtwo_out[rows, :] + norm_back(grad * g1, xhat, r)).astype(BF16)
            return (carry[0] + grad * xhat, carry[1] + grad, carry[2] + dq[0, rows, :].astype(F32),
                    carry[3] + dq[2, rows, :].astype(F32))
        zero = jnp.zeros((32, width), F32)
        sums = lax.fori_loop(0, own // 32, part, (zero, zero, zero, zero))
        for line, value in zip((0, 1, 6, 7), sums):
            small[line:line + 1, :] = jnp.sum(value, axis=0, keepdims=True)
        gathered_g[t] = own_ig[...]
    task(at, norm_one)
    at += 3.0
    ready = at
    for kind in range(3):
        def run(kind=kind):
            value = dot(d_t[kind], normed[...], NN).astype(BF16)
            g0[:, kind // 2, kind % 2] = value.reshape((nt,) + g0.shape[3:])
        task(at, run)
        at += 1.2

    late = at

    pace = PACE
    for n, (k, s) in enumerate(units):
        base = n * pace if k > 0 else max(n * pace, late + 3.0 + (n - nt * (chunks - 1)) * pace)

        def first(k=k, s=s):
            core(k, s).start()

        def second(k=k, s=s):
            core(k, s).wait_recv()
            if k > 0:
                own_copy(k, s).wait()
                add_bf16(s1.at[s, k], rc.at[s, k])
            else:
                s1[s, k] = (g0[s, b0].astype(F32) + rc[s, k].astype(F32)).astype(BF16)
            one(k, s, 0).start()
            one(k, s, 1).start()

        def third(k=k, s=s):
            one(k, s, 0).wait_recv()
            one(k, s, 1).wait_recv()
            add_bf16(s1.at[s, k, b2, :, 0], ra.at[s, k])
            add_bf16(s1.at[s, k, :, b1, 1], rb.at[s, k])
            two(k, s, 0).start()
            two(k, s, 1).start()

        def fourth(k=k, s=s):
            two(k, s, 0).wait_recv()
            two(k, s, 1).wait_recv()
            add_bf16(s1.at[s, k, b2, b1, 0], rz.at[s, k, 0])
            add_bf16(s1.at[s, k, b2, b1, 1], rz.at[s, k, 1])
        task(max(base - 12.0, -10.0) if k > 0 else max(base - 12.0, late + 0.01), first)
        task(base + STEPS[0], second)
        task(base + STEPS[1], third)
        task(base + STEPS[2], fourth)
        if s == nt - 1:
            end_of_chunk = base + STEPS[2]
        else:
            continue

        for hop in range(nt):
            def chain(k=k, hop=hop):
                @pl.when(t == hop)
                def _():
                    for s in reversed(range(nt)):
                        @pl.when(s >= t)
                        def _():
                            if hop > 0:
                                up(k, s).wait_recv()
                                add_bf16(s1.at[s, k, b2, b1], rx.at[s, k])
                            if hop < nt - 1:
                                @pl.when(s > t)
                                def _():
                                    up(k, s).start()

                @pl.when(t == nt - 1 - hop)
                def _():
                    for s in range(nt):
                        if hop > 0:
                            @pl.when(s < t)
                            def _():
                                down(k, s, False).wait_recv()
                                add_bf16(s1.at[s, k, b2, b1], rx.at[s, k])

                            @pl.when(s == t)
                            def _():
                                down(k, s, True).wait_recv()
                                add_bf16(s1.at[s, k, b2, b1], rt.at[k])
                        if hop < nt - 1:
                            @pl.when(s == t - 1)
                            def _():
                                down(k, s, True).start()

                            @pl.when(s < t - 1)
                            def _():
                                down(k, s, False).start()
            task(end_of_chunk + 0.5 + HOP * hop, chain)
        base = end_of_chunk + 0.5 + HOP * nt

        for e, bit in enumerate(extra):
            def more(k=k, e=e, bit=bit):
                swap = remote(s1.at[t, k, b2, b1], rx.at[nt + e, k], xs.at[e, k], xr.at[e, k], dp=flip(d, bit))
                swap.start()
                swap.wait()
                add_bf16(s1.at[t, k, b2, b1], rx.at[nt + e, k])
            task(base + 0.01 * e, more)

        def settle(k=k):
            total[k, b0, b2, b1] = s1[t, k, b2, b1]

        def give_one(k, q):
            if q == 0:
                piece = total.at[k, b0, b2, b1, 0]
                return remote(piece, piece, fs.at[k, 0], fr.at[k, 0], dp=flip(d, 2))
            piece = total.at[k, b0, b2, b1, 1]
            return remote(piece, piece, fs.at[k, 1], fr.at[k, 1], dp=flip(d, 4))

        def give_two(k, q):
            if q == 0:
                piece = total.at[k, b0, b2, :, 0]
                return remote(piece, piece, fs.at[k, 2], fr.at[k, 2], dp=flip(d, 4))
            piece = total.at[k, b0, :, b1, 1]
            return remote(piece, piece, fs.at[k, 3], fr.at[k, 3], dp=flip(d, 2))

        def give_core(k):
            return remote(total.at[k, b0], total.at[k, b0], fs.at[k, 4], fr.at[k, 4], dp=flip(d, 1))

        def spread_one(k=k):
            for q in (0, 1):
                give_one(k, q).start()

        def spread_two(k=k):
            for q in (0, 1):
                give_one(k, q).wait_recv()
            for q in (0, 1):
                give_two(k, q).start()

        def spread_core(k=k):
            for q in (0, 1):
                give_two(k, q).wait_recv()
            give_core(k).start()

        def spread_end(k=k):
            give_core(k).wait()
            for q in (0, 1):
                give_one(k, q).wait_send()
                give_two(k, q).wait_send()
        task(base + 0.5, settle)
        task(base + 1.0, spread_one)
        task(base + 4.0, spread_two)
        task(base + 8.0, spread_core)
        task(1e6, spread_end)

    part = own // PIECES

    def piece_of(ref, n):
        return ref.at[pl.ds(n % PIECES * part, part)]
    z_tasks, z_finish = relay_tasks(
        nt, 2 * PIECES, lambda n: piece_of((result, own_ig)[n // PIECES], n),
        lambda s, n: piece_of(gathered[n // PIECES].at[s], n), (os_, or_),
        lambda n, j: (-5.0, ready)[n // PIECES] + 14.0 / PIECES * (n % PIECES) + 14.0 * j + (0.01 if j == 0 else 1.0),
        lambda *a: None)
    tasks += [(w, 1000 + n, b) for w, n, b in z_tasks]

    exchanges = [("dp", bit) for bit in bits]
    step = 1
    while step < nt:
        exchanges.append(("tensor", step))
        step *= 2
    for e, (axis, bit) in enumerate(exchanges):
        def swap(e=e, axis=axis, bit=bit):
            goal = {axis: flip(lax.axis_index(axis), bit)}
            return remote(small, sr.at[e], ss.at[e], sm.at[e], **goal)

        def begin(swap=swap):
            swap().start()

        def end(e=e, swap=swap):
            swap().wait()
            small[...] = small[...] + sr[e]
        task(late + 1.0 + 5.0 * e, begin)
        task(late + 5.5 + 5.0 * e, end)

    ordered(tasks)
    z_finish()

    @pl.when(t < nt - 1)
    def _():
        halo(0).wait_send()
        halo(2).wait_send()

    @pl.when(t > 0)
    def _():
        halo(1).wait_send()
        halo(3).wait_send()
    for k, s in units:
        core(k, s).wait_send()
        for q in (0, 1):
            one(k, s, q).wait_send()
            two(k, s, q).wait_send()

        @pl.when(s > t)
        def _():
            up(k, s).wait_send()

        @pl.when(s < t)
        def _():
            down(k, s, False).wait_send()


def backward(vmem_arrays, hbm_arrays, nt, extra):
    own, width = hbm_arrays[4].shape
    grads, segments = hbm_arrays[2], vmem_arrays[2]
    small_shape = vmem_arrays[1].shape
    piece, chunks = width // 16, grads.shape[1] + 1
    window = own + 2 * HALO
    dma = pltpu.SemaphoreType.DMA
    hops = 3 + len(extra) + (nt - 1).bit_length()
    vmem, any_ = pl.BlockSpec(memory_space=pltpu.VMEM), pl.BlockSpec(memory_space=pl.ANY)
    unit = (2, 2, 2, piece, width)
    blocks = own // BLOCK

    def low(*dims):
        return pltpu.VMEM(dims, BF16)

    def wide(*dims):
        return pltpu.VMEM(dims, F32)
    return pl.pallas_call(
        functools.partial(backward_kernel, nt, chunks, extra),
        name="backward",
        out_shape=(
            jax.ShapeDtypeStruct((chunks, 2) + unit, BF16),
            jax.ShapeDtypeStruct(small_shape, F32),
            jax.ShapeDtypeStruct((nt, own, width), BF16),
            jax.ShapeDtypeStruct((nt, own, width), BF16),
        ),
        in_specs=[vmem] * len(vmem_arrays) + [any_] * len(hbm_arrays),
        out_specs=(vmem,) * 4,
        scratch_shapes=[
            wide(own, width), low(window, width), low(window, width), low(window, width), low(own, width),
            low(width, own), wide(own, width),
            low(nt, chunks, *unit), low(nt, chunks, *unit),
            low(nt, chunks, 2, piece, width), low(nt, chunks, 2, piece, width), low(nt, chunks, 2, piece, width),
            low(nt + len(extra), chunks, 2, piece, width), low(chunks, 2, piece, width),
            wide(hops, *small_shape), low(nt, 2, *unit), low(nt, 2, *unit),
            low(own, width), low(own, width), pltpu.VMEM((1, segments.shape[1] + 2 * HALO), jnp.int32),
            pltpu.VMEM((1, window), jnp.int32), pltpu.VMEM((window, BLOCK), jnp.int32),
            low(own, width), low(own, width), wide(blocks, 16, 2 * BLOCK),
            low(2, HALO, width), wide(2, HALO // BLOCK, 16, 2 * BLOCK),
            wide(own, width), wide(own, width), low(3, own, width), low(3, width, own),
            wide(own, width), low(own, width),
            dma((nt, chunks)), dma((nt, chunks)), dma((nt, chunks)),
            dma((nt, chunks, 4)), dma((nt, chunks, 4)),
            dma((nt, chunks, 2)), dma((nt, chunks, 2)),
            dma((max(1, len(extra)), chunks)), dma((max(1, len(extra)), chunks)),
            dma((chunks, 5)), dma((chunks, 5)),
            dma((2 * PIECES, nt - 1, 2)), dma((2 * PIECES, nt - 1, 2)),
            dma((hops,)), dma((hops,)), dma((4,)), dma((4,)), dma((3,)), dma((8,)),
        ],
        compiler_params=pltpu.CompilerParams(
            collective_id=2, has_side_effects=True, vmem_limit_bytes=VMEM_LIMIT),
    )(*vmem_arrays, *hbm_arrays)


def finish_kernel(nt, ndp, total_in, small, results, input_grads,
                  results_out, input_grads_out, g1, s1, qkv, qvb, out_w, out_b, g2, s2, up, up_b, down, down_b,
                  total, held, first, second, third, in_sem, out_sem):
    t = lax.axis_index("tensor")
    width = small.shape[1]
    local = width // nt
    scale = 1.0 / ndp
    parts = [pltpu.make_async_copy(total_in.at[k], total.at[k], in_sem.at[k]) for k in range(3)]
    for k in (1, 2, 0):
        parts[k].start()
    stage = [pltpu.make_async_copy(results, held.at[0], in_sem.at[3]), pltpu.make_async_copy(input_grads, held.at[1], in_sem.at[4])]
    for copy in stage:
        copy.start()
    moves = []
    for ref, line in ((g1, 0), (s1, 1), (out_b, 2), (g2, 3), (s2, 4), (down_b, 5)):
        ref[...] = small[line:line + 1, :].reshape(width) * scale
    up_b[...] = small[pl.ds(8 + t, 1), :].reshape(width) * scale
    for place in range(nt):
        @pl.when(t == place)
        def _():
            qvb[...] = small[6:8, place * local:(place + 1) * local] * scale
    for n, goal in enumerate((results_out, input_grads_out)):
        stage[n].wait()
        moves.append(pltpu.make_async_copy(held.at[n], goal, out_sem.at[n]))
        moves[-1].start()
    parts[1].wait()
    second[...] = total[1].reshape(width, width).astype(F32) * scale
    moves.append(pltpu.make_async_copy(second, up, out_sem.at[2]))
    moves[-1].start()
    parts[2].wait()
    third[...] = (total[2].reshape(width, width).astype(F32) * scale).T
    moves.append(pltpu.make_async_copy(third, down, out_sem.at[3]))
    moves[-1].start()
    parts[0].wait()
    first[...] = total[0].reshape(nt, local, width).astype(F32) * scale
    moves.append(pltpu.make_async_copy(first.at[pl.ds(0, 3)], qkv, out_sem.at[4]))
    moves[-1].start()
    moves.append(pltpu.make_async_copy(first.at[3], out_w, out_sem.at[5]))
    moves[-1].start()
    for copy in moves:
        copy.wait()


def finish_up(total, small, results, input_grads, nt, ndp):
    width = small.shape[1]
    local = width // nt
    dma = pltpu.SemaphoreType.DMA
    vmem, any_ = pl.BlockSpec(memory_space=pltpu.VMEM), pl.BlockSpec(memory_space=pl.ANY)

    def shape(*dims):
        return jax.ShapeDtypeStruct(dims, F32)
    return pl.pallas_call(
        functools.partial(finish_kernel, nt, ndp),
        name="finish",
        out_shape=(jax.ShapeDtypeStruct(results.shape, BF16), jax.ShapeDtypeStruct(results.shape, BF16),
                   shape(width), shape(width), shape(3, local, width), shape(2, local), shape(local, width), shape(width),
                   shape(width), shape(width), shape(width, width), shape(width), shape(width, width), shape(width)),
        in_specs=[any_, vmem, any_, any_],
        out_specs=(any_, any_, vmem, vmem, any_, vmem, any_, vmem, vmem, vmem, any_, vmem, any_, vmem),
        scratch_shapes=[pltpu.VMEM(total.shape, BF16), pltpu.VMEM((2,) + results.shape, BF16), pltpu.VMEM((nt, local, width), F32),
                        pltpu.VMEM((width, width), F32), pltpu.VMEM((width, width), F32), dma((5,)), dma((6,))],
        compiler_params=pltpu.CompilerParams(vmem_limit_bytes=VMEM_LIMIT),
    )(total, small, results, input_grads)


def body(tokens_in, segment_ids, first_gain, first_shift, qkv_weight, query_value_bias, out_weight, out_bias,
         second_gain, second_shift, up_weight, up_bias, down_weight, down_bias, cotangent):
    nt, ndp = lax.axis_size("tensor"), lax.axis_size("dp")
    length, width = tokens_in.shape
    (result, hidden, q, k, v, normed, heads_t, grad_two, lse, small, mlp_grads, w_first) = forward(
        (tokens_in, cotangent, segment_ids, first_gain, first_shift, qkv_weight, query_value_bias, out_weight, out_bias,
         second_gain, second_shift, up_weight, up_bias, down_weight, down_bias), nt)
    extra = []
    bit = 8
    while bit < ndp:
        extra.append(bit)
        bit *= 2
    total, small, results, input_grads = backward(
        (lse, small, segment_ids, first_gain, second_gain),
        (cotangent, tokens_in, mlp_grads, w_first, result, hidden, q, k, v, normed, heads_t, grad_two), nt, tuple(extra))
    outs = list(finish_up(total, small, results, input_grads, nt, ndp))
    outs[0], outs[1] = outs[0].reshape(length, width), outs[1].reshape(length, width)
    outs[4] = outs[4].transpose(0, 2, 1)
    return tuple(outs)


def solution(mesh):
    placed = (
        P("dp", None), P("dp", None), P(), P(), P(None, None, "tensor"), P(None, "tensor"), P("tensor", None), P(),
        P(), P(), P(None, "tensor"), P("tensor"), P("tensor", None), P(), P("dp", None),
    )
    return jax.shard_map(
        body,
        mesh=mesh,
        in_specs=placed,
        out_specs=(
            P("dp", None), P("dp", None), P(), P(), P(None, None, "tensor"), P(None, "tensor"), P("tensor", None),
            P(), P(), P(), P(None, "tensor"), P("tensor"), P("tensor", None), P(),
        ),
        check_vma=False,
    )
```

```python
import functools

import jax
import jax.numpy as jnp
from jax import lax
from jax.experimental import pallas as pl
from jax.experimental.pallas import tpu as pltpu
from jax.sharding import PartitionSpec as P

HEAD_DIM = 64
HALO = 256
REACH = 224
BLOCK = 128
EPS = 1e-06
SCALE = HEAD_DIM ** -0.5
F32 = jnp.float32
BF16 = jnp.bfloat16
MESH = pl.DeviceIdType.MESH
VMEM_LIMIT = 60 << 20


def place():
    d, t = lax.axis_index("dp"), lax.axis_index("tensor")
    return d, t, lax.rem(d, 2), lax.rem(d // 2, 2), lax.rem(d // 4, 2)


def flip(d, value):
    return d + value * (1 - 2 * lax.rem(d // value, 2))


def remote(src, dst, send, recv, **axis):
    return pltpu.make_async_remote_copy(
        src_ref=src, dst_ref=dst, send_sem=send, recv_sem=recv,
        device_id=axis, device_id_type=MESH)


def greet(nt, bits, far=False):
    d, t = lax.axis_index("dp"), lax.axis_index("tensor")
    barrier = pltpu.get_barrier_semaphore()

    @pl.when(t > 0)
    def _():
        pl.semaphore_signal(barrier, inc=1, device_id={"tensor": t - 1}, device_id_type=MESH)

    @pl.when(t < nt - 1)
    def _():
        pl.semaphore_signal(barrier, inc=1, device_id={"tensor": t + 1}, device_id_type=MESH)

    for bit in bits:
        pl.semaphore_signal(barrier, inc=1, device_id={"dp": flip(d, bit)}, device_id_type=MESH)
    if far:
        pl.semaphore_signal(barrier, inc=1, device_id={"tensor": flip(t, 2)}, device_id_type=MESH)
    peers = len(bits) + int(far) + (t > 0).astype(jnp.int32) + (t < nt - 1).astype(jnp.int32)
    pl.semaphore_wait(barrier, peers)


def ordered(tasks):
    for _, _, task in sorted(tasks, key=lambda item: item[:2]):
        task()


def relay_tasks(nt, chunks, own, full, sems, start, arrived):
    send, recv = sems
    tasks = []
    t = lax.axis_index("tensor")
    for k in range(chunks):
        for j in range(nt):
            def step(k=k, j=j):
                for way in (0, 1):
                    sign = 1 - 2 * way
                    shard = t - sign * j
                    inside = (shard >= 0) & (shard < nt)
                    if j > 0:
                        @pl.when(inside)
                        def _():
                            remote(full(shard, k), full(shard, k), send.at[k, j - 1, way], recv.at[k, j - 1, way],
                                   tensor=t).wait_recv()
                            arrived(k, j, way, shard)
                    if j < nt - 1:
                        goal = t + sign
                        @pl.when(inside & (goal >= 0) & (goal < nt))
                        def _():
                            source = own(k) if j == 0 else full(shard, k)
                            remote(source, full(shard, k), send.at[k, j, way], recv.at[k, j, way],
                                   tensor=goal).start()
            tasks.append((start(k, j), len(tasks), step))

    def finish():
        for k in range(chunks):
            for j in range(nt - 1):
                for way in (0, 1):
                    sign = 1 - 2 * way
                    shard, goal = t - sign * j, t + sign
                    @pl.when((shard >= 0) & (shard < nt) & (goal >= 0) & (goal < nt))
                    def _():
                        source = own(k) if j == 0 else full(shard, k)
                        remote(source, full(shard, k), send.at[k, j, way], recv.at[k, j, way],
                               tensor=goal).wait_send()
    return tasks, finish


def add_bf16(ref, other):
    ref[...] = (ref[...].astype(F32) + other[...].astype(F32)).astype(BF16)


def stacked(pair):
    lane = lax.broadcasted_iota(jnp.int32, pair.shape, 1)
    zero = jnp.zeros_like(pair)
    return jnp.concatenate([jnp.where(lane < HEAD_DIM, pair, zero), jnp.where(lane < HEAD_DIM, zero, pair)], axis=0)


def dot(a, b, dims):
    return lax.dot_general(a, b, (dims, ((), ())), preferred_element_type=F32)


NN = ((1,), (0,))
NT = ((1,), (1,))


def untangle(both):
    half = both.shape[1] // 2
    return jnp.concatenate([both[:HEAD_DIM, :half], both[HEAD_DIM:, half:]], axis=0).T


def standardize(rows):
    center = rows - jnp.mean(rows, axis=-1, keepdims=True)
    r = lax.rsqrt(jnp.mean(center * center, axis=-1, keepdims=True) + EPS)
    return center * r, r


def norm_back(e, xhat, r):
    return r * (e - jnp.mean(e, axis=-1, keepdims=True) - xhat * jnp.mean(e * xhat, axis=-1, keepdims=True))


def window_segments(segments, padded, row, column):
    length, window = segments.shape[1], row.shape[1]
    padded[...] = jnp.full(padded.shape, -1, jnp.int32)
    padded[:, HALO:HALO + length] = segments[...]
    own = window - 2 * HALO
    for i in range(window // BLOCK):
        first = pl.multiple_of(lax.axis_index("tensor") * own + i * BLOCK, BLOCK)
        line = padded[:, pl.ds(first, BLOCK)]
        row[:, i * BLOCK:(i + 1) * BLOCK] = line
        column[i * BLOCK:(i + 1) * BLOCK, :] = jnp.broadcast_to(line, (BLOCK, BLOCK)).T


def nearest(nt):
    return [sorted(range(nt), key=lambda s: (abs(s - p), s if p < nt // 2 else -s)) for p in range(nt)]


def pick(table, position):
    t = lax.axis_index("tensor")
    return sum((t == p).astype(jnp.int32) * row[position] for p, row in enumerate(table))


def gelu_parts(x):
    cdf = 0.5 * (1.0 + lax.erf(x * (0.5 ** 0.5)))
    pdf = jnp.exp(-0.5 * x * x) * ((2.0 * jnp.pi) ** -0.5)
    return x * cdf, cdf + x * pdf


ATTEND = 0.6
LINE_GAP, LAGS_0 = 2.3, (7.3, 12.9, 16.4)
DIRECT = 3
LINE, PLANE, LEAD, LAGS = 4.3, 4.2, 0.0, (5.6, 12.3, 15.8)


def forward_kernel(nt, chunks, own,
                   tokens_in, cotangent, segments, gain_1, shift_1, qkv_in, qv_bias, out_in, out_bias, gain_2, shift_2,
                   up_in, up_bias, down_in, down_bias,
                   result_out, hidden_out, q_out, k_out, v_out, normed_out, heads_out, gtwo_out, lse_ref, small, grads, w0,
                   result, hidden, q_ref, k_ref, v_ref, heads_t, gtwo, tok, cot, segp, segr, segc, bias, normed, w, bias_all, bias_sem, bias_recv, heads, normed_two, n2t,
                   cot_t, mlp, gbuf, pre_s, gact_s, act, gpre, gsem, zs, zr, ps, pr, cs, cr, ls, out_sem):
    d, t, b0, b1, b2 = place()
    window, width = tok.shape
    local = width // nt
    blocks = own // BLOCK
    local_copies = [pltpu.make_async_copy(qkv_in.at[kind], w.at[t, 0, kind // 2, kind % 2], ls.at[5 + kind])
                    for kind in range(3)] + [
        pltpu.make_async_copy(out_in, w.at[t, 0, 1, 1], ls.at[0]),
        pltpu.make_async_copy(up_in, w.at[t, 1], ls.at[1]),
        pltpu.make_async_copy(down_in, w.at[t, 2], ls.at[2]),
    ]
    for copy in local_copies:
        copy.start()
    cot_copy = pltpu.make_async_copy(cotangent.at[pl.ds(pl.multiple_of(t * own, own), own)], cot, ls.at[3])
    cot_copy.start()

    def token_copy(place):
        rows = own + HALO
        if place == 0:
            return pltpu.make_async_copy(tokens_in.at[pl.ds(0, rows)], tok.at[pl.ds(HALO, rows)], ls.at[4])
        if place == 1:
            return pltpu.make_async_copy(tokens_in.at[pl.ds((nt - 1) * own - HALO, rows)], tok.at[pl.ds(0, rows)], ls.at[4])
        first = pl.multiple_of(t * own - HALO, BLOCK)
        return pltpu.make_async_copy(tokens_in.at[pl.ds(first, window)], tok, ls.at[4])

    def tokens(act):
        @pl.when(t == 0)
        def _():
            act(token_copy(0))

        @pl.when(t == nt - 1)
        def _():
            act(token_copy(1))

        @pl.when((t > 0) & (t < nt - 1))
        def _():
            act(token_copy(2))
    tokens(lambda copy: copy.start())

    @pl.when(t == 0)
    def _():
        tok[0:HALO, :] = jnp.zeros((HALO, width), BF16)

    @pl.when(t == nt - 1)
    def _():
        tok[window - HALO:window, :] = jnp.zeros((HALO, width), BF16)

    barrier = pltpu.get_barrier_semaphore()
    for bit in (1, 2, 4):
        pl.semaphore_signal(barrier, inc=1, device_id={"dp": flip(d, bit)}, device_id_type=MESH)
    for j in range(1, nt):
        pl.semaphore_signal(barrier, inc=1, device_id={"tensor": lax.rem(t + j, nt)}, device_id_type=MESH)
    bias[...] = jnp.zeros(bias.shape, F32)
    bias[0:1, :] = up_bias[...].reshape(1, width)
    bias[1:3, 0:local] = qv_bias[...]
    bias_all[t] = bias[...]
    window_segments(segments, segp, segr, segc)
    for copy in local_copies:
        copy.wait()
    pl.semaphore_wait(barrier, 3 + nt - 1)
    tasks = []

    def task(when, body):
        tasks.append((when, len(tasks), body))

    def bias_send(j):
        return remote(bias, bias_all.at[t], bias_sem.at[j], bias_recv.at[j], tensor=lax.rem(t + j + 1, nt))

    def bias_get(j):
        source = lax.rem(t + nt - j - 1, nt)
        return remote(bias, bias_all.at[source], bias_sem.at[j], bias_recv.at[j], tensor=source)

    parity = lax.rem(b1 + b2, 2)

    def line_piece(shard, n):
        if n < DIRECT:
            return w.at[shard, n, b0, b2, b1]
        k, side = DIRECT + (n - DIRECT) // 2, (n - DIRECT) % 2
        return w.at[shard, k, b0, side, parity if side == 0 else 1 - parity]

    def one(shard, k, q, way, j):
        if k >= DIRECT:
            mine = line_piece(shard, DIRECT + 2 * (k - DIRECT) + q)
            return remote(mine, mine, ps.at[k, j, way, q], pr.at[k, j, way, q], dp=flip(d, 2 + 2 * q))
        if q == 0:
            mine = w.at[shard, k, b0, b2, b1, 0]
            return remote(mine, mine, ps.at[k, j, way, 0], pr.at[k, j, way, 0], dp=flip(d, 2))
        mine = w.at[shard, k, b0, b2, b1, 1]
        return remote(mine, mine, ps.at[k, j, way, 1], pr.at[k, j, way, 1], dp=flip(d, 4))

    def two(shard, k, q, way, j):
        if q == 0:
            mine = w.at[shard, k, b0, b2, :, 0]
            return remote(mine, mine, ps.at[k, j, way, 2], pr.at[k, j, way, 2], dp=flip(d, 4))
        mine = w.at[shard, k, b0, :, b1, 1]
        return remote(mine, mine, ps.at[k, j, way, 3], pr.at[k, j, way, 3], dp=flip(d, 2))

    def core(shard, k, way, j):
        return remote(w.at[shard, k, b0], w.at[shard, k, b0], cs.at[k, j, way], cr.at[k, j, way], dp=flip(d, 1))

    def each(k, j, act):
        for way in (0, 1):
            shard = t - (1 - 2 * way) * (j + 1)

            @pl.when((shard >= 0) & (shard < nt))
            def _():
                act(shard, k, way, j)

    def piece_time(n, j):
        if n < DIRECT:
            return LINE * (n * (nt - 1) + j) + (LINE_GAP if n > 0 else 0.0)
        pair, side = (n - DIRECT) // 2, (n - DIRECT) % 2
        return LINE_GAP + LINE * ((DIRECT + 2 * pair) * (nt - 1) + 2 * j - (j > 0) + side)

    def line_time(k, j):
        return piece_time(k, j) if k < DIRECT else piece_time(DIRECT + 2 * (k - DIRECT) + 1, j)

    z_tasks, z_finish = relay_tasks(
        nt, 2 * chunks - DIRECT, lambda n: line_piece(t, n), line_piece, (zs, zr), piece_time, lambda *a: None)
    tasks += z_tasks
    ready_at = {}
    for k in range(chunks):
        for j in range(nt - 1):
            def begin(k=k, j=j):
                def act(shard, k, way, j):
                    for q in (0, 1):
                        one(shard, k, q, way, j).start()
                each(k, j, act)

            def second(k=k, j=j):
                def act(shard, k, way, j):
                    for q in (0, 1):
                        one(shard, k, q, way, j).wait_recv()
                    for q in (0, 1):
                        two(shard, k, q, way, j).start()
                each(k, j, act)

            def third(k=k, j=j):
                def act(shard, k, way, j):
                    for q in (0, 1):
                        (two if k < DIRECT else one)(shard, k, q, way, j).wait_recv()
                    core(shard, k, way, j).start()
                each(k, j, act)

            def fourth(k=k, j=j):
                def act(shard, k, way, j):
                    core(shard, k, way, j).wait_recv()
                each(k, j, act)
            n = k * (nt - 1) + j
            base = max(line_time(k, j + 1) + 0.1, LEAD + PLANE * n)
            lags = LAGS_0 if k == 0 else LAGS
            skip = 0.0 if k < DIRECT else lags[0]
            task(base, begin)
            if k < DIRECT:
                task(base + lags[0], second)
            task(base + lags[1] - skip, third)
            task(base + lags[2] - skip, fourth)
            ready_at[k, j] = base + lags[2] - skip + 0.1

    def bias_begin():
        for j in range(nt - 1):
            bias_send(j).start()

    def bias_end():
        for j in range(nt - 1):
            bias_get(j).wait_recv()
    task(0.2, bias_begin)
    task(10.0, bias_end)

    g1, s1, ob, g2, s2, db = (ref[...].reshape(1, width) for ref in (gain_1, shift_1, out_bias, gain_2, shift_2, down_bias))

    def tokens_here():
        tokens(lambda copy: copy.wait())
    task(0.4, tokens_here)
    for i in range(window // BLOCK):
        def norm_rows(i=i):
            def part(n, carry):
                rows = pl.ds(pl.multiple_of(i * BLOCK + n * 32, 32), 32)
                xhat, _ = standardize(tok[rows, :].astype(F32))
                normed[rows, :] = (xhat * g1 + s1).astype(BF16)
                return carry
            lax.fori_loop(0, BLOCK // 32, part, 0)
        task(0.5 + 1.0 * i, norm_rows)

    kept = [pltpu.make_async_copy(source, goal, out_sem.at[n]) for n, (source, goal) in enumerate((
        (result, result_out), (hidden, hidden_out), (q_ref, q_out), (k_ref, k_out), (v_ref, v_out),
        (normed.at[pl.ds(HALO, own)], normed_out), (heads_t, heads_out), (gtwo, gtwo_out)))]

    def transposes():
        kept[5].start()
        cot_copy.wait()
        cot_t[...] = cot[...].T
        small[5:6, :] = jnp.sum(cot[...].astype(F32), axis=0, keepdims=True)
    task(7.9, transposes)

    half_rows = window // 2
    group = 2 * local

    def project(u, kind, part):
        rows = slice(part * half_rows, (part + 1) * half_rows)
        weight = w[pl.ds(2 * u, 2), 0, kind // 2, kind % 2].reshape(group, width)
        out = dot(normed[rows, :], weight, NT)
        if kind != 1:
            line = 1 + kind // 2
            out = out + jnp.concatenate([bias_all[2 * u, line:line + 1, :local], bias_all[2 * u + 1, line:line + 1, :local]], axis=1)
        target = (q_ref, k_ref, v_ref)[kind]
        target[rows, pl.ds(pl.multiple_of(u * group, 128), group)] = out.astype(BF16)

    def attention(u, b, only):
        first, count = BLOCK * b + 32, BLOCK + 448
        q0 = HALO + BLOCK * b
        allowed = segc[first:first + count, :] == segr[:, q0:q0 + BLOCK]
        allowed = jnp.concatenate([allowed, allowed], axis=1)

        def pair(j, carry):
            at = u * (group // 128) + j
            cols = pl.ds(pl.multiple_of(at * 128, 128), 128)
            q2 = stacked(q_ref[q0:q0 + BLOCK, cols] * SCALE)
            k2 = k_ref[first:first + count, cols]
            v2 = v_ref[first:first + count, cols]
            s = jnp.where(allowed, dot(k2, q2, NT), -1e9)
            m = jnp.max(s, axis=0, keepdims=True)
            p = jnp.exp(s - m)
            l = jnp.sum(p, axis=0, keepdims=True)
            out = dot(v2.T, p.astype(BF16), NN) * (1.0 / l)
            half = out.shape[1] // 2
            both = jnp.concatenate([out[:HEAD_DIM, :half], out[HEAD_DIM:, half:]], axis=0).astype(BF16)
            heads_t[cols, b * BLOCK:(b + 1) * BLOCK] = both
            heads[b * BLOCK:(b + 1) * BLOCK, cols] = both.T
            lse_ref[b, pl.ds(at, 1), :] = m + jnp.log(l)
            return carry
        pair(only, 0)

    def out_project(u, fresh):
        weight = w[pl.ds(2 * u, 2), 0, 1, 1].reshape(group, width)
        part = dot(heads[:, pl.ds(pl.multiple_of(u * group, 128), group)], weight, NN)
        if fresh:
            hidden[...] = part
        else:
            hidden[...] += part

    first_half = t // 2
    at = 7.0
    for n in range(nt // 2):
        u = lax.rem(first_half + n, nt // 2)
        if n == 0:
            at = max(at, ready_at[0, 0])
        else:
            at = max(at, ready_at[0, nt - 2])
        for kind in range(3):
            for part in range(2):
                def run(u=u, kind=kind, part=part):
                    project(u, kind, part)
                task(at, run)
                at += 0.7
        for b in range(blocks):
            for only in range(group // 128):
                def run(u=u, b=b, only=only):
                    attention(u, b, only)
                task(at, run)
                at += ATTEND

        def run(u=u, n=n):
            out_project(u, n == 0)
        task(at, run)
        at += 0.6

    def keep_heads():
        for n in (2, 3, 4, 6):
            kept[n].start()
    task(at, keep_heads)

    def rows_of(i):
        return slice(i * BLOCK, (i + 1) * BLOCK)

    for i in range(blocks):
        def norm_two(i=i):
            rows = rows_of(i)
            token = tok[HALO + i * BLOCK:HALO + (i + 1) * BLOCK, :].astype(F32)
            whole = hidden[rows, :] + token + ob
            hidden[rows, :] = whole
            xhat, _ = standardize(whole)
            low = (xhat * g2 + s2).astype(BF16)
            normed_two[rows, :] = low
            n2t[:, rows] = low.T
        task(at, norm_two)
        at += 0.7

    def keep_hidden():
        kept[1].start()
    task(at, keep_hidden)
    table = nearest(nt)
    slab = 32

    def grads_out(slot, shard):
        return pltpu.make_async_copy(gbuf.at[slot], grads.at[shard], gsem.at[slot])

    def mlp_steps(position):
        shard, slot = pick(table, position), position % 2

        def up():
            return w[shard, 1].reshape(width, width)

        def down():
            return w[shard, 2].reshape(width, width)

        def begin():
            pre_s[...] = dot(normed_two[...], up(), NN) + bias_all[shard, 0:1, :]

        def begin_back():
            gact_s[...] = dot(cot[...], down(), NT)

        def middle():
            def step(i, total):
                rows = pl.ds(pl.multiple_of(i * slab, slab), slab)
                value, slope = gelu_parts(pre_s[rows, :])
                act[rows, :] = value.astype(BF16)
                low = (gact_s[rows, :] * slope).astype(BF16)
                gpre[rows, :] = low
                return total + low.astype(F32)
            total = lax.fori_loop(0, own // slab, step, jnp.zeros((slab, width), F32))
            small[pl.ds(8 + shard, 1), :] = jnp.sum(total, axis=0, keepdims=True)

        def end():
            if position == 0:
                mlp[...] = dot(act[...], down(), NN)
                gtwo[...] = dot(gpre[...], up(), NT)
            else:
                mlp[...] += dot(act[...], down(), NN)
                gtwo[...] += dot(gpre[...], up(), NT)

        def grad_up():
            if position >= 2:
                grads_out(slot, shard).wait()
            gbuf[slot, 0] = dot(n2t[...], gpre[...], NN).astype(BF16).reshape(gbuf.shape[2:])

        def grad_down():
            gbuf[slot, 1] = dot(cot_t[...], act[...], NN).astype(BF16).reshape(gbuf.shape[2:])
            grads_out(slot, shard).start()
        return (begin, 0.7), (begin_back, 0.7), (middle, 1.0), (end, 1.4), (grad_up, 0.7), (grad_down, 0.7)

    for position in range(nt):
        if position > 0:
            at = max([at] + [ready_at[k, position - 1] for k in range(1, chunks)])
        for run, length in mlp_steps(position):
            task(at, run)
            at += length

    def finish():
        def part(n, carry):
            rows = pl.ds(pl.multiple_of(n * 32, 32), 32)
            result[rows, :] = (hidden[rows, :] + mlp[rows, :] + db).astype(BF16)
            return carry
        kept[7].start()
        lax.fori_loop(0, own // 32, part, 0)
        kept[0].start()
    task(at, finish)

    def keep_copy():
        return pltpu.make_async_copy(w.at[:, 0], w0, ls.at[0])

    def keep_first():
        keep_copy().start()
    task(at - 10.0, keep_first)
    ordered(tasks)
    grads_out(0, 0).wait()
    grads_out(1, 0).wait()
    keep_copy().wait()
    for copy in kept:
        copy.wait()
    for n in (0, 1, 2, 3, 4, 6, 7):
        small[n:n + 1, :] = jnp.zeros((1, width), F32)
    if small.shape[0] > 8 + nt:
        small[8 + nt:, :] = jnp.zeros((small.shape[0] - 8 - nt, width), F32)
    z_finish()
    for j in range(nt - 1):
        bias_send(j).wait_send()
    for k in range(chunks):
        for j in range(nt - 1):
            def end(shard, k, way, j):
                core(shard, k, way, j).wait_send()
                for q in (0, 1):
                    one(shard, k, q, way, j).wait_send()
                    if k < DIRECT:
                        two(shard, k, q, way, j).wait_send()
            each(k, j, end)


def forward(arrays, nt):
    length, width = arrays[0].shape
    own = length // nt
    window = own + 2 * HALO
    piece = width // 16
    unit = (2, 2, 2, 2, piece, width)
    rows = width + 2 * arrays[12].shape[0]
    chunks = rows // (16 * piece)
    lines = 8 + nt + -nt % 8
    dma = pltpu.SemaphoreType.DMA
    vmem, any_ = pl.BlockSpec(memory_space=pltpu.VMEM), pl.BlockSpec(memory_space=pl.ANY)

    def shape(dims, kind):
        return jax.ShapeDtypeStruct(dims, kind)

    def low(*dims):
        return pltpu.VMEM(dims, BF16)

    def wide(*dims):
        return pltpu.VMEM(dims, F32)
    views = list(arrays)
    for n in (7, 11, 13):
        views[n] = arrays[n].reshape(unit[2:] if n == 7 else unit)
    views[5] = arrays[5].transpose(0, 2, 1).reshape((3,) + unit[2:])
    return pl.pallas_call(
        functools.partial(forward_kernel, nt, chunks, own),
        name="forward",
        out_shape=(
            shape((own, width), BF16), shape((own, width), F32),
            shape((window, width), BF16), shape((window, width), BF16), shape((window, width), BF16),
            shape((own, width), BF16), shape((width, own), BF16), shape((own, width), F32),
            shape((own // BLOCK, 8, 2 * BLOCK), F32), shape((lines, width), F32),
            shape((nt, chunks - 1) + unit, BF16), shape((nt,) + unit, BF16),
        ),
        in_specs=[any_, any_] + [vmem] * 3 + [any_, vmem, any_] + [vmem] * 3 + [any_, vmem, any_, vmem],
        out_specs=(any_,) * 8 + (vmem, vmem, any_, any_),
        scratch_shapes=[
            low(own, width), wide(own, width), low(window, width), low(window, width), low(window, width),
            low(width, own), wide(own, width),
            low(window, width), low(own, width), pltpu.VMEM((1, length + 2 * HALO), jnp.int32),
            pltpu.VMEM((1, window), jnp.int32), pltpu.VMEM((window, BLOCK), jnp.int32), wide(8, width),
            low(window, width), low(nt, chunks, *unit), wide(nt, 8, width), dma((nt - 1,)), dma((nt - 1,)),
            low(own, width), low(own, width), low(width, own), low(width, own), wide(own, width),
            low(2, chunks - 1, *unit), wide(own, width), wide(own, width), low(own, width), low(own, width),
            dma((2,)),
            dma((2 * chunks - DIRECT, nt - 1, 2)), dma((2 * chunks - DIRECT, nt - 1, 2)),
            dma((chunks, nt - 1, 2, 4)), dma((chunks, nt - 1, 2, 4)),
            dma((chunks, nt - 1, 2)), dma((chunks, nt - 1, 2)), dma((8,)), dma((8,)),
        ],
        compiler_params=pltpu.CompilerParams(
            collective_id=1, has_side_effects=True, vmem_limit_bytes=VMEM_LIMIT),
    )(*views)


PIECES = 3
OWN_TIME, SIDE_TIME = 2.1, 1.5
PACE, STEPS, HOP = 4.5, (2.8, 8.5, 14.4), 8.0


def backward_kernel(nt, chunks, extra,
                    lse_ref, small1, segments, gain_1, gain_2,
                    cotangent, tokens_in, grads, w0, result, hidden_in, q_in, k_in, v_in, normed_in, heads_in, gtwo_in,
                    total, small, gathered_r, gathered_g,
                    hidden, q_ref, k_ref, v_ref, normed, heads_t, gtwo,
                    s1, rc, ra, rb, rz, rx, rt, sr, g0, w_first, token, cot, segp, segr, segc, branch, g_ref, stats,
                    halo_g, halo_s, dk, dv, dq, d_t, gtwo_out, own_ig,
                    ls, cs, cr, ps, pr, zs, zr, xs, xr, fs, fr, os_, or_, ss, sm, hs, hr, lo, in_sem):
    d, t, b0, b1, b2 = place()
    own, width = hidden.shape
    blocks = own // BLOCK
    gathered = (gathered_r, gathered_g)
    bits = (1, 2, 4) + tuple(extra)
    order = tuple(range(chunks))[::-1]
    units = [(k, s) for k in order for s in range(nt)]

    def own_copy(k, s):
        return pltpu.make_async_copy(grads.at[s, k - 1, b0], s1.at[s, k], ls.at[s, k])

    arrivals = [pltpu.make_async_copy(source, goal, in_sem.at[n]) for n, (source, goal) in enumerate((
        (hidden_in, hidden), (gtwo_in, gtwo), (heads_in, heads_t), (q_in, q_ref), (k_in, k_ref), (v_in, v_ref),
        (normed_in, normed), (result, gathered_r.at[t])))]
    fetch_w = pltpu.make_async_copy(w0, w_first, lo.at[0])
    mine = pl.ds(pl.multiple_of(t * own, own), own)
    fetch_t = pltpu.make_async_copy(tokens_in.at[mine], token, lo.at[1])
    fetch_t.start()
    fetch_c = pltpu.make_async_copy(cotangent.at[mine], cot, lo.at[2])
    fetch_c.start()
    for copy in arrivals[:3]:
        copy.start()
    fetch_w.start()
    for copy in arrivals[3:]:
        copy.start()
    for k, s in units:
        if k > 0:
            own_copy(k, s).start()
    window_segments(segments, segp, segr, segc)
    greet(nt, bits, nt > 2)
    tasks = []

    def task(when, body):
        tasks.append((when, len(tasks), body))

    def core(k, s):
        source = g0.at[s, 1 - b0] if k == 0 else grads.at[s, k - 1, 1 - b0]
        return remote(source, rc.at[s, k], cs.at[s, k], cr.at[s, k], dp=flip(d, 1))

    def one(k, s, q):
        if q == 0:
            return remote(s1.at[s, k, 1 - b2, :, 0], ra.at[s, k], ps.at[s, k, 0], pr.at[s, k, 0], dp=flip(d, 4))
        return remote(s1.at[s, k, :, 1 - b1, 1], rb.at[s, k], ps.at[s, k, 1], pr.at[s, k, 1], dp=flip(d, 2))

    def two(k, s, q):
        if q == 0:
            return remote(s1.at[s, k, b2, 1 - b1, 0], rz.at[s, k, 0], ps.at[s, k, 2], pr.at[s, k, 2], dp=flip(d, 2))
        return remote(s1.at[s, k, 1 - b2, b1, 1], rz.at[s, k, 1], ps.at[s, k, 3], pr.at[s, k, 3], dp=flip(d, 4))

    def up(k, s):
        return remote(s1.at[s, k, b2, b1], rx.at[s, k], zs.at[s, k, 0], zr.at[s, k, 0], tensor=t + 1)

    def down(k, s, last):
        goal = rt.at[k] if last else rx.at[s, k]
        return remote(s1.at[s, k, b2, b1], goal, zs.at[s, k, 1], zr.at[s, k, 1], tensor=t - 1)

    def halo(n):
        if n == 0:
            return remote(g_ref.at[pl.ds(own - REACH, REACH)], halo_g.at[0, pl.ds(HALO - REACH, REACH)],
                          hs.at[0], hr.at[0], tensor=t + 1)
        if n == 1:
            return remote(g_ref.at[pl.ds(0, REACH)], halo_g.at[1, pl.ds(0, REACH)], hs.at[1], hr.at[1], tensor=t - 1)
        span = HALO // BLOCK
        if n == 2:
            return remote(stats.at[pl.ds(blocks - span, span)], halo_s.at[0], hs.at[2], hr.at[2], tensor=t + 1)
        return remote(stats.at[pl.ds(0, span)], halo_s.at[1], hs.at[3], hr.at[3], tensor=t - 1)

    def halo_start():
        @pl.when(t < nt - 1)
        def _():
            halo(0).start()
            halo(2).start()

        @pl.when(t > 0)
        def _():
            halo(1).start()
            halo(3).start()
        pad = HALO - REACH
        halo_g[0, 0:pad, :] = jnp.zeros((pad, width), BF16)
        halo_g[1, REACH:HALO, :] = jnp.zeros((pad, width), BF16)

        @pl.when(t == 0)
        def _():
            halo_g[0] = jnp.zeros((HALO, width), BF16)
            halo_s[0] = jnp.zeros(halo_s.shape[1:], F32)

        @pl.when(t == nt - 1)
        def _():
            halo_g[1] = jnp.zeros((HALO, width), BF16)
            halo_s[1] = jnp.zeros(halo_s.shape[1:], F32)

    def halo_end():
        @pl.when(t > 0)
        def _():
            halo(0).wait_recv()
            halo(2).wait_recv()

        @pl.when(t < nt - 1)
        def _():
            halo(1).wait_recv()
            halo(3).wait_recv()

    def attend_block(w, cols, row):
        q0 = w * BLOCK
        middle = HALO // BLOCK <= w < HALO // BLOCK + blocks
        k0, k1 = max(0, q0 - REACH), q0 + BLOCK + REACH
        if not middle:
            k0, k1 = max(k0, HALO), min(k1, HALO + own)
        q2 = stacked(q_ref[q0:q0 + BLOCK, cols] * SCALE)
        if middle:
            i = w - HALO // BLOCK
            g_rows = g_ref[i * BLOCK:(i + 1) * BLOCK, cols]
            lse, delta = stats[i, pl.ds(row, 1), :], stats[i, pl.ds(8 + row, 1), :]
        else:
            side = int(w > HALO // BLOCK)
            i = w if side == 0 else w - HALO // BLOCK - blocks
            g_rows = halo_g[side, i * BLOCK:(i + 1) * BLOCK, cols]
            lse, delta = halo_s[side, i, pl.ds(row, 1), :], halo_s[side, i, pl.ds(8 + row, 1), :]
        g2 = stacked(g_rows)
        k2, v2 = k_ref[k0:k1, cols], v_ref[k0:k1, cols]
        allowed = segc[k0:k1, :] == segr[:, q0:q0 + BLOCK]
        allowed = jnp.concatenate([allowed, allowed], axis=1)
        s = dot(k2, q2, NT)
        p = jnp.exp(jnp.where(allowed, s - lse, -1e9))
        low = p.astype(BF16)
        ds = (p * (dot(v2, g2, NT) - delta)).astype(BF16)
        o0, o1 = max(k0, HALO), min(k1, HALO + own)
        dst, src = slice(o0 - HALO, o1 - HALO), slice(o0 - k0, o1 - k0)
        dk[dst, cols] += dot(ds[src], q2, NN)
        dv[dst, cols] += dot(low[src], g2, NN)
        if middle:
            out = dot(k2.T, ds, NN) * SCALE
            half = out.shape[1] // 2
            both = jnp.concatenate([out[:HEAD_DIM, :half], out[HEAD_DIM:, half:]], axis=0).astype(BF16)
            d_t[0, cols, i * BLOCK:(i + 1) * BLOCK] = both
            dq[0, i * BLOCK:(i + 1) * BLOCK, cols] = both.T

    def attention(first, count, mine):
        def pair(j, carry):
            cols = pl.ds(pl.multiple_of(j * 128, 128), 128)
            if mine:
                dk[:, cols] = jnp.zeros((own, 128), F32)
                dv[:, cols] = jnp.zeros((own, 128), F32)
                for b in range(blocks):
                    attend_block(HALO // BLOCK + b, cols, j)
            else:
                for w in tuple(range(HALO // BLOCK)) + tuple(range(HALO // BLOCK + blocks, 2 * HALO // BLOCK + blocks)):
                    attend_block(w, cols, j)
                for n, ref in enumerate((dk, dv)):
                    value = ref[:, cols].astype(BF16)
                    dq[1 + n, :, cols] = value
                    d_t[1 + n, cols, :] = value.T
            return carry
        for j in range(first, first + count):
            pair(j, 0)

    g1, g2 = gain_1[...].reshape(1, width), gain_2[...].reshape(1, width)

    def norm_two_back():
        fetch_c.wait()
        arrivals[0].wait()
        arrivals[1].wait()

        def part(n, carry):
            rows = pl.ds(pl.multiple_of(n * 32, 32), 32)
            xhat, r = standardize(hidden[rows, :])
            grad = gtwo[rows, :]
            gh = cot[rows, :].astype(F32) + norm_back(grad * g2, xhat, r)
            gtwo_out[rows, :] = gh
            branch[rows, :] = gh.astype(BF16)
            return carry[0] + gh, carry[1] + grad * xhat, carry[2] + grad
        zero = jnp.zeros((32, width), F32)
        sums = lax.fori_loop(0, own // 32, part, (zero, zero, zero))
        small[...] = small1[...]
        for line, value in zip((2, 3, 4), sums):
            small[line:line + 1, :] = jnp.sum(value, axis=0, keepdims=True)

    def out_back():
        fetch_w.wait()
        arrivals[2].wait()
        outw = w_first[:, 1, 1].reshape(width, width)
        rows = branch[...]
        g_ref[...] = dot(rows, outw, NT).astype(BF16)
        g_t = dot(outw, rows, NT).astype(BF16).astype(F32)
        product = g_t * heads_t[...].astype(F32)
        for b in range(blocks):
            stats[b, 0:8, :] = lse_ref[b]
            for h in range(width // HEAD_DIM):
                line = jnp.sum(product[h * HEAD_DIM:(h + 1) * HEAD_DIM, b * BLOCK:(b + 1) * BLOCK], axis=0, keepdims=True)
                stats[b, 8 + h // 2:9 + h // 2, (h % 2) * BLOCK:(h % 2 + 1) * BLOCK] = line
            stats[b, 8 + width // 128:16, :] = jnp.zeros((8 - width // 128, 2 * BLOCK), F32)

    def out_grad():
        value = dot(heads_t[...], branch[...], NN).astype(BF16)
        g0[:, 1, 1] = value.reshape((nt,) + g0.shape[3:])
    task(0.3, norm_two_back)
    task(3.0, out_back)
    task(5.5, halo_start)
    task(6.0, out_grad)
    at = 7.0
    pairs = width // 128

    def attend_ready():
        for copy in arrivals[3:]:
            copy.wait()
    task(at, attend_ready)
    for first in range(pairs):
        def run(first=first):
            attention(first, 1, True)
        task(at, run)
        at += OWN_TIME
    at = max(at, 14.0)
    task(at, halo_end)
    for first in range(pairs):
        def run(first=first):
            attention(first, 1, False)
        task(at, run)
        at += SIDE_TIME

    def weight_of(kind):
        return w_first[:, kind // 2, kind % 2].reshape(width, width)

    def back_project():
        dk[...] = dot(dq[0], weight_of(0), NN)
        dk[...] += dot(dq[1], weight_of(1), NN)
        dk[...] += dot(dq[2], weight_of(2), NN)
    task(at, back_project)
    at += 2.5

    def norm_one():
        fetch_t.wait()

        def part(n, carry):
            rows = pl.ds(pl.multiple_of(n * 32, 32), 32)
            xhat, r = standardize(token[rows, :].astype(F32))
            grad = dk[rows, :]
            own_ig[rows, :] = (gtwo_out[rows, :] + norm_back(grad * g1, xhat, r)).astype(BF16)
            return (carry[0] + grad * xhat, carry[1] + grad, carry[2] + dq[0, rows, :].astype(F32),
                    carry[3] + dq[2, rows, :].astype(F32))
        zero = jnp.zeros((32, width), F32)
        sums = lax.fori_loop(0, own // 32, part, (zero, zero, zero, zero))
        for line, value in zip((0, 1, 6, 7), sums):
            small[line:line + 1, :] = jnp.sum(value, axis=0, keepdims=True)
        gathered_g[t] = own_ig[...]
    task(at, norm_one)
    at += 3.0
    ready = at
    for kind in range(3):
        def run(kind=kind):
            value = dot(d_t[kind], normed[...], NN).astype(BF16)
            g0[:, kind // 2, kind % 2] = value.reshape((nt,) + g0.shape[3:])
        task(at, run)
        at += 1.2

    late = at

    pace = PACE
    for n, (k, s) in enumerate(units):
        base = n * pace if k > 0 else max(n * pace, late + 0.6 + (n - nt * (chunks - 1)) * pace)

        def first(k=k, s=s):
            core(k, s).start()

        def second(k=k, s=s):
            core(k, s).wait_recv()
            if k > 0:
                own_copy(k, s).wait()
                add_bf16(s1.at[s, k], rc.at[s, k])
            else:
                s1[s, k] = (g0[s, b0].astype(F32) + rc[s, k].astype(F32)).astype(BF16)
            one(k, s, 0).start()
            one(k, s, 1).start()

        def third(k=k, s=s):
            one(k, s, 0).wait_recv()
            one(k, s, 1).wait_recv()
            add_bf16(s1.at[s, k, b2, :, 0], ra.at[s, k])
            add_bf16(s1.at[s, k, :, b1, 1], rb.at[s, k])
            two(k, s, 0).start()
            two(k, s, 1).start()

        def fourth(k=k, s=s):
            two(k, s, 0).wait_recv()
            two(k, s, 1).wait_recv()
            add_bf16(s1.at[s, k, b2, b1, 0], rz.at[s, k, 0])
            add_bf16(s1.at[s, k, b2, b1, 1], rz.at[s, k, 1])
        task(max(base - 14.9, -10.0) if k > 0 else max(base - 12.0, late + 0.01), first)
        task(base + STEPS[0], second)
        task(base + STEPS[1], third)
        task(base + STEPS[2], fourth)
        if s == nt - 1:
            end_of_chunk = base + STEPS[2]
        else:
            continue

        for hop in range(nt):
            def chain(k=k, hop=hop):
                @pl.when(t == hop)
                def _():
                    for s in reversed(range(nt)):
                        @pl.when(s >= t)
                        def _():
                            if hop > 0:
                                up(k, s).wait_recv()
                                add_bf16(s1.at[s, k, b2, b1], rx.at[s, k])
                            if hop < nt - 1:
                                @pl.when(s > t)
                                def _():
                                    up(k, s).start()

                @pl.when(t == nt - 1 - hop)
                def _():
                    for s in range(nt):
                        if hop > 0:
                            @pl.when(s < t)
                            def _():
                                down(k, s, False).wait_recv()
                                add_bf16(s1.at[s, k, b2, b1], rx.at[s, k])

                            @pl.when(s == t)
                            def _():
                                down(k, s, True).wait_recv()
                                add_bf16(s1.at[s, k, b2, b1], rt.at[k])
                        if hop < nt - 1:
                            @pl.when(s == t - 1)
                            def _():
                                down(k, s, True).start()

                            @pl.when(s < t - 1)
                            def _():
                                down(k, s, False).start()
            task(end_of_chunk + 0.5 + HOP * hop, chain)
        base = end_of_chunk + 0.5 + HOP * nt + -2.8

        for e, bit in enumerate(extra):
            def more(k=k, e=e, bit=bit):
                swap = remote(s1.at[t, k, b2, b1], rx.at[nt + e, k], xs.at[e, k], xr.at[e, k], dp=flip(d, bit))
                swap.start()
                swap.wait()
                add_bf16(s1.at[t, k, b2, b1], rx.at[nt + e, k])
            task(base + 0.01 * e, more)

        def settle(k=k):
            total[k, b0, b2, b1] = s1[t, k, b2, b1]

        def give_one(k, q):
            if q == 0:
                piece = total.at[k, b0, b2, b1, 0]
                return remote(piece, piece, fs.at[k, 0], fr.at[k, 0], dp=flip(d, 2))
            piece = total.at[k, b0, b2, b1, 1]
            return remote(piece, piece, fs.at[k, 1], fr.at[k, 1], dp=flip(d, 4))

        def give_two(k, q):
            if q == 0:
                piece = total.at[k, b0, b2, :, 0]
                return remote(piece, piece, fs.at[k, 2], fr.at[k, 2], dp=flip(d, 4))
            piece = total.at[k, b0, :, b1, 1]
            return remote(piece, piece, fs.at[k, 3], fr.at[k, 3], dp=flip(d, 2))

        def give_core(k):
            return remote(total.at[k, b0], total.at[k, b0], fs.at[k, 4], fr.at[k, 4], dp=flip(d, 1))

        def spread_one(k=k):
            for q in (0, 1):
                give_one(k, q).start()

        def spread_two(k=k):
            for q in (0, 1):
                give_one(k, q).wait_recv()
            for q in (0, 1):
                give_two(k, q).start()

        def spread_core(k=k):
            for q in (0, 1):
                give_two(k, q).wait_recv()
            give_core(k).start()

        def spread_end(k=k):
            give_core(k).wait()
            for q in (0, 1):
                give_one(k, q).wait_send()
                give_two(k, q).wait_send()
        task(base + 0.5, settle)
        task(base + 0.6, spread_one)
        task(base + 4.3, spread_two)
        task(base + 9.7, spread_core)
        task(1e6, spread_end)

    part = own // PIECES

    def piece_of(ref, n):
        return ref.at[pl.ds(n % PIECES * part, part)]
    z_tasks, z_finish = relay_tasks(
        nt, 2 * PIECES, lambda n: piece_of((result, own_ig)[n // PIECES], n),
        lambda s, n: piece_of(gathered[n // PIECES].at[s], n), (os_, or_),
        lambda n, j: (-5.0, ready)[n // PIECES] + 20.0 / PIECES * (n % PIECES) + 20.0 * j + (0.01 if j == 0 else 2.6),
        lambda *a: None)
    tasks += [(w, 1000 + n, b) for w, n, b in z_tasks]

    exchanges = [("dp", bit) for bit in bits]
    step = 1
    while step < nt:
        exchanges.append(("tensor", step))
        step *= 2
    for e, (axis, bit) in enumerate(exchanges):
        def swap(e=e, axis=axis, bit=bit):
            goal = {axis: flip(lax.axis_index(axis), bit)}
            return remote(small, sr.at[e], ss.at[e], sm.at[e], **goal)

        def begin(swap=swap):
            swap().start()

        def end(e=e, swap=swap):
            swap().wait()
            small[...] = small[...] + sr[e]
        task(late + 19.1 + 6.7 * e, begin)
        task(late + 24.6 + 6.7 * e, end)

    ordered(tasks)
    z_finish()

    @pl.when(t < nt - 1)
    def _():
        halo(0).wait_send()
        halo(2).wait_send()

    @pl.when(t > 0)
    def _():
        halo(1).wait_send()
        halo(3).wait_send()
    for k, s in units:
        core(k, s).wait_send()
        for q in (0, 1):
            one(k, s, q).wait_send()
            two(k, s, q).wait_send()

        @pl.when(s > t)
        def _():
            up(k, s).wait_send()

        @pl.when(s < t)
        def _():
            down(k, s, False).wait_send()


def backward(vmem_arrays, hbm_arrays, nt, extra):
    own, width = hbm_arrays[4].shape
    grads, segments = hbm_arrays[2], vmem_arrays[2]
    small_shape = vmem_arrays[1].shape
    piece, chunks = width // 16, grads.shape[1] + 1
    window = own + 2 * HALO
    dma = pltpu.SemaphoreType.DMA
    hops = 3 + len(extra) + (nt - 1).bit_length()
    vmem, any_ = pl.BlockSpec(memory_space=pltpu.VMEM), pl.BlockSpec(memory_space=pl.ANY)
    unit = (2, 2, 2, piece, width)
    blocks = own // BLOCK

    def low(*dims):
        return pltpu.VMEM(dims, BF16)

    def wide(*dims):
        return pltpu.VMEM(dims, F32)
    return pl.pallas_call(
        functools.partial(backward_kernel, nt, chunks, extra),
        name="backward",
        out_shape=(
            jax.ShapeDtypeStruct((chunks, 2) + unit, BF16),
            jax.ShapeDtypeStruct(small_shape, F32),
            jax.ShapeDtypeStruct((nt, own, width), BF16),
            jax.ShapeDtypeStruct((nt, own, width), BF16),
        ),
        in_specs=[vmem] * len(vmem_arrays) + [any_] * len(hbm_arrays),
        out_specs=(vmem,) * 4,
        scratch_shapes=[
            wide(own, width), low(window, width), low(window, width), low(window, width), low(own, width),
            low(width, own), wide(own, width),
            low(nt, chunks, *unit), low(nt, chunks, *unit),
            low(nt, chunks, 2, piece, width), low(nt, chunks, 2, piece, width), low(nt, chunks, 2, piece, width),
            low(nt + len(extra), chunks, 2, piece, width), low(chunks, 2, piece, width),
            wide(hops, *small_shape), low(nt, 2, *unit), low(nt, 2, *unit),
            low(own, width), low(own, width), pltpu.VMEM((1, segments.shape[1] + 2 * HALO), jnp.int32),
            pltpu.VMEM((1, window), jnp.int32), pltpu.VMEM((window, BLOCK), jnp.int32),
            low(own, width), low(own, width), wide(blocks, 16, 2 * BLOCK),
            low(2, HALO, width), wide(2, HALO // BLOCK, 16, 2 * BLOCK),
            wide(own, width), wide(own, width), low(3, own, width), low(3, width, own),
            wide(own, width), low(own, width),
            dma((nt, chunks)), dma((nt, chunks)), dma((nt, chunks)),
            dma((nt, chunks, 4)), dma((nt, chunks, 4)),
            dma((nt, chunks, 2)), dma((nt, chunks, 2)),
            dma((max(1, len(extra)), chunks)), dma((max(1, len(extra)), chunks)),
            dma((chunks, 5)), dma((chunks, 5)),
            dma((2 * PIECES, nt - 1, 2)), dma((2 * PIECES, nt - 1, 2)),
            dma((hops,)), dma((hops,)), dma((4,)), dma((4,)), dma((3,)), dma((8,)),
        ],
        compiler_params=pltpu.CompilerParams(
            collective_id=2, has_side_effects=True, vmem_limit_bytes=VMEM_LIMIT),
    )(*vmem_arrays, *hbm_arrays)


def finish_kernel(nt, ndp, total_in, small, results, input_grads,
                  results_out, input_grads_out, g1, s1, qkv, qvb, out_w, out_b, g2, s2, up, up_b, down, down_b,
                  total, held, first, second, third, in_sem, out_sem):
    t = lax.axis_index("tensor")
    width = small.shape[1]
    local = width // nt
    scale = 1.0 / ndp
    parts = [pltpu.make_async_copy(total_in.at[k], total.at[k], in_sem.at[k]) for k in range(3)]
    for k in (1, 2, 0):
        parts[k].start()
    stage = [pltpu.make_async_copy(results, held.at[0], in_sem.at[3]), pltpu.make_async_copy(input_grads, held.at[1], in_sem.at[4])]
    for copy in stage:
        copy.start()
    moves = []
    for ref, line in ((g1, 0), (s1, 1), (out_b, 2), (g2, 3), (s2, 4), (down_b, 5)):
        ref[...] = small[line:line + 1, :].reshape(width) * scale
    up_b[...] = small[pl.ds(8 + t, 1), :].reshape(width) * scale
    for place in range(nt):
        @pl.when(t == place)
        def _():
            qvb[...] = small[6:8, place * local:(place + 1) * local] * scale
    for n, goal in enumerate((results_out, input_grads_out)):
        stage[n].wait()
        moves.append(pltpu.make_async_copy(held.at[n], goal, out_sem.at[n]))
        moves[-1].start()
    parts[1].wait()
    second[...] = total[1].reshape(width, width).astype(F32) * scale
    moves.append(pltpu.make_async_copy(second, up, out_sem.at[2]))
    moves[-1].start()
    parts[2].wait()
    third[...] = (total[2].reshape(width, width).astype(F32) * scale).T
    moves.append(pltpu.make_async_copy(third, down, out_sem.at[3]))
    moves[-1].start()
    parts[0].wait()
    first[...] = total[0].reshape(nt, local, width).astype(F32) * scale
    moves.append(pltpu.make_async_copy(first.at[pl.ds(0, 3)], qkv, out_sem.at[4]))
    moves[-1].start()
    moves.append(pltpu.make_async_copy(first.at[3], out_w, out_sem.at[5]))
    moves[-1].start()
    for copy in moves:
        copy.wait()


def finish_up(total, small, results, input_grads, nt, ndp):
    width = small.shape[1]
    local = width // nt
    dma = pltpu.SemaphoreType.DMA
    vmem, any_ = pl.BlockSpec(memory_space=pltpu.VMEM), pl.BlockSpec(memory_space=pl.ANY)

    def shape(*dims):
        return jax.ShapeDtypeStruct(dims, F32)
    return pl.pallas_call(
        functools.partial(finish_kernel, nt, ndp),
        name="finish",
        out_shape=(jax.ShapeDtypeStruct(results.shape, BF16), jax.ShapeDtypeStruct(results.shape, BF16),
                   shape(width), shape(width), shape(3, local, width), shape(2, local), shape(local, width), shape(width),
                   shape(width), shape(width), shape(width, width), shape(width), shape(width, width), shape(width)),
        in_specs=[any_, vmem, any_, any_],
        out_specs=(any_, any_, vmem, vmem, any_, vmem, any_, vmem, vmem, vmem, any_, vmem, any_, vmem),
        scratch_shapes=[pltpu.VMEM(total.shape, BF16), pltpu.VMEM((2,) + results.shape, BF16), pltpu.VMEM((nt, local, width), F32),
                        pltpu.VMEM((width, width), F32), pltpu.VMEM((width, width), F32), dma((5,)), dma((6,))],
        compiler_params=pltpu.CompilerParams(vmem_limit_bytes=VMEM_LIMIT),
    )(total, small, results, input_grads)


def body(tokens_in, segment_ids, first_gain, first_shift, qkv_weight, query_value_bias, out_weight, out_bias,
         second_gain, second_shift, up_weight, up_bias, down_weight, down_bias, cotangent):
    nt, ndp = lax.axis_size("tensor"), lax.axis_size("dp")
    length, width = tokens_in.shape
    (result, hidden, q, k, v, normed, heads_t, grad_two, lse, small, mlp_grads, w_first) = forward(
        (tokens_in, cotangent, segment_ids, first_gain, first_shift, qkv_weight, query_value_bias, out_weight, out_bias,
         second_gain, second_shift, up_weight, up_bias, down_weight, down_bias), nt)
    extra = []
    bit = 8
    while bit < ndp:
        extra.append(bit)
        bit *= 2
    total, small, results, input_grads = backward(
        (lse, small, segment_ids, first_gain, second_gain),
        (cotangent, tokens_in, mlp_grads, w_first, result, hidden, q, k, v, normed, heads_t, grad_two), nt, tuple(extra))
    outs = list(finish_up(total, small, results, input_grads, nt, ndp))
    outs[0], outs[1] = outs[0].reshape(length, width), outs[1].reshape(length, width)
    outs[4] = outs[4].transpose(0, 2, 1)
    return tuple(outs)


def solution(mesh):
    placed = (
        P("dp", None), P("dp", None), P(), P(), P(None, None, "tensor"), P(None, "tensor"), P("tensor", None), P(),
        P(), P(), P(None, "tensor"), P("tensor"), P("tensor", None), P(), P("dp", None),
    )
    return jax.shard_map(
        body,
        mesh=mesh,
        in_specs=placed,
        out_specs=(
            P("dp", None), P("dp", None), P(), P(), P(None, None, "tensor"), P(None, "tensor"), P("tensor", None),
            P(), P(), P(), P(None, "tensor"), P("tensor"), P("tensor", None), P(),
        ),
        check_vma=False,
    )
```

```python
import functools

import jax
import jax.numpy as jnp
from jax import lax
from jax.experimental import pallas as pl
from jax.experimental.pallas import tpu as pltpu
from jax.sharding import PartitionSpec as P

HEAD_DIM = 64
HALO = 256
REACH = 224
BLOCK = 128
EPS = 1e-06
SCALE = HEAD_DIM ** -0.5
F32 = jnp.float32
BF16 = jnp.bfloat16
MESH = pl.DeviceIdType.MESH
VMEM_LIMIT = 60 << 20


def place():
    d, t = lax.axis_index("dp"), lax.axis_index("tensor")
    return d, t, lax.rem(d, 2), lax.rem(d // 2, 2), lax.rem(d // 4, 2)


def flip(d, value):
    return d + value * (1 - 2 * lax.rem(d // value, 2))


def remote(src, dst, send, recv, **axis):
    return pltpu.make_async_remote_copy(
        src_ref=src, dst_ref=dst, send_sem=send, recv_sem=recv,
        device_id=axis, device_id_type=MESH)


def greet(nt, bits, far=False):
    d, t = lax.axis_index("dp"), lax.axis_index("tensor")
    barrier = pltpu.get_barrier_semaphore()

    @pl.when(t > 0)
    def _():
        pl.semaphore_signal(barrier, inc=1, device_id={"tensor": t - 1}, device_id_type=MESH)

    @pl.when(t < nt - 1)
    def _():
        pl.semaphore_signal(barrier, inc=1, device_id={"tensor": t + 1}, device_id_type=MESH)

    for bit in bits:
        pl.semaphore_signal(barrier, inc=1, device_id={"dp": flip(d, bit)}, device_id_type=MESH)
    if far:
        pl.semaphore_signal(barrier, inc=1, device_id={"tensor": flip(t, 2)}, device_id_type=MESH)
    peers = len(bits) + int(far) + (t > 0).astype(jnp.int32) + (t < nt - 1).astype(jnp.int32)
    pl.semaphore_wait(barrier, peers)


def ordered(tasks):
    for _, _, task in sorted(tasks, key=lambda item: item[:2]):
        task()


def relay_tasks(nt, chunks, own, full, sems, start, arrived):
    send, recv = sems
    tasks = []
    t = lax.axis_index("tensor")
    for k in range(chunks):
        for j in range(nt):
            def step(k=k, j=j):
                for way in (0, 1):
                    sign = 1 - 2 * way
                    shard = t - sign * j
                    inside = (shard >= 0) & (shard < nt)
                    if j > 0:
                        @pl.when(inside)
                        def _():
                            remote(full(shard, k), full(shard, k), send.at[k, j - 1, way], recv.at[k, j - 1, way],
                                   tensor=t).wait_recv()
                            arrived(k, j, way, shard)
                    if j < nt - 1:
                        goal = t + sign
                        @pl.when(inside & (goal >= 0) & (goal < nt))
                        def _():
                            source = own(k) if j == 0 else full(shard, k)
                            remote(source, full(shard, k), send.at[k, j, way], recv.at[k, j, way],
                                   tensor=goal).start()
            tasks.append((start(k, j), len(tasks), step))

    def finish():
        for k in range(chunks):
            for j in range(nt - 1):
                for way in (0, 1):
                    sign = 1 - 2 * way
                    shard, goal = t - sign * j, t + sign
                    @pl.when((shard >= 0) & (shard < nt) & (goal >= 0) & (goal < nt))
                    def _():
                        source = own(k) if j == 0 else full(shard, k)
                        remote(source, full(shard, k), send.at[k, j, way], recv.at[k, j, way],
                               tensor=goal).wait_send()
    return tasks, finish


def add_bf16(ref, other):
    ref[...] = (ref[...].astype(F32) + other[...].astype(F32)).astype(BF16)


def stacked(pair):
    lane = lax.broadcasted_iota(jnp.int32, pair.shape, 1)
    zero = jnp.zeros_like(pair)
    return jnp.concatenate([jnp.where(lane < HEAD_DIM, pair, zero), jnp.where(lane < HEAD_DIM, zero, pair)], axis=0)


def dot(a, b, dims):
    return lax.dot_general(a, b, (dims, ((), ())), preferred_element_type=F32)


NN = ((1,), (0,))
NT = ((1,), (1,))


def untangle(both):
    half = both.shape[1] // 2
    return jnp.concatenate([both[:HEAD_DIM, :half], both[HEAD_DIM:, half:]], axis=0).T


def standardize(rows):
    center = rows - jnp.mean(rows, axis=-1, keepdims=True)
    r = lax.rsqrt(jnp.mean(center * center, axis=-1, keepdims=True) + EPS)
    return center * r, r


def norm_back(e, xhat, r):
    return r * (e - jnp.mean(e, axis=-1, keepdims=True) - xhat * jnp.mean(e * xhat, axis=-1, keepdims=True))


def window_segments(segments, padded, row, column):
    length, window = segments.shape[1], row.shape[1]
    padded[...] = jnp.full(padded.shape, -1, jnp.int32)
    padded[:, HALO:HALO + length] = segments[...]
    own = window - 2 * HALO
    for i in range(window // BLOCK):
        first = pl.multiple_of(lax.axis_index("tensor") * own + i * BLOCK, BLOCK)
        line = padded[:, pl.ds(first, BLOCK)]
        row[:, i * BLOCK:(i + 1) * BLOCK] = line
        column[i * BLOCK:(i + 1) * BLOCK, :] = jnp.broadcast_to(line, (BLOCK, BLOCK)).T


def nearest(nt):
    return [sorted(range(nt), key=lambda s: (abs(s - p), s if p < nt // 2 else -s)) for p in range(nt)]


def pick(table, position):
    t = lax.axis_index("tensor")
    return sum((t == p).astype(jnp.int32) * row[position] for p, row in enumerate(table))


def gelu_parts(x):
    cdf = 0.5 * (1.0 + lax.erf(x * (0.5 ** 0.5)))
    pdf = jnp.exp(-0.5 * x * x) * ((2.0 * jnp.pi) ** -0.5)
    return x * cdf, cdf + x * pdf


ATTEND = 0.6
NORM_TIME = 1.0
LINE_GAP, LAGS_0 = 2.3, (7.3, 12.9, 16.4)
DIRECT = 3
LINE, PLANE, LEAD, LAGS = 4.3, 4.2, 0.0, (5.6, 12.3, 15.8)


def forward_kernel(nt, chunks, own,
                   tokens_in, cotangent, segments, gain_1, shift_1, qkv_in, qv_bias, out_in, out_bias, gain_2, shift_2,
                   up_in, up_bias, down_in, down_bias,
                   result_out, hidden_out, q_out, k_out, v_out, normed_out, heads_out, gtwo_out, lse_ref, small, grads, w0,
                   result, hidden, q_ref, k_ref, v_ref, heads_t, gtwo, tok, cot, segp, segr, segc, bias, normed, w, bias_all, bias_sem, bias_recv, heads, normed_two, n2t,
                   cot_t, mlp, gbuf, pre_s, gact_s, act, gpre, gsem, zs, zr, ps, pr, cs, cr, ls, out_sem):
    d, t, b0, b1, b2 = place()
    window, width = tok.shape
    local = width // nt
    blocks = own // BLOCK
    local_copies = [pltpu.make_async_copy(qkv_in.at[kind], w.at[t, 0, kind // 2, kind % 2], ls.at[5 + kind])
                    for kind in range(3)] + [
        pltpu.make_async_copy(out_in, w.at[t, 0, 1, 1], ls.at[0]),
        pltpu.make_async_copy(up_in, w.at[t, 1], ls.at[1]),
        pltpu.make_async_copy(down_in, w.at[t, 2], ls.at[2]),
    ]
    for copy in local_copies:
        copy.start()
    cot_copy = pltpu.make_async_copy(cotangent.at[pl.ds(pl.multiple_of(t * own, own), own)], cot, ls.at[3])
    cot_copy.start()

    def token_copy(place):
        rows = own + HALO
        if place == 0:
            return pltpu.make_async_copy(tokens_in.at[pl.ds(0, rows)], tok.at[pl.ds(HALO, rows)], ls.at[4])
        if place == 1:
            return pltpu.make_async_copy(tokens_in.at[pl.ds((nt - 1) * own - HALO, rows)], tok.at[pl.ds(0, rows)], ls.at[4])
        first = pl.multiple_of(t * own - HALO, BLOCK)
        return pltpu.make_async_copy(tokens_in.at[pl.ds(first, window)], tok, ls.at[4])

    def tokens(act):
        @pl.when(t == 0)
        def _():
            act(token_copy(0))

        @pl.when(t == nt - 1)
        def _():
            act(token_copy(1))

        @pl.when((t > 0) & (t < nt - 1))
        def _():
            act(token_copy(2))
    tokens(lambda copy: copy.start())

    @pl.when(t == 0)
    def _():
        tok[0:HALO, :] = jnp.zeros((HALO, width), BF16)

    @pl.when(t == nt - 1)
    def _():
        tok[window - HALO:window, :] = jnp.zeros((HALO, width), BF16)

    barrier = pltpu.get_barrier_semaphore()
    for bit in (1, 2, 4):
        pl.semaphore_signal(barrier, inc=1, device_id={"dp": flip(d, bit)}, device_id_type=MESH)
    for j in range(1, nt):
        pl.semaphore_signal(barrier, inc=1, device_id={"tensor": lax.rem(t + j, nt)}, device_id_type=MESH)
    bias[...] = jnp.zeros(bias.shape, F32)
    bias[0:1, :] = up_bias[...].reshape(1, width)
    bias[1:3, 0:local] = qv_bias[...]
    bias_all[t] = bias[...]
    window_segments(segments, segp, segr, segc)
    for copy in local_copies:
        copy.wait()
    pl.semaphore_wait(barrier, 3 + nt - 1)
    tasks = []

    def task(when, body):
        tasks.append((when, len(tasks), body))

    def bias_send(j):
        return remote(bias, bias_all.at[t], bias_sem.at[j], bias_recv.at[j], tensor=lax.rem(t + j + 1, nt))

    def bias_get(j):
        source = lax.rem(t + nt - j - 1, nt)
        return remote(bias, bias_all.at[source], bias_sem.at[j], bias_recv.at[j], tensor=source)

    parity = lax.rem(b1 + b2, 2)

    def line_piece(shard, n):
        if n < DIRECT:
            return w.at[shard, n, b0, b2, b1]
        k, side = DIRECT + (n - DIRECT) // 2, (n - DIRECT) % 2
        return w.at[shard, k, b0, side, parity if side == 0 else 1 - parity]

    def one(shard, k, q, way, j):
        if k >= DIRECT:
            mine = line_piece(shard, DIRECT + 2 * (k - DIRECT) + q)
            return remote(mine, mine, ps.at[k, j, way, q], pr.at[k, j, way, q], dp=flip(d, 2 + 2 * q))
        if q == 0:
            mine = w.at[shard, k, b0, b2, b1, 0]
            return remote(mine, mine, ps.at[k, j, way, 0], pr.at[k, j, way, 0], dp=flip(d, 2))
        mine = w.at[shard, k, b0, b2, b1, 1]
        return remote(mine, mine, ps.at[k, j, way, 1], pr.at[k, j, way, 1], dp=flip(d, 4))

    def two(shard, k, q, way, j):
        if q == 0:
            mine = w.at[shard, k, b0, b2, :, 0]
            return remote(mine, mine, ps.at[k, j, way, 2], pr.at[k, j, way, 2], dp=flip(d, 4))
        mine = w.at[shard, k, b0, :, b1, 1]
        return remote(mine, mine, ps.at[k, j, way, 3], pr.at[k, j, way, 3], dp=flip(d, 2))

    def core(shard, k, way, j):
        return remote(w.at[shard, k, b0], w.at[shard, k, b0], cs.at[k, j, way], cr.at[k, j, way], dp=flip(d, 1))

    def each(k, j, act):
        for way in (0, 1):
            shard = t - (1 - 2 * way) * (j + 1)

            @pl.when((shard >= 0) & (shard < nt))
            def _():
                act(shard, k, way, j)

    def piece_time(n, j):
        if n < DIRECT:
            return LINE * (n * (nt - 1) + j) + (LINE_GAP if n > 0 else 0.0)
        pair, side = (n - DIRECT) // 2, (n - DIRECT) % 2
        return LINE_GAP + LINE * ((DIRECT + 2 * pair) * (nt - 1) + 2 * j - (j > 0) + side)

    def line_time(k, j):
        return piece_time(k, j) if k < DIRECT else piece_time(DIRECT + 2 * (k - DIRECT) + 1, j)

    z_tasks, z_finish = relay_tasks(
        nt, 2 * chunks - DIRECT, lambda n: line_piece(t, n), line_piece, (zs, zr), piece_time, lambda *a: None)
    tasks += z_tasks
    ready_at = {}
    for k in range(chunks):
        for j in range(nt - 1):
            def begin(k=k, j=j):
                def act(shard, k, way, j):
                    for q in (0, 1):
                        one(shard, k, q, way, j).start()
                each(k, j, act)

            def second(k=k, j=j):
                def act(shard, k, way, j):
                    for q in (0, 1):
                        one(shard, k, q, way, j).wait_recv()
                    for q in (0, 1):
                        two(shard, k, q, way, j).start()
                each(k, j, act)

            def third(k=k, j=j):
                def act(shard, k, way, j):
                    for q in (0, 1):
                        (two if k < DIRECT else one)(shard, k, q, way, j).wait_recv()
                    core(shard, k, way, j).start()
                each(k, j, act)

            def fourth(k=k, j=j):
                def act(shard, k, way, j):
                    core(shard, k, way, j).wait_recv()
                each(k, j, act)
            n = k * (nt - 1) + j
            base = max(line_time(k, j + 1) + 0.1, LEAD + PLANE * n)
            lags = LAGS_0 if k == 0 else LAGS
            skip = 0.0 if k < DIRECT else lags[0]
            task(base, begin)
            if k < DIRECT:
                task(base + lags[0], second)
            task(base + lags[1] - skip, third)
            task(base + lags[2] - skip, fourth)
            ready_at[k, j] = base + lags[2] - skip + 0.1

    def bias_begin():
        for j in range(nt - 1):
            bias_send(j).start()

    def bias_end():
        for j in range(nt - 1):
            bias_get(j).wait_recv()
    task(0.2, bias_begin)
    task(10.0, bias_end)

    g1, s1, ob, g2, s2, db = (ref[...].reshape(1, width) for ref in (gain_1, shift_1, out_bias, gain_2, shift_2, down_bias))

    def tokens_here():
        tokens(lambda copy: copy.wait())
    task(0.4, tokens_here)
    for i in range(window // BLOCK):
        def norm_rows(i=i):
            def part(n, carry):
                rows = pl.ds(pl.multiple_of(i * BLOCK + n * 32, 32), 32)
                xhat, _ = standardize(tok[rows, :].astype(F32))
                normed[rows, :] = (xhat * g1 + s1).astype(BF16)
                return carry
            lax.fori_loop(0, BLOCK // 32, part, 0)
        task(0.5 + NORM_TIME * i, norm_rows)

    kept = [pltpu.make_async_copy(source, goal, out_sem.at[n]) for n, (source, goal) in enumerate((
        (result, result_out), (hidden, hidden_out), (q_ref, q_out), (k_ref, k_out), (v_ref, v_out),
        (normed.at[pl.ds(HALO, own)], normed_out), (heads_t, heads_out), (gtwo, gtwo_out)))]

    def transposes():
        kept[5].start()
        cot_copy.wait()
        cot_t[...] = cot[...].T
        small[5:6, :] = jnp.sum(cot[...].astype(F32), axis=0, keepdims=True)
    task(7.6, transposes)

    half_rows = window // 2
    group = 2 * local

    def project(u, kind, part):
        rows = slice(part * half_rows, (part + 1) * half_rows)
        weight = w[pl.ds(2 * u, 2), 0, kind // 2, kind % 2].reshape(group, width)
        out = dot(normed[rows, :], weight, NT)
        if kind != 1:
            line = 1 + kind // 2
            out = out + jnp.concatenate([bias_all[2 * u, line:line + 1, :local], bias_all[2 * u + 1, line:line + 1, :local]], axis=1)
        target = (q_ref, k_ref, v_ref)[kind]
        target[rows, pl.ds(pl.multiple_of(u * group, 128), group)] = out.astype(BF16)

    def attention(u, b, only):
        first, count = BLOCK * b + 32, BLOCK + 448
        q0 = HALO + BLOCK * b
        allowed = segc[first:first + count, :] == segr[:, q0:q0 + BLOCK]
        allowed = jnp.concatenate([allowed, allowed], axis=1)

        def pair(j, carry):
            at = u * (group // 128) + j
            cols = pl.ds(pl.multiple_of(at * 128, 128), 128)
            q2 = stacked(q_ref[q0:q0 + BLOCK, cols] * SCALE)
            k2 = k_ref[first:first + count, cols]
            v2 = v_ref[first:first + count, cols]
            s = jnp.where(allowed, dot(k2, q2, NT), -1e9)
            m = jnp.max(s, axis=0, keepdims=True)
            p = jnp.exp(s - m)
            l = jnp.sum(p, axis=0, keepdims=True)
            out = dot(v2.T, p.astype(BF16), NN) * (1.0 / l)
            half = out.shape[1] // 2
            both = jnp.concatenate([out[:HEAD_DIM, :half], out[HEAD_DIM:, half:]], axis=0).astype(BF16)
            heads_t[cols, b * BLOCK:(b + 1) * BLOCK] = both
            heads[b * BLOCK:(b + 1) * BLOCK, cols] = both.T
            lse_ref[b, pl.ds(at, 1), :] = m + jnp.log(l)
            return carry
        pair(only, 0)

    def out_project(u, fresh):
        weight = w[pl.ds(2 * u, 2), 0, 1, 1].reshape(group, width)
        part = dot(heads[:, pl.ds(pl.multiple_of(u * group, 128), group)], weight, NN)
        if fresh:
            hidden[...] = part
        else:
            hidden[...] += part

    first_half = t // 2
    at = 7.0
    for n in range(nt // 2):
        u = lax.rem(first_half + n, nt // 2)
        if n == 0:
            at = max(at, ready_at[0, 0])
        else:
            at = max(at, ready_at[0, nt - 2])
        for kind in range(3):
            for part in range(2):
                def run(u=u, kind=kind, part=part):
                    project(u, kind, part)
                task(at, run)
                at += 0.7
        for b in range(blocks):
            for only in range(group // 128):
                def run(u=u, b=b, only=only):
                    attention(u, b, only)
                task(at, run)
                at += ATTEND

        def run(u=u, n=n):
            out_project(u, n == 0)
        task(at, run)
        at += 0.6

    def keep_heads():
        for n in (2, 3, 4, 6):
            kept[n].start()
    task(at, keep_heads)

    def rows_of(i):
        return slice(i * BLOCK, (i + 1) * BLOCK)

    for i in range(blocks):
        def norm_two(i=i):
            rows = rows_of(i)
            token = tok[HALO + i * BLOCK:HALO + (i + 1) * BLOCK, :].astype(F32)
            whole = hidden[rows, :] + token + ob
            hidden[rows, :] = whole
            xhat, _ = standardize(whole)
            low = (xhat * g2 + s2).astype(BF16)
            normed_two[rows, :] = low
            n2t[:, rows] = low.T
        task(at, norm_two)
        at += 0.7

    def keep_hidden():
        kept[1].start()
    task(at, keep_hidden)
    table = nearest(nt)
    slab = 32

    def grads_out(slot, shard):
        return pltpu.make_async_copy(gbuf.at[slot], grads.at[shard], gsem.at[slot])

    def mlp_steps(position):
        shard, slot = pick(table, position), position % 2

        def up():
            return w[shard, 1].reshape(width, width)

        def down():
            return w[shard, 2].reshape(width, width)

        def begin():
            pre_s[...] = dot(normed_two[...], up(), NN) + bias_all[shard, 0:1, :]

        def begin_back():
            gact_s[...] = dot(cot[...], down(), NT)

        def middle():
            def step(i, total):
                rows = pl.ds(pl.multiple_of(i * slab, slab), slab)
                value, slope = gelu_parts(pre_s[rows, :])
                act[rows, :] = value.astype(BF16)
                low = (gact_s[rows, :] * slope).astype(BF16)
                gpre[rows, :] = low
                return total + low.astype(F32)
            total = lax.fori_loop(0, own // slab, step, jnp.zeros((slab, width), F32))
            small[pl.ds(8 + shard, 1), :] = jnp.sum(total, axis=0, keepdims=True)

        def end():
            if position == 0:
                mlp[...] = dot(act[...], down(), NN)
                gtwo[...] = dot(gpre[...], up(), NT)
            else:
                mlp[...] += dot(act[...], down(), NN)
                gtwo[...] += dot(gpre[...], up(), NT)

        def grad_up():
            if position >= 2:
                grads_out(slot, shard).wait()
            gbuf[slot, 0] = dot(n2t[...], gpre[...], NN).astype(BF16).reshape(gbuf.shape[2:])

        def grad_down():
            gbuf[slot, 1] = dot(cot_t[...], act[...], NN).astype(BF16).reshape(gbuf.shape[2:])
            grads_out(slot, shard).start()
        return (begin, 0.7), (begin_back, 0.7), (middle, 1.0), (end, 1.4), (grad_up, 0.7), (grad_down, 0.7)

    for position in range(nt):
        if position > 0:
            at = max([at] + [ready_at[k, position - 1] for k in range(1, chunks)])
        for run, length in mlp_steps(position):
            task(at, run)
            at += length

    def finish():
        def part(n, carry):
            rows = pl.ds(pl.multiple_of(n * 32, 32), 32)
            result[rows, :] = (hidden[rows, :] + mlp[rows, :] + db).astype(BF16)
            return carry
        kept[7].start()
        lax.fori_loop(0, own // 32, part, 0)
        kept[0].start()
    task(at, finish)

    def keep_copy():
        return pltpu.make_async_copy(w.at[:, 0], w0, ls.at[0])

    def keep_first():
        keep_copy().start()
    task(at - 10.0, keep_first)
    ordered(tasks)
    grads_out(0, 0).wait()
    grads_out(1, 0).wait()
    keep_copy().wait()
    for copy in kept:
        copy.wait()
    for n in (0, 1, 2, 3, 4, 6, 7):
        small[n:n + 1, :] = jnp.zeros((1, width), F32)
    if small.shape[0] > 8 + nt:
        small[8 + nt:, :] = jnp.zeros((small.shape[0] - 8 - nt, width), F32)
    z_finish()
    for j in range(nt - 1):
        bias_send(j).wait_send()
    for k in range(chunks):
        for j in range(nt - 1):
            def end(shard, k, way, j):
                core(shard, k, way, j).wait_send()
                for q in (0, 1):
                    one(shard, k, q, way, j).wait_send()
                    if k < DIRECT:
                        two(shard, k, q, way, j).wait_send()
            each(k, j, end)


def forward(arrays, nt):
    length, width = arrays[0].shape
    own = length // nt
    window = own + 2 * HALO
    piece = width // 16
    unit = (2, 2, 2, 2, piece, width)
    rows = width + 2 * arrays[12].shape[0]
    chunks = rows // (16 * piece)
    lines = 8 + nt + -nt % 8
    dma = pltpu.SemaphoreType.DMA
    vmem, any_ = pl.BlockSpec(memory_space=pltpu.VMEM), pl.BlockSpec(memory_space=pl.ANY)

    def shape(dims, kind):
        return jax.ShapeDtypeStruct(dims, kind)

    def low(*dims):
        return pltpu.VMEM(dims, BF16)

    def wide(*dims):
        return pltpu.VMEM(dims, F32)
    views = list(arrays)
    for n in (7, 11, 13):
        views[n] = arrays[n].reshape(unit[2:] if n == 7 else unit)
    views[5] = arrays[5].transpose(0, 2, 1).reshape((3,) + unit[2:])
    return pl.pallas_call(
        functools.partial(forward_kernel, nt, chunks, own),
        name="forward",
        out_shape=(
            shape((own, width), BF16), shape((own, width), F32),
            shape((window, width), BF16), shape((window, width), BF16), shape((window, width), BF16),
            shape((own, width), BF16), shape((width, own), BF16), shape((own, width), F32),
            shape((own // BLOCK, 8, 2 * BLOCK), F32), shape((lines, width), F32),
            shape((nt, chunks - 1) + unit, BF16), shape((nt,) + unit, BF16),
        ),
        in_specs=[any_, any_] + [vmem] * 3 + [any_, vmem, any_] + [vmem] * 3 + [any_, vmem, any_, vmem],
        out_specs=(any_,) * 8 + (vmem, vmem, any_, any_),
        scratch_shapes=[
            low(own, width), wide(own, width), low(window, width), low(window, width), low(window, width),
            low(width, own), wide(own, width),
            low(window, width), low(own, width), pltpu.VMEM((1, length + 2 * HALO), jnp.int32),
            pltpu.VMEM((1, window), jnp.int32), pltpu.VMEM((window, BLOCK), jnp.int32), wide(8, width),
            low(window, width), low(nt, chunks, *unit), wide(nt, 8, width), dma((nt - 1,)), dma((nt - 1,)),
            low(own, width), low(own, width), low(width, own), low(width, own), wide(own, width),
            low(2, chunks - 1, *unit), wide(own, width), wide(own, width), low(own, width), low(own, width),
            dma((2,)),
            dma((2 * chunks - DIRECT, nt - 1, 2)), dma((2 * chunks - DIRECT, nt - 1, 2)),
            dma((chunks, nt - 1, 2, 4)), dma((chunks, nt - 1, 2, 4)),
            dma((chunks, nt - 1, 2)), dma((chunks, nt - 1, 2)), dma((8,)), dma((8,)),
        ],
        compiler_params=pltpu.CompilerParams(
            collective_id=1, has_side_effects=True, vmem_limit_bytes=VMEM_LIMIT),
    )(*views)


PIECES = 3
OWN_TIME, SIDE_TIME = 1.7, 1.7
PACE, STEPS, HOP = 4.5, (1.7, 7.0, 13.3), 6.9


def backward_kernel(nt, chunks, extra,
                    lse_ref, small1, segments, gain_1, gain_2,
                    cotangent, tokens_in, grads, w0, result, hidden_in, q_in, k_in, v_in, normed_in, heads_in, gtwo_in,
                    total_out, small, result_all, input_grad_all, total, gathered_r, gathered_g,
                    hidden, q_ref, k_ref, v_ref, normed, heads_t, gtwo,
                    s1, rc, ra, rb, rz, rx, rt, sr, g0, w_first, token, cot, segp, segr, segc, branch, g_ref, stats,
                    halo_g, halo_s, dk, dv, dq, d_t, gtwo_out, own_ig,
                    ls, cs, cr, ps, pr, zs, zr, xs, xr, fs, fr, os_, or_, ss, sm, hs, hr, lo, in_sem, leave_sem):
    d, t, b0, b1, b2 = place()
    own, width = hidden.shape
    blocks = own // BLOCK
    gathered = (gathered_r, gathered_g)
    bits = (1, 2, 4) + tuple(extra)
    order = tuple(range(chunks))[::-1]
    units = [(k, s) for k in order for s in range(nt)]

    def own_copy(k, s):
        return pltpu.make_async_copy(grads.at[s, k - 1, b0], s1.at[s, k], ls.at[s, k])

    arrivals = [pltpu.make_async_copy(source, goal, in_sem.at[n]) for n, (source, goal) in enumerate((
        (hidden_in, hidden), (gtwo_in, gtwo), (heads_in, heads_t), (q_in, q_ref), (k_in, k_ref), (v_in, v_ref),
        (normed_in, normed), (result, gathered_r.at[t])))]
    fetch_w = pltpu.make_async_copy(w0, w_first, lo.at[0])
    mine = pl.ds(pl.multiple_of(t * own, own), own)
    fetch_t = pltpu.make_async_copy(tokens_in.at[mine], token, lo.at[1])
    fetch_t.start()
    fetch_c = pltpu.make_async_copy(cotangent.at[mine], cot, lo.at[2])
    fetch_c.start()
    for copy in arrivals[:3]:
        copy.start()
    fetch_w.start()
    for copy in arrivals[3:]:
        copy.start()
    for k, s in units:
        if k > 0:
            own_copy(k, s).start()
    window_segments(segments, segp, segr, segc)
    greet(nt, bits, nt > 2)
    tasks = []

    def task(when, body):
        tasks.append((when, len(tasks), body))

    def leave(n):
        source, goal = ((gathered_r, result_all), (gathered_g, input_grad_all))[n] if n < 5 else (total.at[n - 5], total_out.at[n - 5])
        return pltpu.make_async_copy(source, goal, leave_sem.at[n])

    def core(k, s):
        source = g0.at[s, 1 - b0] if k == 0 else grads.at[s, k - 1, 1 - b0]
        return remote(source, rc.at[s, k], cs.at[s, k], cr.at[s, k], dp=flip(d, 1))

    def one(k, s, q):
        if q == 0:
            return remote(s1.at[s, k, 1 - b2, :, 0], ra.at[s, k], ps.at[s, k, 0], pr.at[s, k, 0], dp=flip(d, 4))
        return remote(s1.at[s, k, :, 1 - b1, 1], rb.at[s, k], ps.at[s, k, 1], pr.at[s, k, 1], dp=flip(d, 2))

    def two(k, s, q):
        if q == 0:
            return remote(s1.at[s, k, b2, 1 - b1, 0], rz.at[s, k, 0], ps.at[s, k, 2], pr.at[s, k, 2], dp=flip(d, 2))
        return remote(s1.at[s, k, 1 - b2, b1, 1], rz.at[s, k, 1], ps.at[s, k, 3], pr.at[s, k, 3], dp=flip(d, 4))

    def up(k, s):
        return remote(s1.at[s, k, b2, b1], rx.at[s, k], zs.at[s, k, 0], zr.at[s, k, 0], tensor=t + 1)

    def down(k, s, last):
        goal = rt.at[k] if last else rx.at[s, k]
        return remote(s1.at[s, k, b2, b1], goal, zs.at[s, k, 1], zr.at[s, k, 1], tensor=t - 1)

    def halo(n):
        if n == 0:
            return remote(g_ref.at[pl.ds(own - REACH, REACH)], halo_g.at[0, pl.ds(HALO - REACH, REACH)],
                          hs.at[0], hr.at[0], tensor=t + 1)
        if n == 1:
            return remote(g_ref.at[pl.ds(0, REACH)], halo_g.at[1, pl.ds(0, REACH)], hs.at[1], hr.at[1], tensor=t - 1)
        span = HALO // BLOCK
        if n == 2:
            return remote(stats.at[pl.ds(blocks - span, span)], halo_s.at[0], hs.at[2], hr.at[2], tensor=t + 1)
        return remote(stats.at[pl.ds(0, span)], halo_s.at[1], hs.at[3], hr.at[3], tensor=t - 1)

    def halo_start():
        @pl.when(t < nt - 1)
        def _():
            halo(0).start()
            halo(2).start()

        @pl.when(t > 0)
        def _():
            halo(1).start()
            halo(3).start()
        pad = HALO - REACH
        halo_g[0, 0:pad, :] = jnp.zeros((pad, width), BF16)
        halo_g[1, REACH:HALO, :] = jnp.zeros((pad, width), BF16)

        @pl.when(t == 0)
        def _():
            halo_g[0] = jnp.zeros((HALO, width), BF16)
            halo_s[0] = jnp.zeros(halo_s.shape[1:], F32)

        @pl.when(t == nt - 1)
        def _():
            halo_g[1] = jnp.zeros((HALO, width), BF16)
            halo_s[1] = jnp.zeros(halo_s.shape[1:], F32)

    def halo_end():
        @pl.when(t > 0)
        def _():
            halo(0).wait_recv()
            halo(2).wait_recv()

        @pl.when(t < nt - 1)
        def _():
            halo(1).wait_recv()
            halo(3).wait_recv()

    def attend_block(w, cols, row):
        q0 = w * BLOCK
        middle = HALO // BLOCK <= w < HALO // BLOCK + blocks
        k0, k1 = max(0, q0 - REACH), q0 + BLOCK + REACH
        if not middle:
            k0, k1 = max(k0, HALO), min(k1, HALO + own)
        q2 = stacked(q_ref[q0:q0 + BLOCK, cols] * SCALE)
        if middle:
            i = w - HALO // BLOCK
            g_rows = g_ref[i * BLOCK:(i + 1) * BLOCK, cols]
            lse, delta = stats[i, pl.ds(row, 1), :], stats[i, pl.ds(8 + row, 1), :]
        else:
            side = int(w > HALO // BLOCK)
            i = w if side == 0 else w - HALO // BLOCK - blocks
            g_rows = halo_g[side, i * BLOCK:(i + 1) * BLOCK, cols]
            lse, delta = halo_s[side, i, pl.ds(row, 1), :], halo_s[side, i, pl.ds(8 + row, 1), :]
        g2 = stacked(g_rows)
        k2, v2 = k_ref[k0:k1, cols], v_ref[k0:k1, cols]
        allowed = segc[k0:k1, :] == segr[:, q0:q0 + BLOCK]
        allowed = jnp.concatenate([allowed, allowed], axis=1)
        s = dot(k2, q2, NT)
        p = jnp.exp(jnp.where(allowed, s - lse, -1e9))
        low = p.astype(BF16)
        ds = (p * (dot(v2, g2, NT) - delta)).astype(BF16)
        o0, o1 = max(k0, HALO), min(k1, HALO + own)
        dst, src = slice(o0 - HALO, o1 - HALO), slice(o0 - k0, o1 - k0)
        dk[dst, cols] += dot(ds[src], q2, NN)
        dv[dst, cols] += dot(low[src], g2, NN)
        if middle:
            out = dot(k2.T, ds, NN) * SCALE
            half = out.shape[1] // 2
            both = jnp.concatenate([out[:HEAD_DIM, :half], out[HEAD_DIM:, half:]], axis=0).astype(BF16)
            d_t[0, cols, i * BLOCK:(i + 1) * BLOCK] = both
            dq[0, i * BLOCK:(i + 1) * BLOCK, cols] = both.T

    def attention(first, count, mine):
        def pair(j, carry):
            cols = pl.ds(pl.multiple_of(j * 128, 128), 128)
            if mine:
                dk[:, cols] = jnp.zeros((own, 128), F32)
                dv[:, cols] = jnp.zeros((own, 128), F32)
                for b in range(blocks):
                    attend_block(HALO // BLOCK + b, cols, j)
            else:
                for w in tuple(range(HALO // BLOCK)) + tuple(range(HALO // BLOCK + blocks, 2 * HALO // BLOCK + blocks)):
                    attend_block(w, cols, j)
                for n, ref in enumerate((dk, dv)):
                    value = ref[:, cols].astype(BF16)
                    dq[1 + n, :, cols] = value
                    d_t[1 + n, cols, :] = value.T
            return carry
        for j in range(first, first + count):
            pair(j, 0)

    g1, g2 = gain_1[...].reshape(1, width), gain_2[...].reshape(1, width)

    def norm_two_back():
        fetch_c.wait()
        arrivals[0].wait()
        arrivals[1].wait()

        def part(n, carry):
            rows = pl.ds(pl.multiple_of(n * 32, 32), 32)
            xhat, r = standardize(hidden[rows, :])
            grad = gtwo[rows, :]
            gh = cot[rows, :].astype(F32) + norm_back(grad * g2, xhat, r)
            gtwo_out[rows, :] = gh
            branch[rows, :] = gh.astype(BF16)
            return carry[0] + gh, carry[1] + grad * xhat, carry[2] + grad
        zero = jnp.zeros((32, width), F32)
        sums = lax.fori_loop(0, own // 32, part, (zero, zero, zero))
        small[...] = small1[...]
        for line, value in zip((2, 3, 4), sums):
            small[line:line + 1, :] = jnp.sum(value, axis=0, keepdims=True)

    def out_back():
        fetch_w.wait()
        arrivals[2].wait()
        outw = w_first[:, 1, 1].reshape(width, width)
        rows = branch[...]
        g_ref[...] = dot(rows, outw, NT).astype(BF16)
        g_t = dot(outw, rows, NT).astype(BF16).astype(F32)
        product = g_t * heads_t[...].astype(F32)
        for b in range(blocks):
            stats[b, 0:8, :] = lse_ref[b]
            for h in range(width // HEAD_DIM):
                line = jnp.sum(product[h * HEAD_DIM:(h + 1) * HEAD_DIM, b * BLOCK:(b + 1) * BLOCK], axis=0, keepdims=True)
                stats[b, 8 + h // 2:9 + h // 2, (h % 2) * BLOCK:(h % 2 + 1) * BLOCK] = line
            stats[b, 8 + width // 128:16, :] = jnp.zeros((8 - width // 128, 2 * BLOCK), F32)

    def out_grad():
        value = dot(heads_t[...], branch[...], NN).astype(BF16)
        g0[:, 1, 1] = value.reshape((nt,) + g0.shape[3:])
    task(0.3, norm_two_back)
    task(3.0, out_back)
    task(5.5, halo_start)
    task(6.0, out_grad)
    at = 7.0
    pairs = width // 128

    def attend_ready():
        for copy in arrivals[3:]:
            copy.wait()
    task(at, attend_ready)
    for first in range(pairs):
        def run(first=first):
            attention(first, 1, True)
        task(at, run)
        at += OWN_TIME
    at = max(at, 14.0)
    task(at, halo_end)
    for first in range(pairs):
        def run(first=first):
            attention(first, 1, False)
        task(at, run)
        at += SIDE_TIME

    def weight_of(kind):
        return w_first[:, kind // 2, kind % 2].reshape(width, width)

    def back_project():
        dk[...] = dot(dq[0], weight_of(0), NN)
        dk[...] += dot(dq[1], weight_of(1), NN)
        dk[...] += dot(dq[2], weight_of(2), NN)
    task(at, back_project)
    at += 2.5

    def norm_one():
        fetch_t.wait()

        def part(n, carry):
            rows = pl.ds(pl.multiple_of(n * 32, 32), 32)
            xhat, r = standardize(token[rows, :].astype(F32))
            grad = dk[rows, :]
            own_ig[rows, :] = (gtwo_out[rows, :] + norm_back(grad * g1, xhat, r)).astype(BF16)
            return (carry[0] + grad * xhat, carry[1] + grad, carry[2] + dq[0, rows, :].astype(F32),
                    carry[3] + dq[2, rows, :].astype(F32))
        zero = jnp.zeros((32, width), F32)
        sums = lax.fori_loop(0, own // 32, part, (zero, zero, zero, zero))
        for line, value in zip((0, 1, 6, 7), sums):
            small[line:line + 1, :] = jnp.sum(value, axis=0, keepdims=True)
        gathered_g[t] = own_ig[...]
    task(at, norm_one)
    at += 3.0
    ready = at
    for kind in range(3):
        def run(kind=kind):
            value = dot(d_t[kind], normed[...], NN).astype(BF16)
            g0[:, kind // 2, kind % 2] = value.reshape((nt,) + g0.shape[3:])
        task(at, run)
        at += 1.2

    late = at

    pace = PACE
    for n, (k, s) in enumerate(units):
        base = n * pace if k > 0 else max(n * pace, late + 0.0 + (n - nt * (chunks - 1)) * pace)

        def first(k=k, s=s):
            core(k, s).start()

        def second(k=k, s=s):
            core(k, s).wait_recv()
            if k > 0:
                own_copy(k, s).wait()
                add_bf16(s1.at[s, k], rc.at[s, k])
            else:
                s1[s, k] = (g0[s, b0].astype(F32) + rc[s, k].astype(F32)).astype(BF16)
            one(k, s, 0).start()
            one(k, s, 1).start()

        def third(k=k, s=s):
            one(k, s, 0).wait_recv()
            one(k, s, 1).wait_recv()
            add_bf16(s1.at[s, k, b2, :, 0], ra.at[s, k])
            add_bf16(s1.at[s, k, :, b1, 1], rb.at[s, k])
            two(k, s, 0).start()
            two(k, s, 1).start()

        def fourth(k=k, s=s):
            two(k, s, 0).wait_recv()
            two(k, s, 1).wait_recv()
            add_bf16(s1.at[s, k, b2, b1, 0], rz.at[s, k, 0])
            add_bf16(s1.at[s, k, b2, b1, 1], rz.at[s, k, 1])
        task(max(base - 19.9, -10.0) if k > 0 else max(base - 12.0, late + 0.01), first)
        task(base + STEPS[0], second)
        task(base + STEPS[1], third)
        task(base + STEPS[2], fourth)
        if s == nt - 1:
            end_of_chunk = base + STEPS[2]
        else:
            continue

        for hop in range(nt):
            def chain(k=k, hop=hop):
                @pl.when(t == hop)
                def _():
                    for s in reversed(range(nt)):
                        @pl.when(s >= t)
                        def _():
                            if hop > 0:
                                up(k, s).wait_recv()
                                add_bf16(s1.at[s, k, b2, b1], rx.at[s, k])
                            if hop < nt - 1:
                                @pl.when(s > t)
                                def _():
                                    up(k, s).start()

                @pl.when(t == nt - 1 - hop)
                def _():
                    for s in range(nt):
                        if hop > 0:
                            @pl.when(s < t)
                            def _():
                                down(k, s, False).wait_recv()
                                add_bf16(s1.at[s, k, b2, b1], rx.at[s, k])

                            @pl.when(s == t)
                            def _():
                                down(k, s, True).wait_recv()
                                add_bf16(s1.at[s, k, b2, b1], rt.at[k])
                        if hop < nt - 1:
                            @pl.when(s == t - 1)
                            def _():
                                down(k, s, True).start()

                            @pl.when(s < t - 1)
                            def _():
                                down(k, s, False).start()
            task(end_of_chunk + 0.5 + HOP * hop, chain)
        base = end_of_chunk + 0.5 + HOP * nt + -6.2

        for e, bit in enumerate(extra):
            def more(k=k, e=e, bit=bit):
                swap = remote(s1.at[t, k, b2, b1], rx.at[nt + e, k], xs.at[e, k], xr.at[e, k], dp=flip(d, bit))
                swap.start()
                swap.wait()
                add_bf16(s1.at[t, k, b2, b1], rx.at[nt + e, k])
            task(base + 0.01 * e, more)

        def settle(k=k):
            total[k, b0, b2, b1] = s1[t, k, b2, b1]

        def give_one(k, q):
            if q == 0:
                piece = total.at[k, b0, b2, b1, 0]
                return remote(piece, piece, fs.at[k, 0], fr.at[k, 0], dp=flip(d, 2))
            piece = total.at[k, b0, b2, b1, 1]
            return remote(piece, piece, fs.at[k, 1], fr.at[k, 1], dp=flip(d, 4))

        def give_two(k, q):
            if q == 0:
                piece = total.at[k, b0, b2, :, 0]
                return remote(piece, piece, fs.at[k, 2], fr.at[k, 2], dp=flip(d, 4))
            piece = total.at[k, b0, :, b1, 1]
            return remote(piece, piece, fs.at[k, 3], fr.at[k, 3], dp=flip(d, 2))

        def give_core(k):
            return remote(total.at[k, b0], total.at[k, b0], fs.at[k, 4], fr.at[k, 4], dp=flip(d, 1))

        def spread_one(k=k):
            for q in (0, 1):
                give_one(k, q).start()

        def spread_two(k=k):
            for q in (0, 1):
                give_one(k, q).wait_recv()
            for q in (0, 1):
                give_two(k, q).start()

        def spread_core(k=k):
            for q in (0, 1):
                give_two(k, q).wait_recv()
            give_core(k).start()

        def spread_end(k=k):
            give_core(k).wait()
            leave(5 + k).start()
            for q in (0, 1):
                give_one(k, q).wait_send()
                give_two(k, q).wait_send()
        task(base + 0.5, settle)
        task(base + 0.7, spread_one)
        task(base + 5.1, spread_two)
        task(base + 10.6, spread_core)
        task(1e6 if k == order[-1] else base + 16.0, spread_end)

    part = own // PIECES

    def piece_of(ref, n):
        return ref.at[pl.ds(n % PIECES * part, part)]
    z_tasks, z_finish = relay_tasks(
        nt, 2 * PIECES, lambda n: piece_of((result, own_ig)[n // PIECES], n),
        lambda s, n: piece_of(gathered[n // PIECES].at[s], n), (os_, or_),
        lambda n, j: (-5.0, ready)[n // PIECES] + 20.2 / PIECES * (n % PIECES) + 20.2 * j + (0.01 if j == 0 else 0.2),
        lambda *a: None)
    tasks += [(w, 1000 + n, b) for w, n, b in z_tasks]

    def result_done():
        leave(0).start()
    task(max(w for w, n, b in z_tasks[:PIECES * nt]) + 0.1, result_done)

    exchanges = [("dp", bit) for bit in bits]
    step = 1
    while step < nt:
        exchanges.append(("tensor", step))
        step *= 2
    for e, (axis, bit) in enumerate(exchanges):
        def swap(e=e, axis=axis, bit=bit):
            goal = {axis: flip(lax.axis_index(axis), bit)}
            return remote(small, sr.at[e], ss.at[e], sm.at[e], **goal)

        def begin(swap=swap):
            swap().start()

        def end(e=e, swap=swap):
            swap().wait()
            small[...] = small[...] + sr[e]
        task(late + 19.6 + 9.5 * e, begin)
        task(late + 28.4 + 9.5 * e, end)

    ordered(tasks)
    leave(1).start()
    z_finish()
    for n in (0, 1) + tuple(5 + k for k in order):
        leave(n).wait()

    @pl.when(t < nt - 1)
    def _():
        halo(0).wait_send()
        halo(2).wait_send()

    @pl.when(t > 0)
    def _():
        halo(1).wait_send()
        halo(3).wait_send()
    for k, s in units:
        core(k, s).wait_send()
        for q in (0, 1):
            one(k, s, q).wait_send()
            two(k, s, q).wait_send()

        @pl.when(s > t)
        def _():
            up(k, s).wait_send()

        @pl.when(s < t)
        def _():
            down(k, s, False).wait_send()


def backward(vmem_arrays, hbm_arrays, nt, extra):
    own, width = hbm_arrays[4].shape
    grads, segments = hbm_arrays[2], vmem_arrays[2]
    small_shape = vmem_arrays[1].shape
    piece, chunks = width // 16, grads.shape[1] + 1
    window = own + 2 * HALO
    dma = pltpu.SemaphoreType.DMA
    hops = 3 + len(extra) + (nt - 1).bit_length()
    vmem, any_ = pl.BlockSpec(memory_space=pltpu.VMEM), pl.BlockSpec(memory_space=pl.ANY)
    unit = (2, 2, 2, piece, width)
    blocks = own // BLOCK

    def low(*dims):
        return pltpu.VMEM(dims, BF16)

    def wide(*dims):
        return pltpu.VMEM(dims, F32)
    return pl.pallas_call(
        functools.partial(backward_kernel, nt, chunks, extra),
        name="backward",
        out_shape=(
            jax.ShapeDtypeStruct((chunks, 2) + unit, BF16),
            jax.ShapeDtypeStruct(small_shape, F32),
            jax.ShapeDtypeStruct((nt, own, width), BF16),
            jax.ShapeDtypeStruct((nt, own, width), BF16),
        ),
        in_specs=[vmem] * len(vmem_arrays) + [any_] * len(hbm_arrays),
        out_specs=(any_, vmem, any_, any_),
        scratch_shapes=[
            low(chunks, 2, *unit), low(nt, own, width), low(nt, own, width),
            wide(own, width), low(window, width), low(window, width), low(window, width), low(own, width),
            low(width, own), wide(own, width),
            low(nt, chunks, *unit), low(nt, chunks, *unit),
            low(nt, chunks, 2, piece, width), low(nt, chunks, 2, piece, width), low(nt, chunks, 2, piece, width),
            low(nt + len(extra), chunks, 2, piece, width), low(chunks, 2, piece, width),
            wide(hops, *small_shape), low(nt, 2, *unit), low(nt, 2, *unit),
            low(own, width), low(own, width), pltpu.VMEM((1, segments.shape[1] + 2 * HALO), jnp.int32),
            pltpu.VMEM((1, window), jnp.int32), pltpu.VMEM((window, BLOCK), jnp.int32),
            low(own, width), low(own, width), wide(blocks, 16, 2 * BLOCK),
            low(2, HALO, width), wide(2, HALO // BLOCK, 16, 2 * BLOCK),
            wide(own, width), wide(own, width), low(3, own, width), low(3, width, own),
            wide(own, width), low(own, width),
            dma((nt, chunks)), dma((nt, chunks)), dma((nt, chunks)),
            dma((nt, chunks, 4)), dma((nt, chunks, 4)),
            dma((nt, chunks, 2)), dma((nt, chunks, 2)),
            dma((max(1, len(extra)), chunks)), dma((max(1, len(extra)), chunks)),
            dma((chunks, 5)), dma((chunks, 5)),
            dma((2 * PIECES, nt - 1, 2)), dma((2 * PIECES, nt - 1, 2)),
            dma((hops,)), dma((hops,)), dma((4,)), dma((4,)), dma((3,)), dma((8,)), dma((5 + chunks,)),
        ],
        compiler_params=pltpu.CompilerParams(
            collective_id=2, has_side_effects=True, vmem_limit_bytes=VMEM_LIMIT),
    )(*vmem_arrays, *hbm_arrays)


def finish_kernel(nt, ndp, total_in, small, results, input_grads,
                  results_out, input_grads_out, g1, s1, qkv, qvb, out_w, out_b, g2, s2, up, up_b, down, down_b,
                  total, held, first, second, third, in_sem, out_sem):
    t = lax.axis_index("tensor")
    width = small.shape[1]
    local = width // nt
    scale = 1.0 / ndp
    parts = [pltpu.make_async_copy(total_in.at[k], total.at[k], in_sem.at[k]) for k in range(3)]
    for k in (1, 2, 0):
        parts[k].start()
    stage = [pltpu.make_async_copy(results, held.at[0], in_sem.at[3]), pltpu.make_async_copy(input_grads, held.at[1], in_sem.at[4])]
    for copy in stage:
        copy.start()
    moves = []
    for ref, line in ((g1, 0), (s1, 1), (out_b, 2), (g2, 3), (s2, 4), (down_b, 5)):
        ref[...] = small[line:line + 1, :].reshape(width) * scale
    up_b[...] = small[pl.ds(8 + t, 1), :].reshape(width) * scale
    for place in range(nt):
        @pl.when(t == place)
        def _():
            qvb[...] = small[6:8, place * local:(place + 1) * local] * scale
    for n, goal in enumerate((results_out, input_grads_out)):
        stage[n].wait()
        moves.append(pltpu.make_async_copy(held.at[n], goal, out_sem.at[n]))
        moves[-1].start()
    parts[1].wait()
    second[...] = total[1].reshape(width, width).astype(F32) * scale
    moves.append(pltpu.make_async_copy(second, up, out_sem.at[2]))
    moves[-1].start()
    parts[2].wait()
    third[...] = (total[2].reshape(width, width).astype(F32) * scale).T
    moves.append(pltpu.make_async_copy(third, down, out_sem.at[3]))
    moves[-1].start()
    parts[0].wait()
    first[...] = total[0].reshape(nt, local, width).astype(F32) * scale
    moves.append(pltpu.make_async_copy(first.at[pl.ds(0, 3)], qkv, out_sem.at[4]))
    moves[-1].start()
    moves.append(pltpu.make_async_copy(first.at[3], out_w, out_sem.at[5]))
    moves[-1].start()
    for copy in moves:
        copy.wait()


def finish_up(total, small, results, input_grads, nt, ndp):
    width = small.shape[1]
    local = width // nt
    dma = pltpu.SemaphoreType.DMA
    vmem, any_ = pl.BlockSpec(memory_space=pltpu.VMEM), pl.BlockSpec(memory_space=pl.ANY)

    def shape(*dims):
        return jax.ShapeDtypeStruct(dims, F32)
    return pl.pallas_call(
        functools.partial(finish_kernel, nt, ndp),
        name="finish",
        out_shape=(jax.ShapeDtypeStruct(results.shape, BF16), jax.ShapeDtypeStruct(results.shape, BF16),
                   shape(width), shape(width), shape(3, local, width), shape(2, local), shape(local, width), shape(width),
                   shape(width), shape(width), shape(width, width), shape(width), shape(width, width), shape(width)),
        in_specs=[any_, vmem, any_, any_],
        out_specs=(any_, any_, vmem, vmem, any_, vmem, any_, vmem, vmem, vmem, any_, vmem, any_, vmem),
        scratch_shapes=[pltpu.VMEM(total.shape, BF16), pltpu.VMEM((2,) + results.shape, BF16), pltpu.VMEM((nt, local, width), F32),
                        pltpu.VMEM((width, width), F32), pltpu.VMEM((width, width), F32), dma((5,)), dma((6,))],
        compiler_params=pltpu.CompilerParams(vmem_limit_bytes=VMEM_LIMIT),
    )(total, small, results, input_grads)


def body(tokens_in, segment_ids, first_gain, first_shift, qkv_weight, query_value_bias, out_weight, out_bias,
         second_gain, second_shift, up_weight, up_bias, down_weight, down_bias, cotangent):
    nt, ndp = lax.axis_size("tensor"), lax.axis_size("dp")
    length, width = tokens_in.shape
    (result, hidden, q, k, v, normed, heads_t, grad_two, lse, small, mlp_grads, w_first) = forward(
        (tokens_in, cotangent, segment_ids, first_gain, first_shift, qkv_weight, query_value_bias, out_weight, out_bias,
         second_gain, second_shift, up_weight, up_bias, down_weight, down_bias), nt)
    extra = []
    bit = 8
    while bit < ndp:
        extra.append(bit)
        bit *= 2
    total, small, results, input_grads = backward(
        (lse, small, segment_ids, first_gain, second_gain),
        (cotangent, tokens_in, mlp_grads, w_first, result, hidden, q, k, v, normed, heads_t, grad_two), nt, tuple(extra))
    outs = list(finish_up(total, small, results, input_grads, nt, ndp))
    outs[0], outs[1] = outs[0].reshape(length, width), outs[1].reshape(length, width)
    outs[4] = outs[4].transpose(0, 2, 1)
    return tuple(outs)


def solution(mesh):
    placed = (
        P("dp", None), P("dp", None), P(), P(), P(None, None, "tensor"), P(None, "tensor"), P("tensor", None), P(),
        P(), P(), P(None, "tensor"), P("tensor"), P("tensor", None), P(), P("dp", None),
    )
    return jax.shard_map(
        body,
        mesh=mesh,
        in_specs=placed,
        out_specs=(
            P("dp", None), P("dp", None), P(), P(), P(None, None, "tensor"), P(None, "tensor"), P("tensor", None),
            P(), P(), P(), P(None, "tensor"), P("tensor"), P("tensor", None), P(),
        ),
        check_vma=False,
    )
```

```python
import functools

import jax
import jax.numpy as jnp
from jax import lax
from jax.experimental import pallas as pl
from jax.experimental.pallas import tpu as pltpu
from jax.sharding import PartitionSpec as P

HEAD_DIM = 64
HALO = 256
REACH = 224
BLOCK = 128
EPS = 1e-06
SCALE = HEAD_DIM ** -0.5
F32 = jnp.float32
BF16 = jnp.bfloat16
MESH = pl.DeviceIdType.MESH
VMEM_LIMIT = 60 << 20


def place():
    d, t = lax.axis_index("dp"), lax.axis_index("tensor")
    return d, t, lax.rem(d, 2), lax.rem(d // 2, 2), lax.rem(d // 4, 2)


def flip(d, value):
    return d + value * (1 - 2 * lax.rem(d // value, 2))


def remote(src, dst, send, recv, **axis):
    return pltpu.make_async_remote_copy(
        src_ref=src, dst_ref=dst, send_sem=send, recv_sem=recv,
        device_id=axis, device_id_type=MESH)


def greet(nt, bits, far=False):
    d, t = lax.axis_index("dp"), lax.axis_index("tensor")
    barrier = pltpu.get_barrier_semaphore()

    @pl.when(t > 0)
    def _():
        pl.semaphore_signal(barrier, inc=1, device_id={"tensor": t - 1}, device_id_type=MESH)

    @pl.when(t < nt - 1)
    def _():
        pl.semaphore_signal(barrier, inc=1, device_id={"tensor": t + 1}, device_id_type=MESH)

    for bit in bits:
        pl.semaphore_signal(barrier, inc=1, device_id={"dp": flip(d, bit)}, device_id_type=MESH)
    if far:
        pl.semaphore_signal(barrier, inc=1, device_id={"tensor": flip(t, 2)}, device_id_type=MESH)
    peers = len(bits) + int(far) + (t > 0).astype(jnp.int32) + (t < nt - 1).astype(jnp.int32)
    pl.semaphore_wait(barrier, peers)


def ordered(tasks):
    for _, _, task in sorted(tasks, key=lambda item: item[:2]):
        task()


def relay_tasks(nt, chunks, own, full, sems, start, arrived):
    send, recv = sems
    tasks = []
    t = lax.axis_index("tensor")
    for k in range(chunks):
        for j in range(nt):
            def step(k=k, j=j):
                for way in (0, 1):
                    sign = 1 - 2 * way
                    shard = t - sign * j
                    inside = (shard >= 0) & (shard < nt)
                    if j > 0:
                        @pl.when(inside)
                        def _():
                            remote(full(shard, k), full(shard, k), send.at[k, j - 1, way], recv.at[k, j - 1, way],
                                   tensor=t).wait_recv()
                            arrived(k, j, way, shard)
                    if j < nt - 1:
                        goal = t + sign
                        @pl.when(inside & (goal >= 0) & (goal < nt))
                        def _():
                            source = own(k) if j == 0 else full(shard, k)
                            remote(source, full(shard, k), send.at[k, j, way], recv.at[k, j, way],
                                   tensor=goal).start()
            tasks.append((start(k, j), len(tasks), step))

    def finish():
        for k in range(chunks):
            for j in range(nt - 1):
                for way in (0, 1):
                    sign = 1 - 2 * way
                    shard, goal = t - sign * j, t + sign
                    @pl.when((shard >= 0) & (shard < nt) & (goal >= 0) & (goal < nt))
                    def _():
                        source = own(k) if j == 0 else full(shard, k)
                        remote(source, full(shard, k), send.at[k, j, way], recv.at[k, j, way],
                               tensor=goal).wait_send()
    return tasks, finish


def add_bf16(ref, other):
    ref[...] = (ref[...].astype(F32) + other[...].astype(F32)).astype(BF16)


def stacked(pair):
    lane = lax.broadcasted_iota(jnp.int32, pair.shape, 1)
    zero = jnp.zeros_like(pair)
    return jnp.concatenate([jnp.where(lane < HEAD_DIM, pair, zero), jnp.where(lane < HEAD_DIM, zero, pair)], axis=0)


def dot(a, b, dims):
    return lax.dot_general(a, b, (dims, ((), ())), preferred_element_type=F32)


NN = ((1,), (0,))
NT = ((1,), (1,))


def untangle(both):
    half = both.shape[1] // 2
    return jnp.concatenate([both[:HEAD_DIM, :half], both[HEAD_DIM:, half:]], axis=0).T


def standardize(rows):
    center = rows - jnp.mean(rows, axis=-1, keepdims=True)
    r = lax.rsqrt(jnp.mean(center * center, axis=-1, keepdims=True) + EPS)
    return center * r, r


def norm_back(e, xhat, r):
    return r * (e - jnp.mean(e, axis=-1, keepdims=True) - xhat * jnp.mean(e * xhat, axis=-1, keepdims=True))


def window_segments(segments, padded, row, column):
    length, window = segments.shape[1], row.shape[1]
    padded[...] = jnp.full(padded.shape, -1, jnp.int32)
    padded[:, HALO:HALO + length] = segments[...]
    own = window - 2 * HALO
    for i in range(window // BLOCK):
        first = pl.multiple_of(lax.axis_index("tensor") * own + i * BLOCK, BLOCK)
        line = padded[:, pl.ds(first, BLOCK)]
        row[:, i * BLOCK:(i + 1) * BLOCK] = line
        column[i * BLOCK:(i + 1) * BLOCK, :] = jnp.broadcast_to(line, (BLOCK, BLOCK)).T


def nearest(nt):
    return [sorted(range(nt), key=lambda s: (abs(s - p), s if p < nt // 2 else -s)) for p in range(nt)]


def pick(table, position):
    t = lax.axis_index("tensor")
    return sum((t == p).astype(jnp.int32) * row[position] for p, row in enumerate(table))


def gelu_parts(x):
    cdf = 0.5 * (1.0 + lax.erf(x * (0.5 ** 0.5)))
    pdf = jnp.exp(-0.5 * x * x) * ((2.0 * jnp.pi) ** -0.5)
    return x * cdf, cdf + x * pdf


ATTEND = 0.6
NORM_TIME = 1.0
LINE_GAP, LAGS_0 = 2.3, (7.3, 12.9, 16.4)
DIRECT = 3
LINE, PLANE, LEAD, LAGS = 4.3, 4.2, 0.0, (5.6, 12.3, 15.8)


def forward_kernel(nt, chunks, own,
                   tokens_in, cotangent, segments, gain_1, shift_1, qkv_in, qv_bias, out_in, out_bias, gain_2, shift_2,
                   up_in, up_bias, down_in, down_bias,
                   result_out, hidden_out, q_out, k_out, v_out, normed_out, heads_out, gtwo_out, lse_ref, small, grads, w0,
                   result, hidden, q_ref, k_ref, v_ref, heads_t, gtwo, tok, cot, segp, segr, segc, bias, normed, w, bias_all, bias_sem, bias_recv, heads, normed_two, n2t,
                   cot_t, mlp, gbuf, pre_s, gact_s, act, gpre, gsem, zs, zr, ps, pr, cs, cr, ls, out_sem):
    d, t, b0, b1, b2 = place()
    window, width = tok.shape
    local = width // nt
    blocks = own // BLOCK
    local_copies = [pltpu.make_async_copy(qkv_in.at[kind], w.at[t, 0, kind // 2, kind % 2], ls.at[5 + kind])
                    for kind in range(3)] + [
        pltpu.make_async_copy(out_in, w.at[t, 0, 1, 1], ls.at[0]),
        pltpu.make_async_copy(up_in, w.at[t, 1], ls.at[1]),
        pltpu.make_async_copy(down_in, w.at[t, 2], ls.at[2]),
    ]
    for copy in local_copies:
        copy.start()
    cot_copy = pltpu.make_async_copy(cotangent.at[pl.ds(pl.multiple_of(t * own, own), own)], cot, ls.at[3])
    cot_copy.start()

    def token_copy(place):
        rows = own + HALO
        if place == 0:
            return pltpu.make_async_copy(tokens_in.at[pl.ds(0, rows)], tok.at[pl.ds(HALO, rows)], ls.at[4])
        if place == 1:
            return pltpu.make_async_copy(tokens_in.at[pl.ds((nt - 1) * own - HALO, rows)], tok.at[pl.ds(0, rows)], ls.at[4])
        first = pl.multiple_of(t * own - HALO, BLOCK)
        return pltpu.make_async_copy(tokens_in.at[pl.ds(first, window)], tok, ls.at[4])

    def tokens(act):
        @pl.when(t == 0)
        def _():
            act(token_copy(0))

        @pl.when(t == nt - 1)
        def _():
            act(token_copy(1))

        @pl.when((t > 0) & (t < nt - 1))
        def _():
            act(token_copy(2))
    tokens(lambda copy: copy.start())

    @pl.when(t == 0)
    def _():
        tok[0:HALO, :] = jnp.zeros((HALO, width), BF16)

    @pl.when(t == nt - 1)
    def _():
        tok[window - HALO:window, :] = jnp.zeros((HALO, width), BF16)

    barrier = pltpu.get_barrier_semaphore()
    for bit in (1, 2, 4):
        pl.semaphore_signal(barrier, inc=1, device_id={"dp": flip(d, bit)}, device_id_type=MESH)
    for j in range(1, nt):
        pl.semaphore_signal(barrier, inc=1, device_id={"tensor": lax.rem(t + j, nt)}, device_id_type=MESH)
    bias[...] = jnp.zeros(bias.shape, F32)
    bias[0:1, :] = up_bias[...].reshape(1, width)
    bias[1:3, 0:local] = qv_bias[...]
    bias_all[t] = bias[...]
    window_segments(segments, segp, segr, segc)
    for copy in local_copies:
        copy.wait()
    pl.semaphore_wait(barrier, 3 + nt - 1)
    tasks = []

    def task(when, body):
        tasks.append((when, len(tasks), body))

    def bias_send(j):
        return remote(bias, bias_all.at[t], bias_sem.at[j], bias_recv.at[j], tensor=lax.rem(t + j + 1, nt))

    def bias_get(j):
        source = lax.rem(t + nt - j - 1, nt)
        return remote(bias, bias_all.at[source], bias_sem.at[j], bias_recv.at[j], tensor=source)

    parity = lax.rem(b1 + b2, 2)

    def line_piece(shard, n):
        if n < DIRECT:
            return w.at[shard, n, b0, b2, b1]
        k, side = DIRECT + (n - DIRECT) // 2, (n - DIRECT) % 2
        return w.at[shard, k, b0, side, parity if side == 0 else 1 - parity]

    def one(shard, k, q, way, j):
        if k >= DIRECT:
            mine = line_piece(shard, DIRECT + 2 * (k - DIRECT) + q)
            return remote(mine, mine, ps.at[k, j, way, q], pr.at[k, j, way, q], dp=flip(d, 2 + 2 * q))
        if q == 0:
            mine = w.at[shard, k, b0, b2, b1, 0]
            return remote(mine, mine, ps.at[k, j, way, 0], pr.at[k, j, way, 0], dp=flip(d, 2))
        mine = w.at[shard, k, b0, b2, b1, 1]
        return remote(mine, mine, ps.at[k, j, way, 1], pr.at[k, j, way, 1], dp=flip(d, 4))

    def two(shard, k, q, way, j):
        if q == 0:
            mine = w.at[shard, k, b0, b2, :, 0]
            return remote(mine, mine, ps.at[k, j, way, 2], pr.at[k, j, way, 2], dp=flip(d, 4))
        mine = w.at[shard, k, b0, :, b1, 1]
        return remote(mine, mine, ps.at[k, j, way, 3], pr.at[k, j, way, 3], dp=flip(d, 2))

    def core(shard, k, way, j):
        return remote(w.at[shard, k, b0], w.at[shard, k, b0], cs.at[k, j, way], cr.at[k, j, way], dp=flip(d, 1))

    def each(k, j, act):
        for way in (0, 1):
            shard = t - (1 - 2 * way) * (j + 1)

            @pl.when((shard >= 0) & (shard < nt))
            def _():
                act(shard, k, way, j)

    def piece_time(n, j):
        if n < DIRECT:
            return LINE * (n * (nt - 1) + j) + (LINE_GAP if n > 0 else 0.0)
        pair, side = (n - DIRECT) // 2, (n - DIRECT) % 2
        return LINE_GAP + LINE * ((DIRECT + 2 * pair) * (nt - 1) + 2 * j - (j > 0) + side)

    def line_time(k, j):
        return piece_time(k, j) if k < DIRECT else piece_time(DIRECT + 2 * (k - DIRECT) + 1, j)

    z_tasks, z_finish = relay_tasks(
        nt, 2 * chunks - DIRECT, lambda n: line_piece(t, n), line_piece, (zs, zr), piece_time, lambda *a: None)
    tasks += z_tasks
    ready_at = {}
    for k in range(chunks):
        for j in range(nt - 1):
            def begin(k=k, j=j):
                def act(shard, k, way, j):
                    for q in (0, 1):
                        one(shard, k, q, way, j).start()
                each(k, j, act)

            def second(k=k, j=j):
                def act(shard, k, way, j):
                    for q in (0, 1):
                        one(shard, k, q, way, j).wait_recv()
                    for q in (0, 1):
                        two(shard, k, q, way, j).start()
                each(k, j, act)

            def third(k=k, j=j):
                def act(shard, k, way, j):
                    for q in (0, 1):
                        (two if k < DIRECT else one)(shard, k, q, way, j).wait_recv()
                    core(shard, k, way, j).start()
                each(k, j, act)

            def fourth(k=k, j=j):
                def act(shard, k, way, j):
                    core(shard, k, way, j).wait_recv()
                each(k, j, act)
            n = k * (nt - 1) + j
            base = max(line_time(k, j + 1) + 0.1, LEAD + PLANE * n)
            lags = LAGS_0 if k == 0 else LAGS
            skip = 0.0 if k < DIRECT else lags[0]
            task(base, begin)
            if k < DIRECT:
                task(base + lags[0], second)
            task(base + lags[1] - skip, third)
            task(base + lags[2] - skip, fourth)
            ready_at[k, j] = base + lags[2] - skip + 0.1

    def bias_begin():
        for j in range(nt - 1):
            bias_send(j).start()

    def bias_end():
        for j in range(nt - 1):
            bias_get(j).wait_recv()
    task(0.2, bias_begin)
    task(10.0, bias_end)

    g1, s1, ob, g2, s2, db = (ref[...].reshape(1, width) for ref in (gain_1, shift_1, out_bias, gain_2, shift_2, down_bias))

    def tokens_here():
        tokens(lambda copy: copy.wait())
    task(0.4, tokens_here)
    for i in range(window // BLOCK):
        def norm_rows(i=i):
            def part(n, carry):
                rows = pl.ds(pl.multiple_of(i * BLOCK + n * 32, 32), 32)
                xhat, _ = standardize(tok[rows, :].astype(F32))
                normed[rows, :] = (xhat * g1 + s1).astype(BF16)
                return carry
            lax.fori_loop(0, BLOCK // 32, part, 0)
        task(0.5 + NORM_TIME * i, norm_rows)

    kept = [pltpu.make_async_copy(source, goal, out_sem.at[n]) for n, (source, goal) in enumerate((
        (result, result_out), (hidden, hidden_out), (q_ref, q_out), (k_ref, k_out), (v_ref, v_out),
        (normed.at[pl.ds(HALO, own)], normed_out), (heads_t, heads_out), (gtwo, gtwo_out)))]

    def transposes():
        kept[5].start()
        cot_copy.wait()
        cot_t[...] = cot[...].T
        small[5:6, :] = jnp.sum(cot[...].astype(F32), axis=0, keepdims=True)
    task(7.6, transposes)

    half_rows = window // 2
    group = 2 * local

    def project(u, kind, part):
        rows = slice(part * half_rows, (part + 1) * half_rows)
        weight = w[pl.ds(2 * u, 2), 0, kind // 2, kind % 2].reshape(group, width)
        out = dot(normed[rows, :], weight, NT)
        if kind != 1:
            line = 1 + kind // 2
            out = out + jnp.concatenate([bias_all[2 * u, line:line + 1, :local], bias_all[2 * u + 1, line:line + 1, :local]], axis=1)
        target = (q_ref, k_ref, v_ref)[kind]
        target[rows, pl.ds(pl.multiple_of(u * group, 128), group)] = out.astype(BF16)

    def attention(u, b, only):
        first, count = BLOCK * b + 32, BLOCK + 448
        q0 = HALO + BLOCK * b
        allowed = segc[first:first + count, :] == segr[:, q0:q0 + BLOCK]
        allowed = jnp.concatenate([allowed, allowed], axis=1)

        def pair(j, carry):
            at = u * (group // 128) + j
            cols = pl.ds(pl.multiple_of(at * 128, 128), 128)
            q2 = stacked(q_ref[q0:q0 + BLOCK, cols] * SCALE)
            k2 = k_ref[first:first + count, cols]
            v2 = v_ref[first:first + count, cols]
            s = jnp.where(allowed, dot(k2, q2, NT), -1e9)
            m = jnp.max(s, axis=0, keepdims=True)
            p = jnp.exp(s - m)
            l = jnp.sum(p, axis=0, keepdims=True)
            out = dot(v2.T, p.astype(BF16), NN) * (1.0 / l)
            half = out.shape[1] // 2
            both = jnp.concatenate([out[:HEAD_DIM, :half], out[HEAD_DIM:, half:]], axis=0).astype(BF16)
            heads_t[cols, b * BLOCK:(b + 1) * BLOCK] = both
            heads[b * BLOCK:(b + 1) * BLOCK, cols] = both.T
            lse_ref[b, pl.ds(at, 1), :] = m + jnp.log(l)
            return carry
        pair(only, 0)

    def out_project(u, fresh):
        weight = w[pl.ds(2 * u, 2), 0, 1, 1].reshape(group, width)
        part = dot(heads[:, pl.ds(pl.multiple_of(u * group, 128), group)], weight, NN)
        if fresh:
            hidden[...] = part
        else:
            hidden[...] += part

    first_half = t // 2
    at = 7.0
    for n in range(nt // 2):
        u = lax.rem(first_half + n, nt // 2)
        if n == 0:
            at = max(at, ready_at[0, 0])
        else:
            at = max(at, ready_at[0, nt - 2])
        for kind in range(3):
            for part in range(2):
                def run(u=u, kind=kind, part=part):
                    project(u, kind, part)
                task(at, run)
                at += 0.7
        for b in range(blocks):
            for only in range(group // 128):
                def run(u=u, b=b, only=only):
                    attention(u, b, only)
                task(at, run)
                at += ATTEND

        def run(u=u, n=n):
            out_project(u, n == 0)
        task(at, run)
        at += 0.6

    def keep_heads():
        for n in (2, 3, 4, 6):
            kept[n].start()
    task(at, keep_heads)

    def rows_of(i):
        return slice(i * BLOCK, (i + 1) * BLOCK)

    for i in range(blocks):
        def norm_two(i=i):
            rows = rows_of(i)
            token = tok[HALO + i * BLOCK:HALO + (i + 1) * BLOCK, :].astype(F32)
            whole = hidden[rows, :] + token + ob
            hidden[rows, :] = whole
            xhat, _ = standardize(whole)
            low = (xhat * g2 + s2).astype(BF16)
            normed_two[rows, :] = low
            n2t[:, rows] = low.T
        task(at, norm_two)
        at += 0.7

    def keep_hidden():
        kept[1].start()
    task(at, keep_hidden)
    table = nearest(nt)
    slab = 32

    def grads_out(slot, shard):
        return pltpu.make_async_copy(gbuf.at[slot], grads.at[shard], gsem.at[slot])

    def mlp_steps(position):
        shard, slot = pick(table, position), position % 2

        def up():
            return w[shard, 1].reshape(width, width)

        def down():
            return w[shard, 2].reshape(width, width)

        def begin():
            pre_s[...] = dot(normed_two[...], up(), NN) + bias_all[shard, 0:1, :]

        def begin_back():
            gact_s[...] = dot(cot[...], down(), NT)

        def middle():
            def step(i, total):
                rows = pl.ds(pl.multiple_of(i * slab, slab), slab)
                value, slope = gelu_parts(pre_s[rows, :])
                act[rows, :] = value.astype(BF16)
                low = (gact_s[rows, :] * slope).astype(BF16)
                gpre[rows, :] = low
                return total + low.astype(F32)
            total = lax.fori_loop(0, own // slab, step, jnp.zeros((slab, width), F32))
            small[pl.ds(8 + shard, 1), :] = jnp.sum(total, axis=0, keepdims=True)

        def end():
            if position == 0:
                mlp[...] = dot(act[...], down(), NN)
                gtwo[...] = dot(gpre[...], up(), NT)
            else:
                mlp[...] += dot(act[...], down(), NN)
                gtwo[...] += dot(gpre[...], up(), NT)

        def grad_up():
            if position >= 2:
                grads_out(slot, shard).wait()
            gbuf[slot, 0] = dot(n2t[...], gpre[...], NN).astype(BF16).reshape(gbuf.shape[2:])

        def grad_down():
            gbuf[slot, 1] = dot(cot_t[...], act[...], NN).astype(BF16).reshape(gbuf.shape[2:])
            grads_out(slot, shard).start()
        return (begin, 0.7), (begin_back, 0.7), (middle, 1.0), (end, 1.4), (grad_up, 0.7), (grad_down, 0.7)

    for position in range(nt):
        if position > 0:
            at = max([at] + [ready_at[k, position - 1] for k in range(1, chunks)])
        for run, length in mlp_steps(position):
            task(at, run)
            at += length

    def finish():
        def part(n, carry):
            rows = pl.ds(pl.multiple_of(n * 32, 32), 32)
            result[rows, :] = (hidden[rows, :] + mlp[rows, :] + db).astype(BF16)
            return carry
        kept[7].start()
        lax.fori_loop(0, own // 32, part, 0)
        kept[0].start()
    task(at, finish)

    def keep_copy():
        return pltpu.make_async_copy(w.at[:, 0], w0, ls.at[0])

    def keep_first():
        keep_copy().start()
    task(at - 10.0, keep_first)
    ordered(tasks)
    grads_out(0, 0).wait()
    grads_out(1, 0).wait()
    keep_copy().wait()
    for copy in kept:
        copy.wait()
    for n in (0, 1, 2, 3, 4, 6, 7):
        small[n:n + 1, :] = jnp.zeros((1, width), F32)
    if small.shape[0] > 8 + nt:
        small[8 + nt:, :] = jnp.zeros((small.shape[0] - 8 - nt, width), F32)
    z_finish()
    for j in range(nt - 1):
        bias_send(j).wait_send()
    for k in range(chunks):
        for j in range(nt - 1):
            def end(shard, k, way, j):
                core(shard, k, way, j).wait_send()
                for q in (0, 1):
                    one(shard, k, q, way, j).wait_send()
                    if k < DIRECT:
                        two(shard, k, q, way, j).wait_send()
            each(k, j, end)


def forward(arrays, nt):
    length, width = arrays[0].shape
    own = length // nt
    window = own + 2 * HALO
    piece = width // 16
    unit = (2, 2, 2, 2, piece, width)
    rows = width + 2 * arrays[12].shape[0]
    chunks = rows // (16 * piece)
    lines = 8 + nt + -nt % 8
    dma = pltpu.SemaphoreType.DMA
    vmem, any_ = pl.BlockSpec(memory_space=pltpu.VMEM), pl.BlockSpec(memory_space=pl.ANY)

    def shape(dims, kind):
        return jax.ShapeDtypeStruct(dims, kind)

    def low(*dims):
        return pltpu.VMEM(dims, BF16)

    def wide(*dims):
        return pltpu.VMEM(dims, F32)
    views = list(arrays)
    for n in (7, 11, 13):
        views[n] = arrays[n].reshape(unit[2:] if n == 7 else unit)
    views[5] = arrays[5].transpose(0, 2, 1).reshape((3,) + unit[2:])
    return pl.pallas_call(
        functools.partial(forward_kernel, nt, chunks, own),
        name="forward",
        out_shape=(
            shape((own, width), BF16), shape((own, width), F32),
            shape((window, width), BF16), shape((window, width), BF16), shape((window, width), BF16),
            shape((own, width), BF16), shape((width, own), BF16), shape((own, width), F32),
            shape((own // BLOCK, 8, 2 * BLOCK), F32), shape((lines, width), F32),
            shape((nt, chunks - 1) + unit, BF16), shape((nt,) + unit, BF16),
        ),
        in_specs=[any_, any_] + [vmem] * 3 + [any_, vmem, any_] + [vmem] * 3 + [any_, vmem, any_, vmem],
        out_specs=(any_,) * 8 + (vmem, vmem, any_, any_),
        scratch_shapes=[
            low(own, width), wide(own, width), low(window, width), low(window, width), low(window, width),
            low(width, own), wide(own, width),
            low(window, width), low(own, width), pltpu.VMEM((1, length + 2 * HALO), jnp.int32),
            pltpu.VMEM((1, window), jnp.int32), pltpu.VMEM((window, BLOCK), jnp.int32), wide(8, width),
            low(window, width), low(nt, chunks, *unit), wide(nt, 8, width), dma((nt - 1,)), dma((nt - 1,)),
            low(own, width), low(own, width), low(width, own), low(width, own), wide(own, width),
            low(2, chunks - 1, *unit), wide(own, width), wide(own, width), low(own, width), low(own, width),
            dma((2,)),
            dma((2 * chunks - DIRECT, nt - 1, 2)), dma((2 * chunks - DIRECT, nt - 1, 2)),
            dma((chunks, nt - 1, 2, 4)), dma((chunks, nt - 1, 2, 4)),
            dma((chunks, nt - 1, 2)), dma((chunks, nt - 1, 2)), dma((8,)), dma((8,)),
        ],
        compiler_params=pltpu.CompilerParams(
            collective_id=1, has_side_effects=True, vmem_limit_bytes=VMEM_LIMIT),
    )(*views)


PIECES = 3
OWN_TIME, SIDE_TIME = 1.4, 1.4
PACE, STEPS, HOP = 4.5, (2.2, 7.5, 14.4), 7.6


def backward_kernel(nt, chunks, extra,
                    lse_ref, small1, segments, gain_1, gain_2,
                    cotangent, tokens_in, grads, w0, result, hidden_in, q_in, k_in, v_in, normed_in, heads_in, gtwo_in,
                    total_out, small, result_all, input_grad_all, total, gathered_r, gathered_g,
                    hidden, q_ref, k_ref, v_ref, normed, heads_t, gtwo,
                    s1, rc, ra, rb, rz, rx, rt, sr, g0, w_first, token, cot, segp, segr, segc, branch, g_ref, stats,
                    halo_g, halo_s, dk, dv, dq, d_t, gtwo_out, own_ig,
                    ls, cs, cr, ps, pr, zs, zr, xs, xr, fs, fr, os_, or_, ss, sm, hs, hr, lo, in_sem, leave_sem):
    d, t, b0, b1, b2 = place()
    own, width = hidden.shape
    blocks = own // BLOCK
    gathered = (gathered_r, gathered_g)
    bits = (1, 2, 4) + tuple(extra)
    order = tuple(range(chunks))[::-1]
    units = [(k, s) for k in order for s in range(nt)]

    def own_copy(k, s):
        return pltpu.make_async_copy(grads.at[s, k - 1, b0], s1.at[s, k], ls.at[s, k])

    arrivals = [pltpu.make_async_copy(source, goal, in_sem.at[n]) for n, (source, goal) in enumerate((
        (hidden_in, hidden), (gtwo_in, gtwo), (heads_in, heads_t), (q_in, q_ref), (k_in, k_ref), (v_in, v_ref),
        (normed_in, normed), (result, gathered_r.at[t])))]
    fetch_w = pltpu.make_async_copy(w0, w_first, lo.at[0])
    mine = pl.ds(pl.multiple_of(t * own, own), own)
    fetch_t = pltpu.make_async_copy(tokens_in.at[mine], token, lo.at[1])
    fetch_t.start()
    fetch_c = pltpu.make_async_copy(cotangent.at[mine], cot, lo.at[2])
    fetch_c.start()
    for copy in arrivals[:3]:
        copy.start()
    fetch_w.start()
    for copy in arrivals[3:]:
        copy.start()
    for k, s in units:
        if k > 0:
            own_copy(k, s).start()
    window_segments(segments, segp, segr, segc)
    greet(nt, bits, nt > 2)
    tasks = []

    def task(when, body):
        tasks.append((when, len(tasks), body))

    def leave(n):
        source, goal = ((gathered_r, result_all), (gathered_g, input_grad_all))[n] if n < 5 else (total.at[n - 5], total_out.at[n - 5])
        return pltpu.make_async_copy(source, goal, leave_sem.at[n])

    def core(k, s):
        source = g0.at[s, 1 - b0] if k == 0 else grads.at[s, k - 1, 1 - b0]
        return remote(source, rc.at[s, k], cs.at[s, k], cr.at[s, k], dp=flip(d, 1))

    def one(k, s, q):
        if q == 0:
            return remote(s1.at[s, k, 1 - b2, :, 0], ra.at[s, k], ps.at[s, k, 0], pr.at[s, k, 0], dp=flip(d, 4))
        return remote(s1.at[s, k, :, 1 - b1, 1], rb.at[s, k], ps.at[s, k, 1], pr.at[s, k, 1], dp=flip(d, 2))

    def two(k, s, q):
        if q == 0:
            return remote(s1.at[s, k, b2, 1 - b1, 0], rz.at[s, k, 0], ps.at[s, k, 2], pr.at[s, k, 2], dp=flip(d, 2))
        return remote(s1.at[s, k, 1 - b2, b1, 1], rz.at[s, k, 1], ps.at[s, k, 3], pr.at[s, k, 3], dp=flip(d, 4))

    def up(k, s):
        return remote(s1.at[s, k, b2, b1], rx.at[s, k], zs.at[s, k, 0], zr.at[s, k, 0], tensor=t + 1)

    def down(k, s, last):
        goal = rt.at[k] if last else rx.at[s, k]
        return remote(s1.at[s, k, b2, b1], goal, zs.at[s, k, 1], zr.at[s, k, 1], tensor=t - 1)

    def halo(n):
        if n == 0:
            return remote(g_ref.at[pl.ds(own - REACH, REACH)], halo_g.at[0, pl.ds(HALO - REACH, REACH)],
                          hs.at[0], hr.at[0], tensor=t + 1)
        if n == 1:
            return remote(g_ref.at[pl.ds(0, REACH)], halo_g.at[1, pl.ds(0, REACH)], hs.at[1], hr.at[1], tensor=t - 1)
        span = HALO // BLOCK
        if n == 2:
            return remote(stats.at[pl.ds(blocks - span, span)], halo_s.at[0], hs.at[2], hr.at[2], tensor=t + 1)
        return remote(stats.at[pl.ds(0, span)], halo_s.at[1], hs.at[3], hr.at[3], tensor=t - 1)

    def halo_start():
        @pl.when(t < nt - 1)
        def _():
            halo(0).start()
            halo(2).start()

        @pl.when(t > 0)
        def _():
            halo(1).start()
            halo(3).start()
        pad = HALO - REACH
        halo_g[0, 0:pad, :] = jnp.zeros((pad, width), BF16)
        halo_g[1, REACH:HALO, :] = jnp.zeros((pad, width), BF16)

        @pl.when(t == 0)
        def _():
            halo_g[0] = jnp.zeros((HALO, width), BF16)
            halo_s[0] = jnp.zeros(halo_s.shape[1:], F32)

        @pl.when(t == nt - 1)
        def _():
            halo_g[1] = jnp.zeros((HALO, width), BF16)
            halo_s[1] = jnp.zeros(halo_s.shape[1:], F32)

    def halo_end():
        @pl.when(t > 0)
        def _():
            halo(0).wait_recv()
            halo(2).wait_recv()

        @pl.when(t < nt - 1)
        def _():
            halo(1).wait_recv()
            halo(3).wait_recv()

    def attend_block(w, cols, row):
        q0 = w * BLOCK
        middle = HALO // BLOCK <= w < HALO // BLOCK + blocks
        k0, k1 = max(0, q0 - REACH), q0 + BLOCK + REACH
        if not middle:
            k0, k1 = max(k0, HALO), min(k1, HALO + own)
        q2 = stacked(q_ref[q0:q0 + BLOCK, cols] * SCALE)
        if middle:
            i = w - HALO // BLOCK
            g_rows = g_ref[i * BLOCK:(i + 1) * BLOCK, cols]
            lse, delta = stats[i, pl.ds(row, 1), :], stats[i, pl.ds(8 + row, 1), :]
        else:
            side = int(w > HALO // BLOCK)
            i = w if side == 0 else w - HALO // BLOCK - blocks
            g_rows = halo_g[side, i * BLOCK:(i + 1) * BLOCK, cols]
            lse, delta = halo_s[side, i, pl.ds(row, 1), :], halo_s[side, i, pl.ds(8 + row, 1), :]
        g2 = stacked(g_rows)
        k2, v2 = k_ref[k0:k1, cols], v_ref[k0:k1, cols]
        allowed = segc[k0:k1, :] == segr[:, q0:q0 + BLOCK]
        allowed = jnp.concatenate([allowed, allowed], axis=1)
        s = dot(k2, q2, NT)
        p = jnp.exp(jnp.where(allowed, s - lse, -1e9))
        low = p.astype(BF16)
        ds = (p * (dot(v2, g2, NT) - delta)).astype(BF16)
        o0, o1 = max(k0, HALO), min(k1, HALO + own)
        dst, src = slice(o0 - HALO, o1 - HALO), slice(o0 - k0, o1 - k0)
        dk[dst, cols] += dot(ds[src], q2, NN)
        dv[dst, cols] += dot(low[src], g2, NN)
        if middle:
            out = dot(k2.T, ds, NN) * SCALE
            half = out.shape[1] // 2
            both = jnp.concatenate([out[:HEAD_DIM, :half], out[HEAD_DIM:, half:]], axis=0).astype(BF16)
            d_t[0, cols, i * BLOCK:(i + 1) * BLOCK] = both
            dq[0, i * BLOCK:(i + 1) * BLOCK, cols] = both.T

    def attention(first, count, mine):
        def pair(j, carry):
            cols = pl.ds(pl.multiple_of(j * 128, 128), 128)
            if mine:
                dk[:, cols] = jnp.zeros((own, 128), F32)
                dv[:, cols] = jnp.zeros((own, 128), F32)
                for b in range(blocks):
                    attend_block(HALO // BLOCK + b, cols, j)
            else:
                for w in tuple(range(HALO // BLOCK)) + tuple(range(HALO // BLOCK + blocks, 2 * HALO // BLOCK + blocks)):
                    attend_block(w, cols, j)
                for n, ref in enumerate((dk, dv)):
                    value = ref[:, cols].astype(BF16)
                    dq[1 + n, :, cols] = value
                    d_t[1 + n, cols, :] = value.T
            return carry
        for j in range(first, first + count):
            pair(j, 0)

    g1, g2 = gain_1[...].reshape(1, width), gain_2[...].reshape(1, width)

    def norm_two_back():
        fetch_c.wait()
        arrivals[0].wait()
        arrivals[1].wait()

        def part(n, carry):
            rows = pl.ds(pl.multiple_of(n * 32, 32), 32)
            xhat, r = standardize(hidden[rows, :])
            grad = gtwo[rows, :]
            gh = cot[rows, :].astype(F32) + norm_back(grad * g2, xhat, r)
            gtwo_out[rows, :] = gh
            branch[rows, :] = gh.astype(BF16)
            return carry[0] + gh, carry[1] + grad * xhat, carry[2] + grad
        zero = jnp.zeros((32, width), F32)
        sums = lax.fori_loop(0, own // 32, part, (zero, zero, zero))
        small[...] = small1[...]
        for line, value in zip((2, 3, 4), sums):
            small[line:line + 1, :] = jnp.sum(value, axis=0, keepdims=True)

    def out_back():
        fetch_w.wait()
        arrivals[2].wait()
        outw = w_first[:, 1, 1].reshape(width, width)
        rows = branch[...]
        g_ref[...] = dot(rows, outw, NT).astype(BF16)
        g_t = dot(outw, rows, NT).astype(BF16).astype(F32)
        product = g_t * heads_t[...].astype(F32)
        for b in range(blocks):
            stats[b, 0:8, :] = lse_ref[b]
            for h in range(width // HEAD_DIM):
                line = jnp.sum(product[h * HEAD_DIM:(h + 1) * HEAD_DIM, b * BLOCK:(b + 1) * BLOCK], axis=0, keepdims=True)
                stats[b, 8 + h // 2:9 + h // 2, (h % 2) * BLOCK:(h % 2 + 1) * BLOCK] = line
            stats[b, 8 + width // 128:16, :] = jnp.zeros((8 - width // 128, 2 * BLOCK), F32)

    def out_grad():
        value = dot(heads_t[...], branch[...], NN).astype(BF16)
        g0[:, 1, 1] = value.reshape((nt,) + g0.shape[3:])
    task(0.3, norm_two_back)
    task(3.0, out_back)
    task(5.5, halo_start)
    task(6.0, out_grad)
    at = 7.0
    pairs = width // 128

    def attend_ready():
        for copy in arrivals[3:]:
            copy.wait()
    task(at, attend_ready)
    for first in range(pairs):
        def run(first=first):
            attention(first, 1, True)
        task(at, run)
        at += OWN_TIME
    at = max(at, 18.4)
    task(at, halo_end)
    for first in range(pairs):
        def run(first=first):
            attention(first, 1, False)
        task(at, run)
        at += SIDE_TIME

    def weight_of(kind):
        return w_first[:, kind // 2, kind % 2].reshape(width, width)

    def back_project():
        dk[...] = dot(dq[0], weight_of(0), NN)
        dk[...] += dot(dq[1], weight_of(1), NN)
        dk[...] += dot(dq[2], weight_of(2), NN)
    task(at, back_project)
    at += 2.5

    def norm_one():
        fetch_t.wait()

        def part(n, carry):
            rows = pl.ds(pl.multiple_of(n * 32, 32), 32)
            xhat, r = standardize(token[rows, :].astype(F32))
            grad = dk[rows, :]
            own_ig[rows, :] = (gtwo_out[rows, :] + norm_back(grad * g1, xhat, r)).astype(BF16)
            return (carry[0] + grad * xhat, carry[1] + grad, carry[2] + dq[0, rows, :].astype(F32),
                    carry[3] + dq[2, rows, :].astype(F32))
        zero = jnp.zeros((32, width), F32)
        sums = lax.fori_loop(0, own // 32, part, (zero, zero, zero, zero))
        for line, value in zip((0, 1, 6, 7), sums):
            small[line:line + 1, :] = jnp.sum(value, axis=0, keepdims=True)
        gathered_g[t] = own_ig[...]
    task(at, norm_one)
    at += 3.0
    ready = at
    for kind in range(3):
        def run(kind=kind):
            value = dot(d_t[kind], normed[...], NN).astype(BF16)
            g0[:, kind // 2, kind % 2] = value.reshape((nt,) + g0.shape[3:])
        task(at, run)
        at += 1.2

    late = at

    pace = PACE
    for n, (k, s) in enumerate(units):
        base = n * pace if k > 0 else max(n * pace, late + 0.4 + (n - nt * (chunks - 1)) * pace)

        def first(k=k, s=s):
            core(k, s).start()

        def second(k=k, s=s):
            core(k, s).wait_recv()
            if k > 0:
                own_copy(k, s).wait()
                add_bf16(s1.at[s, k], rc.at[s, k])
            else:
                s1[s, k] = (g0[s, b0].astype(F32) + rc[s, k].astype(F32)).astype(BF16)
            one(k, s, 0).start()
            one(k, s, 1).start()

        def third(k=k, s=s):
            one(k, s, 0).wait_recv()
            one(k, s, 1).wait_recv()
            add_bf16(s1.at[s, k, b2, :, 0], ra.at[s, k])
            add_bf16(s1.at[s, k, :, b1, 1], rb.at[s, k])
            two(k, s, 0).start()
            two(k, s, 1).start()

        def fourth(k=k, s=s):
            two(k, s, 0).wait_recv()
            two(k, s, 1).wait_recv()
            add_bf16(s1.at[s, k, b2, b1, 0], rz.at[s, k, 0])
            add_bf16(s1.at[s, k, b2, b1, 1], rz.at[s, k, 1])
        task(max(base - 8.1, -10.0) if k > 0 else max(base - 12.0, late + 0.01), first)
        task(base + STEPS[0], second)
        task(base + STEPS[1], third)
        task(base + STEPS[2], fourth)
        if s == nt - 1:
            end_of_chunk = base + STEPS[2]
        else:
            continue

        for hop in range(nt):
            def chain(k=k, hop=hop):
                @pl.when(t == hop)
                def _():
                    for s in reversed(range(nt)):
                        @pl.when(s >= t)
                        def _():
                            if hop > 0:
                                up(k, s).wait_recv()
                                add_bf16(s1.at[s, k, b2, b1], rx.at[s, k])
                            if hop < nt - 1:
                                @pl.when(s > t)
                                def _():
                                    up(k, s).start()

                @pl.when(t == nt - 1 - hop)
                def _():
                    for s in range(nt):
                        if hop > 0:
                            @pl.when(s < t)
                            def _():
                                down(k, s, False).wait_recv()
                                add_bf16(s1.at[s, k, b2, b1], rx.at[s, k])

                            @pl.when(s == t)
                            def _():
                                down(k, s, True).wait_recv()
                                add_bf16(s1.at[s, k, b2, b1], rt.at[k])
                        if hop < nt - 1:
                            @pl.when(s == t - 1)
                            def _():
                                down(k, s, True).start()

                            @pl.when(s < t - 1)
                            def _():
                                down(k, s, False).start()
            task(end_of_chunk + 0.5 + HOP * hop, chain)
        base = end_of_chunk + 0.5 + HOP * nt + -5.8

        for e, bit in enumerate(extra):
            def more(k=k, e=e, bit=bit):
                swap = remote(s1.at[t, k, b2, b1], rx.at[nt + e, k], xs.at[e, k], xr.at[e, k], dp=flip(d, bit))
                swap.start()
                swap.wait()
                add_bf16(s1.at[t, k, b2, b1], rx.at[nt + e, k])
            task(base + 0.01 * e, more)

        def settle(k=k):
            total[k, b0, b2, b1] = s1[t, k, b2, b1]

        def give_one(k, q):
            if q == 0:
                piece = total.at[k, b0, b2, b1, 0]
                return remote(piece, piece, fs.at[k, 0], fr.at[k, 0], dp=flip(d, 2))
            piece = total.at[k, b0, b2, b1, 1]
            return remote(piece, piece, fs.at[k, 1], fr.at[k, 1], dp=flip(d, 4))

        def give_two(k, q):
            if q == 0:
                piece = total.at[k, b0, b2, :, 0]
                return remote(piece, piece, fs.at[k, 2], fr.at[k, 2], dp=flip(d, 4))
            piece = total.at[k, b0, :, b1, 1]
            return remote(piece, piece, fs.at[k, 3], fr.at[k, 3], dp=flip(d, 2))

        def give_core(k):
            return remote(total.at[k, b0], total.at[k, b0], fs.at[k, 4], fr.at[k, 4], dp=flip(d, 1))

        def spread_one(k=k):
            for q in (0, 1):
                give_one(k, q).start()

        def spread_two(k=k):
            for q in (0, 1):
                give_one(k, q).wait_recv()
            for q in (0, 1):
                give_two(k, q).start()

        def spread_core(k=k):
            for q in (0, 1):
                give_two(k, q).wait_recv()
            give_core(k).start()

        def spread_end(k=k):
            give_core(k).wait()
            leave(5 + k).start()
            for q in (0, 1):
                give_one(k, q).wait_send()
                give_two(k, q).wait_send()
        task(base + 0.5, settle)
        task(base + 3.9, spread_one)
        task(base + 5.3, spread_two)
        task(base + 13.3, spread_core)
        task(1e6 if k == order[-1] else base + 16.0, spread_end)

    part = own // PIECES

    def piece_of(ref, n):
        return ref.at[pl.ds(n % PIECES * part, part)]
    z_tasks, z_finish = relay_tasks(
        nt, 2 * PIECES, lambda n: piece_of((result, own_ig)[n // PIECES], n),
        lambda s, n: piece_of(gathered[n // PIECES].at[s], n), (os_, or_),
        lambda n, j: (-5.0, ready)[n // PIECES] + 20.4 / PIECES * (n % PIECES) + 20.4 * j + (0.01 if j == 0 else 0.1),
        lambda *a: None)
    tasks += [(w, 1000 + n, b) for w, n, b in z_tasks]

    def result_done():
        leave(0).start()
    task(max(w for w, n, b in z_tasks[:PIECES * nt]) + 0.1, result_done)

    exchanges = [("dp", bit) for bit in bits]
    step = 1
    while step < nt:
        exchanges.append(("tensor", step))
        step *= 2
    for e, (axis, bit) in enumerate(exchanges):
        def swap(e=e, axis=axis, bit=bit):
            goal = {axis: flip(lax.axis_index(axis), bit)}
            return remote(small, sr.at[e], ss.at[e], sm.at[e], **goal)

        def begin(swap=swap):
            swap().start()

        def end(e=e, swap=swap):
            swap().wait()
            small[...] = small[...] + sr[e]
        task(late + 21.1 + 9.9 * e, begin)
        task(late + 29.9 + 9.9 * e, end)

    ordered(tasks)
    leave(1).start()
    z_finish()
    for n in (0, 1) + tuple(5 + k for k in order):
        leave(n).wait()

    @pl.when(t < nt - 1)
    def _():
        halo(0).wait_send()
        halo(2).wait_send()

    @pl.when(t > 0)
    def _():
        halo(1).wait_send()
        halo(3).wait_send()
    for k, s in units:
        core(k, s).wait_send()
        for q in (0, 1):
            one(k, s, q).wait_send()
            two(k, s, q).wait_send()

        @pl.when(s > t)
        def _():
            up(k, s).wait_send()

        @pl.when(s < t)
        def _():
            down(k, s, False).wait_send()


def backward(vmem_arrays, hbm_arrays, nt, extra):
    own, width = hbm_arrays[4].shape
    grads, segments = hbm_arrays[2], vmem_arrays[2]
    small_shape = vmem_arrays[1].shape
    piece, chunks = width // 16, grads.shape[1] + 1
    window = own + 2 * HALO
    dma = pltpu.SemaphoreType.DMA
    hops = 3 + len(extra) + (nt - 1).bit_length()
    vmem, any_ = pl.BlockSpec(memory_space=pltpu.VMEM), pl.BlockSpec(memory_space=pl.ANY)
    unit = (2, 2, 2, piece, width)
    blocks = own // BLOCK

    def low(*dims):
        return pltpu.VMEM(dims, BF16)

    def wide(*dims):
        return pltpu.VMEM(dims, F32)
    return pl.pallas_call(
        functools.partial(backward_kernel, nt, chunks, extra),
        name="backward",
        out_shape=(
            jax.ShapeDtypeStruct((chunks, 2) + unit, BF16),
            jax.ShapeDtypeStruct(small_shape, F32),
            jax.ShapeDtypeStruct((nt, own, width), BF16),
            jax.ShapeDtypeStruct((nt, own, width), BF16),
        ),
        in_specs=[vmem] * len(vmem_arrays) + [any_] * len(hbm_arrays),
        out_specs=(any_, vmem, any_, any_),
        scratch_shapes=[
            low(chunks, 2, *unit), low(nt, own, width), low(nt, own, width),
            wide(own, width), low(window, width), low(window, width), low(window, width), low(own, width),
            low(width, own), wide(own, width),
            low(nt, chunks, *unit), low(nt, chunks, *unit),
            low(nt, chunks, 2, piece, width), low(nt, chunks, 2, piece, width), low(nt, chunks, 2, piece, width),
            low(nt + len(extra), chunks, 2, piece, width), low(chunks, 2, piece, width),
            wide(hops, *small_shape), low(nt, 2, *unit), low(nt, 2, *unit),
            low(own, width), low(own, width), pltpu.VMEM((1, segments.shape[1] + 2 * HALO), jnp.int32),
            pltpu.VMEM((1, window), jnp.int32), pltpu.VMEM((window, BLOCK), jnp.int32),
            low(own, width), low(own, width), wide(blocks, 16, 2 * BLOCK),
            low(2, HALO, width), wide(2, HALO // BLOCK, 16, 2 * BLOCK),
            wide(own, width), wide(own, width), low(3, own, width), low(3, width, own),
            wide(own, width), low(own, width),
            dma((nt, chunks)), dma((nt, chunks)), dma((nt, chunks)),
            dma((nt, chunks, 4)), dma((nt, chunks, 4)),
            dma((nt, chunks, 2)), dma((nt, chunks, 2)),
            dma((max(1, len(extra)), chunks)), dma((max(1, len(extra)), chunks)),
            dma((chunks, 5)), dma((chunks, 5)),
            dma((2 * PIECES, nt - 1, 2)), dma((2 * PIECES, nt - 1, 2)),
            dma((hops,)), dma((hops,)), dma((4,)), dma((4,)), dma((3,)), dma((8,)), dma((5 + chunks,)),
        ],
        compiler_params=pltpu.CompilerParams(
            collective_id=2, has_side_effects=True, vmem_limit_bytes=VMEM_LIMIT),
    )(*vmem_arrays, *hbm_arrays)


def finish_kernel(nt, ndp, total_in, small, results, input_grads,
                  results_out, input_grads_out, g1, s1, qkv, qvb, out_w, out_b, g2, s2, up, up_b, down, down_b,
                  total, held, first, second, third, in_sem, out_sem):
    t = lax.axis_index("tensor")
    width = small.shape[1]
    local = width // nt
    scale = 1.0 / ndp
    parts = [pltpu.make_async_copy(total_in.at[k], total.at[k], in_sem.at[k]) for k in range(3)]
    for k in (1, 2, 0):
        parts[k].start()
    stage = [pltpu.make_async_copy(results, held.at[0], in_sem.at[3]), pltpu.make_async_copy(input_grads, held.at[1], in_sem.at[4])]
    for copy in stage:
        copy.start()
    moves = []
    for ref, line in ((g1, 0), (s1, 1), (out_b, 2), (g2, 3), (s2, 4), (down_b, 5)):
        ref[...] = small[line:line + 1, :].reshape(width) * scale
    up_b[...] = small[pl.ds(8 + t, 1), :].reshape(width) * scale
    for place in range(nt):
        @pl.when(t == place)
        def _():
            qvb[...] = small[6:8, place * local:(place + 1) * local] * scale
    for n, goal in enumerate((results_out, input_grads_out)):
        stage[n].wait()
        moves.append(pltpu.make_async_copy(held.at[n], goal, out_sem.at[n]))
        moves[-1].start()
    parts[1].wait()
    second[...] = total[1].reshape(width, width).astype(F32) * scale
    moves.append(pltpu.make_async_copy(second, up, out_sem.at[2]))
    moves[-1].start()
    parts[2].wait()
    third[...] = (total[2].reshape(width, width).astype(F32) * scale).T
    moves.append(pltpu.make_async_copy(third, down, out_sem.at[3]))
    moves[-1].start()
    parts[0].wait()
    first[...] = total[0].reshape(nt, local, width).astype(F32) * scale
    moves.append(pltpu.make_async_copy(first.at[pl.ds(0, 3)], qkv, out_sem.at[4]))
    moves[-1].start()
    moves.append(pltpu.make_async_copy(first.at[3], out_w, out_sem.at[5]))
    moves[-1].start()
    for copy in moves:
        copy.wait()


def finish_up(total, small, results, input_grads, nt, ndp):
    width = small.shape[1]
    local = width // nt
    dma = pltpu.SemaphoreType.DMA
    vmem, any_ = pl.BlockSpec(memory_space=pltpu.VMEM), pl.BlockSpec(memory_space=pl.ANY)

    def shape(*dims):
        return jax.ShapeDtypeStruct(dims, F32)
    return pl.pallas_call(
        functools.partial(finish_kernel, nt, ndp),
        name="finish",
        out_shape=(jax.ShapeDtypeStruct(results.shape, BF16), jax.ShapeDtypeStruct(results.shape, BF16),
                   shape(width), shape(width), shape(3, local, width), shape(2, local), shape(local, width), shape(width),
                   shape(width), shape(width), shape(width, width), shape(width), shape(width, width), shape(width)),
        in_specs=[any_, vmem, any_, any_],
        out_specs=(any_, any_, vmem, vmem, any_, vmem, any_, vmem, vmem, vmem, any_, vmem, any_, vmem),
        scratch_shapes=[pltpu.VMEM(total.shape, BF16), pltpu.VMEM((2,) + results.shape, BF16), pltpu.VMEM((nt, local, width), F32),
                        pltpu.VMEM((width, width), F32), pltpu.VMEM((width, width), F32), dma((5,)), dma((6,))],
        compiler_params=pltpu.CompilerParams(vmem_limit_bytes=VMEM_LIMIT),
    )(total, small, results, input_grads)


def body(tokens_in, segment_ids, first_gain, first_shift, qkv_weight, query_value_bias, out_weight, out_bias,
         second_gain, second_shift, up_weight, up_bias, down_weight, down_bias, cotangent):
    nt, ndp = lax.axis_size("tensor"), lax.axis_size("dp")
    length, width = tokens_in.shape
    (result, hidden, q, k, v, normed, heads_t, grad_two, lse, small, mlp_grads, w_first) = forward(
        (tokens_in, cotangent, segment_ids, first_gain, first_shift, qkv_weight, query_value_bias, out_weight, out_bias,
         second_gain, second_shift, up_weight, up_bias, down_weight, down_bias), nt)
    extra = []
    bit = 8
    while bit < ndp:
        extra.append(bit)
        bit *= 2
    total, small, results, input_grads = backward(
        (lse, small, segment_ids, first_gain, second_gain),
        (cotangent, tokens_in, mlp_grads, w_first, result, hidden, q, k, v, normed, heads_t, grad_two), nt, tuple(extra))
    outs = list(finish_up(total, small, results, input_grads, nt, ndp))
    outs[0], outs[1] = outs[0].reshape(length, width), outs[1].reshape(length, width)
    outs[4] = outs[4].transpose(0, 2, 1)
    return tuple(outs)


def solution(mesh):
    placed = (
        P("dp", None), P("dp", None), P(), P(), P(None, None, "tensor"), P(None, "tensor"), P("tensor", None), P(),
        P(), P(), P(None, "tensor"), P("tensor"), P("tensor", None), P(), P("dp", None),
    )
    return jax.shard_map(
        body,
        mesh=mesh,
        in_specs=placed,
        out_specs=(
            P("dp", None), P("dp", None), P(), P(), P(None, None, "tensor"), P(None, "tensor"), P("tensor", None),
            P(), P(), P(), P(None, "tensor"), P("tensor"), P("tensor", None), P(),
        ),
        check_vma=False,
    )
```
